32 devices in a mesh: ctx: 16 (over z, y, core), fsdp: 2 (over x).
Axes of the slice: x: 2, y: 2, z: 4, core: 2. Of those that a mesh axis runs over, the one named last changes fastest.
Arguments:
- tokens: bfloat16 [4096, 768], P(('fsdp', 'ctx')), may hold values from -6 to 6
- encoded: bfloat16 [4096, 768], P(('fsdp', 'ctx')), may hold values from -6 to 6
- cotangent: bfloat16 [4096, 768], P(('fsdp', 'ctx')), may hold values from -6 to 6
- tgt_lengths: int32 [2, 6], P('fsdp'), may hold values from 1 to 1984, 2048 in all within a row
- enc_lengths: int32 [2, 6], P('fsdp'), may hold values from 1 to 1984, 2048 in all within a row
- deal: int32 [2, 6], P('fsdp'), may hold values from 0 to 5, each once within a row
- ln_self: float32 [768], P('fsdp'), may hold values from 0.1 to 1.9
- ln_cross: float32 [768], P('fsdp'), may hold values from 0.1 to 1.9
- ln_ffn: float32 [768], P('fsdp'), may hold values from 0.1 to 1.9
- bias_table: float32 [32, 12], P('fsdp'), may hold values from -4 to 4
- self_query: float32 [768, 768], P('fsdp'), may hold values from -0.0546875 to 0.0546875
- self_key: float32 [768, 768], P('fsdp'), may hold values from -0.21875 to 0.21875
- self_value: float32 [768, 768], P('fsdp'), may hold values from -0.21875 to 0.21875
- self_output: float32 [768, 768], P('fsdp'), may hold values from -1.25 to 1.25
- cross_query: float32 [768, 768], P('fsdp'), may hold values from -0.0546875 to 0.0546875
- cross_key: float32 [768, 768], P('fsdp'), may hold values from -0.21875 to 0.21875
- cross_value: float32 [768, 768], P('fsdp'), may hold values from -0.21875 to 0.21875
- cross_output: float32 [768, 768], P('fsdp'), may hold values from -1.25 to 1.25
- ffn_inner: float32 [768, 3072], P('fsdp'), may hold values from -0.21875 to 0.21875
- ffn_outer: float32 [3072, 768], P('fsdp'), may hold values from -0.109375 to 0.109375
Outputs:
- output: float32 [4096, 768], P(('fsdp', 'ctx'))
- tokens_grad: float32 [4096, 768], P(('fsdp', 'ctx'))
- encoded_grad: float32 [4096, 768], P(('fsdp', 'ctx'))
- ln_self_grad: float32 [768], P('fsdp')
- ln_cross_grad: float32 [768], P('fsdp')
- ln_ffn_grad: float32 [768], P('fsdp')
- bias_table_grad: float32 [32, 12], P('fsdp')
- self_query_grad: float32 [768, 768], P('fsdp')
- self_key_grad: float32 [768, 768], P('fsdp')
- self_value_grad: float32 [768, 768], P('fsdp')
- self_output_grad: float32 [768, 768], P('fsdp')
- cross_query_grad: float32 [768, 768], P('fsdp')
- cross_key_grad: float32 [768, 768], P('fsdp')
- cross_value_grad: float32 [768, 768], P('fsdp')
- cross_output_grad: float32 [768, 768], P('fsdp')
- ffn_inner_grad: float32 [768, 3072], P('fsdp')
- ffn_outer_grad: float32 [3072, 768], P('fsdp')
The draws below stay inside these ranges and needn't reach their ends.
Inputs may be any that keep to these rules, and one draw needn't show every extreme that they name: `tgt_lengths`: each row holds the lengths of the 6 target sequences of one group in packed order, summing to 2048; the longest is exactly 1984. `enc_lengths`: each row holds the lengths of the 6 encoder sequences of one group in packed order, summing to 2048; the longest is exactly 1984. `deal`: each row is a permutation of the 6 encoder sequences of the group.
All inputs are finite; a program needn't handle non-finite values.
Results may differ from the reference program's by a relative error of at most 0.03.
The reference program's roundings to bfloat16 on the way count: a program that leaves them out, or rounds other values in their place, can miss the bound.
Values may be sent and summed in bfloat16 or wider, within the bound.
No kernel may reach another device: no remote copies, remote signals or barrier semaphores. Data moves between devices by JAX's collectives and lax.ppermute only.
A program may use at most 192 MiB of HBM per device.

```python
import math
import jax
import jax.numpy as jnp
import numpy as np
from jax import lax

D = 768
HEADS = 12
HEAD_DIM = 64
FF = 3072
BUCKETS = 32
TOK_DEV = 128
ENC_DEV = 128
NSEQ = 6
GROUP = 2048
ENC_GROUP = 2048
MAXLEN = 1984
ENC_MAX = 1984
TOKENS = 4096
ENC_TOKENS = 4096
N_CTX = 16
N_FSDP = 2


def level_of(own_key, shape, cuts, least, high):
    def one(axis_at, parts):
        heights = jax.random.uniform(jax.random.fold_in(jax.random.fold_in(own_key, 6), axis_at), (parts,), jnp.float32, least / len(cuts), high / len(cuts))
        return jnp.repeat(jnp.exp(heights), shape[axis_at] // parts).reshape((-1,) + (1,) * (len(shape) - axis_at - 1))

    loudness = one(*cuts[0])
    for cut in cuts[1:]:
        loudness = loudness * one(*cut)
    return loudness


def split_up(amount, total, bound, slope):
    portions = [(1 << 20) // math.isqrt(rank ** slope) + 1 for rank in range(2, amount + 1)]
    rest, holding = total - bound - (amount - 1), [1] * (amount - 1)
    while rest > 0:
        candidates = [i for i in range(amount - 1) if holding[i] < bound]
        pool, left = sum([portions[i] for i in candidates]), rest
        for i in candidates:
            addition = min(bound - holding[i], max(1, left * portions[i] // pool), rest)
            holding[i] = holding[i] + addition
            rest = rest - addition
    return np.array([bound] + holding)


def ragged(key, number_of, total, bound, slope):
    if number_of == 2:
        one = jax.random.randint(key, (), max(1, total - bound), min(bound, total - 1) + 1)
        return jnp.stack([one, total - one])
    tallies = jnp.asarray(split_up(number_of, total, bound, slope), jnp.int32)
    twos = (number_of - 1) // 2
    donor, sink = tallies[1:1 + 2 * twos:2], tallies[2:2 + 2 * twos:2]
    margin = jnp.minimum(donor - 1, bound - sink)
    shifted = jax.random.randint(jax.random.fold_in(key, 1), (twos,), 0, 1 << 20) % (margin + 1)
    tallies = tallies.at[1:1 + 2 * twos:2].set(donor - shifted).at[2:2 + 2 * twos:2].set(sink + shifted)
    return tallies[jax.random.permutation(jax.random.fold_in(key, 2), number_of)]


def centred(rng, dims, width, most, cuts=(), kind=jnp.bfloat16):
    factor_of = level_of(rng, dims, cuts, -0.22, 0.18) if cuts else 1.0
    drawn = jax.random.normal(rng, dims, jnp.float32) * width * factor_of
    return jnp.minimum(jnp.maximum(drawn, -most), most).astype(kind)


def setup_inputs(seed: int = 0) -> dict:
    streams_of = jax.random.split(jax.random.key(seed), 21)
    tokens = centred(streams_of[0], (TOKENS, D), 1.0, 6.0, ((0, 32),))
    encoded = centred(streams_of[1], (ENC_TOKENS, D), 1.0, 6.0, ((0, 32),))
    cotangent = centred(streams_of[2], (TOKENS, D), 1.0, 6.0, ((0, 32),))
    tgt_lengths = jax.vmap(lambda own: ragged(own, NSEQ, GROUP, MAXLEN, 2))(jax.random.split(streams_of[3], N_FSDP)).reshape((N_FSDP, NSEQ)).astype(jnp.int32)
    enc_lengths = jax.vmap(lambda own: ragged(own, NSEQ, ENC_GROUP, ENC_MAX, 2))(jax.random.split(streams_of[4], N_FSDP)).reshape((N_FSDP, NSEQ)).astype(jnp.int32)
    deal = jax.vmap(lambda own: jax.random.permutation(own, NSEQ))(jax.random.split(streams_of[5], N_FSDP)).reshape((N_FSDP, NSEQ)).astype(jnp.int32)
    ln_self = jnp.clip(1.0 + 0.18 * jax.random.normal(streams_of[6], (D,), jnp.float32), 0.1, 1.9)
    ln_cross = jnp.clip(1.0 + 0.18 * jax.random.normal(streams_of[7], (D,), jnp.float32), 0.1, 1.9)
    ln_ffn = jnp.clip(1.0 + 0.18 * jax.random.normal(streams_of[8], (D,), jnp.float32), 0.1, 1.9)
    bias_table = centred(streams_of[9], (BUCKETS, HEADS), 1.0, 4.0, ((0, 2),), jnp.float32)
    self_query = centred(streams_of[10], (D, D), (16 * D) ** -0.5, 0.0546875, ((0, 2),), jnp.float32)
    self_key = centred(streams_of[11], (D, D), D ** -0.5, 0.21875, ((0, 2),), jnp.float32)
    self_value = centred(streams_of[12], (D, D), D ** -0.5, 0.21875, ((0, 2),), jnp.float32)
    self_output = centred(streams_of[13], (D, D), (D // 32) ** -0.5, 1.25, ((0, 2),), jnp.float32)
    cross_query = centred(streams_of[14], (D, D), (16 * D) ** -0.5, 0.0546875, ((0, 2),), jnp.float32)
    cross_key = centred(streams_of[15], (D, D), D ** -0.5, 0.21875, ((0, 2),), jnp.float32)
    cross_value = centred(streams_of[16], (D, D), D ** -0.5, 0.21875, ((0, 2),), jnp.float32)
    cross_output = centred(streams_of[17], (D, D), (D // 32) ** -0.5, 1.25, ((0, 2),), jnp.float32)
    ffn_inner = centred(streams_of[18], (D, FF), D ** -0.5, 0.21875, ((0, 2),), jnp.float32)
    ffn_outer = centred(streams_of[19], (FF, D), FF ** -0.5, 0.109375, ((0, 2),), jnp.float32)
    return dict(tokens=tokens, encoded=encoded, cotangent=cotangent, tgt_lengths=tgt_lengths, enc_lengths=enc_lengths, deal=deal, ln_self=ln_self, ln_cross=ln_cross, ln_ffn=ln_ffn, bias_table=bias_table, self_query=self_query, self_key=self_key, self_value=self_value, self_output=self_output, cross_query=cross_query, cross_key=cross_key, cross_value=cross_value, cross_output=cross_output, ffn_inner=ffn_inner, ffn_outer=ffn_outer)


@jax.custom_vjp
def low(v):
    return lax.optimization_barrier(v.astype(jnp.bfloat16)).astype(jnp.float32)

@jax.custom_vjp
def low_back(v):
    return v

def low_keep(v):
    return (low(v), None)

def low_pass(kept, grad):
    return (grad,)

def back_keep(v):
    return (v, None)

def back_low(kept, grad):
    return (low(grad),)
low.defvjp(low_keep, low_pass)
low_back.defvjp(back_keep, back_low)
EPS = 1e-06
NEG = -1e+30
HIGH = lax.Precision.HIGHEST
GELU_C = 0.7978845608028654
GELU_A = 0.044715

def gelu_tanh(value):
    return 0.5 * value * (1.0 + jnp.tanh(GELU_C * (value + GELU_A * value * value * value)))

def bucket_edges():
    edges = []
    for level in range(1, 16):
        distance = 16
        while int(math.log(distance / 16.0) / math.log(8.0) * 16.0) < level:
            distance += 1
        edges.append(distance)
    return edges

def bucket_of(distance):
    clipped = jnp.maximum(distance, 0).astype(jnp.int32)
    large = jnp.full(clipped.shape, 16, jnp.int32)
    for edge in bucket_edges():
        large = large + (clipped >= edge).astype(jnp.int32)
    return jnp.where(clipped < 16, clipped, large)

def seg_ids(index, lengths):
    ends = jnp.cumsum(lengths).astype(jnp.int32)
    return lax.optimization_barrier(jnp.sum((index[:, None] >= ends[None, :]).astype(jnp.int32), axis=1)).astype(jnp.int32)

def rms_norm(value, gain):
    return value * lax.rsqrt(lax.optimization_barrier(jnp.mean(value * value, axis=-1, keepdims=True)) + EPS) * gain

def matmul(left, right):
    return jnp.dot(left, right, precision=HIGH)

def attention(query, keys, values, allowed_fn, bias_fn):
    group_rows = query.shape[0]
    block = math.gcd(group_rows, 512)
    count = group_rows // block
    key_heads = keys.reshape(keys.shape[0], HEADS, HEAD_DIM)
    value_heads = values.reshape(values.shape[0], HEADS, HEAD_DIM)

    def one_block(inputs):
        q_block, start = inputs
        q_heads = q_block.reshape(block, HEADS, HEAD_DIM)
        q_index = start + jnp.arange(block, dtype=jnp.int32)
        scores = jnp.einsum('qhd,khd->hqk', q_heads, key_heads, precision=HIGH)
        if bias_fn is not None:
            scores = scores + bias_fn(q_index)
        scores = low_back(scores)
        allowed = allowed_fn(q_index)
        scores = jnp.where(allowed[None], scores, NEG)
        probs = low(jax.nn.softmax(scores, axis=-1))
        result = jnp.einsum('hqk,khd->qhd', probs, value_heads, precision=HIGH)
        return result.reshape(block, HEADS * HEAD_DIM)
    starts = jnp.arange(count, dtype=jnp.int32) * block
    blocks = lax.map(jax.checkpoint(one_block), (query.reshape(count, block, query.shape[1]), starts))
    return blocks.reshape(group_rows, query.shape[1])

def reference(tokens, encoded, cotangent, tgt_lengths, enc_lengths, deal, ln_self, ln_cross, ln_ffn, bias_table, self_query, self_key, self_value, self_output, cross_query, cross_key, cross_value, cross_output, ffn_inner, ffn_outer):
    group_rows = TOK_DEV * N_CTX
    enc_group = ENC_DEV * N_CTX

    def forward(x_all, enc_all, gain_self, gain_cross, gain_ffn, table, w_sq, w_sk, w_sv, w_so, w_cq, w_ck, w_cv, w_co, w_inner, w_outer):
        gain_self = low(gain_self)
        gain_cross = low(gain_cross)
        gain_ffn = low(gain_ffn)
        table = low(table)
        w_sq, w_sk, w_sv, w_so = (low(w_sq), low(w_sk), low(w_sv), low(w_so))
        w_cq, w_ck, w_cv, w_co = (low(w_cq), low(w_ck), low(w_cv), low(w_co))
        w_inner, w_outer = (low(w_inner), low(w_outer))
        results = []
        for group in range(N_FSDP):
            lengths = tgt_lengths[group]
            enc_sizes = enc_lengths[group]
            pairing = deal[group]
            x_start = x_all[group * group_rows:(group + 1) * group_rows]
            enc_rows = enc_all[group * enc_group:(group + 1) * enc_group]
            key_index = jnp.arange(group_rows, dtype=jnp.int32)
            key_seg = seg_ids(key_index, lengths)
            enc_seg = seg_ids(jnp.arange(enc_group, dtype=jnp.int32), enc_sizes)

            def self_allowed(q_index, key_index=key_index, key_seg=key_seg, lengths=lengths):
                q_seg = seg_ids(q_index, lengths)
                return (q_seg[:, None] == key_seg[None, :]) & (key_index[None, :] <= q_index[:, None])

            def self_bias(q_index, key_index=key_index):
                buckets = bucket_of(q_index[:, None] - key_index[None, :])
                return jnp.transpose(jnp.take(table, buckets, axis=0), (2, 0, 1))

            def cross_allowed(q_index, lengths=lengths, pairing=pairing, enc_seg=enc_seg):
                q_seg = seg_ids(q_index, lengths)
                choose = q_seg[:, None] == jnp.arange(NSEQ, dtype=jnp.int32)[None, :]
                paired = lax.optimization_barrier(jnp.sum(jnp.where(choose, pairing[None, :], 0), axis=1)).astype(jnp.int32)
                return enc_seg[None, :] == paired[:, None]
            h_one = low(rms_norm(x_start, gain_self))
            q_one = low_back(low(matmul(h_one, w_sq)))
            k_one = low_back(low(matmul(h_one, w_sk)))
            v_one = low_back(low(matmul(h_one, w_sv)))
            att_one = low_back(low(attention(q_one, k_one, v_one, self_allowed, self_bias)))
            x_mid = x_start + low_back(matmul(att_one, w_so))
            h_two = low(rms_norm(x_mid, gain_cross))
            q_two = low_back(low(matmul(h_two, w_cq)))
            k_two = low_back(low(matmul(enc_rows, w_ck)))
            v_two = low_back(low(matmul(enc_rows, w_cv)))
            att_two = low_back(low(attention(q_two, k_two, v_two, cross_allowed, None)))
            x_late = x_mid + low_back(matmul(att_two, w_co))
            h_three = low(rms_norm(x_late, gain_ffn))
            pre_act = low_back(matmul(h_three, w_inner))
            hidden = low(gelu_tanh(pre_act))
            results.append(x_late + low_back(matmul(hidden, w_outer)))
        return jnp.concatenate(results, axis=0)
    output, pullback = jax.vjp(forward, tokens.astype(jnp.float32), encoded.astype(jnp.float32), ln_self, ln_cross, ln_ffn, bias_table, self_query, self_key, self_value, self_output, cross_query, cross_key, cross_value, cross_output, ffn_inner, ffn_outer)
    grads = pullback(cotangent.astype(jnp.float32))
    return (output, grads[0], grads[1], grads[2], grads[3], grads[4], grads[5], grads[6], grads[7], grads[8], grads[9], grads[10], grads[11], grads[12], grads[13], grads[14], grads[15])
```

```python
import functools
import math

import jax
import jax.numpy as jnp
import numpy as np
from jax import lax
from jax.experimental import pallas as pl
from jax.experimental.pallas import tpu as pltpu
from jax.sharding import Mesh
from jax.sharding import PartitionSpec as P

HEADS = 12
HEAD_DIM = 64
BUCKETS = 32
EPS = 1e-06
NEG = -1e30
GELU_C = 0.7978845608028654
GELU_A = 0.044715

LOCAL = HEADS // 2
PAIRS = LOCAL // 2
HALF = LOCAL * HEAD_DIM
ROWS = 256
VMEM_LIMIT = 56 << 20

F32 = jnp.float32
BF16 = jnp.bfloat16


def bucket_edges():
    edges = []
    for level in range(1, 16):
        distance = 16
        while int(math.log(distance / 16.0) / math.log(8.0) * 16.0) < level:
            distance += 1
        edges.append(distance)
    return edges


def buckets_of(distances):
    clipped = np.maximum(np.asarray(distances), 0)
    large = np.full(clipped.shape, 16)
    for edge in bucket_edges():
        large = large + (clipped >= edge)
    return np.where(clipped < 16, clipped, large)


LANES = np.arange(2 * ROWS)
QK_DISTANCE = np.where(LANES <= ROWS, ROWS - LANES, 3 * ROWS - LANES)
KQ_DISTANCE = LANES
QK_ONEHOT = np.eye(BUCKETS, dtype=np.float32)[buckets_of(QK_DISTANCE)]
KQ_ONEHOT = np.eye(BUCKETS, dtype=np.float32)[buckets_of(KQ_DISTANCE)]


def dot_nt(left, right):
    return lax.dot_general(left, right, (((1,), (1,)), ((), ())), preferred_element_type=F32)


def dot_tn(left, right):
    return lax.dot_general(left, right, (((0,), (0,)), ((), ())), preferred_element_type=F32)


def dot_nn(left, right):
    return lax.dot_general(left, right, (((1,), (0,)), ((), ())), preferred_element_type=F32)


def spans(ref):
    starts, ends, at = [], [], jnp.int32(0)
    for i in range(ref.shape[1]):
        starts.append(at)
        at = at + ref[0, i]
        ends.append(at)
    return starts, ends


def seg_of(index, ends):
    found = jnp.zeros(index.shape, jnp.int32)
    for end in ends[:-1]:
        found = found + (index >= end).astype(jnp.int32)
    return found


def iota(shape, axis):
    return lax.broadcasted_iota(jnp.int32, shape, axis)


def split_pair(pair):
    low = iota(pair.shape, 1) < HEAD_DIM
    zero = jnp.zeros_like(pair)
    return jnp.concatenate([jnp.where(low, pair, zero), jnp.where(low, zero, pair)], axis=0)


def join_pair(both):
    rows = both.shape[0] // 2
    low = iota((rows, both.shape[1]), 1) < HEAD_DIM
    return jnp.where(low, both[:rows], both[rows:])


def fill_tiles(bias_ref, tiles, first, second):
    for h in range(LOCAL):
        rolled = pltpu.roll(
            jnp.broadcast_to(bias_ref[h : h + 1, :], (ROWS, 2 * ROWS)), 0, 1, stride=1, stride_axis=0
        )
        tiles[first, h] = rolled[:, :ROWS]
        tiles[second, h] = rolled[:, ROWS:]
        tiles[0, h] = jnp.broadcast_to(bias_ref[h : h + 1, 2 * ROWS - 1 :], (ROWS, ROWS))


def softmax_and_values(s_scr, mx_scr, l_scr, acc_scr, values, visit, o_ref, lse_ref):
    lse = jnp.zeros((ROWS, 128), F32)
    lane = iota((ROWS, 128), 1)
    for p in range(PAIRS):
        peak = jnp.max(mx_scr[p], axis=1, keepdims=True)
        l_scr[...] = jnp.zeros_like(l_scr)
        acc_scr[...] = jnp.zeros_like(acc_scr)

        def block(j, p=p, peak=peak):
            at = pl.multiple_of(j * ROWS, ROWS)
            weights = jnp.exp(s_scr[p, :, pl.ds(at, ROWS)] - peak)
            l_scr[...] += weights
            acc_scr[...] += dot_nn(weights.astype(BF16), values(at, p))

        visit(block)
        total = jnp.sum(l_scr[...], axis=1, keepdims=True)
        o_ref[:, 128 * p : 128 * p + 128] = join_pair(acc_scr[...] / total)
        both = peak + jnp.log(total)
        lse = jnp.where(lane == 2 * p, both[:ROWS], lse)
        lse = jnp.where(lane == 2 * p + 1, both[ROWS:], lse)
    lse_ref[...] = lse


def self_forward_kernel(chip_ref, len_ref, bias_ref, qkv_ref, o_ref, lse_ref, tiles, qs, s_scr, mx_scr, l_scr, acc_scr):
    chip = chip_ref[0]
    starts, ends = spans(len_ref)
    base = pl.multiple_of(chip * ROWS, ROWS)
    first = jnp.int32(0)
    for end in ends[:-1]:
        first = jnp.where(base >= end, end, first)
    j_min = first // ROWS
    fill_tiles(bias_ref, tiles, 1, 2)
    for p in range(PAIRS):
        qs[p] = split_pair(qkv_ref[pl.ds(base, ROWS), 128 * p : 128 * p + 128])
    mx_scr[...] = jnp.full_like(mx_scr, NEG)
    q_row = base + iota((ROWS, 1), 0)
    q_seg = seg_of(q_row, ends)

    def scores(j, _):
        at = pl.multiple_of(j * ROWS, ROWS)
        k_row = at + iota((1, ROWS), 1)
        allowed = (q_seg == seg_of(k_row, ends)) & (k_row <= q_row)
        masked = jnp.where(allowed, 0.0, NEG)
        tile = jnp.maximum(j - chip + 2, 0)
        for p in range(PAIRS):
            keys = qkv_ref[pl.ds(at, ROWS), HALF + 128 * p : HALF + 128 * p + 128]
            raw = dot_nt(qs[p], keys)
            for i in range(2):
                rows = slice(i * ROWS, (i + 1) * ROWS)
                value = raw[rows] + (tiles[tile, 2 * p + i] + masked)
                s_scr[p, rows, pl.ds(at, ROWS)] = value
                mx_scr[p, rows] = jnp.maximum(mx_scr[p, rows], value)
        return 0

    lax.fori_loop(j_min, chip + 1, scores, 0)

    def visit(block):
        lax.fori_loop(j_min, chip + 1, lambda j, c: (block(j), c)[1], 0)

    softmax_and_values(
        s_scr, mx_scr, l_scr, acc_scr,
        lambda at, p: qkv_ref[pl.ds(at, ROWS), 2 * HALF + 128 * p : 2 * HALF + 128 * p + 128],
        visit, o_ref, lse_ref,
    )


def cross_flags(chip, len_ref, enc_ref, deal_ref):
    starts, ends = spans(len_ref)
    e_starts, e_ends = spans(enc_ref)
    base = chip * ROWS
    ranges = []
    for i in range(len(ends)):
        live = (starts[i] < base + ROWS) & (ends[i] > base)
        low, high = jnp.int32(0), jnp.int32(0)
        for e in range(len(e_ends)):
            hit = deal_ref[0, i] == e
            low = jnp.where(hit, e_starts[e], low)
            high = jnp.where(hit, e_ends[e], high)
        ranges.append((live, low, high))

    def wanted(at):
        found = jnp.bool_(False)
        for live, low, high in ranges:
            found = found | (live & (low < at + ROWS) & (high > at))
        return found

    q_seg = seg_of(base + iota((ROWS, 1), 0), ends)
    q_pair = jnp.zeros((ROWS, 1), jnp.int32)
    for i in range(len(ends)):
        q_pair = q_pair + jnp.where(q_seg == i, deal_ref[0, i], 0)
    return wanted, q_pair, e_ends


def cross_forward_kernel(chip_ref, len_ref, enc_ref, deal_ref, q_ref, kv_ref, o_ref, lse_ref, qs, s_scr, mx_scr, l_scr, acc_scr):
    chip = chip_ref[0]
    wanted, q_pair, e_ends = cross_flags(chip, len_ref, enc_ref, deal_ref)
    for p in range(PAIRS):
        qs[p] = split_pair(q_ref[:, 128 * p : 128 * p + 128])
    mx_scr[...] = jnp.full_like(mx_scr, NEG)
    blocks = kv_ref.shape[0] // ROWS

    def visit(block):
        def body(j, c):
            @pl.when(wanted(j * ROWS))
            def _():
                block(j)

            return c

        lax.fori_loop(0, blocks, body, 0)

    def scores(j):
        at = pl.multiple_of(j * ROWS, ROWS)
        k_row = at + iota((1, ROWS), 1)
        masked = jnp.where(q_pair == seg_of(k_row, e_ends), 0.0, NEG)
        for p in range(PAIRS):
            raw = dot_nt(qs[p], kv_ref[pl.ds(at, ROWS), 128 * p : 128 * p + 128])
            for i in range(2):
                rows = slice(i * ROWS, (i + 1) * ROWS)
                value = raw[rows] + masked
                s_scr[p, rows, pl.ds(at, ROWS)] = value
                mx_scr[p, rows] = jnp.maximum(mx_scr[p, rows], value)

    visit(scores)
    softmax_and_values(
        s_scr, mx_scr, l_scr, acc_scr,
        lambda at, p: kv_ref[pl.ds(at, ROWS), HALF + 128 * p : HALF + 128 * p + 128],
        visit, o_ref, lse_ref,
    )


def row_stats(go_ref, o_ref, lse_ref, gs, lse_scr, delta_scr):
    lane = iota((ROWS, 128), 1)
    low = lane < HEAD_DIM
    deltas = jnp.zeros((ROWS, 128), F32)
    for p in range(PAIRS):
        columns = slice(128 * p, 128 * p + 128)
        grads = go_ref[:, columns]
        gs[p] = split_pair(grads)
        product = grads.astype(F32) * o_ref[:, columns]
        for i in range(2):
            part = jnp.where(low if i == 0 else ~low, product, 0.0)
            delta = jnp.sum(part, axis=1, keepdims=True)
            rows = slice(i * ROWS, (i + 1) * ROWS)
            delta_scr[p, rows] = jnp.broadcast_to(delta, (ROWS, 128))
            lse_scr[p, rows] = jnp.broadcast_to(
                jnp.sum(jnp.where(lane == 2 * p + i, lse_ref[...], 0.0), axis=1, keepdims=True), (ROWS, 128)
            )
            deltas = jnp.where(lane == 8 + 2 * p + i, delta, deltas)
    return deltas


def self_query_grad_kernel(
    chip_ref, len_ref, bias_ref, qkv_ref, go_ref, o_ref, lse_ref, dq_ref, stat_ref, dist_ref,
    tiles, qs, gs, lse_scr, delta_scr, dq_scr, ds_scr,
):
    chip = chip_ref[0]
    starts, ends = spans(len_ref)
    base = pl.multiple_of(chip * ROWS, ROWS)
    first = jnp.int32(0)
    for end in ends[:-1]:
        first = jnp.where(base >= end, end, first)
    fill_tiles(bias_ref, tiles, 1, 2)
    deltas = row_stats(go_ref, o_ref, lse_ref, gs, lse_scr, delta_scr)
    stats = jnp.where(iota((ROWS, 128), 1) < 8, lse_ref[...], deltas)
    stat_ref[...] = jnp.transpose(stats)[:16]
    for p in range(PAIRS):
        qs[p] = split_pair(qkv_ref[pl.ds(base, ROWS), 128 * p : 128 * p + 128])
    dq_scr[...] = jnp.zeros_like(dq_scr)
    ds_scr[...] = jnp.zeros_like(ds_scr)
    q_row = base + iota((ROWS, 1), 0)
    q_seg = seg_of(q_row, ends)

    def block(j, _):
        at = pl.multiple_of(j * ROWS, ROWS)
        k_row = at + iota((1, ROWS), 1)
        allowed = (q_seg == seg_of(k_row, ends)) & (k_row <= q_row)
        masked = jnp.where(allowed, 0.0, NEG)
        tile = jnp.maximum(j - chip + 2, 0)
        for p in range(PAIRS):
            keys = qkv_ref[pl.ds(at, ROWS), HALF + 128 * p : HALF + 128 * p + 128]
            values = qkv_ref[pl.ds(at, ROWS), 2 * HALF + 128 * p : 2 * HALF + 128 * p + 128]
            raw = dot_nt(qs[p], keys)
            dprobs = dot_nt(gs[p], values)
            grads = []
            for i in range(2):
                rows = slice(i * ROWS, (i + 1) * ROWS)
                value = raw[rows] + (tiles[tile, 2 * p + i] + masked)
                probs = jnp.exp(value - lse_scr[p, rows, :1])
                ds = (probs * (dprobs[rows] - delta_scr[p, rows, :1])).astype(BF16)
                ds_scr[tile, 2 * p + i] += ds.astype(F32)
                grads.append(ds)
            dq_scr[p] += dot_nn(jnp.concatenate(grads, axis=0), keys)
        return 0

    lax.fori_loop(first // ROWS, chip + 1, block, 0)
    dist_ref[...] = jnp.zeros_like(dist_ref)
    lanes = iota((1, 2 * ROWS), 1)
    for p in range(PAIRS):
        dq_ref[:, 128 * p : 128 * p + 128] = join_pair(dq_scr[p]).astype(BF16)
    for h in range(LOCAL):
        folded = jnp.concatenate([ds_scr[1, h], ds_scr[2, h]], axis=1)
        rows = ROWS
        while rows > 1:
            rows //= 2
            folded = folded[:rows] + pltpu.roll(folded[rows:], 2 * ROWS - rows, 1)
        far = jnp.sum(jnp.sum(ds_scr[0, h], axis=0, keepdims=True), axis=1, keepdims=True)
        dist_ref[h : h + 1, :] = folded + jnp.where(lanes == 2 * ROWS - 1, far, 0.0)


def self_key_grad_kernel(chip_ref, len_ref, bias_ref, qkv_ref, go_ref, stat_ref, dkv_ref, tiles, ks, vs, dk_scr, dv_scr):
    chip = chip_ref[0]
    starts, ends = spans(len_ref)
    base = pl.multiple_of(chip * ROWS, ROWS)
    last = ends[-1]
    for end in reversed(ends[:-1]):
        last = jnp.where(base + ROWS - 1 < end, end, last)
    fill_tiles(bias_ref, tiles, 2, 1)
    for p in range(PAIRS):
        ks[p] = split_pair(qkv_ref[pl.ds(base, ROWS), HALF + 128 * p : HALF + 128 * p + 128])
        vs[p] = split_pair(qkv_ref[pl.ds(base, ROWS), 2 * HALF + 128 * p : 2 * HALF + 128 * p + 128])
    dk_scr[...] = jnp.zeros_like(dk_scr)
    dv_scr[...] = jnp.zeros_like(dv_scr)
    k_row = base + iota((ROWS, 1), 0)
    k_seg = seg_of(k_row, ends)

    def block(i, _):
        at = pl.multiple_of(i * ROWS, ROWS)
        q_row = at + iota((1, ROWS), 1)
        allowed = (k_seg == seg_of(q_row, ends)) & (k_row <= q_row)
        masked = jnp.where(allowed, 0.0, NEG)
        tile = jnp.maximum(2 - (i - chip), 0)
        for p in range(PAIRS):
            queries = qkv_ref[pl.ds(at, ROWS), 128 * p : 128 * p + 128]
            grads = go_ref[pl.ds(at, ROWS), 128 * p : 128 * p + 128]
            raw = dot_nt(ks[p], queries)
            dprobs = dot_nt(vs[p], grads)
            weights, dscores = [], []
            for e in range(2):
                rows = slice(e * ROWS, (e + 1) * ROWS)
                h = 2 * p + e
                value = raw[rows] + (tiles[tile, h] + masked)
                probs = jnp.exp(value - stat_ref[i, h : h + 1, :])
                weights.append(probs.astype(BF16))
                dscores.append((probs * (dprobs[rows] - stat_ref[i, 8 + h : 9 + h, :])).astype(BF16))
            dv_scr[p] += dot_nn(jnp.concatenate(weights, axis=0), grads)
            dk_scr[p] += dot_nn(jnp.concatenate(dscores, axis=0), queries)
        return 0

    lax.fori_loop(chip, (last - 1) // ROWS + 1, block, 0)
    for p in range(PAIRS):
        dkv_ref[:, 128 * p : 128 * p + 128] = join_pair(dk_scr[p]).astype(BF16)
        dkv_ref[:, HALF + 128 * p : HALF + 128 * p + 128] = join_pair(dv_scr[p]).astype(BF16)


def cross_grad_kernel(
    chip_ref, len_ref, enc_ref, deal_ref, q_ref, go_ref, o_ref, lse_ref, kv_ref, dq_ref, dkv_ref,
    qs, gs, lse_scr, delta_scr, dq_scr,
):
    chip = chip_ref[0]
    wanted, q_pair, e_ends = cross_flags(chip, len_ref, enc_ref, deal_ref)
    row_stats(go_ref, o_ref, lse_ref, gs, lse_scr, delta_scr)
    for p in range(PAIRS):
        qs[p] = split_pair(q_ref[:, 128 * p : 128 * p + 128])
    dq_scr[...] = jnp.zeros_like(dq_scr)

    def block(j, c):
        at = pl.multiple_of(j * ROWS, ROWS)
        hit = wanted(at)

        @pl.when(hit)
        def _():
            k_row = at + iota((1, ROWS), 1)
            masked = jnp.where(q_pair == seg_of(k_row, e_ends), 0.0, NEG)
            for p in range(PAIRS):
                columns = slice(128 * p, 128 * p + 128)
                v_columns = slice(HALF + 128 * p, HALF + 128 * p + 128)
                keys = kv_ref[pl.ds(at, ROWS), columns]
                raw = dot_nt(qs[p], keys)
                dprobs = dot_nt(gs[p], kv_ref[pl.ds(at, ROWS), v_columns])
                weights, dscores = [], []
                for i in range(2):
                    rows = slice(i * ROWS, (i + 1) * ROWS)
                    probs = jnp.exp(raw[rows] + masked - lse_scr[p, rows, :1])
                    weights.append(probs.astype(BF16))
                    dscores.append((probs * (dprobs[rows] - delta_scr[p, rows, :1])).astype(BF16))
                ds = jnp.concatenate(dscores, axis=0)
                dq_scr[p] += dot_nn(ds, keys)
                dkv_ref[pl.ds(at, ROWS), columns] = dot_tn(ds, qs[p]).astype(BF16)
                dkv_ref[pl.ds(at, ROWS), v_columns] = dot_tn(jnp.concatenate(weights, axis=0), gs[p]).astype(BF16)

        @pl.when(jnp.logical_not(hit))
        def _():
            dkv_ref[pl.ds(at, ROWS), :] = jnp.zeros((ROWS, 2 * HALF), BF16)

        return c

    lax.fori_loop(0, kv_ref.shape[0] // ROWS, block, 0)
    for p in range(PAIRS):
        dq_ref[:, 128 * p : 128 * p + 128] = join_pair(dq_scr[p]).astype(BF16)


SMEM = pl.BlockSpec(memory_space=pltpu.SMEM)
VMEM = pl.BlockSpec(memory_space=pltpu.VMEM)


def call(kernel, scalars, arrays, outs, scratch, flops):
    moved = sum(a.size * a.dtype.itemsize for a in arrays) + sum(math.prod(s) * jnp.dtype(d).itemsize for s, d in outs)
    return pl.pallas_call(
        kernel,
        out_shape=[jax.ShapeDtypeStruct(s, d) for s, d in outs],
        in_specs=[SMEM] * len(scalars) + [VMEM] * len(arrays),
        out_specs=[VMEM] * len(outs),
        scratch_shapes=[pltpu.VMEM(s, d) for s, d in scratch],
        compiler_params=pltpu.CompilerParams(vmem_limit_bytes=VMEM_LIMIT),
        cost_estimate=pl.CostEstimate(flops=flops, transcendentals=flops // 256, bytes_accessed=moved),
    )(*scalars, *arrays)


TILES = ((3, LOCAL, ROWS, ROWS), F32)
STACK = ((PAIRS, 2 * ROWS, 128), BF16)
COLUMN = ((PAIRS, 2 * ROWS, 128), F32)


def self_forward(chip, lengths, bias, qkv):
    n = qkv.shape[0]
    return call(
        self_forward_kernel, (chip, lengths), (bias, qkv),
        [((ROWS, HALF), F32), ((ROWS, 128), F32)],
        [TILES, STACK, ((PAIRS, 2 * ROWS, n), F32), ((PAIRS, 2 * ROWS, ROWS), F32), ((2 * ROWS, ROWS), F32), ((2 * ROWS, 128), F32)],
        8 * ROWS * n * HALF,
    )


def cross_forward(chip, lengths, enc, deal, query, kv):
    n = kv.shape[0]
    return call(
        cross_forward_kernel, (chip, lengths, enc, deal), (query, kv),
        [((ROWS, HALF), F32), ((ROWS, 128), F32)],
        [STACK, ((PAIRS, 2 * ROWS, n), F32), ((PAIRS, 2 * ROWS, ROWS), F32), ((2 * ROWS, ROWS), F32), ((2 * ROWS, 128), F32)],
        8 * ROWS * n * HALF,
    )


def self_query_grad(chip, lengths, bias, qkv, go, attn, lse):
    n = qkv.shape[0]
    return call(
        self_query_grad_kernel, (chip, lengths), (bias, qkv, go, attn, lse),
        [((ROWS, HALF), BF16), ((16, ROWS), F32), ((8, 2 * ROWS), F32)],
        [TILES, STACK, STACK, COLUMN, COLUMN, COLUMN, TILES],
        12 * ROWS * n * HALF,
    )


def self_key_grad(chip, lengths, bias, qkv, go, stats):
    n = qkv.shape[0]
    return call(
        self_key_grad_kernel, (chip, lengths), (bias, qkv, go, stats),
        [((ROWS, 2 * HALF), BF16)],
        [TILES, STACK, STACK, COLUMN, COLUMN],
        16 * ROWS * n * HALF,
    )[0]


def cross_grad(chip, lengths, enc, deal, query, go, attn, lse, kv):
    n = kv.shape[0]
    return call(
        cross_grad_kernel, (chip, lengths, enc, deal), (query, go, attn, lse, kv),
        [((ROWS, HALF), BF16), ((n, 2 * HALF), BF16)],
        [STACK, STACK, COLUMN, COLUMN, COLUMN],
        20 * ROWS * n * HALF,
    )


def swap_core(value):
    return lax.ppermute(value, "core", [(0, 1), (1, 0)])


def by_core(own, other, axis):
    core = lax.axis_index("core")
    return jnp.where(
        core == 0, jnp.concatenate([own, other], axis=axis), jnp.concatenate([other, own], axis=axis)
    )


def both_cores(own, axis):
    return by_core(own, swap_core(own), axis)


def gather_fsdp(own):
    count = lax.axis_size("fsdp")
    if count != 2:
        return lax.all_gather(own, "fsdp", axis=0, tiled=True)
    other = lax.ppermute(own, "fsdp", [(0, 1), (1, 0)])
    return jnp.where(
        lax.axis_index("fsdp") == 0,
        jnp.concatenate([own, other], axis=0),
        jnp.concatenate([other, own], axis=0),
    )


def scatter_fsdp(terms):
    count = lax.axis_size("fsdp")
    if count != 2:
        return lax.psum_scatter(terms, "fsdp", scatter_dimension=0, tiled=True)
    index = lax.axis_index("fsdp")
    rows = terms.shape[0] // 2
    other = lax.dynamic_slice_in_dim(terms, (1 - index) * rows, rows, 0).astype(BF16)
    own = lax.dynamic_slice_in_dim(terms, index * rows, rows, 0)
    return own + lax.ppermute(other, "fsdp", [(0, 1), (1, 0)]).astype(F32)


def spread(value, axes):
    count = lax.axis_size(axes)
    return lax.all_to_all(jnp.broadcast_to(value[None], (count,) + value.shape), axes, 0, 0, tiled=True)


CHIPS = ("z", "y")


def gather_rows(own):
    blocks = spread(own, CHIPS)
    other = swap_core(blocks)
    core = lax.axis_index("core")
    both = jnp.where(
        core == 0, jnp.stack([blocks, other], axis=1), jnp.stack([other, blocks], axis=1)
    )
    return both.reshape(-1, own.shape[1])


def sum_over(value, axis):
    count = lax.axis_size(axis)
    parts = value.reshape((count, value.shape[0] // count) + value.shape[1:])
    return jnp.sum(lax.all_to_all(parts, axis, 0, 0, tiled=True).astype(F32), axis=0)


def reduce_chips(value):
    rows = value.shape[0]
    part = sum_over(value.astype(BF16), "y").astype(BF16)
    part = sum_over(part, "z").astype(BF16)
    part = spread(part, "z").reshape((-1,) + value.shape[1:])
    return spread(part, "y").reshape((rows,) + value.shape[1:])


def inverse_rms(value):
    return lax.rsqrt(jnp.mean(value * value, axis=-1, keepdims=True) + EPS)


def rms_backward(value, inverse, gain, grad):
    scaled = grad * gain
    cubed = inverse * inverse * inverse
    dvalue = inverse * scaled - value * cubed * jnp.mean(scaled * value, axis=-1, keepdims=True)
    return (dvalue, jnp.sum(grad * value * inverse, axis=0))


def gelu_parts(value):
    tangent = jnp.tanh(GELU_C * (value + GELU_A * value * value * value))
    result = 0.5 * value * (1.0 + tangent)
    slope = 0.5 * (1.0 + tangent) + 0.5 * value * (1.0 - tangent * tangent) * GELU_C * (
        1.0 + 3.0 * GELU_A * value * value
    )
    return (result, slope)


def on_device(
    tokens, encoded, cotangent, tgt_lengths, enc_lengths, deal,
    ln_self, ln_cross, ln_ffn, bias_table,
    self_query, self_key, self_value, self_output,
    cross_query, cross_key, cross_value, cross_output,
    ffn_inner, ffn_outer,
):
    core = lax.axis_index("core")
    fsdp = lax.axis_index("fsdp")
    n_fsdp = lax.axis_size("fsdp")
    chip = lax.axis_index(CHIPS)
    chip_ref = chip.reshape(1).astype(jnp.int32)
    rows, width = tokens.shape
    hidden_half = ffn_inner.shape[1] // 2
    unit = hidden_half // n_fsdp

    def mine(value, axis):
        size = value.shape[axis] // 2
        return lax.dynamic_slice_in_dim(value, core * size, size, axis)

    small = jnp.concatenate(
        [ln_self, ln_cross, ln_ffn, bias_table.reshape(-1)], axis=0
    ).astype(BF16)[None]
    small = gather_fsdp(small)
    part = width // n_fsdp
    gain_self = small[:, :part].reshape(-1).astype(F32)
    gain_cross = small[:, part : 2 * part].reshape(-1).astype(F32)
    gain_ffn = small[:, 2 * part : 3 * part].reshape(-1).astype(F32)
    table = small[:, 3 * part :].reshape(BUCKETS, HEADS)
    table = lax.dynamic_slice_in_dim(table, core * LOCAL, LOCAL, 1).astype(F32)
    pad = jnp.zeros((2, 2 * ROWS), F32)
    highest = functools.partial(jnp.einsum, "bh,tb->ht", precision=lax.Precision.HIGHEST)
    bias_qk = jnp.concatenate([highest(table, QK_ONEHOT), pad], axis=0)
    bias_kq = jnp.concatenate([highest(table, KQ_ONEHOT), pad], axis=0)

    def gather_columns(*weights):
        return gather_fsdp(jnp.concatenate([mine(w, 1).astype(BF16) for w in weights], axis=1))

    w_qkv = gather_columns(self_query, self_key, self_value)
    w_rest = gather_columns(self_output, cross_query, cross_key, cross_value, cross_output)
    w_cq = w_rest[:, HALF : 2 * HALF]
    w_ckv = w_rest[:, 2 * HALF : 4 * HALF]
    w_so = both_cores(w_rest[:, :HALF], 1)
    w_co = both_cores(w_rest[:, 4 * HALF :], 1)
    inner_units = ffn_inner.reshape(ffn_inner.shape[0], n_fsdp, 2, unit)
    inner_units = lax.dynamic_index_in_dim(inner_units, core, 2, keepdims=False)
    w_inner = gather_fsdp(inner_units.reshape(ffn_inner.shape[0], hidden_half).astype(BF16))
    w_outer = gather_fsdp(mine(ffn_outer, 0).astype(BF16))

    x_group = gather_rows(tokens)
    e_group = gather_rows(encoded)
    cot = both_cores(cotangent, 0).astype(F32)
    cot_low = both_cores(cotangent, 0)

    x_wide = x_group.astype(F32)
    h_group = (x_wide * inverse_rms(x_wide) * gain_self).astype(BF16)
    qkv = dot_nn(h_group, w_qkv).astype(BF16)
    attn_self, lse_self = self_forward(chip_ref, tgt_lengths, bias_qk, qkv)
    attn_self_full = both_cores(attn_self.astype(BF16), 1)
    x_chip = lax.dynamic_slice_in_dim(x_group, chip * ROWS, ROWS, 0).astype(F32)
    h_chip = lax.dynamic_slice_in_dim(h_group, chip * ROWS, ROWS, 0)
    e_chip = lax.dynamic_slice_in_dim(e_group, chip * ROWS, ROWS, 0)
    x_mid = x_chip + dot_nn(attn_self_full, w_so)

    inv_cross = inverse_rms(x_mid)
    in_cross = (x_mid * inv_cross * gain_cross).astype(BF16)
    q_cross = dot_nn(in_cross, w_cq).astype(BF16)
    kv_cross = dot_nn(e_group, w_ckv).astype(BF16)
    attn_cross, lse_cross = cross_forward(chip_ref, tgt_lengths, enc_lengths, deal, q_cross, kv_cross)
    attn_cross_full = both_cores(attn_cross.astype(BF16), 1)
    x_late = x_mid + dot_nn(attn_cross_full, w_co)

    inv_ffn = inverse_rms(x_late)
    in_ffn = (x_late * inv_ffn * gain_ffn).astype(BF16)
    pre_act = dot_nn(in_ffn, w_inner)
    activated, slope = gelu_parts(pre_act)
    hidden = activated.astype(BF16)
    out_part = dot_nn(hidden, w_outer)

    def across(partial):
        other = lax.dynamic_slice_in_dim(partial, (1 - core) * rows, rows, 0)
        return mine(partial, 0) + swap_core(other)

    output = mine(x_late, 0) + across(out_part)

    d_outer = dot_tn(hidden, cot_low)
    d_pre = (dot_nt(cot_low, w_outer) * slope).astype(BF16)
    d_inner = dot_tn(in_ffn, d_pre)
    e_ffn = dot_nt(d_pre, w_inner)
    e_ffn = e_ffn + swap_core(e_ffn)
    dx_ffn, d_gain_ffn = rms_backward(x_late, inv_ffn, gain_ffn, e_ffn)
    grad_late = cot + dx_ffn
    late_low = grad_late.astype(BF16)

    d_co = dot_tn(attn_cross_full, mine(late_low, 1))
    go_cross = dot_nt(late_low, mine(w_co, 0)).astype(BF16)
    dq_cross, dkv_part = cross_grad(
        chip_ref, tgt_lengths, enc_lengths, deal, q_cross, go_cross, attn_cross, lse_cross, kv_cross
    )
    dkv_cross = sum_over(dkv_part, CHIPS).astype(BF16)
    d_cq = dot_tn(in_cross, dq_cross)
    e_cross = dot_nt(dq_cross, w_cq)
    e_cross = e_cross + swap_core(e_cross)
    dx_cross, d_gain_cross = rms_backward(x_mid, inv_cross, gain_cross, e_cross)
    grad_mid = grad_late + dx_cross
    mid_low = grad_mid.astype(BF16)
    d_ckv = dot_tn(e_chip, dkv_cross)
    enc_grad = across(dot_nt(dkv_cross, w_ckv))

    d_so = dot_tn(attn_self_full, mine(mid_low, 1))
    w_so_rows = mine(w_so, 0)
    go_self = dot_nt(mid_low, w_so_rows).astype(BF16)
    dq_self, stats, dist = self_query_grad(chip_ref, tgt_lengths, bias_qk, qkv, go_self, attn_self, lse_self)
    go_group = dot_nt(gather_rows(mine(mid_low, 0)), w_so_rows).astype(BF16)
    stats_group = spread(stats, CHIPS).reshape((-1,) + stats.shape)
    dkv_self = self_key_grad(chip_ref, tgt_lengths, bias_kq, qkv, go_group, stats_group)
    d_table = jnp.einsum("ht,tb->bh", dist[:LOCAL], QK_ONEHOT, precision=lax.Precision.HIGHEST)
    dqkv = jnp.concatenate([dq_self, dkv_self], axis=1)
    d_qkv = dot_tn(h_chip, dqkv)
    e_self = across(dot_nt(dqkv, w_qkv))
    x_own = tokens.astype(F32)
    dx_self, d_gain_self = rms_backward(x_own, inverse_rms(x_own), gain_self, e_self)
    grad_tokens = mine(grad_mid, 0) + dx_self

    def finish_columns(*grads):
        done = reduce_chips(scatter_fsdp(jnp.concatenate(grads, axis=1)))
        own, other = done.astype(F32), swap_core(done).astype(F32)
        return [
            by_core(own[:, i : i + HALF], other[:, i : i + HALF], 1) for i in range(0, done.shape[1], HALF)
        ]

    g_outer = reduce_chips(scatter_fsdp(d_outer))
    g_outer = both_cores(g_outer, 0).astype(F32)
    g_inner = reduce_chips(scatter_fsdp(d_inner)).reshape(-1, n_fsdp, 1, unit)
    g_inner = both_cores(g_inner, 2).reshape(ffn_inner.shape).astype(F32)
    g_co, g_cq, g_ck, g_cv = finish_columns(d_co, d_cq, d_ckv)
    g_so, g_sq, g_sk, g_sv = finish_columns(d_so, d_qkv)

    own_table = jnp.zeros((BUCKETS, 2, LOCAL), F32)
    own_table = lax.dynamic_update_slice(own_table, d_table[:, None], (0, core, 0))
    vector = jnp.concatenate(
        [d_gain_self, 0.5 * d_gain_cross, 0.5 * d_gain_ffn, own_table.reshape(-1)], axis=0
    )
    vector = lax.psum(vector, ("z", "y", "core", "fsdp"))

    def owned(value):
        size = value.shape[0] // n_fsdp
        return lax.dynamic_slice_in_dim(value, fsdp * size, size, 0)

    return (
        output, grad_tokens, enc_grad,
        owned(vector[:width]), owned(vector[width : 2 * width]), owned(vector[2 * width : 3 * width]),
        owned(vector[3 * width :].reshape(BUCKETS, HEADS)),
        g_sq, g_sk, g_sv, g_so, g_cq, g_ck, g_cv, g_co, g_inner, g_outer,
    )


def solution(mesh):
    n_ctx, n_fsdp = mesh.shape["ctx"], mesh.shape["fsdp"]
    n_z = 4
    grid = Mesh(mesh.devices.reshape(n_z, n_ctx // (2 * n_z), 2, n_fsdp), ("z", "y", "core", "fsdp"))
    by_rows = P(("fsdp", "z", "y", "core"), None)
    split = P("fsdp", None)
    vector = P("fsdp")
    in_specs = (by_rows,) * 3 + (split,) * 3 + (vector,) * 3 + (split,) * 11
    out_specs = (by_rows,) * 3 + (vector,) * 3 + (split,) * 11
    return jax.shard_map(on_device, mesh=grid, in_specs=in_specs, out_specs=out_specs, check_vma=False)
```

```python
import functools
import math

import jax
import jax.numpy as jnp
import numpy as np
from jax import lax
from jax.experimental import pallas as pl
from jax.experimental.pallas import tpu as pltpu
from jax.sharding import Mesh
from jax.sharding import PartitionSpec as P

HEADS = 12
HEAD_DIM = 64
BUCKETS = 32
EPS = 1e-06
NEG = -1e30
GELU_C = 0.7978845608028654
GELU_A = 0.044715

LOCAL = HEADS // 2
PAIRS = LOCAL // 2
HALF = LOCAL * HEAD_DIM
ROWS = 256
VMEM_LIMIT = 56 << 20

F32 = jnp.float32
BF16 = jnp.bfloat16


def bucket_edges():
    edges = []
    for level in range(1, 16):
        distance = 16
        while int(math.log(distance / 16.0) / math.log(8.0) * 16.0) < level:
            distance += 1
        edges.append(distance)
    return edges


def buckets_of(distances):
    clipped = np.maximum(np.asarray(distances), 0)
    large = np.full(clipped.shape, 16)
    for edge in bucket_edges():
        large = large + (clipped >= edge)
    return np.where(clipped < 16, clipped, large)


LANES = np.arange(2 * ROWS)
QK_DISTANCE = np.where(LANES <= ROWS, ROWS - LANES, 3 * ROWS - LANES)
KQ_DISTANCE = LANES
QK_ONEHOT = np.eye(BUCKETS, dtype=np.float32)[buckets_of(QK_DISTANCE)]
KQ_ONEHOT = np.eye(BUCKETS, dtype=np.float32)[buckets_of(KQ_DISTANCE)]


def dot_nt(left, right):
    return lax.dot_general(left, right, (((1,), (1,)), ((), ())), preferred_element_type=F32)


def dot_tn(left, right):
    return lax.dot_general(left, right, (((0,), (0,)), ((), ())), preferred_element_type=F32)


def dot_nn(left, right):
    return lax.dot_general(left, right, (((1,), (0,)), ((), ())), preferred_element_type=F32)


def spans(ref):
    starts, ends, at = [], [], jnp.int32(0)
    for i in range(ref.shape[1]):
        starts.append(at)
        at = at + ref[0, i]
        ends.append(at)
    return starts, ends


def seg_of(index, ends):
    found = jnp.zeros(index.shape, jnp.int32)
    for end in ends[:-1]:
        found = found + (index >= end).astype(jnp.int32)
    return found


def iota(shape, axis):
    return lax.broadcasted_iota(jnp.int32, shape, axis)


def split_pair(pair):
    low = iota(pair.shape, 1) < HEAD_DIM
    zero = jnp.zeros_like(pair)
    return jnp.concatenate([jnp.where(low, pair, zero), jnp.where(low, zero, pair)], axis=0)


def join_pair(both):
    rows = both.shape[0] // 2
    low = iota((rows, both.shape[1]), 1) < HEAD_DIM
    return jnp.where(low, both[:rows], both[rows:])


def fill_tiles(bias_ref, tiles, first, second):
    for h in range(LOCAL):
        rolled = pltpu.roll(
            jnp.broadcast_to(bias_ref[h : h + 1, :], (ROWS, 2 * ROWS)), 0, 1, stride=1, stride_axis=0
        )
        tiles[first, h] = rolled[:, :ROWS]
        tiles[second, h] = rolled[:, ROWS:]
        tiles[0, h] = jnp.broadcast_to(bias_ref[h : h + 1, 2 * ROWS - 1 :], (ROWS, ROWS))


def lanes_of(p):
    return pl.ds(pl.multiple_of(p * 128, 128), 128)


def each_pair(body):
    lax.fori_loop(0, PAIRS, lambda p, c: (body(p), c)[1], 0)


def rms_inverse(value):
    return lax.rsqrt(jnp.mean(value * value, axis=-1, keepdims=True) + EPS)


def attend(p, queries, keys, values, visit, extra, s_scr, mx_scr, l_scr, acc_scr, qs, o_ref, low_ref, lse_ref):
    qs[...] = split_pair(queries)
    mx_scr[...] = jnp.full_like(mx_scr, NEG)

    def scores(j):
        at = pl.multiple_of(j * ROWS, ROWS)
        raw = dot_nt(qs[...], keys(at))
        for i in range(2):
            rows = slice(i * ROWS, (i + 1) * ROWS)
            value = raw[rows] + extra(j, at, 2 * p + i)
            s_scr[rows, pl.ds(at, ROWS)] = value
            mx_scr[rows] = jnp.maximum(mx_scr[rows], value)

    visit(scores)
    peak = jnp.max(mx_scr[...], axis=1, keepdims=True)
    l_scr[...] = jnp.zeros_like(l_scr)
    acc_scr[...] = jnp.zeros_like(acc_scr)

    def weigh(j):
        at = pl.multiple_of(j * ROWS, ROWS)
        weights = jnp.exp(s_scr[:, pl.ds(at, ROWS)] - peak)
        l_scr[...] += weights
        acc_scr[...] += dot_nn(weights.astype(BF16), values(at))

    visit(weigh)
    total = jnp.sum(l_scr[...], axis=1, keepdims=True)
    result = join_pair(acc_scr[...] / total)
    o_ref[:, lanes_of(p)] = result
    low_ref[:, lanes_of(p)] = result.astype(BF16)
    both = peak + jnp.log(total)
    lane = iota((ROWS, 128), 1)
    lse = jnp.where(lane == 2 * p, both[:ROWS], lse_ref[...])
    lse_ref[...] = jnp.where(lane == 2 * p + 1, both[ROWS:], lse)


ATTEND = lambda n: [
    ((2 * ROWS, n), F32), ((2 * ROWS, ROWS), F32), ((2 * ROWS, ROWS), F32), ((2 * ROWS, 128), F32), ((2 * ROWS, 128), BF16),
]


def set_rows(target, parts, side):
    if len(parts) == 1:
        target[...] = parts[0][...]
        return
    rows = parts[0].shape[0]
    target[pl.ds(pl.multiple_of(side * rows, rows), rows), :] = parts[0][...]
    target[pl.ds(pl.multiple_of((1 - side) * rows, rows), rows), :] = parts[1][...]


def first_of(base, ends):
    first = jnp.int32(0)
    for end in ends[:-1]:
        first = jnp.where(base >= end, end, first)
    return first


def self_stage_kernel(n_parts, at_ref, len_ref, xe_ref, gain_ref, bias_ref, *refs):
    parts, refs = refs[:n_parts], refs[n_parts:]
    qkv_ref, w_ref, o_ref, low_ref, lse_ref, tiles, mask, s_scr, mx_scr, l_scr, acc_scr, qs = refs
    chip, side = at_ref[0], at_ref[2]
    set_rows(w_ref, parts, side)
    fill_tiles(bias_ref, tiles, 1, 2)
    width = w_ref.shape[0]
    step = 512

    def body(i, c):
        at = pl.multiple_of(i * step, step)
        wide = xe_ref[pl.ds(at, step), :width].astype(F32)
        value = (wide * rms_inverse(wide) * gain_ref[...]).astype(BF16)
        result = dot_nn(value, w_ref[...])
        for j in range(qkv_ref.shape[0]):
            qkv_ref[j, pl.ds(at, step), :] = result[:, 128 * j : 128 * j + 128].astype(BF16)
        return c

    lax.fori_loop(0, xe_ref.shape[0] // step, body, 0)

    starts, ends = spans(len_ref)
    base = pl.multiple_of(chip * ROWS, ROWS)
    j_min = first_of(base, ends) // ROWS
    q_row = base + iota((ROWS, 1), 0)
    q_seg = seg_of(q_row, ends)
    lse_ref[...] = jnp.zeros_like(lse_ref)

    def fill_mask(j, c):
        at = pl.multiple_of(j * ROWS, ROWS)
        k_row = at + iota((1, ROWS), 1)
        mask[:, pl.ds(at, ROWS)] = jnp.where((q_seg == seg_of(k_row, ends)) & (k_row <= q_row), 0.0, NEG)
        return c

    lax.fori_loop(j_min, chip + 1, fill_mask, 0)

    def visit(block):
        lax.fori_loop(j_min, chip + 1, lambda j, c: (block(j), c)[1], 0)

    def extra(j, at, h):
        return tiles[jnp.maximum(j - chip + 2, 0), h] + mask[:, pl.ds(at, ROWS)]

    each_pair(
        lambda p: attend(
            p, qkv_ref[p, pl.ds(base, ROWS), :],
            lambda at: qkv_ref[PAIRS + p, pl.ds(at, ROWS), :],
            lambda at: qkv_ref[2 * PAIRS + p, pl.ds(at, ROWS), :],
            visit, extra, s_scr, mx_scr, l_scr, acc_scr, qs, o_ref, low_ref, lse_ref,
        )
    )


def add_heads(low_ref, other_ref, w_ref, core):
    own = pl.ds(pl.multiple_of(core * HALF, HALF), HALF)
    other = pl.ds(pl.multiple_of((1 - core) * HALF, HALF), HALF)
    return dot_nn(low_ref[...], w_ref[own, :]) + dot_nn(other_ref[...], w_ref[other, :])


def cross_stage_kernel(n_parts, at_ref, len_ref, enc_ref, deal_ref, xe_ref, gain_ref, low_ref, other_ref, *refs):
    outs, mates, parts, refs = refs[:n_parts], refs[n_parts : 2 * n_parts], refs[2 * n_parts : 3 * n_parts], refs[3 * n_parts :]
    mid_ref, in_ref, q_ref, kv_ref, o_ref, low2_ref, lse_ref, so_ref, co_ref, wc_ref, refs = *refs[:10], refs[10:]
    mask, s_scr, mx_scr, l_scr, acc_scr, qs = refs
    chip, core, side = at_ref[0], at_ref[1], at_ref[2]
    set_rows(wc_ref, parts, side)
    for pieces, column in ((outs, core), (mates, 1 - core)):
        lanes = pl.ds(pl.multiple_of(column * HALF, 128), HALF)
        for i, piece in enumerate(pieces):
            rows = piece.shape[0]
            at = pl.multiple_of((side if i == 0 else 1 - side) * rows, rows) if n_parts > 1 else 0
            so_ref[pl.ds(at, rows), lanes] = piece[:, :HALF]
            co_ref[pl.ds(at, rows), lanes] = piece[:, HALF:]
    width = so_ref.shape[0]
    base = pl.multiple_of(chip * ROWS, ROWS)
    mid = xe_ref[pl.ds(base, ROWS), :width].astype(F32) + add_heads(low_ref, other_ref, so_ref, core)
    mid_ref[...] = mid
    normed = (mid * rms_inverse(mid) * gain_ref[...]).astype(BF16)
    in_ref[...] = normed
    q_ref[...] = dot_nn(normed, wc_ref[:, :HALF]).astype(BF16)
    step = 512

    def body(i, c):
        at = pl.multiple_of(i * step, step)
        result = dot_nn(xe_ref[pl.ds(at, step), width:], wc_ref[:, HALF:])
        for j in range(kv_ref.shape[0]):
            kv_ref[j, pl.ds(at, step), :] = result[:, 128 * j : 128 * j + 128].astype(BF16)
        return c

    lax.fori_loop(0, xe_ref.shape[0] // step, body, 0)
    wanted, q_pair, e_ends = cross_flags(chip, len_ref, enc_ref, deal_ref)
    lse_ref[...] = jnp.zeros_like(lse_ref)

    def visit(block):
        def body(j, c):
            @pl.when(wanted(j * ROWS))
            def _():
                block(j)

            return c

        lax.fori_loop(0, kv_ref.shape[1] // ROWS, body, 0)

    def fill_mask(j):
        at = pl.multiple_of(j * ROWS, ROWS)
        mask[:, pl.ds(at, ROWS)] = jnp.where(q_pair == seg_of(at + iota((1, ROWS), 1), e_ends), 0.0, NEG)

    visit(fill_mask)
    each_pair(
        lambda p: attend(
            p, q_ref[:, lanes_of(p)],
            lambda at: kv_ref[p, pl.ds(at, ROWS), :],
            lambda at: kv_ref[PAIRS + p, pl.ds(at, ROWS), :],
            visit, lambda j, at, h: mask[:, pl.ds(at, ROWS)],
            s_scr, mx_scr, l_scr, acc_scr, qs, o_ref, low2_ref, lse_ref,
        )
    )


def gelu_parts(value):
    tangent = jnp.tanh(GELU_C * (value + GELU_A * value * value * value))
    result = 0.5 * value * (1.0 + tangent)
    slope = 0.5 * (1.0 + tangent) + 0.5 * value * (1.0 - tangent * tangent) * GELU_C * (
        1.0 + 3.0 * GELU_A * value * value
    )
    return (result, slope)


def own_rows(core, rows):
    return pl.ds(pl.multiple_of(core * rows, rows), rows)


def ffn_stage_kernel(n_parts, at_ref, mid_ref, gain_ref, low_ref, other_ref, co_ref, cot_ref, mate_ref, *refs):
    inner, outer, refs = refs[:n_parts], refs[n_parts : 2 * n_parts], refs[2 * n_parts :]
    late_ref, in_ref, hid_ref, dpre_ref, cot_out, keep_ref, send_ref, e_ref, wi_ref, wo_ref, part_scr = refs
    core, side = at_ref[1], at_ref[2]
    rows = cot_ref.shape[0]
    set_rows(wi_ref, inner, side)
    set_rows(wo_ref, outer, side)
    cot_out[own_rows(core, rows), :] = cot_ref[...]
    cot_out[own_rows(1 - core, rows), :] = mate_ref[...]
    late = mid_ref[...] + add_heads(low_ref, other_ref, co_ref, core)
    late_ref[...] = late
    normed = (late * rms_inverse(late) * gain_ref[...]).astype(BF16)
    in_ref[...] = normed
    columns = 512

    def body(i, c):
        at = pl.multiple_of(i * columns, columns)
        activated, slope = gelu_parts(dot_nn(normed, wi_ref[:, pl.ds(at, columns)]))
        hid_ref[:, pl.ds(at, columns)] = activated.astype(BF16)
        grads = dot_nt(cot_out[...], wo_ref[pl.ds(at, columns), :])
        dpre_ref[:, pl.ds(at, columns)] = (grads * slope).astype(BF16)
        return c

    lax.fori_loop(0, wi_ref.shape[1] // columns, body, 0)
    e_ref[...] = dot_nt(dpre_ref[...], wi_ref[...])
    part_scr[...] = dot_nn(hid_ref[...], wo_ref[...])
    keep_ref[...] = part_scr[own_rows(core, rows), :] + late_ref[own_rows(core, rows), :]
    send_ref[...] = part_scr[own_rows(1 - core, rows), :]


def ffn_grads_kernel(n_sides, at_ref, hid_ref, cot_ref, in_ref, dpre_ref, *outs):
    side = at_ref[2]
    rows = in_ref.shape[1] // n_sides
    width = cot_ref.shape[1]
    if n_sides != 2:
        outs[0][...] = dot_tn(hid_ref[...], cot_ref[...])
        outs[1][...] = dot_tn(in_ref[...], dpre_ref[...])
        return
    keep_ref, send_ref = outs
    for owner in range(2):
        for mine, target in ((True, keep_ref), (False, send_ref)):

            @pl.when((side == owner) == mine)
            def _():
                for part in range(2):
                    units = slice((2 * owner + part) * rows, (2 * owner + part + 1) * rows)
                    block = dot_tn(hid_ref[:, units], cot_ref[...])
                    target[:, part * width : (part + 1) * width] = block.astype(target.dtype)
                block = dot_tn(in_ref[:, owner * rows : (owner + 1) * rows], dpre_ref[...])
                target[:, 2 * width :] = block.astype(target.dtype)


def norm_grad(value, gain, grad):
    inverse = rms_inverse(value)
    scaled = grad * gain
    cubed = inverse * inverse * inverse
    dvalue = inverse * scaled - value * cubed * jnp.mean(scaled * value, axis=-1, keepdims=True)
    return dvalue, jnp.sum(grad * value * inverse, axis=0, keepdims=True)


def cross_flags(chip, len_ref, enc_ref, deal_ref):
    starts, ends = spans(len_ref)
    e_starts, e_ends = spans(enc_ref)
    base = chip * ROWS
    ranges = []
    for i in range(len(ends)):
        live = (starts[i] < base + ROWS) & (ends[i] > base)
        low, high = jnp.int32(0), jnp.int32(0)
        for e in range(len(e_ends)):
            hit = deal_ref[0, i] == e
            low = jnp.where(hit, e_starts[e], low)
            high = jnp.where(hit, e_ends[e], high)
        ranges.append((live, low, high))

    def wanted(at):
        found = jnp.bool_(False)
        for live, low, high in ranges:
            found = found | (live & (low < at + ROWS) & (high > at))
        return found

    q_seg = seg_of(base + iota((ROWS, 1), 0), ends)
    q_pair = jnp.zeros((ROWS, 1), jnp.int32)
    for i in range(len(ends)):
        q_pair = q_pair + jnp.where(q_seg == i, deal_ref[0, i], 0)
    return wanted, q_pair, e_ends


def row_stats(go_ref, o_ref, lse_ref, gs, lse_scr, delta_scr, stat_scr):
    lane = iota((ROWS, 128), 1)
    low = lane < HEAD_DIM
    stat_scr[...] = lse_ref[...]

    def pair(p):
        grads = go_ref[:, lanes_of(p)]
        gs[p] = split_pair(grads)
        product = grads.astype(F32) * o_ref[:, lanes_of(p)]
        for i in range(2):
            part = jnp.where(low if i == 0 else ~low, product, 0.0)
            delta = jnp.sum(part, axis=1, keepdims=True)
            rows = slice(i * ROWS, (i + 1) * ROWS)
            delta_scr[p, rows] = jnp.broadcast_to(delta, (ROWS, 128))
            lse_scr[p, rows] = jnp.broadcast_to(
                jnp.sum(jnp.where(lane == 2 * p + i, lse_ref[...], 0.0), axis=1, keepdims=True), (ROWS, 128)
            )
            stat_scr[...] = jnp.where(lane == 8 + 2 * p + i, delta, stat_scr[...])

    each_pair(pair)


def self_query_grad_kernel(
    at_ref, len_ref, bias_ref, qkv_ref, go_ref, o_ref, lse_ref, dq_ref, dist_ref,
    tiles, qs, gs, lse_scr, delta_scr, dq_scr, ds_scr, stat_scr,
):
    chip = at_ref[0]
    starts, ends = spans(len_ref)
    base = pl.multiple_of(chip * ROWS, ROWS)
    first = first_of(base, ends)
    fill_tiles(bias_ref, tiles, 1, 2)
    row_stats(go_ref, o_ref, lse_ref, gs, lse_scr, delta_scr, stat_scr)

    def start(p):
        qs[p] = split_pair(qkv_ref[p, pl.ds(base, ROWS), :])

    each_pair(start)
    dq_scr[...] = jnp.zeros_like(dq_scr)
    ds_scr[...] = jnp.zeros_like(ds_scr)
    q_row = base + iota((ROWS, 1), 0)
    q_seg = seg_of(q_row, ends)

    def block(j, _):
        at = pl.multiple_of(j * ROWS, ROWS)
        k_row = at + iota((1, ROWS), 1)
        allowed = (q_seg == seg_of(k_row, ends)) & (k_row <= q_row)
        masked = jnp.where(allowed, 0.0, NEG)
        tile = jnp.maximum(j - chip + 2, 0)

        def pair(p):
            keys = qkv_ref[PAIRS + p, pl.ds(at, ROWS), :]
            raw = dot_nt(qs[p], keys)
            dprobs = dot_nt(gs[p], qkv_ref[2 * PAIRS + p, pl.ds(at, ROWS), :])
            grads = []
            for i in range(2):
                rows = slice(i * ROWS, (i + 1) * ROWS)
                value = raw[rows] + (tiles[tile, 2 * p + i] + masked)
                probs = jnp.exp(value - lse_scr[p, rows, :1])
                ds = (probs * (dprobs[rows] - delta_scr[p, rows, :1])).astype(BF16)
                ds_scr[tile, 2 * p + i] += ds.astype(F32)
                grads.append(ds)
            dq_scr[p] += dot_nn(jnp.concatenate(grads, axis=0), keys)

        each_pair(pair)
        return 0

    lax.fori_loop(first // ROWS, chip + 1, block, 0)
    dist_ref[...] = jnp.zeros_like(dist_ref)
    lanes = iota((1, 2 * ROWS), 1)
    for p in range(PAIRS):
        dq_ref[:, 128 * p : 128 * p + 128] = join_pair(dq_scr[p]).astype(BF16)

    def fold(h, c):
        folded = jnp.concatenate([ds_scr[1, h], ds_scr[2, h]], axis=1)
        rows = ROWS
        while rows > 1:
            rows //= 2
            folded = folded[:rows] + pltpu.roll(folded[rows:], 2 * ROWS - rows, 1)
        far = jnp.sum(jnp.sum(ds_scr[0, h], axis=0, keepdims=True), axis=1, keepdims=True)
        dist_ref[pl.ds(h, 1), :] = folded + jnp.where(lanes == 2 * ROWS - 1, far, 0.0)
        return c

    lax.fori_loop(0, LOCAL, fold, 0)


def self_key_stage_kernel(
    at_ref, len_ref, bias_ref, qkv_ref, message_ref, so_ref, dq_ref, w_ref, x_ref, gain_ref, ckv_ref, small_ref,
    grads_ref, keep_ref, send_ref,
    go_ref, stat_ref, tiles, ks, vs, dk_scr, dv_scr, dqkv_scr, h_scr, e_scr,
):
    chip, core = at_ref[0], at_ref[1]
    starts, ends = spans(len_ref)
    base = pl.multiple_of(chip * ROWS, ROWS)
    last = ends[-1]
    for end in reversed(ends[:-1]):
        last = jnp.where(base + ROWS - 1 < end, end, last)
    stop = (last - 1) // ROWS + 1
    fill_tiles(bias_ref, tiles, 2, 1)
    heads = own_rows(core, HALF)
    half = ROWS // 2

    def receive(i, c):
        both = [message_ref[2 * i + e, :half, :] for e in range(2)]
        result = dot_nt(jnp.concatenate(both, axis=0), so_ref[heads, :])
        for p in range(PAIRS):
            go_ref[p, pl.ds(pl.multiple_of(i * ROWS, ROWS), ROWS), :] = result[:, 128 * p : 128 * p + 128].astype(BF16)
        parts = message_ref[2 * i + core, half:, :].astype(F32)
        stat_ref[i] = parts[:, :ROWS] + parts[:, ROWS : 2 * ROWS] + parts[:, 2 * ROWS :]
        return c

    lax.fori_loop(chip, stop, receive, 0)

    def start(p):
        ks[p] = split_pair(qkv_ref[PAIRS + p, pl.ds(base, ROWS), :])
        vs[p] = split_pair(qkv_ref[2 * PAIRS + p, pl.ds(base, ROWS), :])

    each_pair(start)
    dk_scr[...] = jnp.zeros_like(dk_scr)
    dv_scr[...] = jnp.zeros_like(dv_scr)
    k_row = base + iota((ROWS, 1), 0)
    k_seg = seg_of(k_row, ends)

    def block(i, _):
        at = pl.multiple_of(i * ROWS, ROWS)
        q_row = at + iota((1, ROWS), 1)
        allowed = (k_seg == seg_of(q_row, ends)) & (k_row <= q_row)
        masked = jnp.where(allowed, 0.0, NEG)
        tile = jnp.maximum(2 - (i - chip), 0)

        def pair(p):
            queries = qkv_ref[p, pl.ds(at, ROWS), :]
            grads = go_ref[p, pl.ds(at, ROWS), :]
            raw = dot_nt(ks[p], queries)
            dprobs = dot_nt(vs[p], grads)
            weights, dscores = [], []
            for e in range(2):
                rows = slice(e * ROWS, (e + 1) * ROWS)
                h = 2 * p + e
                value = raw[rows] + (tiles[tile, h] + masked)
                probs = jnp.exp(value - stat_ref[i, pl.ds(h, 1), :])
                weights.append(probs.astype(BF16))
                dscores.append((probs * (dprobs[rows] - stat_ref[i, pl.ds(8 + h, 1), :])).astype(BF16))
            dv_scr[p] += dot_nn(jnp.concatenate(weights, axis=0), grads)
            dk_scr[p] += dot_nn(jnp.concatenate(dscores, axis=0), queries)

        each_pair(pair)
        return 0

    lax.fori_loop(chip, stop, block, 0)
    dqkv_scr[:, :HALF] = dq_ref[...]
    for p in range(PAIRS):
        dqkv_scr[:, HALF + 128 * p : HALF + 128 * p + 128] = join_pair(dk_scr[p]).astype(BF16)
        dqkv_scr[:, 2 * HALF + 128 * p : 2 * HALF + 128 * p + 128] = join_pair(dv_scr[p]).astype(BF16)
    e_scr[...] = dot_nt(dqkv_scr[...], w_ref[...])
    keep_ref[...] = e_scr[own_rows(core, half), :]
    send_ref[...] = e_scr[own_rows(1 - core, half), :]
    wide = x_ref[...].astype(F32)
    scaled = wide * rms_inverse(wide)
    h_scr[...] = (scaled * gain_ref[...]).astype(BF16)
    dgain = jnp.sum(e_scr[...] * scaled, axis=0, keepdims=True)
    dgain = jnp.transpose(jnp.where(iota((128, dgain.shape[1]), 0) == 0, dgain, 0.0))
    columns = grads_ref.shape[1]
    grads_ref[:, columns - 128 :] = (small_ref[...] + dgain).astype(BF16)
    grads_ref[:, 3 * HALF : columns - 128] = ckv_ref[...]
    step = 256
    for i in range(0, h_scr.shape[1], step):
        grads_ref[i : i + step, : 3 * HALF] = dot_tn(h_scr[:, i : i + step], dqkv_scr[...]).astype(BF16)


def cross_grad_stage_kernel(
    at_ref, len_ref, enc_ref, deal_ref,
    e_ref, other_ref, late_ref, gain_ref, cot_ref, co_ref, q_ref, o_ref, lse_ref, kv_ref, wc_ref,
    grad_ref, low_ref, dgain_ref, dq_ref, dkv_ref, part_ref,
    go_ref, qs, gs, lse_scr, delta_scr, dq_scr, stat_scr,
):
    chip, core = at_ref[0], at_ref[1]
    dvalue, dgain = norm_grad(late_ref[...], gain_ref[...], e_ref[...] + other_ref[...])
    dgain_ref[...] = dgain
    grad = cot_ref[...].astype(F32) + dvalue
    grad_ref[...] = grad
    low_ref[...] = grad.astype(BF16)
    go_ref[...] = dot_nt(low_ref[...], co_ref[own_rows(core, HALF), :]).astype(BF16)
    wanted, q_pair, e_ends = cross_flags(chip, len_ref, enc_ref, deal_ref)
    row_stats(go_ref, o_ref, lse_ref, gs, lse_scr, delta_scr, stat_scr)

    def start(p):
        qs[p] = split_pair(q_ref[:, lanes_of(p)])

    each_pair(start)
    dq_scr[...] = jnp.zeros_like(dq_scr)

    def block(j, c):
        at = pl.multiple_of(j * ROWS, ROWS)
        hit = wanted(at)

        @pl.when(hit)
        def _():
            k_row = at + iota((1, ROWS), 1)
            masked = jnp.where(q_pair == seg_of(k_row, e_ends), 0.0, NEG)

            def pair(p):
                keys = kv_ref[p, pl.ds(at, ROWS), :]
                raw = dot_nt(qs[p], keys)
                dprobs = dot_nt(gs[p], kv_ref[PAIRS + p, pl.ds(at, ROWS), :])
                weights, dscores = [], []
                for i in range(2):
                    rows = slice(i * ROWS, (i + 1) * ROWS)
                    probs = jnp.exp(raw[rows] + masked - lse_scr[p, rows, :1])
                    weights.append(probs.astype(BF16))
                    dscores.append((probs * (dprobs[rows] - delta_scr[p, rows, :1])).astype(BF16))
                ds = jnp.concatenate(dscores, axis=0)
                dq_scr[p] += dot_nn(ds, keys)
                dkv_ref[pl.ds(at, ROWS), lanes_of(p)] = dot_tn(ds, qs[p]).astype(BF16)
                dkv_ref[pl.ds(at, ROWS), lanes_of(PAIRS + p)] = dot_tn(jnp.concatenate(weights, axis=0), gs[p]).astype(BF16)

            each_pair(pair)

        @pl.when(jnp.logical_not(hit))
        def _():
            dkv_ref[pl.ds(at, ROWS), :] = jnp.zeros((ROWS, 2 * HALF), BF16)

        return c

    lax.fori_loop(0, kv_ref.shape[1] // ROWS, block, 0)
    for p in range(PAIRS):
        dq_ref[:, 128 * p : 128 * p + 128] = join_pair(dq_scr[p]).astype(BF16)
    part_ref[...] = dot_nt(dq_ref[...], wc_ref[:, :HALF])


def self_grad_start_kernel(
    at_ref, e_ref, other_ref, mid_ref, gain_ref, late_grad_ref, so_ref, o_ref, lse_ref,
    grad_ref, low_ref, dgain_ref, go_ref, message_ref,
    stat_scr,
):
    core = at_ref[1]
    dvalue, dgain = norm_grad(mid_ref[...], gain_ref[...], e_ref[...] + other_ref[...])
    dgain_ref[...] = dgain
    grad = late_grad_ref[...] + dvalue
    grad_ref[...] = grad
    low_ref[...] = grad.astype(BF16)
    go_ref[...] = dot_nt(low_ref[...], so_ref[own_rows(core, HALF), :]).astype(BF16)
    half = ROWS // 2
    message_ref[:half, :] = low_ref[own_rows(core, half), :]
    lane = iota((ROWS, 128), 1)
    stat_scr[...] = lse_ref[...]

    def pair(p):
        product = go_ref[:, lanes_of(p)].astype(F32) * o_ref[:, lanes_of(p)]
        for i in range(2):
            part = jnp.where((lane < HEAD_DIM) if i == 0 else (lane >= HEAD_DIM), product, 0.0)
            stat_scr[...] = jnp.where(lane == 8 + 2 * p + i, jnp.sum(part, axis=1, keepdims=True), stat_scr[...])

    each_pair(pair)
    rest = jnp.transpose(stat_scr[...])[:16]
    for part in range(3):
        high = rest.astype(BF16)
        message_ref[half:, part * ROWS : (part + 1) * ROWS] = high
        rest = rest - high.astype(F32)


def projection_grads_kernel(at_ref, low2_ref, other2_ref, b2_ref, in_ref, dq_ref, low1_ref, other1_ref, b1_ref, out_ref):
    core = at_ref[1]
    lanes = pl.ds(pl.multiple_of(core * HALF, 128), HALF)
    for at, own, other, grad in ((0, low2_ref, other2_ref, b2_ref), (2 * HALF, low1_ref, other1_ref, b1_ref)):
        grads = grad[:, lanes]
        for side, part in ((core, own), (1 - core, other)):
            out_ref[own_rows(side, HALF), at : at + HALF] = dot_tn(part[...], grads).astype(BF16)
    out_ref[:, HALF : 2 * HALF] = dot_tn(in_ref[...], dq_ref[...]).astype(BF16)


def encoder_grads_kernel(at_ref, dkv_ref, e_ref, wc_ref, grads_ref, keep_ref, send_ref, low_scr, e_scr):
    core = at_ref[1]
    half = ROWS // 2
    low_scr[...] = dkv_ref[...].astype(BF16)
    e_scr[...] = dot_nt(low_scr[...], wc_ref[:, HALF:])
    keep_ref[...] = e_scr[own_rows(core, half), :]
    send_ref[...] = e_scr[own_rows(1 - core, half), :]
    grads_ref[...] = dot_tn(e_ref[...], low_scr[...]).astype(BF16)


def token_grads_kernel(at_ref, e_ref, other_ref, x_ref, gain_ref, grad_ref, out_ref):
    dvalue, _ = norm_grad(x_ref[...].astype(F32), gain_ref[...], e_ref[...] + other_ref[...])
    out_ref[...] = grad_ref[own_rows(at_ref[1], out_ref.shape[0]), :] + dvalue


def finish_columns_kernel(at_ref, own_ref, other_ref, *outs):
    core = at_ref[1]
    for i, out in enumerate(outs):
        columns = slice(i * HALF, (i + 1) * HALF)
        out[:, pl.ds(pl.multiple_of(core * HALF, 128), HALF)] = own_ref[:, columns].astype(F32)
        out[:, pl.ds(pl.multiple_of((1 - core) * HALF, 128), HALF)] = other_ref[:, columns].astype(F32)


def finish_ffn_kernel(order, parts_ref, outer_ref, inner_ref):
    rows = parts_ref.shape[1]
    side = inner_ref.shape[0]
    width = outer_ref.shape[1]
    unit = inner_ref.shape[1] // 4
    for i, (core, place) in enumerate(order):
        at = place * rows
        for half in range(2):
            top = (2 * core + half) * side + at
            outer_ref[top : top + rows, :] = parts_ref[i, :, half * width : (half + 1) * width].astype(F32)
            lanes = slice((2 * half + core) * unit, (2 * half + core + 1) * unit)
            inner_ref[at : at + rows, lanes] = parts_ref[i, :, 2 * width + half * unit : 2 * width + (half + 1) * unit].astype(F32)


def finish_gathered_kernel(order, parts_ref, *outs):
    rows = parts_ref.shape[1]
    for i, (core, place) in enumerate(order):
        for j, out in enumerate(outs):
            out[place * rows : (place + 1) * rows, core * HALF : (core + 1) * HALF] = parts_ref[
                i, :, j * HALF : (j + 1) * HALF
            ].astype(F32)


def pack_kernel(groups, core_ref, *refs):
    count = sum(groups)
    ins, outs = list(refs[:count]), refs[count:]
    for size, out in zip(groups, outs):
        at = 0
        for _ in range(size):
            part = ins.pop(0)
            out[:, at : at + part.shape[1]] = part[...].astype(BF16)
            at += part.shape[1]


SMEM = pl.BlockSpec(memory_space=pltpu.SMEM)
VMEM = pl.BlockSpec(memory_space=pltpu.VMEM)


def call(kernel, scalars, arrays, outs, scratch, flops):
    moved = sum(a.size * a.dtype.itemsize for a in arrays) + sum(math.prod(s) * jnp.dtype(d).itemsize for s, d in outs)
    return pl.pallas_call(
        kernel,
        out_shape=[jax.ShapeDtypeStruct(s, d) for s, d in outs],
        in_specs=[SMEM] * len(scalars) + [VMEM] * len(arrays),
        out_specs=[VMEM] * len(outs),
        scratch_shapes=[pltpu.VMEM(s, d) for s, d in scratch],
        compiler_params=pltpu.CompilerParams(vmem_limit_bytes=VMEM_LIMIT),
        cost_estimate=pl.CostEstimate(flops=flops, transcendentals=0, bytes_accessed=moved),
    )(*scalars, *arrays)


TILES = ((3, LOCAL, ROWS, ROWS), F32)
STACK = ((PAIRS, 2 * ROWS, 128), BF16)
COLUMN = ((PAIRS, 2 * ROWS, 128), F32)
LANE = ((ROWS, 128), F32)


def pack(core, groups):
    flat = [item for group in groups for item in group]
    return pl.pallas_call(
        functools.partial(pack_kernel, [len(g) for g in groups]),
        grid_spec=pltpu.PrefetchScalarGridSpec(
            num_scalar_prefetch=1,
            grid=(1,),
            in_specs=[
                pl.BlockSpec(shape, functools.partial(lambda index, i, c: index(c[0]), index)) for _, shape, index in flat
            ],
            out_specs=[
                pl.BlockSpec((g[0][1][0], sum(s[1] for _, s, _ in g)), lambda i, c: (0, 0)) for g in groups
            ],
        ),
        out_shape=[jax.ShapeDtypeStruct((g[0][1][0], sum(s[1] for _, s, _ in g)), BF16) for g in groups],
        compiler_params=pltpu.CompilerParams(vmem_limit_bytes=VMEM_LIMIT),
    )(core, *(w for w, _, _ in flat))


def swap_core(value):
    return lax.ppermute(value, "core", [(0, 1), (1, 0)])


def gather_fsdp(own):
    count = lax.axis_size("fsdp")
    if count != 2:
        return [lax.all_gather(own, "fsdp", axis=0, tiled=True)]
    return [own, lax.ppermute(own, "fsdp", [(0, 1), (1, 0)])]


CHIPS = ("z", "y")
GROUP = ("z", "y", "core")


def gather_rows(own):
    return lax.all_gather(own, GROUP, axis=0, tiled=True)


def bits_of(axis):
    return range((lax.axis_size(axis) - 1).bit_length())


def swap_bit(value, axis, bit):
    return lax.ppermute(value, axis, [(i, i ^ (1 << bit)) for i in range(lax.axis_size(axis))])


def halve(value, axis, bit):
    side = (lax.axis_index(axis) >> bit) & 1
    keep = lax.dynamic_index_in_dim(value, side, 0, keepdims=False).astype(F32)
    send = lax.dynamic_index_in_dim(value, 1 - side, 0, keepdims=False).astype(BF16)
    return keep + swap_bit(send, axis, bit).astype(F32)


def steps_of(*axes):
    return [(axis, bit) for axis in axes for bit in bits_of(axis)]


def scatter(value, steps):
    for axis, bit in steps:
        value = halve(value.reshape((2, value.shape[0] // 2) + value.shape[1:]), axis, bit)
    return value


def scatter_fsdp(terms):
    return scatter(terms, [("fsdp", bit) for bit in reversed(bits_of("fsdp"))])


def scatter_chips(value):
    nz, ny = lax.axis_size("z"), lax.axis_size("y")
    value = value.reshape((nz, ny, value.shape[0] // (nz * ny)) + value.shape[1:])
    value = jnp.swapaxes(value, 0, 1)
    value = value.reshape((nz * ny,) + value.shape[2:])
    steps = [(axis, bit) for axis in ("y", "z") for bit in reversed(bits_of(axis))]
    return scatter(value, steps)[0]


def after(value, *earlier):
    return lax.optimization_barrier((value, *earlier))[0]


def on_device(
    tokens, encoded, cotangent, tgt_lengths, enc_lengths, deal,
    ln_self, ln_cross, ln_ffn, bias_table,
    self_query, self_key, self_value, self_output,
    cross_query, cross_key, cross_value, cross_output,
    ffn_inner, ffn_outer,
):
    core = lax.axis_index("core")
    fsdp = lax.axis_index("fsdp")
    n_fsdp = lax.axis_size("fsdp")
    chip = lax.axis_index(CHIPS)
    at = jnp.stack([chip, core, fsdp]).astype(jnp.int32)
    core_ref = core.reshape(1).astype(jnp.int32)
    rows, width = tokens.shape
    n = 2 * rows * lax.axis_size(CHIPS)
    side = width // n_fsdp
    hidden_half = ffn_inner.shape[1] // 2
    unit = hidden_half // n_fsdp
    wide, flat = ((ROWS, width), F32), ((ROWS, width), BF16)

    def column(weight):
        return (weight, (side, HALF), lambda c: (0, c))

    (qkv_own,) = pack(core_ref, [[column(w) for w in (self_query, self_key, self_value)]])
    w_qkv = gather_fsdp(qkv_own)
    if unit % 128 == 0:
        inner_items = [(ffn_inner, (side, unit), functools.partial(lambda o, c: (0, 2 * o + c), o)) for o in range(n_fsdp)]
    else:
        inner_units = ffn_inner.reshape(side, n_fsdp, 2, unit)
        inner_units = lax.dynamic_index_in_dim(inner_units, core, 2, keepdims=False).reshape(side, hidden_half)
        inner_items = [(inner_units, (side, hidden_half), lambda c: (0, 0))]
    out_own, cross_own, inner_own, outer_own = pack(
        core_ref,
        [
            [column(w) for w in (self_output, cross_output)],
            [column(w) for w in (cross_query, cross_key, cross_value)],
            inner_items,
            [(ffn_outer, (unit, width), lambda c: (c, 0))],
        ],
    )
    w_out = gather_fsdp(out_own)
    w_cross = gather_fsdp(cross_own)
    inner_own, outer_own = after((inner_own, outer_own), w_cross[-1])
    w_inner, w_outer = gather_fsdp(inner_own), gather_fsdp(outer_own)
    w_out_mate = [swap_core(w) for w in w_out]
    cot_mate = swap_core(cotangent)

    small = jnp.concatenate([ln_self, ln_cross, ln_ffn, bias_table.reshape(-1)], axis=0).astype(BF16)[None]
    small = gather_fsdp(small)
    if len(small) == 2:
        small = jnp.where(fsdp == 0, jnp.concatenate(small, axis=0), jnp.concatenate(small[::-1], axis=0))
    else:
        small = small[0]
    gain_self, gain_cross, gain_ffn = (
        small[:, i * side : (i + 1) * side].reshape(1, width).astype(F32) for i in range(3)
    )
    table = small[:, 3 * side :].reshape(BUCKETS, HEADS)
    table = lax.dynamic_slice_in_dim(table, core * LOCAL, LOCAL, 1).astype(F32)
    onehots = np.concatenate([QK_ONEHOT, KQ_ONEHOT], axis=0)
    biases = jnp.einsum("bh,tb->ht", table, onehots, precision=lax.Precision.HIGHEST)
    biases = jnp.pad(biases, ((0, 2), (0, 0)))
    bias_qk, bias_kq = biases[:, : 2 * ROWS], biases[:, 2 * ROWS :]

    xe = gather_rows(jnp.concatenate([tokens, encoded], axis=1))
    qkv, w_qkv, attn_self, low_self, lse_self = call(
        functools.partial(self_stage_kernel, len(w_qkv)), (at, tgt_lengths), (xe, gain_self, bias_qk, *w_qkv),
        [((3 * PAIRS, n, 128), BF16), ((width, 3 * HALF), BF16), ((ROWS, HALF), F32), ((ROWS, HALF), BF16), LANE],
        [TILES, ((ROWS, n), F32), *ATTEND(n)],
        2 * n * width * 3 * HALF + 4 * ROWS * n * HALF,
    )
    low_self_other = swap_core(low_self)

    x_mid, in_cross, q_cross, kv_cross, attn_cross, low_cross, lse_cross, w_so, w_co, w_cross = call(
        functools.partial(cross_stage_kernel, len(w_out)), (at, tgt_lengths, enc_lengths, deal),
        (xe, gain_cross, low_self, low_self_other, *w_out, *w_out_mate, *w_cross),
        [
            wide, flat, ((ROWS, HALF), BF16), ((2 * PAIRS, n, 128), BF16), ((ROWS, HALF), F32), ((ROWS, HALF), BF16), LANE,
            ((width, width), BF16), ((width, width), BF16), ((width, 3 * HALF), BF16),
        ],
        [((ROWS, n), F32), *ATTEND(n)],
        2 * n * width * 2 * HALF + 4 * ROWS * n * HALF,
    )
    low_cross_other = swap_core(low_cross)

    half_rows = ((rows, width), F32)
    x_late, in_ffn, hidden, d_pre, cot, out_keep, out_send, e_ffn = call(
        functools.partial(ffn_stage_kernel, len(w_inner)), (at,),
        (x_mid, gain_ffn, low_cross, low_cross_other, w_co, cotangent, cot_mate, *w_inner, *w_outer),
        [wide, flat, ((ROWS, hidden_half), BF16), ((ROWS, hidden_half), BF16), flat, half_rows, half_rows, wide],
        [((width, hidden_half), BF16), ((hidden_half, width), BF16), wide],
        8 * ROWS * width * hidden_half,
    )
    e_ffn_other = swap_core(e_ffn)
    ffn_out = (
        [((side, 4 * width), F32), ((side, 4 * width), BF16)]
        if n_fsdp == 2
        else [((hidden_half, width), F32), ((width, hidden_half), F32)]
    )
    first = call(
        functools.partial(ffn_grads_kernel, n_fsdp), (at,), (hidden, cot, in_ffn, d_pre), ffn_out, [],
        4 * ROWS * width * hidden_half,
    )
    if n_fsdp == 2:
        first_other = lax.ppermute(first[1], "fsdp", [(0, 1), (1, 0)])
        e_ffn = after(e_ffn, first[1])
    output = out_keep + swap_core(out_send)

    grad_late, late_low, d_gain_ffn, dq_cross, dkv_part, e_cross = call(
        cross_grad_stage_kernel, (at, tgt_lengths, enc_lengths, deal),
        (e_ffn, e_ffn_other, x_late, gain_ffn, cot, w_co, q_cross, attn_cross, lse_cross, kv_cross, w_cross),
        [wide, flat, ((1, width), F32), ((ROWS, HALF), BF16), ((n, 2 * HALF), BF16), wide],
        [((ROWS, HALF), BF16), STACK, STACK, COLUMN, COLUMN, COLUMN, LANE],
        10 * ROWS * n * HALF,
    )
    e_cross_other = swap_core(e_cross)

    grad_mid, mid_low, d_gain_cross, go_self, message = call(
        self_grad_start_kernel, (at,), (e_cross, e_cross_other, x_mid, gain_cross, grad_late, w_so, attn_self, lse_self),
        [wide, flat, ((1, width), F32), ((ROWS, HALF), BF16), ((rows + 16, width), BF16)], [LANE],
        2 * ROWS * width * HALF,
    )
    message = lax.all_gather(message, GROUP, axis=0)
    (second,) = call(
        projection_grads_kernel, (at,),
        (low_cross, low_cross_other, late_low, in_cross, dq_cross, low_self, low_self_other, mid_low),
        [((width, 3 * HALF), BF16)], [], 6 * ROWS * width * HALF,
    )
    dq_self, dist = call(
        self_query_grad_kernel, (at, tgt_lengths), (bias_qk, qkv, after(go_self, second), attn_self, lse_self),
        [((ROWS, HALF), BF16), ((8, 2 * ROWS), F32)],
        [TILES, STACK, STACK, COLUMN, COLUMN, COLUMN, TILES, LANE],
        6 * ROWS * n * HALF,
    )
    x_chip = lax.dynamic_slice(xe, (chip * ROWS, 0), (ROWS, width))
    e_chip = lax.dynamic_slice(xe, (chip * ROWS, width), (ROWS, width))
    d_table = jnp.einsum("ht,tb->bh", dist[:LOCAL], QK_ONEHOT, precision=lax.Precision.HIGHEST)
    d_table = jnp.zeros((BUCKETS, 2, LOCAL), F32).at[:, core].set(d_table).reshape(n_fsdp, -1, HEADS)
    d_table = jnp.pad(d_table, ((0, 0), (0, side - d_table.shape[1]), (0, 0))).reshape(width, HEADS)
    none = jnp.zeros((width, 1), F32)
    small = [none, 0.5 * d_gain_cross.reshape(width, 1), 0.5 * d_gain_ffn.reshape(width, 1), d_table]
    small = jnp.pad(jnp.concatenate(small, axis=1), ((0, 0), (0, 128 - 3 - HEADS)))

    dkv_cross = scatter_chips(dkv_part)
    d_ckv, enc_keep, enc_send = call(
        encoder_grads_kernel, (at,), (dkv_cross, e_chip, w_cross),
        [((width, 2 * HALF), BF16), half_rows, half_rows], [((ROWS, 2 * HALF), BF16), wide],
        8 * ROWS * width * HALF,
    )
    enc_grad = enc_keep + swap_core(enc_send)

    steps = steps_of("y", "z")
    if n_fsdp == 2:
        first = first[0] + first_other.astype(F32)
    else:
        outer = first[0].reshape(n_fsdp, 2, side, width)
        first = jnp.concatenate([outer[:, 0], outer[:, 1], first[1].reshape(n_fsdp, side, hidden_half)], axis=2)
        first = scatter_fsdp(first)[0]
    second = scatter_fsdp(after(second, first).reshape(n_fsdp, side, -1))[0]
    first = scatter(first, steps[:1])
    second = scatter(second, steps[:1])

    d_qkv, e_keep, e_send = call(
        self_key_stage_kernel, (at, tgt_lengths),
        (bias_kq, qkv, after(message, dq_self), w_so, dq_self, w_qkv, x_chip, gain_self, d_ckv, small),
        [((width, 5 * HALF + 128), BF16), half_rows, half_rows],
        [
            ((PAIRS, n, 128), BF16), ((n // ROWS, 16, ROWS), F32), TILES, STACK, STACK, COLUMN, COLUMN,
            ((ROWS, 3 * HALF), BF16), flat, wide,
        ],
        8 * ROWS * n * HALF,
    )
    (grad_tokens,) = call(
        token_grads_kernel, (at,), (e_keep, swap_core(e_send), tokens, gain_self, grad_mid),
        [half_rows], [], 10 * rows * width,
    )

    def reduced(joined):
        count = n_fsdp * lax.axis_size(CHIPS)
        joined = joined.reshape(count, -1, joined.shape[1])
        terms = lax.all_to_all(joined, ("fsdp",) + CHIPS, 0, 0, tiled=True)
        total = jnp.sum(terms.astype(F32), axis=0).astype(BF16)
        copies = jnp.broadcast_to(total[None], (lax.axis_size(CHIPS),) + total.shape)
        own = lax.all_to_all(copies, CHIPS, 0, 0, tiled=True).reshape(-1, joined.shape[2])
        return own, swap_core(own)

    third = reduced(d_qkv)
    first = scatter(first, steps[1:]).astype(BF16)
    second = scatter(second, steps[1:]).astype(BF16)
    first = lax.all_gather(first, GROUP, axis=0)
    second = lax.all_gather(second, GROUP, axis=0)

    nz, ny = lax.axis_size("z"), lax.axis_size("y")
    order = []
    for z in range(nz):
        for y in range(ny):
            place = 0
            for axis, bit in steps:
                place = 2 * place + (((z if axis == "z" else y) >> bit) & 1)
            order += [(0, place), (1, place)]
    matrix = ((side, width), F32)
    g_co, g_cq, g_so = call(
        functools.partial(finish_gathered_kernel, order), (), (second,), [matrix] * 3, [], 6 * side * width
    )
    g_sq, g_sk, g_sv, g_ck, g_cv = call(finish_columns_kernel, (at,), third, [matrix] * 5, [], 10 * side * width)
    if n_fsdp == 2:
        g_outer, g_inner = call(
            functools.partial(finish_ffn_kernel, order), (), (first,),
            [(ffn_outer.shape, F32), (ffn_inner.shape, F32)], [], 8 * side * width,
        )
    else:
        places = np.argsort([2 * place + c for c, place in order])
        first = first[places].reshape(nz * ny, 2, -1, first.shape[2])
        pair = jnp.swapaxes(first, 0, 1).reshape(2, side, -1).astype(F32)
        g_outer = pair[:, :, : 2 * width].reshape(2, side, 2, width)
        g_outer = jnp.swapaxes(g_outer, 1, 2).reshape(ffn_outer.shape)
        g_inner = jnp.transpose(pair[:, :, 2 * width :].reshape(2, side, n_fsdp, unit), (1, 2, 0, 3))
        g_inner = g_inner.reshape(ffn_inner.shape)
    vectors = third[0][:, -128:].astype(F32) + third[1][:, -128:].astype(F32)

    return (
        output, grad_tokens, enc_grad,
        vectors[:, 0], vectors[:, 1], vectors[:, 2], vectors[: bias_table.shape[0], 3 : 3 + HEADS],
        g_sq, g_sk, g_sv, g_so, g_cq, g_ck, g_cv, g_co, g_inner, g_outer,
    )


def solution(mesh):
    n_ctx, n_fsdp = mesh.shape["ctx"], mesh.shape["fsdp"]
    n_z = 4
    grid = Mesh(mesh.devices.reshape(n_z, n_ctx // (2 * n_z), 2, n_fsdp), ("z", "y", "core", "fsdp"))
    by_rows = P(("fsdp", "z", "y", "core"), None)
    split = P("fsdp", None)
    vector = P("fsdp")
    in_specs = (by_rows,) * 3 + (split,) * 3 + (vector,) * 3 + (split,) * 11
    out_specs = (by_rows,) * 3 + (vector,) * 3 + (split,) * 11
    return jax.shard_map(on_device, mesh=grid, in_specs=in_specs, out_specs=out_specs, check_vma=False)
```

```python
import functools
import math

import jax
import jax.numpy as jnp
import numpy as np
from jax import lax
from jax.experimental import pallas as pl
from jax.experimental.pallas import tpu as pltpu
from jax.sharding import Mesh
from jax.sharding import PartitionSpec as P

HEADS = 12
HEAD_DIM = 64
BUCKETS = 32
EPS = 1e-06
NEG = -1e30
GELU_C = 0.7978845608028654
GELU_A = 0.044715

LOCAL = HEADS // 2
PAIRS = LOCAL // 2
HALF = LOCAL * HEAD_DIM
ROWS = 256
VMEM_LIMIT = 56 << 20

F32 = jnp.float32
BF16 = jnp.bfloat16


def bucket_edges():
    edges = []
    for level in range(1, 16):
        distance = 16
        while int(math.log(distance / 16.0) / math.log(8.0) * 16.0) < level:
            distance += 1
        edges.append(distance)
    return edges


def buckets_of(distances):
    clipped = np.maximum(np.asarray(distances), 0)
    large = np.full(clipped.shape, 16)
    for edge in bucket_edges():
        large = large + (clipped >= edge)
    return np.where(clipped < 16, clipped, large)


LANES = np.arange(2 * ROWS)
QK_DISTANCE = np.where(LANES <= ROWS, ROWS - LANES, 3 * ROWS - LANES)
KQ_DISTANCE = LANES
QK_ONEHOT = np.eye(BUCKETS, dtype=np.float32)[buckets_of(QK_DISTANCE)]
KQ_ONEHOT = np.eye(BUCKETS, dtype=np.float32)[buckets_of(KQ_DISTANCE)]


def dot_nt(left, right):
    return lax.dot_general(left, right, (((1,), (1,)), ((), ())), preferred_element_type=F32)


def dot_tn(left, right):
    return lax.dot_general(left, right, (((0,), (0,)), ((), ())), preferred_element_type=F32)


def dot_nn(left, right):
    return lax.dot_general(left, right, (((1,), (0,)), ((), ())), preferred_element_type=F32)


def spans(ref):
    starts, ends, at = [], [], jnp.int32(0)
    for i in range(ref.shape[1]):
        starts.append(at)
        at = at + ref[0, i]
        ends.append(at)
    return starts, ends


def seg_of(index, ends):
    found = jnp.zeros(index.shape, jnp.int32)
    for end in ends[:-1]:
        found = found + (index >= end).astype(jnp.int32)
    return found


def iota(shape, axis):
    return lax.broadcasted_iota(jnp.int32, shape, axis)


def split_pair(pair):
    low = iota(pair.shape, 1) < HEAD_DIM
    zero = jnp.zeros_like(pair)
    return jnp.concatenate([jnp.where(low, pair, zero), jnp.where(low, zero, pair)], axis=0)


def join_pair(both):
    rows = both.shape[0] // 2
    low = iota((rows, both.shape[1]), 1) < HEAD_DIM
    return jnp.where(low, both[:rows], both[rows:])


def tiles_kernel(bias_ref, tiles_ref):
    def head(h, c):
        for which in range(2):
            row = bias_ref[pl.ds(8 * which + h, 1), :]
            rolled = pltpu.roll(jnp.broadcast_to(row, (ROWS, 2 * ROWS)), 0, 1, stride=1, stride_axis=0)
            first, second = (1, 2) if which == 0 else (2, 1)
            tiles_ref[which, first, h] = rolled[:, :ROWS].astype(BF16)
            tiles_ref[which, second, h] = rolled[:, ROWS:].astype(BF16)
            tiles_ref[which, 0, h] = jnp.broadcast_to(row[:, 2 * ROWS - 1 :], (ROWS, ROWS)).astype(BF16)
        return c

    lax.fori_loop(0, LOCAL, head, 0)


def lanes_of(p):
    return slice(p * 128, p * 128 + 128) if isinstance(p, int) else pl.ds(pl.multiple_of(p * 128, 128), 128)


def each_pair(body):
    for p in range(PAIRS):
        body(p)


def rms_inverse(value):
    return lax.rsqrt(jnp.mean(value * value, axis=-1, keepdims=True) + EPS)


def together(n):
    return PAIRS if n <= 2048 else 1


def attend(queries, keys, values, visit_scores, visit, s_scr, mx_scr, l_scr, acc_scr, qs, o_ref, low_ref, lse_ref):
    count = s_scr.shape[0]
    lse_ref[...] = jnp.zeros_like(lse_ref)
    lane = iota((ROWS, 128), 1)

    def group(g):
        for c in range(count):
            qs[c] = split_pair(queries(g * count + c))
        mx_scr[...] = jnp.full_like(mx_scr, NEG)

        def scores(j, extra):
            at = pl.multiple_of(j * ROWS, ROWS)
            raws = [dot_nt(qs[c], keys(g * count + c, at)) for c in range(count)]
            for c in range(count):
                for i in range(2):
                    rows = slice(i * ROWS, (i + 1) * ROWS)
                    value = extra(2 * (g * count + c) + i, raws[c][rows])
                    s_scr[c, rows, pl.ds(at, ROWS)] = value
                    mx_scr[c, rows] = jnp.maximum(mx_scr[c, rows], jnp.maximum(value[:, :128], value[:, 128:]))

        visit_scores(scores)
        for c in range(count):
            mx_scr[c] = jnp.broadcast_to(jnp.max(mx_scr[c], axis=1, keepdims=True), mx_scr.shape[1:])
        l_scr[...] = jnp.zeros_like(l_scr)
        acc_scr[...] = jnp.zeros_like(acc_scr)

        def weigh(j):
            at = pl.multiple_of(j * ROWS, ROWS)
            for c in range(count):
                weights = jnp.exp(s_scr[c, :, pl.ds(at, ROWS)] - mx_scr[c, :, :1])
                l_scr[c] += weights[:, :128] + weights[:, 128:]
                acc_scr[c] += dot_nn(weights.astype(BF16), values(g * count + c, at))

        visit(weigh)
        for c in range(count):
            p = g * count + c
            total = jnp.sum(l_scr[c], axis=1, keepdims=True)
            result = join_pair(acc_scr[c] / total)
            o_ref[:, lanes_of(p)] = result
            low_ref[:, lanes_of(p)] = result.astype(BF16)
            both = mx_scr[c, :, :1] + jnp.log(total)
            lse = jnp.where(lane == 2 * p, both[:ROWS], lse_ref[...])
            lse_ref[...] = jnp.where(lane == 2 * p + 1, both[ROWS:], lse)

    if count == PAIRS:
        group(0)
    else:
        lax.fori_loop(0, PAIRS // count, lambda g, c: (group(g), c)[1], 0)


ATTEND = lambda n: [
    ((together(n), 2 * ROWS, n), F32), ((together(n), 2 * ROWS, 128), F32), ((together(n), 2 * ROWS, 128), F32),
    ((together(n), 2 * ROWS, 128), F32), ((together(n), 2 * ROWS, 128), BF16),
]


def set_rows(target, parts, side):
    if len(parts) == 1:
        target[...] = parts[0][...]
        return
    rows = parts[0].shape[0]
    target[pl.ds(pl.multiple_of(side * rows, rows), rows), :] = parts[0][...]
    target[pl.ds(pl.multiple_of((1 - side) * rows, rows), rows), :] = parts[1][...]


def first_of(base, ends):
    first = jnp.int32(0)
    for end in ends[:-1]:
        first = jnp.where(base >= end, end, first)
    return first


def self_stage_kernel(n_parts, at_ref, len_ref, xe_ref, gain_ref, tiles, *refs):
    parts, refs = refs[:n_parts], refs[n_parts:]
    qkv_ref, w_ref, o_ref, low_ref, lse_ref, s_scr, mx_scr, l_scr, acc_scr, qs = refs
    chip, side = at_ref[0], at_ref[2]
    set_rows(w_ref, parts, side)
    width = w_ref.shape[0]
    step = 512

    def body(i, c):
        at = pl.multiple_of(i * step, step)
        wide = xe_ref[pl.ds(at, step), :width].astype(F32)
        value = (wide * rms_inverse(wide) * gain_ref[...]).astype(BF16)
        result = dot_nn(value, w_ref[...])
        for j in range(qkv_ref.shape[0]):
            qkv_ref[j, pl.ds(at, step), :] = result[:, 128 * j : 128 * j + 128].astype(BF16)
        return c

    lax.fori_loop(0, xe_ref.shape[0] // step, body, 0)

    starts, ends = spans(len_ref)
    base = pl.multiple_of(chip * ROWS, ROWS)
    j_min = first_of(base, ends) // ROWS
    full_from = first_of(base + ROWS - 1, ends)
    q_row = base + iota((ROWS, 1), 0)
    q_seg = seg_of(q_row, ends)

    def visit(block):
        lax.fori_loop(j_min, chip + 1, lambda j, c: (block(j), c)[1], 0)

    def visit_scores(block):
        def body(j, c):
            at = pl.multiple_of(j * ROWS, ROWS)
            plain = (at >= full_from) & (j < chip - 1)

            @pl.when(plain)
            def _():
                block(j, lambda h, raw: raw + tiles[0, 0, h, :1, :1].astype(F32))

            @pl.when(jnp.logical_not(plain))
            def _():
                k_row = at + iota((1, ROWS), 1)
                masked = jnp.where((q_seg == seg_of(k_row, ends)) & (k_row <= q_row), 0.0, NEG)
                tile = jnp.maximum(j - chip + 2, 0)
                block(j, lambda h, raw: raw + (tiles[0, tile, h].astype(F32) + masked))

            return c

        lax.fori_loop(j_min, chip + 1, body, 0)

    attend(
        lambda p: qkv_ref[p, pl.ds(base, ROWS), :],
        lambda p, at: qkv_ref[PAIRS + p, pl.ds(at, ROWS), :],
        lambda p, at: qkv_ref[2 * PAIRS + p, pl.ds(at, ROWS), :],
        visit_scores, visit, s_scr, mx_scr, l_scr, acc_scr, qs, o_ref, low_ref, lse_ref,
    )


def add_heads(low_ref, other_ref, w_ref, core):
    own = pl.ds(pl.multiple_of(core * HALF, HALF), HALF)
    other = pl.ds(pl.multiple_of((1 - core) * HALF, HALF), HALF)
    return dot_nn(low_ref[...], w_ref[own, :]) + dot_nn(other_ref[...], w_ref[other, :])


def cross_stage_kernel(n_parts, at_ref, len_ref, enc_ref, deal_ref, xe_ref, gain_ref, low_ref, other_ref, *refs):
    outs, mates, parts, refs = refs[:n_parts], refs[n_parts : 2 * n_parts], refs[2 * n_parts : 3 * n_parts], refs[3 * n_parts :]
    mid_ref, in_ref, q_ref, kv_ref, o_ref, low2_ref, lse_ref, so_ref, co_ref, wc_ref, refs = *refs[:10], refs[10:]
    s_scr, mx_scr, l_scr, acc_scr, qs = refs
    chip, core, side = at_ref[0], at_ref[1], at_ref[2]
    set_rows(wc_ref, parts, side)
    for pieces, column in ((outs, core), (mates, 1 - core)):
        lanes = pl.ds(pl.multiple_of(column * HALF, 128), HALF)
        for i, piece in enumerate(pieces):
            rows = piece.shape[0]
            at = pl.multiple_of((side if i == 0 else 1 - side) * rows, rows) if n_parts > 1 else 0
            so_ref[pl.ds(at, rows), lanes] = piece[:, :HALF]
            co_ref[pl.ds(at, rows), lanes] = piece[:, HALF:]
    width = so_ref.shape[0]
    base = pl.multiple_of(chip * ROWS, ROWS)
    mid = xe_ref[pl.ds(base, ROWS), :width].astype(F32) + add_heads(low_ref, other_ref, so_ref, core)
    mid_ref[...] = mid
    normed = (mid * rms_inverse(mid) * gain_ref[...]).astype(BF16)
    in_ref[...] = normed
    q_ref[...] = dot_nn(normed, wc_ref[:, :HALF]).astype(BF16)
    step = 512

    def body(i, c):
        at = pl.multiple_of(i * step, step)
        result = dot_nn(xe_ref[pl.ds(at, step), width:], wc_ref[:, HALF:])
        for j in range(kv_ref.shape[0]):
            kv_ref[j, pl.ds(at, step), :] = result[:, 128 * j : 128 * j + 128].astype(BF16)
        return c

    lax.fori_loop(0, xe_ref.shape[0] // step, body, 0)
    wanted, q_pair, e_ends = cross_flags(chip, len_ref, enc_ref, deal_ref)

    def visit(block):
        def body(j, c):
            @pl.when(wanted(j * ROWS))
            def _():
                block(j)

            return c

        lax.fori_loop(0, kv_ref.shape[1] // ROWS, body, 0)

    def visit_scores(block):
        def with_mask(j):
            masked = jnp.where(q_pair == seg_of(j * ROWS + iota((1, ROWS), 1), e_ends), 0.0, NEG)
            block(j, lambda h, raw: raw + masked)

        visit(with_mask)

    attend(
        lambda p: q_ref[:, lanes_of(p)],
        lambda p, at: kv_ref[p, pl.ds(at, ROWS), :],
        lambda p, at: kv_ref[PAIRS + p, pl.ds(at, ROWS), :],
        visit_scores, visit, s_scr, mx_scr, l_scr, acc_scr, qs, o_ref, low2_ref, lse_ref,
    )


def gelu_parts(value):
    tangent = jnp.tanh(GELU_C * (value + GELU_A * value * value * value))
    result = 0.5 * value * (1.0 + tangent)
    slope = 0.5 * (1.0 + tangent) + 0.5 * value * (1.0 - tangent * tangent) * GELU_C * (
        1.0 + 3.0 * GELU_A * value * value
    )
    return (result, slope)


def own_rows(core, rows):
    return pl.ds(pl.multiple_of(core * rows, rows), rows)


def ffn_stage_kernel(n_parts, at_ref, mid_ref, gain_ref, low_ref, other_ref, co_ref, cot_ref, mate_ref, *refs):
    inner, outer, refs = refs[:n_parts], refs[n_parts : 2 * n_parts], refs[2 * n_parts :]
    late_ref, in_ref, hid_ref, dpre_ref, cot_out, keep_ref, send_ref, e_ref, wi_ref, wo_ref, part_scr = refs
    core, side = at_ref[1], at_ref[2]
    rows = cot_ref.shape[0]
    set_rows(wi_ref, inner, side)
    set_rows(wo_ref, outer, side)
    cot_out[own_rows(core, rows), :] = cot_ref[...]
    cot_out[own_rows(1 - core, rows), :] = mate_ref[...]
    late = mid_ref[...] + add_heads(low_ref, other_ref, co_ref, core)
    late_ref[...] = late
    normed = (late * rms_inverse(late) * gain_ref[...]).astype(BF16)
    in_ref[...] = normed
    columns = 512

    def body(i, c):
        at = pl.multiple_of(i * columns, columns)
        activated, slope = gelu_parts(dot_nn(normed, wi_ref[:, pl.ds(at, columns)]))
        hid_ref[:, pl.ds(at, columns)] = activated.astype(BF16)
        grads = dot_nt(cot_out[...], wo_ref[pl.ds(at, columns), :])
        dpre_ref[:, pl.ds(at, columns)] = (grads * slope).astype(BF16)
        return c

    lax.fori_loop(0, wi_ref.shape[1] // columns, body, 0)
    e_ref[...] = dot_nt(dpre_ref[...], wi_ref[...])
    part_scr[...] = dot_nn(hid_ref[...], wo_ref[...])
    keep_ref[...] = part_scr[own_rows(core, rows), :] + late_ref[own_rows(core, rows), :]
    send_ref[...] = part_scr[own_rows(1 - core, rows), :]


def ffn_grads_kernel(n_sides, at_ref, hid_ref, cot_ref, in_ref, dpre_ref, *outs):
    side = at_ref[2]
    rows = in_ref.shape[1] // n_sides
    width = cot_ref.shape[1]
    if n_sides != 2:
        outs[0][...] = dot_tn(hid_ref[...], cot_ref[...])
        outs[1][...] = dot_tn(in_ref[...], dpre_ref[...])
        return
    keep_ref, send_ref = outs
    for owner in range(2):
        for mine, target in ((True, keep_ref), (False, send_ref)):

            @pl.when((side == owner) == mine)
            def _():
                for part in range(2):
                    units = slice((2 * owner + part) * rows, (2 * owner + part + 1) * rows)
                    block = dot_tn(hid_ref[:, units], cot_ref[...])
                    target[:, part * width : (part + 1) * width] = block.astype(target.dtype)
                block = dot_tn(in_ref[:, owner * rows : (owner + 1) * rows], dpre_ref[...])
                target[:, 2 * width :] = block.astype(target.dtype)


def norm_grad(value, gain, grad):
    inverse = rms_inverse(value)
    scaled = grad * gain
    cubed = inverse * inverse * inverse
    dvalue = inverse * scaled - value * cubed * jnp.mean(scaled * value, axis=-1, keepdims=True)
    return dvalue, jnp.sum(grad * value * inverse, axis=0, keepdims=True)


def cross_flags(chip, len_ref, enc_ref, deal_ref):
    starts, ends = spans(len_ref)
    e_starts, e_ends = spans(enc_ref)
    base = chip * ROWS
    ranges = []
    for i in range(len(ends)):
        live = (starts[i] < base + ROWS) & (ends[i] > base)
        low, high = jnp.int32(0), jnp.int32(0)
        for e in range(len(e_ends)):
            hit = deal_ref[0, i] == e
            low = jnp.where(hit, e_starts[e], low)
            high = jnp.where(hit, e_ends[e], high)
        ranges.append((live, low, high))

    def wanted(at):
        found = jnp.bool_(False)
        for live, low, high in ranges:
            found = found | (live & (low < at + ROWS) & (high > at))
        return found

    q_seg = seg_of(base + iota((ROWS, 1), 0), ends)
    q_pair = jnp.zeros((ROWS, 1), jnp.int32)
    for i in range(len(ends)):
        q_pair = q_pair + jnp.where(q_seg == i, deal_ref[0, i], 0)
    return wanted, q_pair, e_ends


def row_stats(go_ref, o_ref, lse_ref, gs, lse_scr, delta_scr, stat_scr):
    lane = iota((ROWS, 128), 1)
    low = lane < HEAD_DIM
    stat_scr[...] = lse_ref[...]

    def pair(p):
        grads = go_ref[:, lanes_of(p)]
        gs[p] = split_pair(grads)
        product = grads.astype(F32) * o_ref[:, lanes_of(p)]
        for i in range(2):
            part = jnp.where(low if i == 0 else ~low, product, 0.0)
            delta = jnp.sum(part, axis=1, keepdims=True)
            rows = slice(i * ROWS, (i + 1) * ROWS)
            delta_scr[p, rows] = jnp.broadcast_to(delta, (ROWS, 128))
            lse_scr[p, rows] = jnp.broadcast_to(
                jnp.sum(jnp.where(lane == 2 * p + i, lse_ref[...], 0.0), axis=1, keepdims=True), (ROWS, 128)
            )
            stat_scr[...] = jnp.where(lane == 8 + 2 * p + i, delta, stat_scr[...])

    each_pair(pair)


def self_query_grad_kernel(
    at_ref, len_ref, tiles, qkv_ref, go_ref, o_ref, lse_ref, dq_ref, dist_ref,
    qs, gs, lse_scr, delta_scr, dq_scr, ds_scr, far_scr, stat_scr,
):
    chip = at_ref[0]
    starts, ends = spans(len_ref)
    base = pl.multiple_of(chip * ROWS, ROWS)
    first = first_of(base, ends)
    row_stats(go_ref, o_ref, lse_ref, gs, lse_scr, delta_scr, stat_scr)

    def start(p):
        qs[p] = split_pair(qkv_ref[p, pl.ds(base, ROWS), :])

    each_pair(start)
    dq_scr[...] = jnp.zeros_like(dq_scr)
    ds_scr[...] = jnp.zeros_like(ds_scr)
    far_scr[...] = jnp.zeros_like(far_scr)
    full_from = first_of(base + ROWS - 1, ends)
    q_row = base + iota((ROWS, 1), 0)
    q_seg = seg_of(q_row, ends)

    def block(j, _):
        at = pl.multiple_of(j * ROWS, ROWS)
        plain = (at >= full_from) & (j < chip - 1)

        def gradients(extra, near):
            raws = [dot_nt(qs[p], qkv_ref[PAIRS + p, pl.ds(at, ROWS), :]) for p in range(PAIRS)]
            dprobs = [dot_nt(gs[p], qkv_ref[2 * PAIRS + p, pl.ds(at, ROWS), :]) for p in range(PAIRS)]
            for p in range(PAIRS):
                grads = []
                for i in range(2):
                    h = 2 * p + i
                    rows = slice(i * ROWS, (i + 1) * ROWS)
                    probs = jnp.exp(extra(h, raws[p][rows]) - lse_scr[p, rows, :1])
                    ds = (probs * (dprobs[p][rows] - delta_scr[p, rows, :1])).astype(BF16)
                    if near is None:
                        far_scr[h] += jnp.sum(ds.astype(F32).reshape(ROWS // 8, 8, ROWS), axis=0)
                    else:
                        ds_scr[near, h] += ds.astype(F32)
                    grads.append(ds)
                dq_scr[p] += dot_nn(jnp.concatenate(grads, axis=0), qkv_ref[PAIRS + p, pl.ds(at, ROWS), :])

        @pl.when(plain)
        def _():
            gradients(lambda h, raw: raw + tiles[0, 0, h, :1, :1].astype(F32), None)

        @pl.when(jnp.logical_not(plain))
        def _():
            k_row = at + iota((1, ROWS), 1)
            masked = jnp.where((q_seg == seg_of(k_row, ends)) & (k_row <= q_row), 0.0, NEG)
            tile = jnp.maximum(j - chip + 2, 0)
            gradients(lambda h, raw: raw + (tiles[0, tile, h].astype(F32) + masked), tile)

        return 0

    lax.fori_loop(first // ROWS, chip + 1, block, 0)
    dist_ref[...] = jnp.zeros_like(dist_ref)
    lanes = iota((1, 2 * ROWS), 1)
    for p in range(PAIRS):
        dq_ref[:, 128 * p : 128 * p + 128] = join_pair(dq_scr[p]).astype(BF16)

    def fold(h, c):
        folded = jnp.concatenate([ds_scr[1, h], ds_scr[2, h]], axis=1)
        rows = ROWS
        while rows > 1:
            rows //= 2
            folded = folded[:rows] + pltpu.roll(folded[rows:], 2 * ROWS - rows, 1)
        far = jnp.sum(ds_scr[0, h], axis=0, keepdims=True) + jnp.sum(far_scr[h], axis=0, keepdims=True)
        far = jnp.sum(far, axis=1, keepdims=True)
        dist_ref[pl.ds(h, 1), :] = folded + jnp.where(lanes == 2 * ROWS - 1, far, 0.0)
        return c

    lax.fori_loop(0, LOCAL, fold, 0)


def self_key_stage_kernel(
    n_sides, at_ref, len_ref, tiles, qkv_ref, message_ref, so_ref, dq_ref, w_ref, x_ref, gain_ref, small_ref,
    keep_ref, send_ref, *refs,
):
    *outs, go_ref, stat_ref, ks, vs, dk_scr, dv_scr, dqkv_scr, h_scr, e_scr, grads_ref = refs
    chip, core = at_ref[0], at_ref[1]
    starts, ends = spans(len_ref)
    base = pl.multiple_of(chip * ROWS, ROWS)
    last = ends[-1]
    for end in reversed(ends[:-1]):
        last = jnp.where(base + ROWS - 1 < end, end, last)
    stop = (last - 1) // ROWS + 1
    full_to = ends[-1]
    for end in reversed(ends[:-1]):
        full_to = jnp.where(base < end, end, full_to)
    heads = own_rows(core, HALF)
    half = ROWS // 2

    def receive(i, c):
        both = [message_ref[2 * i + e, :half, :] for e in range(2)]
        result = dot_nt(jnp.concatenate(both, axis=0), so_ref[heads, :])
        for p in range(PAIRS):
            go_ref[p, pl.ds(pl.multiple_of(i * ROWS, ROWS), ROWS), :] = result[:, 128 * p : 128 * p + 128].astype(BF16)
        parts = message_ref[2 * i + core, half:, :].astype(F32)
        stat_ref[i] = parts[:, :ROWS] + parts[:, ROWS : 2 * ROWS] + parts[:, 2 * ROWS :]
        return c

    lax.fori_loop(chip, stop, receive, 0)

    def start(p):
        ks[p] = split_pair(qkv_ref[PAIRS + p, pl.ds(base, ROWS), :])
        vs[p] = split_pair(qkv_ref[2 * PAIRS + p, pl.ds(base, ROWS), :])

    each_pair(start)
    dk_scr[...] = jnp.zeros_like(dk_scr)
    dv_scr[...] = jnp.zeros_like(dv_scr)
    k_row = base + iota((ROWS, 1), 0)
    k_seg = seg_of(k_row, ends)

    def block(i, _):
        at = pl.multiple_of(i * ROWS, ROWS)
        plain = (at + ROWS <= full_to) & (i > chip + 1)

        def gradients(extra):
            raws = [dot_nt(ks[p], qkv_ref[p, pl.ds(at, ROWS), :]) for p in range(PAIRS)]
            dprobs = [dot_nt(vs[p], go_ref[p, pl.ds(at, ROWS), :]) for p in range(PAIRS)]
            for p in range(PAIRS):
                weights, dscores = [], []
                for e in range(2):
                    rows = slice(e * ROWS, (e + 1) * ROWS)
                    h = 2 * p + e
                    probs = jnp.exp(extra(h, raws[p][rows]) - stat_ref[i, h : h + 1, :])
                    weights.append(probs.astype(BF16))
                    dscores.append((probs * (dprobs[p][rows] - stat_ref[i, 8 + h : 9 + h, :])).astype(BF16))
                dv_scr[p] += dot_nn(jnp.concatenate(weights, axis=0), go_ref[p, pl.ds(at, ROWS), :])
                dk_scr[p] += dot_nn(jnp.concatenate(dscores, axis=0), qkv_ref[p, pl.ds(at, ROWS), :])

        @pl.when(plain)
        def _():
            gradients(lambda h, raw: raw + tiles[1, 0, h, :1, :1].astype(F32))

        @pl.when(jnp.logical_not(plain))
        def _():
            q_row = at + iota((1, ROWS), 1)
            masked = jnp.where((k_seg == seg_of(q_row, ends)) & (k_row <= q_row), 0.0, NEG)
            tile = jnp.maximum(2 - (i - chip), 0)
            gradients(lambda h, raw: raw + (tiles[1, tile, h].astype(F32) + masked))

        return 0

    lax.fori_loop(chip, stop, block, 0)
    dqkv_scr[:, :HALF] = dq_ref[...]
    for p in range(PAIRS):
        dqkv_scr[:, HALF + 128 * p : HALF + 128 * p + 128] = join_pair(dk_scr[p]).astype(BF16)
        dqkv_scr[:, 2 * HALF + 128 * p : 2 * HALF + 128 * p + 128] = join_pair(dv_scr[p]).astype(BF16)
    e_scr[...] = dot_nt(dqkv_scr[...], w_ref[...])
    keep_ref[...] = e_scr[own_rows(core, half), :]
    send_ref[...] = e_scr[own_rows(1 - core, half), :]
    wide = x_ref[...].astype(F32)
    scaled = wide * rms_inverse(wide)
    h_scr[...] = (scaled * gain_ref[...]).astype(BF16)
    dgain = jnp.sum(e_scr[...] * scaled, axis=0, keepdims=True)
    dgain = jnp.transpose(jnp.where(iota((128, dgain.shape[1]), 0) == 0, dgain, 0.0))
    columns = grads_ref.shape[1]
    grads_ref[:, columns - 128 :] = (small_ref[...] + dgain).astype(BF16)
    step = 256
    for i in range(0, h_scr.shape[1], step):
        grads_ref[i : i + step, : 2 * HALF] = dot_tn(h_scr[:, i : i + step], dqkv_scr[:, HALF:]).astype(BF16)
    give(n_sides, at_ref[2], grads_ref, outs)


def cross_grad_stage_kernel(
    at_ref, len_ref, enc_ref, deal_ref, place_ref,
    e_ref, other_ref, late_ref, gain_ref, cot_ref, co_ref, q_ref, o_ref, lse_ref, kv_ref, wc_ref,
    grad_ref, low_ref, dgain_ref, dq_ref, keep_ref, send_ref, part_ref,
    go_ref, qs, gs, lse_scr, delta_scr, dq_scr, stat_scr, block_scr,
):
    chip, core = at_ref[0], at_ref[1]
    dvalue, dgain = norm_grad(late_ref[...], gain_ref[...], e_ref[...] + other_ref[...])
    dgain_ref[...] = dgain
    grad = cot_ref[...].astype(F32) + dvalue
    grad_ref[...] = grad
    low_ref[...] = grad.astype(BF16)
    go_ref[...] = dot_nt(low_ref[...], co_ref[own_rows(core, HALF), :]).astype(BF16)
    wanted, q_pair, e_ends = cross_flags(chip, len_ref, enc_ref, deal_ref)
    row_stats(go_ref, o_ref, lse_ref, gs, lse_scr, delta_scr, stat_scr)

    def start(p):
        qs[p] = split_pair(q_ref[:, lanes_of(p)])

    each_pair(start)
    dq_scr[...] = jnp.zeros_like(dq_scr)

    half = keep_ref.shape[0] // ROWS

    def block(j, c):
        at = pl.multiple_of(j * ROWS, ROWS)
        hit = wanted(at)
        upper = (place_ref[j] >= half).astype(jnp.int32)
        to = pl.multiple_of((place_ref[j] - upper * half) * ROWS, ROWS)

        def gradients(target):
            k_row = at + iota((1, ROWS), 1)
            masked = jnp.where(q_pair == seg_of(k_row, e_ends), 0.0, NEG)
            raws = [dot_nt(qs[p], kv_ref[p, pl.ds(at, ROWS), :]) for p in range(PAIRS)]
            dprobs = [dot_nt(gs[p], kv_ref[PAIRS + p, pl.ds(at, ROWS), :]) for p in range(PAIRS)]
            for p in range(PAIRS):
                weights, dscores = [], []
                for i in range(2):
                    rows = slice(i * ROWS, (i + 1) * ROWS)
                    probs = jnp.exp(raws[p][rows] + masked - lse_scr[p, rows, :1])
                    weights.append(probs.astype(BF16))
                    dscores.append((probs * (dprobs[p][rows] - delta_scr[p, rows, :1])).astype(BF16))
                ds = jnp.concatenate(dscores, axis=0)
                dq_scr[p] += dot_nn(ds, kv_ref[p, pl.ds(at, ROWS), :])
                target[:, lanes_of(p)] = dot_tn(ds, qs[p]).astype(BF16)
                target[:, lanes_of(PAIRS + p)] = dot_tn(jnp.concatenate(weights, axis=0), gs[p]).astype(BF16)

        @pl.when(hit)
        def _():
            gradients(block_scr)

        @pl.when(jnp.logical_not(hit))
        def _():
            block_scr[...] = jnp.zeros_like(block_scr)

        for mine, target in ((True, keep_ref), (False, send_ref)):

            @pl.when((upper == at_ref[3]) == mine)
            def _():
                target[pl.ds(to, ROWS), :] = block_scr[...]

        return c

    lax.fori_loop(0, kv_ref.shape[1] // ROWS, block, 0)
    for p in range(PAIRS):
        dq_ref[:, 128 * p : 128 * p + 128] = join_pair(dq_scr[p]).astype(BF16)
    part_ref[...] = dot_nt(dq_ref[...], wc_ref[:, :HALF])


def self_grad_start_kernel(
    at_ref, e_ref, other_ref, mid_ref, gain_ref, late_grad_ref, so_ref, o_ref, lse_ref,
    grad_ref, low_ref, dgain_ref, go_ref, message_ref,
    stat_scr,
):
    core = at_ref[1]
    dvalue, dgain = norm_grad(mid_ref[...], gain_ref[...], e_ref[...] + other_ref[...])
    dgain_ref[...] = dgain
    grad = late_grad_ref[...] + dvalue
    grad_ref[...] = grad
    low_ref[...] = grad.astype(BF16)
    go_ref[...] = dot_nt(low_ref[...], so_ref[own_rows(core, HALF), :]).astype(BF16)
    half = ROWS // 2
    message_ref[:half, :] = low_ref[own_rows(core, half), :]
    lane = iota((ROWS, 128), 1)
    stat_scr[...] = lse_ref[...]

    def pair(p):
        product = go_ref[:, lanes_of(p)].astype(F32) * o_ref[:, lanes_of(p)]
        for i in range(2):
            part = jnp.where((lane < HEAD_DIM) if i == 0 else (lane >= HEAD_DIM), product, 0.0)
            stat_scr[...] = jnp.where(lane == 8 + 2 * p + i, jnp.sum(part, axis=1, keepdims=True), stat_scr[...])

    each_pair(pair)
    rest = jnp.transpose(stat_scr[...])[:16]
    for part in range(3):
        high = rest.astype(BF16)
        message_ref[half:, part * ROWS : (part + 1) * ROWS] = high
        rest = rest - high.astype(F32)


def projection_grads_kernel(
    n_sides, at_ref, low2_ref, other2_ref, b2_ref, in_ref, dq2_ref, low1_ref, other1_ref, b1_ref, x_ref, gain_ref, dq1_ref, *outs
):
    *outs, out_ref = outs
    core, side = at_ref[1], at_ref[2]
    lanes = pl.ds(pl.multiple_of(core * HALF, 128), HALF)
    for at, own, other, grad in ((0, low2_ref, other2_ref, b2_ref), (2 * HALF, low1_ref, other1_ref, b1_ref)):
        grads = grad[:, lanes]
        for which, part in ((core, own), (1 - core, other)):
            out_ref[own_rows(which, HALF), at : at + HALF] = dot_tn(part[...], grads).astype(BF16)
    out_ref[:, HALF : 2 * HALF] = dot_tn(in_ref[...], dq2_ref[...]).astype(BF16)
    wide = x_ref[...].astype(F32)
    normed = (wide * rms_inverse(wide) * gain_ref[...]).astype(BF16)
    out_ref[:, 3 * HALF :] = dot_tn(normed, dq1_ref[...]).astype(BF16)
    give(n_sides, side, out_ref, outs)


def give(n_sides, side, value, outs):
    if n_sides == 2:
        rows = value.shape[0] // 2
        outs[0][...] = value[own_rows(side, rows), :]
        outs[1][...] = value[own_rows(1 - side, rows), :]
    else:
        outs[0][...] = value[...]


def encoder_grads_kernel(n_sides, at_ref, dkv_ref, e_ref, wc_ref, keep_ref, send_ref, *outs):
    *outs, low_scr, e_scr, grads_ref = outs
    core = at_ref[1]
    half = ROWS // 2
    low_scr[...] = dkv_ref[...].astype(BF16)
    e_scr[...] = dot_nt(low_scr[...], wc_ref[:, HALF:])
    keep_ref[...] = e_scr[own_rows(core, half), :]
    send_ref[...] = e_scr[own_rows(1 - core, half), :]
    grads_ref[...] = dot_tn(e_ref[...], low_scr[...]).astype(BF16)
    give(n_sides, at_ref[2], grads_ref, outs)


def token_grads_kernel(at_ref, e_ref, other_ref, x_ref, gain_ref, grad_ref, out_ref):
    dvalue, _ = norm_grad(x_ref[...].astype(F32), gain_ref[...], e_ref[...] + other_ref[...])
    out_ref[...] = grad_ref[own_rows(at_ref[1], out_ref.shape[0]), :] + dvalue


def finish_late_kernel(count, at_ref, place_ref, own_ref, other_ref, *outs):
    *outs, small = outs
    core, place = at_ref[1], place_ref[0]
    rows = own_ref.shape[0] // count
    columns = slice(len(outs) * HALF, len(outs) * HALF + 128)
    for i in range(count):
        part = slice(i * rows, (i + 1) * rows)
        to = pl.ds(pl.multiple_of((place ^ i) * rows, rows), rows)
        for j, out in enumerate(outs):
            lanes = slice(j * HALF, (j + 1) * HALF)
            out[to, own_lanes(core)] = own_ref[part, lanes].astype(F32)
            out[to, own_lanes(1 - core)] = other_ref[part, lanes].astype(F32)
        small[to, :] = own_ref[part, columns].astype(F32) + other_ref[part, columns].astype(F32)


def own_lanes(core):
    return pl.ds(pl.multiple_of(core * HALF, 128), HALF)


def finish_kernel(order, parts_ref, outer_ref, inner_ref, *outs):
    rows = parts_ref.shape[1]
    width = outer_ref.shape[1]
    side = inner_ref.shape[0]
    unit = inner_ref.shape[1] // 4
    for i in range(parts_ref.shape[0]):
        core, at = i % 2, (i // 2) * rows
        for half in range(2):
            top = (2 * core + half) * side + at
            outer_ref[top : top + rows, :] = parts_ref[i, :, half * width : (half + 1) * width].astype(F32)
            lanes = slice((2 * half + core) * unit, (2 * half + core + 1) * unit)
            inner_ref[at : at + rows, lanes] = parts_ref[i, :, 2 * width + half * unit : 2 * width + (half + 1) * unit].astype(F32)
    finish_columns_kernel(order, 4 * width, parts_ref, *outs)


def finish_columns_kernel(order, skip, parts_ref, *outs):
    rows = parts_ref.shape[1]
    for i, (core, place) in enumerate(order):
        at = slice(place * rows, (place + 1) * rows)
        for j, out in enumerate(outs):
            columns = slice(skip + j * HALF, skip + (j + 1) * HALF)
            out[at, core * HALF : (core + 1) * HALF] = parts_ref[i, :, columns].astype(F32)


def pack_kernel(groups, core_ref, *refs):
    count = sum(groups)
    ins, outs = list(refs[:count]), refs[count:]
    for size, out in zip(groups, outs):
        at = 0
        for _ in range(size):
            part = ins.pop(0)
            out[:, at : at + part.shape[1]] = part[...].astype(BF16)
            at += part.shape[1]


SMEM = pl.BlockSpec(memory_space=pltpu.SMEM)
VMEM = pl.BlockSpec(memory_space=pltpu.VMEM)


def call(kernel, scalars, arrays, outs, scratch, flops):
    moved = sum(a.size * a.dtype.itemsize for a in arrays) + sum(math.prod(s) * jnp.dtype(d).itemsize for s, d in outs)
    return pl.pallas_call(
        kernel,
        out_shape=[jax.ShapeDtypeStruct(s, d) for s, d in outs],
        in_specs=[SMEM] * len(scalars) + [VMEM] * len(arrays),
        out_specs=[VMEM] * len(outs),
        scratch_shapes=[pltpu.VMEM(s, d) for s, d in scratch],
        compiler_params=pltpu.CompilerParams(vmem_limit_bytes=VMEM_LIMIT),
        cost_estimate=pl.CostEstimate(flops=1, transcendentals=0, bytes_accessed=1),
    )(*scalars, *arrays)


TILES = ((3, LOCAL, ROWS, ROWS), F32)
FAR = ((LOCAL, 8, ROWS), F32)
STACK = ((PAIRS, 2 * ROWS, 128), BF16)
COLUMN = ((PAIRS, 2 * ROWS, 128), F32)
LANE = ((ROWS, 128), F32)


def pack(core, groups):
    flat = [item for group in groups for item in group]
    return pl.pallas_call(
        functools.partial(pack_kernel, [len(g) for g in groups]),
        grid_spec=pltpu.PrefetchScalarGridSpec(
            num_scalar_prefetch=1,
            grid=(1,),
            in_specs=[
                pl.BlockSpec(shape, functools.partial(lambda index, i, c: index(c[0]), index)) for _, shape, index in flat
            ],
            out_specs=[
                pl.BlockSpec((g[0][1][0], sum(s[1] for _, s, _ in g)), lambda i, c: (0, 0)) for g in groups
            ],
        ),
        out_shape=[jax.ShapeDtypeStruct((g[0][1][0], sum(s[1] for _, s, _ in g)), BF16) for g in groups],
        compiler_params=pltpu.CompilerParams(vmem_limit_bytes=VMEM_LIMIT),
    )(core, *(w for w, _, _ in flat))


def swap_core(value):
    return lax.ppermute(value, "core", [(0, 1), (1, 0)])


def gather_fsdp(own):
    count = lax.axis_size("fsdp")
    if count != 2:
        return [lax.all_gather(own, "fsdp", axis=0, tiled=True)]
    return [own, lax.ppermute(own, "fsdp", [(0, 1), (1, 0)])]


CHIPS = ("z", "y")
GROUP = ("z", "y", "core")


def gather_rows(own):
    return lax.all_gather(own, GROUP, axis=0, tiled=True)


def bits_of(axis):
    return range((lax.axis_size(axis) - 1).bit_length())


def swap_bit(value, axis, bit):
    return lax.ppermute(value, axis, [(i, i ^ (1 << bit)) for i in range(lax.axis_size(axis))])


def parted(terms, axis, bit):
    side = (lax.axis_index(axis) >> bit) & 1
    rows = terms[0].shape[0] // 2

    def half(which):
        return [lax.dynamic_slice_in_dim(t, which * rows, rows, 0) for t in terms]

    return half(side), total(half(1 - side)).astype(BF16)


def halve(terms, axis, bit):
    keep, send = parted(terms, axis, bit)
    return keep + [swap_bit(send, axis, bit)]


def total(terms):
    return sum(t.astype(F32) for t in terms[1:]) + terms[0].astype(F32)


def steps_of(*axes):
    return [(axis, bit) for axis in axes for bit in bits_of(axis)]


def scatter(terms, steps):
    for axis, bit in steps:
        terms = halve(terms, axis, bit)
    return terms


def scatter_fsdp(terms):
    return scatter(terms, [("fsdp", bit) for bit in reversed(bits_of("fsdp"))])


def places(steps):
    nz, ny = lax.axis_size("z"), lax.axis_size("y")
    found = []
    for z in range(nz):
        for y in range(ny):
            place = 0
            for axis, bit in steps:
                place = 2 * place + (((z if axis == "z" else y) >> bit) & 1)
            found.append(place)
    return found


def after(value, *earlier):
    return lax.optimization_barrier((value, *earlier))[0]


def on_device(
    tokens, encoded, cotangent, tgt_lengths, enc_lengths, deal,
    ln_self, ln_cross, ln_ffn, bias_table,
    self_query, self_key, self_value, self_output,
    cross_query, cross_key, cross_value, cross_output,
    ffn_inner, ffn_outer,
):
    core = lax.axis_index("core")
    fsdp = lax.axis_index("fsdp")
    n_fsdp = lax.axis_size("fsdp")
    chip = lax.axis_index(CHIPS)
    steps = steps_of("y", "z")
    y_side = (lax.axis_index("y") >> steps[0][1]) & 1
    at = jnp.stack([chip, core, fsdp, y_side]).astype(jnp.int32)
    core_ref = core.reshape(1).astype(jnp.int32)
    rows, width = tokens.shape
    n = 2 * rows * lax.axis_size(CHIPS)
    side = width // n_fsdp
    hidden_half = ffn_inner.shape[1] // 2
    unit = hidden_half // n_fsdp
    wide, flat = ((ROWS, width), F32), ((ROWS, width), BF16)

    def column(weight):
        return (weight, (side, HALF), lambda c: (0, c))

    (qkv_own,) = pack(core_ref, [[column(w) for w in (self_query, self_key, self_value)]])
    w_qkv = gather_fsdp(qkv_own)
    if unit % 128 == 0:
        inner_items = [(ffn_inner, (side, unit), functools.partial(lambda o, c: (0, 2 * o + c), o)) for o in range(n_fsdp)]
    else:
        inner_units = ffn_inner.reshape(side, n_fsdp, 2, unit)
        inner_units = lax.dynamic_index_in_dim(inner_units, core, 2, keepdims=False).reshape(side, hidden_half)
        inner_items = [(inner_units, (side, hidden_half), lambda c: (0, 0))]
    out_own, cross_own, inner_own, outer_own = pack(
        core_ref,
        [
            [column(w) for w in (self_output, cross_output)],
            [column(w) for w in (cross_query, cross_key, cross_value)],
            inner_items,
            [(ffn_outer, (unit, width), lambda c: (c, 0))],
        ],
    )
    w_out = gather_fsdp(out_own)
    w_cross = gather_fsdp(cross_own)
    inner_own, outer_own = after((inner_own, outer_own), w_cross[-1])
    w_inner, w_outer = gather_fsdp(inner_own), gather_fsdp(outer_own)
    w_out_mate = [swap_core(w) for w in w_out]
    cot_mate = swap_core(cotangent)

    small = jnp.concatenate([ln_self, ln_cross, ln_ffn, bias_table.reshape(-1)], axis=0).astype(BF16)[None]
    small = gather_fsdp(small)
    if len(small) == 2:
        small = jnp.where(fsdp == 0, jnp.concatenate(small, axis=0), jnp.concatenate(small[::-1], axis=0))
    else:
        small = small[0]
    gain_self, gain_cross, gain_ffn = (
        small[:, i * side : (i + 1) * side].reshape(1, width).astype(F32) for i in range(3)
    )
    table = small[:, 3 * side :].reshape(BUCKETS, HEADS)
    table = lax.dynamic_slice_in_dim(table, core * LOCAL, LOCAL, 1).astype(F32)
    onehots = np.concatenate([QK_ONEHOT, KQ_ONEHOT], axis=0)
    biases = jnp.einsum("bh,tb->ht", table, onehots, precision=lax.Precision.HIGHEST)
    biases = jnp.pad(biases.reshape(LOCAL, 2, 2 * ROWS).swapaxes(0, 1), ((0, 0), (0, 2), (0, 0)))
    (tiles,) = call(tiles_kernel, (), (biases.reshape(16, 2 * ROWS),), [((2, *TILES[0]), BF16)], [], 1)

    xe = gather_rows(jnp.concatenate([tokens, encoded], axis=1))
    qkv, w_qkv, attn_self, low_self, lse_self = call(
        functools.partial(self_stage_kernel, len(w_qkv)), (at, tgt_lengths), (xe, gain_self, tiles, *w_qkv),
        [((3 * PAIRS, n, 128), BF16), ((width, 3 * HALF), BF16), ((ROWS, HALF), F32), ((ROWS, HALF), BF16), LANE],
        ATTEND(n),
        2 * n * width * 3 * HALF + 4 * ROWS * n * HALF,
    )
    low_self_other = swap_core(low_self)

    x_mid, in_cross, q_cross, kv_cross, attn_cross, low_cross, lse_cross, w_so, w_co, w_cross = call(
        functools.partial(cross_stage_kernel, len(w_out)), (at, tgt_lengths, enc_lengths, deal),
        (xe, gain_cross, low_self, low_self_other, *w_out, *w_out_mate, *w_cross),
        [
            wide, flat, ((ROWS, HALF), BF16), ((2 * PAIRS, n, 128), BF16), ((ROWS, HALF), F32), ((ROWS, HALF), BF16), LANE,
            ((width, width), BF16), ((width, width), BF16), ((width, 3 * HALF), BF16),
        ],
        ATTEND(n),
        2 * n * width * 2 * HALF + 4 * ROWS * n * HALF,
    )
    low_cross_other = swap_core(low_cross)

    half_rows = ((rows, width), F32)
    x_late, in_ffn, hidden, d_pre, cot, out_keep, out_send, e_ffn = call(
        functools.partial(ffn_stage_kernel, len(w_inner)), (at,),
        (x_mid, gain_ffn, low_cross, low_cross_other, w_co, cotangent, cot_mate, *w_inner, *w_outer),
        [wide, flat, ((ROWS, hidden_half), BF16), ((ROWS, hidden_half), BF16), flat, half_rows, half_rows, wide],
        [((width, hidden_half), BF16), ((hidden_half, width), BF16), wide],
        8 * ROWS * width * hidden_half,
    )
    e_ffn_other = swap_core(e_ffn)
    output = out_keep + swap_core(out_send)

    place = places(steps)
    place_ref = jnp.asarray(np.array(place, np.int32))
    grad_late, late_low, d_gain_ffn, dq_cross, dkv_keep, dkv_send, e_cross = call(
        cross_grad_stage_kernel, (at, tgt_lengths, enc_lengths, deal, place_ref),
        (e_ffn, e_ffn_other, x_late, gain_ffn, cot, w_co, q_cross, attn_cross, lse_cross, kv_cross, w_cross),
        [wide, flat, ((1, width), F32), ((ROWS, HALF), BF16), ((n // 2, 2 * HALF), BF16), ((n // 2, 2 * HALF), BF16), wide],
        [((ROWS, HALF), BF16), STACK, STACK, COLUMN, COLUMN, COLUMN, LANE, ((ROWS, 2 * HALF), BF16)],
        10 * ROWS * n * HALF,
    )
    e_cross_other = swap_core(e_cross)
    dkv_got = swap_bit(dkv_send, *steps[0])

    grad_mid, mid_low, d_gain_cross, go_self, message = call(
        self_grad_start_kernel, (at,), (e_cross, e_cross_other, x_mid, gain_cross, grad_late, w_so, attn_self, lse_self),
        [wide, flat, ((1, width), F32), ((ROWS, HALF), BF16), ((rows + 16, width), BF16)], [LANE],
        2 * ROWS * width * HALF,
    )
    ffn_out = (
        [((side, 4 * width), BF16), ((side, 4 * width), BF16)]
        if n_fsdp == 2
        else [((hidden_half, width), F32), ((width, hidden_half), F32)]
    )
    first = call(
        functools.partial(ffn_grads_kernel, n_fsdp), (at,), (hidden, cot, in_ffn, after(d_pre, message)), ffn_out, [],
        4 * ROWS * width * hidden_half,
    )
    if n_fsdp == 2:
        first_other = lax.ppermute(first[1], "fsdp", [(0, 1), (1, 0)])
        go_self = after(go_self, first[1])
    message = lax.all_gather(message, GROUP, axis=0)
    x_chip = lax.dynamic_slice(xe, (chip * ROWS, 0), (ROWS, width))
    e_chip = lax.dynamic_slice(xe, (chip * ROWS, width), (ROWS, width))
    dq_self, dist = call(
        self_query_grad_kernel, (at, tgt_lengths), (tiles, qkv, go_self, attn_self, lse_self),
        [((ROWS, HALF), BF16), ((8, 2 * ROWS), F32)],
        [STACK, STACK, COLUMN, COLUMN, COLUMN, TILES, FAR, LANE],
        6 * ROWS * n * HALF,
    )
    def given(columns):
        return [((width // 2, columns), BF16)] * 2 if n_fsdp == 2 else [((width, columns), BF16)]

    def over_fsdp(parts):
        if n_fsdp == 2:
            return [parts[0], lax.ppermute(parts[1], "fsdp", [(0, 1), (1, 0)])]
        return scatter_fsdp(parts)

    second = call(
        functools.partial(projection_grads_kernel, n_fsdp), (at,),
        (low_cross, low_cross_other, late_low, in_cross, dq_cross, low_self, low_self_other, mid_low, x_chip, gain_self, dq_self),
        given(4 * HALF), [((width, 4 * HALF), BF16)], 8 * ROWS * width * HALF,
    )
    d_table = jnp.einsum("ht,tb->bh", dist[:LOCAL], QK_ONEHOT, precision=lax.Precision.HIGHEST)
    d_table = jnp.zeros((BUCKETS, 2, LOCAL), F32).at[:, core].set(d_table).reshape(n_fsdp, -1, HEADS)
    d_table = jnp.pad(d_table, ((0, 0), (0, side - d_table.shape[1]), (0, 0))).reshape(width, HEADS)
    none = jnp.zeros((width, 1), F32)
    small = [none, 0.5 * d_gain_cross.reshape(width, 1), 0.5 * d_gain_ffn.reshape(width, 1), d_table]
    small = jnp.pad(jnp.concatenate(small, axis=1), ((0, 0), (0, 128 - 3 - HEADS)))

    if n_fsdp == 2:
        first = [first[0], first_other]
    else:
        outer = first[0].reshape(n_fsdp, 2, side, width)
        first = jnp.concatenate([outer[:, 0], outer[:, 1], first[1].reshape(n_fsdp, side, hidden_half)], axis=2)
        first = scatter_fsdp([first.reshape(width, -1)])
    *y_steps, z_near, z_far = steps
    dkv_cross = scatter([dkv_keep, dkv_got], y_steps[1:])
    dkv_keep, dkv_sent = parted(after(dkv_cross, second[-1]), *z_near)
    dkv_near = swap_bit(dkv_sent, *z_near)
    first = total(after(first, dkv_sent)).astype(BF16)
    second = over_fsdp(after(second, first))

    e_keep, e_send, *fourth = call(
        functools.partial(self_key_stage_kernel, n_fsdp), (at, tgt_lengths),
        (tiles, qkv, after(message, first), w_so, dq_self, w_qkv, x_chip, gain_self, small),
        [half_rows, half_rows, *given(2 * HALF + 128)],
        [
            ((PAIRS, n, 128), BF16), ((n // ROWS, 16, ROWS), F32), STACK, STACK, COLUMN, COLUMN,
            ((ROWS, 3 * HALF), BF16), flat, wide, ((width, 2 * HALF + 128), BF16),
        ],
        8 * ROWS * n * HALF,
    )
    first = lax.psum_scatter(after(first, message), CHIPS, scatter_dimension=0, tiled=True)
    fourth_sent = fourth[-1]
    fourth = over_fsdp(fourth)
    dkv_keep, dkv_sent = parted(dkv_keep + [after(dkv_near, fourth_sent)], *z_far)
    dkv_far = swap_bit(dkv_sent, *z_far)
    second_keep, second_sent = parted(after(second, dkv_sent), *y_steps[0])
    second_got = swap_bit(second_sent, *y_steps[0])
    enc_keep, enc_send, *third = call(
        functools.partial(encoder_grads_kernel, n_fsdp), (at,),
        (total(dkv_keep + [after(dkv_far, second_sent)]), e_chip, w_cross),
        [half_rows, half_rows, *given(2 * HALF)],
        [((ROWS, 2 * HALF), BF16), wide, ((width, 2 * HALF), BF16)], 8 * ROWS * width * HALF,
    )
    third_sent = third[-1]
    third = over_fsdp(third)
    (grad_tokens,) = call(
        token_grads_kernel, (at,), (e_keep, swap_core(after(e_send, third_sent)), tokens, gain_self, grad_mid),
        [half_rows], [], 10 * rows * width,
    )
    enc_grad = enc_keep + swap_core(after(enc_send, third_sent))

    second_got, third, fourth = after((second_got, third, fourth), grad_tokens, enc_grad)
    second = scatter(second_keep + [second_got], y_steps[1:])
    second_keep, second_sent = parted(second, *z_near)
    second_got = swap_bit(second_sent, *z_near)
    late = [jnp.concatenate([total(third), total(after(fourth, second_sent))], axis=1)]
    late_keep, late_sent = parted(late, *y_steps[0])
    late_got = swap_bit(late_sent, *y_steps[0])
    first = after(first, late_sent)
    second_keep, second_sent = parted(second_keep + [after(second_got, late_sent)], *z_far)
    second_got = swap_bit(second_sent, *z_far)
    late = scatter(late_keep + [after(late_got, second_sent)], y_steps[1:])
    late_keep, late_sent = parted(late, *z_near)
    late_got = swap_bit(late_sent, *z_near)
    second = total(second_keep + [after(second_got, late_sent)]).astype(BF16)
    late = total(halve(late_keep + [after(late_got, second)], *z_far)).astype(BF16)
    early = lax.all_gather(jnp.concatenate([first, second], axis=1), GROUP, axis=0)
    for axis, bit in reversed(steps):
        late = jnp.concatenate([late, swap_bit(late, axis, bit)], axis=0)
    late_other = swap_core(late)
    early = after(early, late_other)

    matrix = ((side, width), F32)
    own_place = place_ref[chip].reshape(1)
    if side // len(place) % 8 == 0:
        g_ck, g_cv, g_sk, g_sv, small = call(
            functools.partial(finish_late_kernel, len(place)), (at, own_place), (late, late_other),
            [matrix] * 4 + [((side, 128), F32)], [], 8 * side * width,
        )
    else:
        blocks = jnp.stack([late, late_other]).reshape(2, len(place), side // len(place), -1)
        blocks = jnp.take(blocks, own_place[0] ^ jnp.arange(len(place), dtype=jnp.int32), axis=1)
        blocks = jnp.where(core == 0, blocks, blocks[::-1]).astype(F32).reshape(2, side, -1)
        g_ck, g_cv, g_sk, g_sv = (
            jnp.swapaxes(blocks[:, :, i : i + HALF], 0, 1).reshape(side, width) for i in range(0, 4 * HALF, HALF)
        )
        small = jnp.sum(blocks[:, :, 4 * HALF :], axis=0)
    order = [(c, p) for p in place for c in range(2)]
    if n_fsdp == 2:
        g_outer, g_inner, g_co, g_cq, g_so, g_sq = call(
            functools.partial(finish_kernel, order), (), (early,),
            [(ffn_outer.shape, F32), (ffn_inner.shape, F32), *[matrix] * 4], [], 8 * side * width,
        )
    else:
        pair = jnp.swapaxes(early.reshape(len(place), 2, -1, early.shape[2]), 0, 1).reshape(2, side, -1).astype(F32)
        g_outer = pair[:, :, : 2 * width].reshape(2, side, 2, width)
        g_outer = jnp.swapaxes(g_outer, 1, 2).reshape(ffn_outer.shape)
        g_inner = jnp.transpose(pair[:, :, 2 * width : 4 * width].reshape(2, side, n_fsdp, unit), (1, 2, 0, 3))
        g_inner = g_inner.reshape(ffn_inner.shape)
        g_co, g_cq, g_so, g_sq = call(
            functools.partial(finish_columns_kernel, order, 4 * width), (), (early,), [matrix] * 4, [], 8 * side * width
        )

    return (
        output, grad_tokens, enc_grad,
        small[:, 0], small[:, 1], small[:, 2], small[: bias_table.shape[0], 3 : 3 + HEADS],
        g_sq, g_sk, g_sv, g_so, g_cq, g_ck, g_cv, g_co, g_inner, g_outer,
    )


def solution(mesh):
    n_ctx, n_fsdp = mesh.shape["ctx"], mesh.shape["fsdp"]
    n_z = 4
    grid = Mesh(mesh.devices.reshape(n_z, n_ctx // (2 * n_z), 2, n_fsdp), ("z", "y", "core", "fsdp"))
    by_rows = P(("fsdp", "z", "y", "core"), None)
    split = P("fsdp", None)
    vector = P("fsdp")
    in_specs = (by_rows,) * 3 + (split,) * 3 + (vector,) * 3 + (split,) * 11
    out_specs = (by_rows,) * 3 + (vector,) * 3 + (split,) * 11
    return jax.shard_map(on_device, mesh=grid, in_specs=in_specs, out_specs=out_specs, check_vma=False)
```

```python
import functools
import math

import jax
import jax.numpy as jnp
import numpy as np
from jax import lax
from jax.experimental import pallas as pl
from jax.experimental.pallas import tpu as pltpu
from jax.sharding import Mesh
from jax.sharding import PartitionSpec as P

HEADS = 12
HEAD_DIM = 64
BUCKETS = 32
EPS = 1e-06
NEG = -1e30
GELU_C = 0.7978845608028654
GELU_A = 0.044715

LOCAL = HEADS // 2
PAIRS = LOCAL // 2
HALF = LOCAL * HEAD_DIM
ROWS = 256
VMEM_LIMIT = 56 << 20

F32 = jnp.float32
BF16 = jnp.bfloat16


def bucket_edges():
    edges = []
    for level in range(1, 16):
        distance = 16
        while int(math.log(distance / 16.0) / math.log(8.0) * 16.0) < level:
            distance += 1
        edges.append(distance)
    return edges


def buckets_of(distances):
    clipped = np.maximum(np.asarray(distances), 0)
    large = np.full(clipped.shape, 16)
    for edge in bucket_edges():
        large = large + (clipped >= edge)
    return np.where(clipped < 16, clipped, large)


LANES = np.arange(2 * ROWS)
QK_DISTANCE = np.where(LANES <= ROWS, ROWS - LANES, 3 * ROWS - LANES)
KQ_DISTANCE = LANES
QK_ONEHOT = np.eye(BUCKETS, dtype=np.float32)[buckets_of(QK_DISTANCE)]
KQ_ONEHOT = np.eye(BUCKETS, dtype=np.float32)[buckets_of(KQ_DISTANCE)]


def dot_nt(left, right):
    return lax.dot_general(left, right, (((1,), (1,)), ((), ())), preferred_element_type=F32)


def dot_tn(left, right):
    return lax.dot_general(left, right, (((0,), (0,)), ((), ())), preferred_element_type=F32)


def dot_nn(left, right):
    return lax.dot_general(left, right, (((1,), (0,)), ((), ())), preferred_element_type=F32)


def spans(ref):
    starts, ends, at = [], [], jnp.int32(0)
    for i in range(ref.shape[1]):
        starts.append(at)
        at = at + ref[0, i]
        ends.append(at)
    return starts, ends


def seg_of(index, ends):
    found = jnp.zeros(index.shape, jnp.int32)
    for end in ends[:-1]:
        found = found + (index >= end).astype(jnp.int32)
    return found


def iota(shape, axis):
    return lax.broadcasted_iota(jnp.int32, shape, axis)


def split_pair(pair, sub=ROWS):
    low = iota((sub, pair.shape[1]), 1) < HEAD_DIM
    zero = jnp.zeros((sub, pair.shape[1]), pair.dtype)
    parts = []
    for at in range(0, pair.shape[0], sub):
        part = pair[at : at + sub]
        parts += [jnp.where(low, part, zero), jnp.where(low, zero, part)]
    return jnp.concatenate(parts, axis=0)


def head_rows(both, e, sub=ROWS):
    parts = [both[at + e * sub : at + (e + 1) * sub] for at in range(0, both.shape[0], 2 * sub)]
    return parts[0] if len(parts) == 1 else jnp.concatenate(parts, axis=0)


def join_pair(both, sub=ROWS):
    first = head_rows(both, 0, sub)
    return jnp.where(iota(first.shape, 1) < HEAD_DIM, first, head_rows(both, 1, sub))


def tiles_kernel(bias_ref, tiles_ref):
    def head(h, c):
        for which in range(2):
            row = bias_ref[pl.ds(8 * which + h, 1), :]
            rolled = pltpu.roll(jnp.broadcast_to(row, (ROWS, 2 * ROWS)), 0, 1, stride=1, stride_axis=0)
            first, second = (1, 2) if which == 0 else (2, 1)
            tiles_ref[which, first, h] = rolled[:, :ROWS].astype(BF16)
            tiles_ref[which, second, h] = rolled[:, ROWS:].astype(BF16)
            tiles_ref[which, 0, h] = jnp.broadcast_to(row[:, 2 * ROWS - 1 :], (ROWS, ROWS)).astype(BF16)
        return c

    lax.fori_loop(0, LOCAL, head, 0)


def lanes_of(p):
    return slice(p * 128, p * 128 + 128) if isinstance(p, int) else pl.ds(pl.multiple_of(p * 128, 128), 128)


def each_pair(body):
    for p in range(PAIRS):
        body(p)


def rms_inverse(value):
    return lax.rsqrt(jnp.mean(value * value, axis=-1, keepdims=True) + EPS)


def together(n):
    return PAIRS if n <= 2048 else 1


def attend(queries, keys, values, visit_scores, visit, sub, step, s_scr, mx_scr, l_scr, acc_scr, qs, o_ref, low_ref, lse_ref):
    count = s_scr.shape[0]
    lse_ref[...] = jnp.zeros_like(lse_ref)
    lane = iota((ROWS, 128), 1)

    def group(g):
        for c in range(count):
            qs[c] = split_pair(queries(g * count + c), sub)
        mx_scr[...] = jnp.full_like(mx_scr, NEG)

        def scores(j, rows, extra):
            at = pl.multiple_of(j * step, step)
            raws = [dot_nt(qs[c, rows], keys(g * count + c, at)) for c in range(count)]
            for c in range(count):
                value = extra(g * count + c, raws[c])
                s_scr[c, rows, pl.ds(at, step)] = value
                mx_scr[c, rows] = functools.reduce(
                    jnp.maximum, [value[:, i : i + 128] for i in range(0, step, 128)], mx_scr[c, rows]
                )

        visit_scores(scores)
        for c in range(count):
            mx_scr[c] = jnp.broadcast_to(jnp.max(mx_scr[c], axis=1, keepdims=True), mx_scr.shape[1:])
        l_scr[...] = jnp.zeros_like(l_scr)
        acc_scr[...] = jnp.zeros_like(acc_scr)

        def weigh(j, rows):
            at = pl.multiple_of(j * step, step)
            for c in range(count):
                weights = jnp.exp(s_scr[c, rows, pl.ds(at, step)] - mx_scr[c, rows, :1])
                l_scr[c, rows] += sum(weights[:, i : i + 128] for i in range(128, step, 128)) + weights[:, :128]
                acc_scr[c, rows] += dot_nn(weights.astype(BF16), values(g * count + c, at))

        visit(weigh)
        for c in range(count):
            p = g * count + c
            total = jnp.sum(l_scr[c], axis=1, keepdims=True)
            result = join_pair(acc_scr[c] / total, sub)
            o_ref[:, lanes_of(p)] = result
            low_ref[:, lanes_of(p)] = result.astype(BF16)
            both = mx_scr[c, :, :1] + jnp.log(total)
            lse = jnp.where(lane == 2 * p, head_rows(both, 0, sub), lse_ref[...])
            lse_ref[...] = jnp.where(lane == 2 * p + 1, head_rows(both, 1, sub), lse)

    if count == PAIRS:
        group(0)
    else:
        lax.fori_loop(0, PAIRS // count, lambda g, c: (group(g), c)[1], 0)


ATTEND = lambda n: [
    ((together(n), 2 * ROWS, n), F32), ((together(n), 2 * ROWS, 128), F32), ((together(n), 2 * ROWS, 128), F32),
    ((together(n), 2 * ROWS, 128), F32), ((together(n), 2 * ROWS, 128), BF16),
]


def set_rows(target, parts, side):
    if len(parts) == 1:
        target[...] = parts[0][...]
        return
    rows = parts[0].shape[0]
    target[pl.ds(pl.multiple_of(side * rows, rows), rows), :] = parts[0][...]
    target[pl.ds(pl.multiple_of((1 - side) * rows, rows), rows), :] = parts[1][...]


def first_of(base, ends):
    first = jnp.int32(0)
    for end in ends[:-1]:
        first = jnp.where(base >= end, end, first)
    return first


def self_stage_kernel(n_parts, at_ref, len_ref, xe_ref, gain_ref, tiles, *refs):
    parts, refs = refs[:n_parts], refs[n_parts:]
    qkv_ref, w_ref, o_ref, low_ref, lse_ref, s_scr, mx_scr, l_scr, acc_scr, qs = refs
    chip, side = at_ref[0], at_ref[2]
    set_rows(w_ref, parts, side)
    width = w_ref.shape[0]
    step = 512

    def body(i, c):
        at = pl.multiple_of(i * step, step)
        wide = xe_ref[pl.ds(at, step), :width].astype(F32)
        value = (wide * rms_inverse(wide) * gain_ref[...]).astype(BF16)
        result = dot_nn(value, w_ref[...])
        for j in range(qkv_ref.shape[0]):
            qkv_ref[j, pl.ds(at, step), :] = result[:, 128 * j : 128 * j + 128].astype(BF16)
        return c

    lax.fori_loop(0, xe_ref.shape[0] // step, body, 0)

    starts, ends = spans(len_ref)
    base = pl.multiple_of(chip * ROWS, ROWS)
    j_min = first_of(base, ends) // ROWS
    full_from = first_of(base + ROWS - 1, ends)
    q_row = base + iota((ROWS, 1), 0)
    q_seg = seg_of(q_row, ends)

    rows = slice(0, 2 * ROWS)

    def visit(block):
        lax.fori_loop(j_min, chip + 1, lambda j, c: (block(j, rows), c)[1], 0)

    def visit_scores(block):
        def body(j, c):
            at = pl.multiple_of(j * ROWS, ROWS)
            plain = (at >= full_from) & (j < chip - 1)

            def with_bias(bias):
                def extra(p, raw):
                    return jnp.concatenate([raw[:ROWS] + bias(2 * p), raw[ROWS:] + bias(2 * p + 1)], axis=0)

                block(j, rows, extra)

            @pl.when(plain)
            def _():
                with_bias(lambda h: tiles[0, 0, h, :1, :1].astype(F32))

            @pl.when(jnp.logical_not(plain))
            def _():
                k_row = at + iota((1, ROWS), 1)
                masked = jnp.where((q_seg == seg_of(k_row, ends)) & (k_row <= q_row), 0.0, NEG)
                tile = jnp.maximum(j - chip + 2, 0)
                with_bias(lambda h: tiles[0, tile, h].astype(F32) + masked)

            return c

        lax.fori_loop(j_min, chip + 1, body, 0)

    attend(
        lambda p: qkv_ref[p, pl.ds(base, ROWS), :],
        lambda p, at: qkv_ref[PAIRS + p, pl.ds(at, ROWS), :],
        lambda p, at: qkv_ref[2 * PAIRS + p, pl.ds(at, ROWS), :],
        visit_scores, visit, ROWS, ROWS, s_scr, mx_scr, l_scr, acc_scr, qs, o_ref, low_ref, lse_ref,
    )


def add_heads(low_ref, other_ref, w_ref, core):
    own = pl.ds(pl.multiple_of(core * HALF, HALF), HALF)
    other = pl.ds(pl.multiple_of((1 - core) * HALF, HALF), HALF)
    return dot_nn(low_ref[...], w_ref[own, :]) + dot_nn(other_ref[...], w_ref[other, :])


def cross_stage_kernel(n_parts, at_ref, len_ref, enc_ref, deal_ref, xe_ref, gain_ref, low_ref, other_ref, *refs):
    outs, mates, parts, refs = refs[:n_parts], refs[n_parts : 2 * n_parts], refs[2 * n_parts : 3 * n_parts], refs[3 * n_parts :]
    mid_ref, in_ref, q_ref, kv_ref, o_ref, low2_ref, lse_ref, so_ref, co_ref, wc_ref, refs = *refs[:10], refs[10:]
    s_scr, mx_scr, l_scr, acc_scr, qs = refs
    chip, core, side = at_ref[0], at_ref[1], at_ref[2]
    set_rows(wc_ref, parts, side)
    for pieces, column in ((outs, core), (mates, 1 - core)):
        lanes = pl.ds(pl.multiple_of(column * HALF, 128), HALF)
        for i, piece in enumerate(pieces):
            rows = piece.shape[0]
            at = pl.multiple_of((side if i == 0 else 1 - side) * rows, rows) if n_parts > 1 else 0
            so_ref[pl.ds(at, rows), lanes] = piece[:, :HALF]
            co_ref[pl.ds(at, rows), lanes] = piece[:, HALF:]
    width = so_ref.shape[0]
    base = pl.multiple_of(chip * ROWS, ROWS)
    mid = xe_ref[pl.ds(base, ROWS), :width].astype(F32) + add_heads(low_ref, other_ref, so_ref, core)
    mid_ref[...] = mid
    normed = (mid * rms_inverse(mid) * gain_ref[...]).astype(BF16)
    in_ref[...] = normed
    q_ref[...] = dot_nn(normed, wc_ref[:, :HALF]).astype(BF16)
    step = 512

    def body(i, c):
        at = pl.multiple_of(i * step, step)
        result = dot_nn(xe_ref[pl.ds(at, step), width:], wc_ref[:, HALF:])
        for j in range(kv_ref.shape[0]):
            kv_ref[j, pl.ds(at, step), :] = result[:, 128 * j : 128 * j + 128].astype(BF16)
        return c

    lax.fori_loop(0, xe_ref.shape[0] // step, body, 0)
    _, over, mask = cross_flags(chip, len_ref, enc_ref, deal_ref)
    blocks = kv_ref.shape[1] // KEYS

    def visit(block):
        over(blocks, lambda j, r: block(j, stacked(r)))

    def visit_scores(block):
        def body(j, r):
            masked = mask(j, r)
            block(j, stacked(r), lambda p, raw: raw + jnp.concatenate([masked, masked], axis=0))

        over(blocks, body)

    attend(
        lambda p: q_ref[:, lanes_of(p)],
        lambda p, at: kv_ref[p, pl.ds(at, KEYS), :],
        lambda p, at: kv_ref[PAIRS + p, pl.ds(at, KEYS), :],
        visit_scores, visit, SUB, KEYS, s_scr, mx_scr, l_scr, acc_scr, qs, o_ref, low2_ref, lse_ref,
    )


def gelu_parts(value):
    tangent = jnp.tanh(GELU_C * (value + GELU_A * value * value * value))
    result = 0.5 * value * (1.0 + tangent)
    slope = 0.5 * (1.0 + tangent) + 0.5 * value * (1.0 - tangent * tangent) * GELU_C * (
        1.0 + 3.0 * GELU_A * value * value
    )
    return (result, slope)


def own_rows(core, rows):
    return pl.ds(pl.multiple_of(core * rows, rows), rows)


def ffn_stage_kernel(n_parts, at_ref, mid_ref, gain_ref, low_ref, other_ref, co_ref, cot_ref, mate_ref, *refs):
    inner, outer, refs = refs[:n_parts], refs[n_parts : 2 * n_parts], refs[2 * n_parts :]
    late_ref, in_ref, hid_ref, dpre_ref, cot_out, keep_ref, send_ref, e_ref, wi_ref, wo_ref, part_scr = refs
    core, side = at_ref[1], at_ref[2]
    rows = cot_ref.shape[0]
    set_rows(wi_ref, inner, side)
    set_rows(wo_ref, outer, side)
    cot_out[own_rows(core, rows), :] = cot_ref[...]
    cot_out[own_rows(1 - core, rows), :] = mate_ref[...]
    late = mid_ref[...] + add_heads(low_ref, other_ref, co_ref, core)
    late_ref[...] = late
    normed = (late * rms_inverse(late) * gain_ref[...]).astype(BF16)
    in_ref[...] = normed
    columns = 512

    def body(i, c):
        at = pl.multiple_of(i * columns, columns)
        activated, slope = gelu_parts(dot_nn(normed, wi_ref[:, pl.ds(at, columns)]))
        hid_ref[:, pl.ds(at, columns)] = activated.astype(BF16)
        grads = dot_nt(cot_out[...], wo_ref[pl.ds(at, columns), :])
        dpre_ref[:, pl.ds(at, columns)] = (grads * slope).astype(BF16)
        return c

    lax.fori_loop(0, wi_ref.shape[1] // columns, body, 0)
    e_ref[...] = dot_nt(dpre_ref[...], wi_ref[...])
    part_scr[...] = dot_nn(hid_ref[...], wo_ref[...])
    keep_ref[...] = part_scr[own_rows(core, rows), :] + late_ref[own_rows(core, rows), :]
    send_ref[...] = part_scr[own_rows(1 - core, rows), :]


def ffn_grads_kernel(n_sides, at_ref, hid_ref, cot_ref, in_ref, dpre_ref, *outs):
    side = at_ref[2]
    rows = in_ref.shape[1] // n_sides
    width = cot_ref.shape[1]
    if n_sides != 2:
        outs[0][...] = dot_tn(hid_ref[...], cot_ref[...])
        outs[1][...] = dot_tn(in_ref[...], dpre_ref[...])
        return
    keep_ref, send_ref = outs
    for owner in range(2):
        for mine, target in ((True, keep_ref), (False, send_ref)):

            @pl.when((side == owner) == mine)
            def _():
                for part in range(2):
                    units = slice((2 * owner + part) * rows, (2 * owner + part + 1) * rows)
                    block = dot_tn(hid_ref[:, units], cot_ref[...])
                    target[:, part * width : (part + 1) * width] = block.astype(target.dtype)
                block = dot_tn(in_ref[:, owner * rows : (owner + 1) * rows], dpre_ref[...])
                target[:, 2 * width :] = block.astype(target.dtype)


def norm_grad(value, gain, grad):
    inverse = rms_inverse(value)
    scaled = grad * gain
    cubed = inverse * inverse * inverse
    dvalue = inverse * scaled - value * cubed * jnp.mean(scaled * value, axis=-1, keepdims=True)
    return dvalue, jnp.sum(grad * value * inverse, axis=0, keepdims=True)


KEYS = 2 * ROWS
SUB = ROWS // 2


def cross_flags(chip, len_ref, enc_ref, deal_ref):
    starts, ends = spans(len_ref)
    e_starts, e_ends = spans(enc_ref)
    base = chip * ROWS
    ranges = []
    for i in range(len(ends)):
        low, high = jnp.int32(0), jnp.int32(0)
        for e in range(len(e_ends)):
            hit = deal_ref[0, i] == e
            low = jnp.where(hit, e_starts[e], low)
            high = jnp.where(hit, e_ends[e], high)
        ranges.append((starts[i], ends[i], low, high))

    def wanted(at, first, count):
        found = jnp.bool_(False)
        for start, end, low, high in ranges:
            live = (start < base + first + count) & (end > base + first)
            found = found | (live & (low < at + KEYS) & (high > at))
        return found

    def visit(blocks, body):
        def inner(j, c):
            for r in range(ROWS // SUB):

                @pl.when(wanted(j * KEYS, r * SUB, SUB))
                def _():
                    body(j, r)

            return c

        lax.fori_loop(0, blocks, inner, 0)

    q_seg = seg_of(base + iota((ROWS, 1), 0), ends)
    q_pair = jnp.zeros((ROWS, 1), jnp.int32)
    for i in range(len(ends)):
        q_pair = q_pair + jnp.where(q_seg == i, deal_ref[0, i], 0)

    def mask(j, r):
        k_seg = seg_of(j * KEYS + iota((1, KEYS), 1), e_ends)
        return jnp.where(q_pair[r * SUB : (r + 1) * SUB] == k_seg, 0.0, NEG)

    return wanted, visit, mask


def stacked(r):
    return slice(2 * r * SUB, 2 * (r + 1) * SUB)


def row_stats(go_ref, o_ref, lse_ref, gs, lse_scr, delta_scr, sub=ROWS):
    lane = iota((ROWS, 128), 1)
    low = lane < HEAD_DIM
    for p in range(PAIRS):
        grads = go_ref[:, lanes_of(p)]
        gs[p] = split_pair(grads, sub)
        product = grads.astype(F32) * o_ref[:, lanes_of(p)]
        for i in range(2):
            part = jnp.where(low if i == 0 else ~low, product, 0.0)
            delta = jnp.sum(part, axis=1, keepdims=True)
            lse = jnp.sum(jnp.where(lane == 2 * p + i, lse_ref[...], 0.0), axis=1, keepdims=True)
            for at in range(0, ROWS, sub):
                rows = slice(2 * at + i * sub, 2 * at + (i + 1) * sub)
                delta_scr[p, rows] = jnp.broadcast_to(delta[at : at + sub], (sub, 128))
                lse_scr[p, rows] = jnp.broadcast_to(lse[at : at + sub], (sub, 128))


def self_query_grad_kernel(
    at_ref, len_ref, tiles, qkv_ref, go_ref, o_ref, lse_ref, dq_ref, dist_ref,
    qs, gs, lse_scr, delta_scr, dq_scr, ds_scr, far_scr,
):
    chip = at_ref[0]
    starts, ends = spans(len_ref)
    base = pl.multiple_of(chip * ROWS, ROWS)
    first = first_of(base, ends)
    row_stats(go_ref, o_ref, lse_ref, gs, lse_scr, delta_scr)

    def start(p):
        qs[p] = split_pair(qkv_ref[p, pl.ds(base, ROWS), :])

    each_pair(start)
    dq_scr[...] = jnp.zeros_like(dq_scr)
    ds_scr[...] = jnp.zeros_like(ds_scr)
    far_scr[...] = jnp.zeros_like(far_scr)
    full_from = first_of(base + ROWS - 1, ends)
    q_row = base + iota((ROWS, 1), 0)
    q_seg = seg_of(q_row, ends)

    def block(j, _):
        at = pl.multiple_of(j * ROWS, ROWS)
        plain = (at >= full_from) & (j < chip - 1)

        def gradients(extra, near):
            raws = [dot_nt(qs[p], qkv_ref[PAIRS + p, pl.ds(at, ROWS), :]) for p in range(PAIRS)]
            dprobs = [dot_nt(gs[p], qkv_ref[2 * PAIRS + p, pl.ds(at, ROWS), :]) for p in range(PAIRS)]
            for p in range(PAIRS):
                grads = []
                for i in range(2):
                    h = 2 * p + i
                    rows = slice(i * ROWS, (i + 1) * ROWS)
                    probs = jnp.exp(extra(h, raws[p][rows]) - lse_scr[p, rows, :1])
                    ds = (probs * (dprobs[p][rows] - delta_scr[p, rows, :1])).astype(BF16)
                    if near is None:
                        far_scr[h] += jnp.sum(ds.astype(F32).reshape(ROWS // 8, 8, ROWS), axis=0)
                    else:
                        ds_scr[near, h] += ds.astype(F32)
                    grads.append(ds)
                dq_scr[p] += dot_nn(jnp.concatenate(grads, axis=0), qkv_ref[PAIRS + p, pl.ds(at, ROWS), :])

        @pl.when(plain)
        def _():
            gradients(lambda h, raw: raw + tiles[0, 0, h, :1, :1].astype(F32), None)

        @pl.when(jnp.logical_not(plain))
        def _():
            k_row = at + iota((1, ROWS), 1)
            masked = jnp.where((q_seg == seg_of(k_row, ends)) & (k_row <= q_row), 0.0, NEG)
            tile = jnp.maximum(j - chip + 2, 0)
            gradients(lambda h, raw: raw + (tiles[0, tile, h].astype(F32) + masked), tile)

        return 0

    lax.fori_loop(first // ROWS, chip + 1, block, 0)
    dist_ref[...] = jnp.zeros_like(dist_ref)
    lanes = iota((1, 2 * ROWS), 1)
    for p in range(PAIRS):
        dq_ref[:, 128 * p : 128 * p + 128] = join_pair(dq_scr[p]).astype(BF16)

    def fold(h, c):
        folded = jnp.concatenate([ds_scr[1, h], ds_scr[2, h]], axis=1)
        rows = ROWS
        while rows > 1:
            rows //= 2
            folded = folded[:rows] + pltpu.roll(folded[rows:], 2 * ROWS - rows, 1)
        far = jnp.sum(ds_scr[0, h], axis=0, keepdims=True) + jnp.sum(far_scr[h], axis=0, keepdims=True)
        far = jnp.sum(far, axis=1, keepdims=True)
        dist_ref[pl.ds(h, 1), :] = folded + jnp.where(lanes == 2 * ROWS - 1, far, 0.0)
        return c

    lax.fori_loop(0, LOCAL, fold, 0)


def self_key_stage_kernel(
    n_sides, at_ref, len_ref, tiles, qkv_ref, message_ref, so_ref, dq_ref, w_ref, x_ref, gain_ref, small_ref,
    keep_ref, send_ref, *refs,
):
    *outs, go_ref, stat_ref, ks, vs, dk_scr, dv_scr, dqkv_scr, h_scr, e_scr, grads_ref = refs
    chip, core = at_ref[0], at_ref[1]
    starts, ends = spans(len_ref)
    base = pl.multiple_of(chip * ROWS, ROWS)
    last = ends[-1]
    for end in reversed(ends[:-1]):
        last = jnp.where(base + ROWS - 1 < end, end, last)
    stop = (last - 1) // ROWS + 1
    full_to = ends[-1]
    for end in reversed(ends[:-1]):
        full_to = jnp.where(base < end, end, full_to)
    heads = own_rows(core, HALF)
    half = ROWS // 2

    def receive(i, c):
        both = [message_ref[2 * i + e, :half, :] for e in range(2)]
        result = dot_nt(jnp.concatenate(both, axis=0), so_ref[heads, :])
        for p in range(PAIRS):
            go_ref[p, pl.ds(pl.multiple_of(i * ROWS, ROWS), ROWS), :] = result[:, 128 * p : 128 * p + 128].astype(BF16)
        parts = message_ref[2 * i + core, half:, :].astype(F32)
        stat_ref[i] = parts[:, :ROWS] + parts[:, ROWS : 2 * ROWS] + parts[:, 2 * ROWS :]
        return c

    lax.fori_loop(chip, stop, receive, 0)

    def start(p):
        ks[p] = split_pair(qkv_ref[PAIRS + p, pl.ds(base, ROWS), :])
        vs[p] = split_pair(qkv_ref[2 * PAIRS + p, pl.ds(base, ROWS), :])

    each_pair(start)
    dk_scr[...] = jnp.zeros_like(dk_scr)
    dv_scr[...] = jnp.zeros_like(dv_scr)
    k_row = base + iota((ROWS, 1), 0)
    k_seg = seg_of(k_row, ends)

    def block(i, _):
        at = pl.multiple_of(i * ROWS, ROWS)
        plain = (at + ROWS <= full_to) & (i > chip + 1)

        def gradients(extra):
            raws = [dot_nt(ks[p], qkv_ref[p, pl.ds(at, ROWS), :]) for p in range(PAIRS)]
            dprobs = [dot_nt(vs[p], go_ref[p, pl.ds(at, ROWS), :]) for p in range(PAIRS)]
            for p in range(PAIRS):
                weights, dscores = [], []
                for e in range(2):
                    rows = slice(e * ROWS, (e + 1) * ROWS)
                    h = 2 * p + e
                    probs = jnp.exp(extra(h, raws[p][rows]) - stat_ref[i, h : h + 1, :])
                    weights.append(probs.astype(BF16))
                    dscores.append((probs * (dprobs[p][rows] - stat_ref[i, 8 + h : 9 + h, :])).astype(BF16))
                dv_scr[p] += dot_nn(jnp.concatenate(weights, axis=0), go_ref[p, pl.ds(at, ROWS), :])
                dk_scr[p] += dot_nn(jnp.concatenate(dscores, axis=0), qkv_ref[p, pl.ds(at, ROWS), :])

        @pl.when(plain)
        def _():
            gradients(lambda h, raw: raw + tiles[1, 0, h, :1, :1].astype(F32))

        @pl.when(jnp.logical_not(plain))
        def _():
            q_row = at + iota((1, ROWS), 1)
            masked = jnp.where((k_seg == seg_of(q_row, ends)) & (k_row <= q_row), 0.0, NEG)
            tile = jnp.maximum(2 - (i - chip), 0)
            gradients(lambda h, raw: raw + (tiles[1, tile, h].astype(F32) + masked))

        return 0

    lax.fori_loop(chip, stop, block, 0)
    dqkv_scr[:, :HALF] = dq_ref[...]
    for p in range(PAIRS):
        dqkv_scr[:, HALF + 128 * p : HALF + 128 * p + 128] = join_pair(dk_scr[p]).astype(BF16)
        dqkv_scr[:, 2 * HALF + 128 * p : 2 * HALF + 128 * p + 128] = join_pair(dv_scr[p]).astype(BF16)
    e_scr[...] = dot_nt(dqkv_scr[...], w_ref[...])
    keep_ref[...] = e_scr[own_rows(core, half), :]
    send_ref[...] = e_scr[own_rows(1 - core, half), :]
    wide = x_ref[...].astype(F32)
    scaled = wide * rms_inverse(wide)
    h_scr[...] = (scaled * gain_ref[...]).astype(BF16)
    dgain = jnp.sum(e_scr[...] * scaled, axis=0, keepdims=True)
    dgain = jnp.transpose(jnp.where(iota((128, dgain.shape[1]), 0) == 0, dgain, 0.0))
    columns = grads_ref.shape[1]
    grads_ref[:, columns - 128 :] = (small_ref[...] + dgain).astype(BF16)
    step = 256
    for i in range(0, h_scr.shape[1], step):
        grads_ref[i : i + step, : 2 * HALF] = dot_tn(h_scr[:, i : i + step], dqkv_scr[:, HALF:]).astype(BF16)
    give(n_sides, at_ref[2], grads_ref, outs)


def cross_grad_stage_kernel(
    at_ref, len_ref, enc_ref, deal_ref, place_ref,
    e_ref, other_ref, late_ref, gain_ref, cot_ref, co_ref, q_ref, o_ref, lse_ref, kv_ref, wc_ref,
    grad_ref, low_ref, dgain_ref, dq_ref, keep_ref, send_ref, part_ref,
    go_ref, qs, gs, lse_scr, delta_scr, dq_scr, block_scr,
):
    chip, core = at_ref[0], at_ref[1]
    dvalue, dgain = norm_grad(late_ref[...], gain_ref[...], e_ref[...] + other_ref[...])
    dgain_ref[...] = dgain
    grad = cot_ref[...].astype(F32) + dvalue
    grad_ref[...] = grad
    low_ref[...] = grad.astype(BF16)
    go_ref[...] = dot_nt(low_ref[...], co_ref[own_rows(core, HALF), :]).astype(BF16)
    wanted, _, mask = cross_flags(chip, len_ref, enc_ref, deal_ref)
    row_stats(go_ref, o_ref, lse_ref, gs, lse_scr, delta_scr, SUB)
    for p in range(PAIRS):
        qs[p] = split_pair(q_ref[:, lanes_of(p)], SUB)
    dq_scr[...] = jnp.zeros_like(dq_scr)
    half = keep_ref.shape[0] // ROWS

    def gradients(j, rows, masked):
        at = pl.multiple_of(j * KEYS, KEYS)
        raws = [dot_nt(qs[p, rows], kv_ref[p, pl.ds(at, KEYS), :]) for p in range(PAIRS)]
        dprobs = [dot_nt(gs[p, rows], kv_ref[PAIRS + p, pl.ds(at, KEYS), :]) for p in range(PAIRS)]
        for p in range(PAIRS):
            probs = jnp.exp(raws[p] + masked - lse_scr[p, rows, :1])
            ds = (probs * (dprobs[p] - delta_scr[p, rows, :1])).astype(BF16)
            dq_scr[p, rows] += dot_nn(ds, kv_ref[p, pl.ds(at, KEYS), :])
            block_scr[:, lanes_of(p)] += dot_tn(ds, qs[p, rows])
            block_scr[:, lanes_of(PAIRS + p)] += dot_tn(probs.astype(BF16), gs[p, rows])

    def block(j, c):
        at = pl.multiple_of(j * KEYS, KEYS)
        hit = wanted(at, 0, ROWS)

        @pl.when(hit)
        def _():
            block_scr[...] = jnp.zeros_like(block_scr)
            for r in range(ROWS // SUB):

                @pl.when(wanted(at, r * SUB, SUB))
                def _():
                    masked = mask(j, r)
                    gradients(j, stacked(r), jnp.concatenate([masked, masked], axis=0))

        for i in range(KEYS // ROWS):
            place = place_ref[j * (KEYS // ROWS) + i]
            upper = (place >= half).astype(jnp.int32)
            to = pl.ds(pl.multiple_of((place - upper * half) * ROWS, ROWS), ROWS)
            for mine, target in ((True, keep_ref), (False, send_ref)):
                here = (upper == at_ref[3]) == mine

                @pl.when(here & hit)
                def _():
                    target[to, :] = block_scr[i * ROWS : (i + 1) * ROWS, :].astype(BF16)

                @pl.when(here & jnp.logical_not(hit))
                def _():
                    target[to, :] = jnp.zeros((ROWS, 2 * HALF), BF16)

        return c

    lax.fori_loop(0, kv_ref.shape[1] // KEYS, block, 0)
    for p in range(PAIRS):
        dq_ref[:, 128 * p : 128 * p + 128] = join_pair(dq_scr[p], SUB).astype(BF16)
    part_ref[...] = dot_nt(dq_ref[...], wc_ref[:, :HALF])


def self_grad_start_kernel(
    at_ref, e_ref, other_ref, mid_ref, gain_ref, late_grad_ref, so_ref, o_ref, lse_ref,
    grad_ref, low_ref, dgain_ref, go_ref, message_ref,
    stat_scr,
):
    core = at_ref[1]
    dvalue, dgain = norm_grad(mid_ref[...], gain_ref[...], e_ref[...] + other_ref[...])
    dgain_ref[...] = dgain
    grad = late_grad_ref[...] + dvalue
    grad_ref[...] = grad
    low_ref[...] = grad.astype(BF16)
    go_ref[...] = dot_nt(low_ref[...], so_ref[own_rows(core, HALF), :]).astype(BF16)
    half = ROWS // 2
    message_ref[:half, :] = low_ref[own_rows(core, half), :]
    lane = iota((ROWS, 128), 1)
    stat_scr[...] = lse_ref[...]

    def pair(p):
        product = go_ref[:, lanes_of(p)].astype(F32) * o_ref[:, lanes_of(p)]
        for i in range(2):
            part = jnp.where((lane < HEAD_DIM) if i == 0 else (lane >= HEAD_DIM), product, 0.0)
            stat_scr[...] = jnp.where(lane == 8 + 2 * p + i, jnp.sum(part, axis=1, keepdims=True), stat_scr[...])

    each_pair(pair)
    rest = jnp.transpose(stat_scr[...])[:16]
    for part in range(3):
        high = rest.astype(BF16)
        message_ref[half:, part * ROWS : (part + 1) * ROWS] = high
        rest = rest - high.astype(F32)


def projection_grads_kernel(
    n_sides, at_ref, low2_ref, other2_ref, b2_ref, in_ref, dq2_ref, low1_ref, other1_ref, b1_ref, x_ref, gain_ref, dq1_ref, *outs
):
    *outs, out_ref = outs
    core, side = at_ref[1], at_ref[2]
    lanes = pl.ds(pl.multiple_of(core * HALF, 128), HALF)
    for at, own, other, grad in ((0, low2_ref, other2_ref, b2_ref), (2 * HALF, low1_ref, other1_ref, b1_ref)):
        grads = grad[:, lanes]
        for which, part in ((core, own), (1 - core, other)):
            out_ref[own_rows(which, HALF), at : at + HALF] = dot_tn(part[...], grads).astype(BF16)
    out_ref[:, HALF : 2 * HALF] = dot_tn(in_ref[...], dq2_ref[...]).astype(BF16)
    wide = x_ref[...].astype(F32)
    normed = (wide * rms_inverse(wide) * gain_ref[...]).astype(BF16)
    out_ref[:, 3 * HALF :] = dot_tn(normed, dq1_ref[...]).astype(BF16)
    give(n_sides, side, out_ref, outs)


def give(n_sides, side, value, outs):
    if n_sides == 2:
        rows = value.shape[0] // 2
        outs[0][...] = value[own_rows(side, rows), :]
        outs[1][...] = value[own_rows(1 - side, rows), :]
    else:
        outs[0][...] = value[...]


def encoder_grads_kernel(n_sides, at_ref, dkv_ref, e_ref, wc_ref, keep_ref, send_ref, *outs):
    *outs, low_scr, e_scr, grads_ref = outs
    core = at_ref[1]
    half = ROWS // 2
    low_scr[...] = dkv_ref[...].astype(BF16)
    e_scr[...] = dot_nt(low_scr[...], wc_ref[:, HALF:])
    keep_ref[...] = e_scr[own_rows(core, half), :]
    send_ref[...] = e_scr[own_rows(1 - core, half), :]
    grads_ref[...] = dot_tn(e_ref[...], low_scr[...]).astype(BF16)
    give(n_sides, at_ref[2], grads_ref, outs)


def token_grads_kernel(at_ref, e_ref, other_ref, x_ref, gain_ref, grad_ref, out_ref):
    dvalue, _ = norm_grad(x_ref[...].astype(F32), gain_ref[...], e_ref[...] + other_ref[...])
    out_ref[...] = grad_ref[own_rows(at_ref[1], out_ref.shape[0]), :] + dvalue


def finish_late_kernel(count, at_ref, place_ref, own_ref, other_ref, *refs):
    *outs, one, two, three, table, small = refs
    core, place = at_ref[1], place_ref[0]
    rows = own_ref.shape[0] // count
    columns = slice(len(outs) * HALF, len(outs) * HALF + 128)
    for i in range(count):
        part = slice(i * rows, (i + 1) * rows)
        to = pl.ds(pl.multiple_of((place ^ i) * rows, rows), rows)
        for j, out in enumerate(outs):
            lanes = slice(j * HALF, (j + 1) * HALF)
            out[to, own_lanes(core)] = own_ref[part, lanes].astype(F32)
            out[to, own_lanes(1 - core)] = other_ref[part, lanes].astype(F32)
        small[to, :] = own_ref[part, columns].astype(F32) + other_ref[part, columns].astype(F32)
    turned = jnp.transpose(small[...])
    for i, out in enumerate((one, two, three)):
        out[...] = turned[i]
    table[...] = small[: table.shape[0], 3 : 3 + HEADS]


def own_lanes(core):
    return pl.ds(pl.multiple_of(core * HALF, 128), HALF)


def finish_kernel(order, parts_ref, outer_ref, inner_ref, *outs):
    rows = parts_ref.shape[1]
    width = outer_ref.shape[1]
    side = inner_ref.shape[0]
    unit = inner_ref.shape[1] // 4
    for i, (core, place) in enumerate(order):
        at = place * rows
        for half in range(2):
            top = (2 * core + half) * side + at
            outer_ref[top : top + rows, :] = parts_ref[i, :, half * width : (half + 1) * width].astype(F32)
            lanes = slice((2 * half + core) * unit, (2 * half + core + 1) * unit)
            inner_ref[at : at + rows, lanes] = parts_ref[i, :, 2 * width + half * unit : 2 * width + (half + 1) * unit].astype(F32)
    finish_columns_kernel(order, 4 * width, parts_ref, *outs)


def finish_columns_kernel(order, skip, parts_ref, *outs):
    rows = parts_ref.shape[1]
    for i, (core, place) in enumerate(order):
        at = slice(place * rows, (place + 1) * rows)
        for j, out in enumerate(outs):
            columns = slice(skip + j * HALF, skip + (j + 1) * HALF)
            out[at, core * HALF : (core + 1) * HALF] = parts_ref[i, :, columns].astype(F32)


def pack_kernel(groups, core_ref, *refs):
    count = sum(groups)
    ins, outs = list(refs[:count]), refs[count:]
    for size, out in zip(groups, outs):
        at = 0
        for _ in range(size):
            part = ins.pop(0)
            out[:, at : at + part.shape[1]] = part[...].astype(BF16)
            at += part.shape[1]


SMEM = pl.BlockSpec(memory_space=pltpu.SMEM)
VMEM = pl.BlockSpec(memory_space=pltpu.VMEM)


def call(kernel, scalars, arrays, outs, scratch, flops):
    moved = sum(a.size * a.dtype.itemsize for a in arrays) + sum(math.prod(s) * jnp.dtype(d).itemsize for s, d in outs)
    return pl.pallas_call(
        kernel,
        out_shape=[jax.ShapeDtypeStruct(s, d) for s, d in outs],
        in_specs=[SMEM] * len(scalars) + [VMEM] * len(arrays),
        out_specs=[VMEM] * len(outs),
        scratch_shapes=[pltpu.VMEM(s, d) for s, d in scratch],
        compiler_params=pltpu.CompilerParams(vmem_limit_bytes=VMEM_LIMIT),
        cost_estimate=pl.CostEstimate(flops=1, transcendentals=0, bytes_accessed=1),
    )(*scalars, *arrays)


TILES = ((3, LOCAL, ROWS, ROWS), F32)
FAR = ((LOCAL, 8, ROWS), F32)
STACK = ((PAIRS, 2 * ROWS, 128), BF16)
COLUMN = ((PAIRS, 2 * ROWS, 128), F32)
LANE = ((ROWS, 128), F32)


def pack(core, groups):
    flat = [item for group in groups for item in group]
    return pl.pallas_call(
        functools.partial(pack_kernel, [len(g) for g in groups]),
        grid_spec=pltpu.PrefetchScalarGridSpec(
            num_scalar_prefetch=1,
            grid=(1,),
            in_specs=[
                pl.BlockSpec(shape, functools.partial(lambda index, i, c: index(c[0]), index)) for _, shape, index in flat
            ],
            out_specs=[
                pl.BlockSpec((g[0][1][0], sum(s[1] for _, s, _ in g)), lambda i, c: (0, 0)) for g in groups
            ],
        ),
        out_shape=[jax.ShapeDtypeStruct((g[0][1][0], sum(s[1] for _, s, _ in g)), BF16) for g in groups],
        compiler_params=pltpu.CompilerParams(vmem_limit_bytes=VMEM_LIMIT),
    )(core, *(w for w, _, _ in flat))


def swap_core(value):
    return lax.ppermute(value, "core", [(0, 1), (1, 0)])


def gather_fsdp(own):
    count = lax.axis_size("fsdp")
    if count != 2:
        return [lax.all_gather(own, "fsdp", axis=0, tiled=True)]
    return [own, lax.ppermute(own, "fsdp", [(0, 1), (1, 0)])]


CHIPS = ("z", "y")
GROUP = ("z", "y", "core")


def gather_rows(own):
    return lax.all_gather(own, GROUP, axis=0, tiled=True)


def bits_of(axis):
    return range((lax.axis_size(axis) - 1).bit_length())


def swap_bit(value, axis, bit):
    return lax.ppermute(value, axis, [(i, i ^ (1 << bit)) for i in range(lax.axis_size(axis))])


def parted(terms, axis, bit):
    side = (lax.axis_index(axis) >> bit) & 1
    rows = terms[0].shape[0] // 2

    def half(which):
        return [lax.dynamic_slice_in_dim(t, which * rows, rows, 0) for t in terms]

    return half(side), total(half(1 - side)).astype(BF16)


def halve(terms, axis, bit):
    keep, send = parted(terms, axis, bit)
    return keep + [swap_bit(send, axis, bit)]


def total(terms):
    return sum(t.astype(F32) for t in terms[1:]) + terms[0].astype(F32)


def steps_of(*axes):
    return [(axis, bit) for axis in axes for bit in bits_of(axis)]


def scatter(terms, steps):
    for axis, bit in steps:
        terms = halve(terms, axis, bit)
    return terms


def scatter_fsdp(terms):
    return scatter(terms, [("fsdp", bit) for bit in reversed(bits_of("fsdp"))])


def places(steps):
    nz, ny = lax.axis_size("z"), lax.axis_size("y")
    found = []
    for z in range(nz):
        for y in range(ny):
            place = 0
            for axis, bit in steps:
                place = 2 * place + (((z if axis == "z" else y) >> bit) & 1)
            found.append(place)
    return found


def after(value, *earlier):
    return lax.optimization_barrier((value, *earlier))[0]


def on_device(
    tokens, encoded, cotangent, tgt_lengths, enc_lengths, deal,
    ln_self, ln_cross, ln_ffn, bias_table,
    self_query, self_key, self_value, self_output,
    cross_query, cross_key, cross_value, cross_output,
    ffn_inner, ffn_outer,
):
    core = lax.axis_index("core")
    fsdp = lax.axis_index("fsdp")
    n_fsdp = lax.axis_size("fsdp")
    chip = lax.axis_index(CHIPS)
    steps = steps_of("y", "z")
    y_side = (lax.axis_index("y") >> steps[0][1]) & 1
    at = jnp.stack([chip, core, fsdp, y_side]).astype(jnp.int32)
    core_ref = core.reshape(1).astype(jnp.int32)
    rows, width = tokens.shape
    n = 2 * rows * lax.axis_size(CHIPS)
    side = width // n_fsdp
    hidden_half = ffn_inner.shape[1] // 2
    unit = hidden_half // n_fsdp
    wide, flat = ((ROWS, width), F32), ((ROWS, width), BF16)

    def column(weight):
        return (weight, (side, HALF), lambda c: (0, c))

    (qkv_own,) = pack(core_ref, [[column(w) for w in (self_query, self_key, self_value)]])
    w_qkv = gather_fsdp(qkv_own)
    if unit % 128 == 0:
        inner_items = [(ffn_inner, (side, unit), functools.partial(lambda o, c: (0, 2 * o + c), o)) for o in range(n_fsdp)]
    else:
        inner_units = ffn_inner.reshape(side, n_fsdp, 2, unit)
        inner_units = lax.dynamic_index_in_dim(inner_units, core, 2, keepdims=False).reshape(side, hidden_half)
        inner_items = [(inner_units, (side, hidden_half), lambda c: (0, 0))]
    out_own, cross_own, inner_own, outer_own = pack(
        after(core_ref, qkv_own),
        [
            [column(w) for w in (self_output, cross_output)],
            [column(w) for w in (cross_query, cross_key, cross_value)],
            inner_items,
            [(ffn_outer, (unit, width), lambda c: (c, 0))],
        ],
    )
    w_out = gather_fsdp(out_own)
    w_cross = gather_fsdp(cross_own)
    inner_own, outer_own = after((inner_own, outer_own), w_cross[-1])
    w_inner, w_outer = gather_fsdp(inner_own), gather_fsdp(outer_own)
    w_out_mate = [swap_core(w) for w in w_out]
    cot_mate = swap_core(cotangent)

    small = jnp.concatenate([ln_self, ln_cross, ln_ffn, bias_table.reshape(-1)], axis=0).astype(BF16)[None]
    small = gather_fsdp(small)
    if len(small) == 2:
        small = jnp.where(fsdp == 0, jnp.concatenate(small, axis=0), jnp.concatenate(small[::-1], axis=0))
    else:
        small = small[0]
    gain_self, gain_cross, gain_ffn = (
        small[:, i * side : (i + 1) * side].reshape(1, width).astype(F32) for i in range(3)
    )
    table = small[:, 3 * side :].reshape(BUCKETS, HEADS)
    table = lax.dynamic_slice_in_dim(table, core * LOCAL, LOCAL, 1).astype(F32)
    onehots = np.concatenate([QK_ONEHOT, KQ_ONEHOT], axis=0)
    biases = jnp.einsum("bh,tb->ht", table, onehots, precision=lax.Precision.HIGHEST)
    biases = jnp.pad(biases.reshape(LOCAL, 2, 2 * ROWS).swapaxes(0, 1), ((0, 0), (0, 2), (0, 0)))
    (tiles,) = call(tiles_kernel, (), (biases.reshape(16, 2 * ROWS),), [((2, *TILES[0]), BF16)], [], 1)

    xe = gather_rows(jnp.concatenate([tokens, encoded], axis=1))
    qkv, w_qkv, attn_self, low_self, lse_self = call(
        functools.partial(self_stage_kernel, len(w_qkv)), (at, tgt_lengths), (xe, gain_self, tiles, *w_qkv),
        [((3 * PAIRS, n, 128), BF16), ((width, 3 * HALF), BF16), ((ROWS, HALF), F32), ((ROWS, HALF), BF16), LANE],
        ATTEND(n),
        2 * n * width * 3 * HALF + 4 * ROWS * n * HALF,
    )
    low_self_other = swap_core(low_self)

    x_mid, in_cross, q_cross, kv_cross, attn_cross, low_cross, lse_cross, w_so, w_co, w_cross = call(
        functools.partial(cross_stage_kernel, len(w_out)), (at, tgt_lengths, enc_lengths, deal),
        (xe, gain_cross, low_self, low_self_other, *w_out, *w_out_mate, *w_cross),
        [
            wide, flat, ((ROWS, HALF), BF16), ((2 * PAIRS, n, 128), BF16), ((ROWS, HALF), F32), ((ROWS, HALF), BF16), LANE,
            ((width, width), BF16), ((width, width), BF16), ((width, 3 * HALF), BF16),
        ],
        ATTEND(n),
        2 * n * width * 2 * HALF + 4 * ROWS * n * HALF,
    )
    low_cross_other = swap_core(low_cross)

    half_rows = ((rows, width), F32)
    x_late, in_ffn, hidden, d_pre, cot, out_keep, out_send, e_ffn = call(
        functools.partial(ffn_stage_kernel, len(w_inner)), (at,),
        (x_mid, gain_ffn, low_cross, low_cross_other, w_co, cotangent, cot_mate, *w_inner, *w_outer),
        [wide, flat, ((ROWS, hidden_half), BF16), ((ROWS, hidden_half), BF16), flat, half_rows, half_rows, wide],
        [((width, hidden_half), BF16), ((hidden_half, width), BF16), wide],
        8 * ROWS * width * hidden_half,
    )
    e_ffn_other = swap_core(e_ffn)
    output = out_keep + swap_core(out_send)

    place = places(steps)
    place_ref = jnp.asarray(np.array(place, np.int32))
    nz, ny = lax.axis_size("z"), lax.axis_size("y")
    y_place = [p // nz for p in place[:ny]]
    key_place_ref = jnp.asarray(np.array([y_place[y] * nz + z for z in range(nz) for y in range(ny)], np.int32))
    grad_late, late_low, d_gain_ffn, dq_cross, dkv_keep, dkv_send, e_cross = call(
        cross_grad_stage_kernel, (at, tgt_lengths, enc_lengths, deal, key_place_ref),
        (e_ffn, e_ffn_other, x_late, gain_ffn, cot, w_co, q_cross, attn_cross, lse_cross, kv_cross, w_cross),
        [wide, flat, ((1, width), F32), ((ROWS, HALF), BF16), ((n // 2, 2 * HALF), BF16), ((n // 2, 2 * HALF), BF16), wide],
        [((ROWS, HALF), BF16), STACK, STACK, COLUMN, COLUMN, COLUMN, ((KEYS, 2 * HALF), F32)],
        10 * ROWS * n * HALF,
    )
    e_cross_other = swap_core(e_cross)
    dkv_got = swap_bit(dkv_send, *steps[0])

    grad_mid, mid_low, d_gain_cross, go_self, message = call(
        self_grad_start_kernel, (at,), (e_cross, e_cross_other, x_mid, gain_cross, grad_late, w_so, attn_self, lse_self),
        [wide, flat, ((1, width), F32), ((ROWS, HALF), BF16), ((rows + 16, width), BF16)], [LANE],
        2 * ROWS * width * HALF,
    )
    ffn_out = (
        [((side, 4 * width), BF16), ((side, 4 * width), BF16)]
        if n_fsdp == 2
        else [((hidden_half, width), F32), ((width, hidden_half), F32)]
    )
    first = call(
        functools.partial(ffn_grads_kernel, n_fsdp), (at,), (hidden, cot, in_ffn, after(d_pre, message)), ffn_out, [],
        4 * ROWS * width * hidden_half,
    )
    if n_fsdp == 2:
        first_other = lax.ppermute(first[1], "fsdp", [(0, 1), (1, 0)])
        go_self = after(go_self, first[1])
    message = lax.all_gather(message, GROUP, axis=0)
    x_chip = lax.dynamic_slice(xe, (chip * ROWS, 0), (ROWS, width))
    e_chip = lax.dynamic_slice(xe, (chip * ROWS, width), (ROWS, width))
    dq_self, dist = call(
        self_query_grad_kernel, (at, tgt_lengths), (tiles, qkv, go_self, attn_self, lse_self),
        [((ROWS, HALF), BF16), ((8, 2 * ROWS), F32)],
        [STACK, STACK, COLUMN, COLUMN, COLUMN, TILES, FAR],
        6 * ROWS * n * HALF,
    )
    def given(columns):
        return [((width // 2, columns), BF16)] * 2 if n_fsdp == 2 else [((width, columns), BF16)]

    def over_fsdp(parts):
        if n_fsdp == 2:
            return [parts[0], lax.ppermute(parts[1], "fsdp", [(0, 1), (1, 0)])]
        return scatter_fsdp(parts)

    second = call(
        functools.partial(projection_grads_kernel, n_fsdp), (at,),
        (low_cross, low_cross_other, late_low, in_cross, dq_cross, low_self, low_self_other, mid_low, x_chip, gain_self, dq_self),
        given(4 * HALF), [((width, 4 * HALF), BF16)], 8 * ROWS * width * HALF,
    )
    d_table = jnp.einsum("ht,tb->bh", dist[:LOCAL], QK_ONEHOT, precision=lax.Precision.HIGHEST)
    d_table = jnp.zeros((BUCKETS, 2, LOCAL), F32).at[:, core].set(d_table).reshape(n_fsdp, -1, HEADS)
    d_table = jnp.pad(d_table, ((0, 0), (0, side - d_table.shape[1]), (0, 0))).reshape(width, HEADS)
    none = jnp.zeros((width, 1), F32)
    small = [none, 0.5 * d_gain_cross.reshape(width, 1), 0.5 * d_gain_ffn.reshape(width, 1), d_table]
    small = jnp.pad(jnp.concatenate(small, axis=1), ((0, 0), (0, 128 - 3 - HEADS)))

    if n_fsdp == 2:
        first = [first[0], first_other]
    else:
        outer = first[0].reshape(n_fsdp, 2, side, width)
        first = jnp.concatenate([outer[:, 0], outer[:, 1], first[1].reshape(n_fsdp, side, hidden_half)], axis=2)
        first = scatter_fsdp([first.reshape(width, -1)])
    *y_steps, z_near, z_far = steps
    dkv_cross = scatter(after([dkv_keep, dkv_got], second[-1]), y_steps[1:])
    dkv_cross = total(dkv_cross).astype(BF16)
    first_keep, first_sent = parted(after(first, dkv_cross), *y_steps[0])
    first_got = swap_bit(first_sent, *y_steps[0])
    second = over_fsdp(after(second, first_sent))
    dkv_cross = lax.psum_scatter(dkv_cross, "z", scatter_dimension=0, tiled=True)

    e_keep, e_send, *fourth = call(
        functools.partial(self_key_stage_kernel, n_fsdp), (at, tgt_lengths),
        (tiles, qkv, after(message, first_sent), w_so, dq_self, w_qkv, x_chip, gain_self, small),
        [half_rows, half_rows, *given(2 * HALF + 128)],
        [
            ((PAIRS, n, 128), BF16), ((n // ROWS, 16, ROWS), F32), STACK, STACK, COLUMN, COLUMN,
            ((ROWS, 3 * HALF), BF16), flat, wide, ((width, 2 * HALF + 128), BF16),
        ],
        8 * ROWS * n * HALF,
    )
    fourth_sent = fourth[-1]
    fourth = over_fsdp(fourth)
    first = scatter(first_keep + [after(first_got, fourth_sent)], y_steps[1:])
    first_keep, first_sent = parted(first, *z_near)
    first_got = swap_bit(first_sent, *z_near)
    second, fourth = after((second, fourth), first_sent)
    second = jnp.concatenate([total(second), total(fourth)], axis=1).astype(BF16)
    second_keep, second_sent = parted([second], *y_steps[0])
    second_got = swap_bit(second_sent, *y_steps[0])
    enc_keep, enc_send, *third = call(
        functools.partial(encoder_grads_kernel, n_fsdp), (at,), (after(dkv_cross, second_sent), e_chip, w_cross),
        [half_rows, half_rows, *given(2 * HALF)],
        [((ROWS, 2 * HALF), BF16), wide, ((width, 2 * HALF), BF16)], 8 * ROWS * width * HALF,
    )
    third_sent = third[-1]
    third = over_fsdp(third)
    first_keep, first_sent = parted(first_keep + [after(first_got, third_sent)], *z_far)
    first_got = swap_bit(first_sent, *z_far)
    (grad_tokens,) = call(
        token_grads_kernel, (at,), (e_keep, swap_core(after(e_send, first_sent)), tokens, gain_self, grad_mid),
        [half_rows], [], 10 * rows * width,
    )
    enc_grad = enc_keep + swap_core(after(enc_send, first_sent))

    second = scatter(second_keep + [after(second_got, grad_tokens, enc_grad)], y_steps[1:])
    second_keep, second_sent = parted(second, *z_near)
    second_got = swap_bit(second_sent, *z_near)
    late_keep, late_sent = parted(after(third, second_sent), *y_steps[0])
    late_got = swap_bit(late_sent, *y_steps[0])
    first = total(first_keep + [after(first_got, late_sent)]).astype(BF16)
    second_keep, second_sent = parted(second_keep + [after(second_got, first)], *z_far)
    second_got = swap_bit(second_sent, *z_far)
    late = scatter(late_keep + [after(late_got, second_sent)], y_steps[1:])
    late_keep, late_sent = parted(late, *z_near)
    late_got = swap_bit(late_sent, *z_near)
    second = total(second_keep + [after(second_got, late_sent)]).astype(BF16)
    early = lax.all_gather(jnp.concatenate([first, second[:, : 4 * HALF]], axis=1), GROUP, axis=0)
    late = total(halve(late_keep + [after(late_got, second)], *z_far)).astype(BF16)
    late = jnp.concatenate([late, second[:, 4 * HALF :]], axis=1)
    for axis, bit in reversed(steps):
        late = jnp.concatenate([late, swap_bit(late, axis, bit)], axis=0)
    late_other = swap_core(late)
    early = after(early, late_other)

    matrix = ((side, width), F32)
    own_place = place_ref[chip].reshape(1)
    if side // len(place) % 8 == 0:
        g_ck, g_cv, g_sk, g_sv, *gains, g_table = call(
            functools.partial(finish_late_kernel, len(place)), (at, own_place), (late, late_other),
            [matrix] * 4 + [((side,), F32)] * 3 + [(bias_table.shape, F32)], [((side, 128), F32)], 8 * side * width,
        )
    else:
        blocks = jnp.stack([late, late_other]).reshape(2, len(place), side // len(place), -1)
        blocks = jnp.take(blocks, own_place[0] ^ jnp.arange(len(place), dtype=jnp.int32), axis=1)
        blocks = jnp.where(core == 0, blocks, blocks[::-1]).astype(F32).reshape(2, side, -1)
        g_ck, g_cv, g_sk, g_sv = (
            jnp.swapaxes(blocks[:, :, i : i + HALF], 0, 1).reshape(side, width) for i in range(0, 4 * HALF, HALF)
        )
        small = jnp.sum(blocks[:, :, 4 * HALF :], axis=0)
        gains = [small[:, i] for i in range(3)]
        g_table = small[: bias_table.shape[0], 3 : 3 + HEADS]
    order = [(c, p) for p in place for c in range(2)]
    if n_fsdp == 2:
        g_outer, g_inner, g_co, g_cq, g_so, g_sq = call(
            functools.partial(finish_kernel, order), (), (early,),
            [(ffn_outer.shape, F32), (ffn_inner.shape, F32), *[matrix] * 4], [], 8 * side * width,
        )
    else:
        sources = np.argsort([2 * p + c for c, p in order])
        pair = jnp.swapaxes(early[sources].reshape(len(place), 2, -1, early.shape[2]), 0, 1)
        pair = pair.reshape(2, side, -1).astype(F32)
        g_outer = pair[:, :, : 2 * width].reshape(2, side, 2, width)
        g_outer = jnp.swapaxes(g_outer, 1, 2).reshape(ffn_outer.shape)
        g_inner = jnp.transpose(pair[:, :, 2 * width : 4 * width].reshape(2, side, n_fsdp, unit), (1, 2, 0, 3))
        g_inner = g_inner.reshape(ffn_inner.shape)
        g_co, g_cq, g_so, g_sq = call(
            functools.partial(finish_columns_kernel, order, 4 * width), (), (early,), [matrix] * 4, [], 8 * side * width
        )

    return (
        output, grad_tokens, enc_grad,
        *gains, g_table,
        g_sq, g_sk, g_sv, g_so, g_cq, g_ck, g_cv, g_co, g_inner, g_outer,
    )


def solution(mesh):
    n_ctx, n_fsdp = mesh.shape["ctx"], mesh.shape["fsdp"]
    n_z = 4
    grid = Mesh(mesh.devices.reshape(n_z, n_ctx // (2 * n_z), 2, n_fsdp), ("z", "y", "core", "fsdp"))
    by_rows = P(("fsdp", "z", "y", "core"), None)
    split = P("fsdp", None)
    vector = P("fsdp")
    in_specs = (by_rows,) * 3 + (split,) * 3 + (vector,) * 3 + (split,) * 11
    out_specs = (by_rows,) * 3 + (vector,) * 3 + (split,) * 11
    return jax.shard_map(on_device, mesh=grid, in_specs=in_specs, out_specs=out_specs, check_vma=False)
```

```python
import functools
import math

import jax
import jax.numpy as jnp
import numpy as np
from jax import lax
from jax.experimental import pallas as pl
from jax.experimental.pallas import tpu as pltpu
from jax.sharding import Mesh
from jax.sharding import PartitionSpec as P

HEADS = 12
HEAD_DIM = 64
BUCKETS = 32
EPS = 1e-06
NEG = -1e30
GELU_C = 0.7978845608028654
GELU_A = 0.044715

LOCAL = HEADS // 2
PAIRS = LOCAL // 2
HALF = LOCAL * HEAD_DIM
ROWS = 256
VMEM_LIMIT = 56 << 20

F32 = jnp.float32
BF16 = jnp.bfloat16


def bucket_edges():
    edges = []
    for level in range(1, 16):
        distance = 16
        while int(math.log(distance / 16.0) / math.log(8.0) * 16.0) < level:
            distance += 1
        edges.append(distance)
    return edges


def buckets_of(distances):
    clipped = np.maximum(np.asarray(distances), 0)
    large = np.full(clipped.shape, 16)
    for edge in bucket_edges():
        large = large + (clipped >= edge)
    return np.where(clipped < 16, clipped, large)


LANES = np.arange(2 * ROWS)
QK_DISTANCE = np.where(LANES <= ROWS, ROWS - LANES, 3 * ROWS - LANES)
KQ_DISTANCE = LANES
QK_ONEHOT = np.eye(BUCKETS, dtype=np.float32)[buckets_of(QK_DISTANCE)]
KQ_ONEHOT = np.eye(BUCKETS, dtype=np.float32)[buckets_of(KQ_DISTANCE)]


def dot_nt(left, right):
    return lax.dot_general(left, right, (((1,), (1,)), ((), ())), preferred_element_type=F32)


def dot_tn(left, right):
    return lax.dot_general(left, right, (((0,), (0,)), ((), ())), preferred_element_type=F32)


def dot_nn(left, right):
    return lax.dot_general(left, right, (((1,), (0,)), ((), ())), preferred_element_type=F32)


def spans(ref):
    starts, ends, at = [], [], jnp.int32(0)
    for i in range(ref.shape[1]):
        starts.append(at)
        at = at + ref[0, i]
        ends.append(at)
    return starts, ends


def seg_of(index, ends):
    found = jnp.zeros(index.shape, jnp.int32)
    for end in ends[:-1]:
        found = found + (index >= end).astype(jnp.int32)
    return found


def iota(shape, axis):
    return lax.broadcasted_iota(jnp.int32, shape, axis)


def split_pair(pair, sub=ROWS):
    low = iota((sub, pair.shape[1]), 1) < HEAD_DIM
    zero = jnp.zeros((sub, pair.shape[1]), pair.dtype)
    parts = []
    for at in range(0, pair.shape[0], sub):
        part = pair[at : at + sub]
        parts += [jnp.where(low, part, zero), jnp.where(low, zero, part)]
    return jnp.concatenate(parts, axis=0)


def head_rows(both, e, sub=ROWS):
    parts = [both[at + e * sub : at + (e + 1) * sub] for at in range(0, both.shape[0], 2 * sub)]
    return parts[0] if len(parts) == 1 else jnp.concatenate(parts, axis=0)


def join_pair(both, sub=ROWS):
    first = head_rows(both, 0, sub)
    return jnp.where(iota(first.shape, 1) < HEAD_DIM, first, head_rows(both, 1, sub))


def tiles_kernel(bias_ref, tiles_ref):
    def head(h, c):
        for which in range(2):
            row = bias_ref[pl.ds(8 * which + h, 1), :]
            rolled = pltpu.roll(jnp.broadcast_to(row, (ROWS, 2 * ROWS)), 0, 1, stride=1, stride_axis=0)
            first, second = (1, 2) if which == 0 else (2, 1)
            tiles_ref[which, first, h] = rolled[:, :ROWS].astype(BF16)
            tiles_ref[which, second, h] = rolled[:, ROWS:].astype(BF16)
            tiles_ref[which, 0, h] = jnp.broadcast_to(row[:, 2 * ROWS - 1 :], (ROWS, ROWS)).astype(BF16)
        return c

    lax.fori_loop(0, LOCAL, head, 0)


def lanes_of(p):
    return slice(p * 128, p * 128 + 128) if isinstance(p, int) else pl.ds(pl.multiple_of(p * 128, 128), 128)


def each_pair(body):
    for p in range(PAIRS):
        body(p)


def rms_inverse(value):
    return lax.rsqrt(jnp.mean(value * value, axis=-1, keepdims=True) + EPS)


def together(n):
    return PAIRS if n <= 2048 else 1


def attend(queries, keys, values, visit_scores, visit, sub, step, s_scr, mx_scr, l_scr, acc_scr, qs, o_ref, low_ref, lse_ref):
    count = s_scr.shape[0]
    lse_ref[...] = jnp.zeros_like(lse_ref)
    lane = iota((ROWS, 128), 1)

    def group(g):
        for c in range(count):
            qs[c] = split_pair(queries(g * count + c), sub)
        mx_scr[...] = jnp.full_like(mx_scr, NEG)

        def scores(j, rows, extra):
            at = pl.multiple_of(j * step, step)
            raws = [dot_nt(qs[c, rows], keys(g * count + c, at)) for c in range(count)]
            for c in range(count):
                value = extra(g * count + c, raws[c])
                s_scr[c, rows, pl.ds(at, step)] = value
                mx_scr[c, rows] = functools.reduce(
                    jnp.maximum, [value[:, i : i + 128] for i in range(0, step, 128)], mx_scr[c, rows]
                )

        visit_scores(scores)
        for c in range(count):
            mx_scr[c] = jnp.broadcast_to(jnp.max(mx_scr[c], axis=1, keepdims=True), mx_scr.shape[1:])
        l_scr[...] = jnp.zeros_like(l_scr)
        acc_scr[...] = jnp.zeros_like(acc_scr)

        def weigh(j, rows):
            at = pl.multiple_of(j * step, step)
            for c in range(count):
                weights = jnp.exp(s_scr[c, rows, pl.ds(at, step)] - mx_scr[c, rows, :1])
                l_scr[c, rows] += sum(weights[:, i : i + 128] for i in range(128, step, 128)) + weights[:, :128]
                acc_scr[c, rows] += dot_nn(weights.astype(BF16), values(g * count + c, at))

        visit(weigh)
        for c in range(count):
            p = g * count + c
            total = jnp.sum(l_scr[c], axis=1, keepdims=True)
            result = join_pair(acc_scr[c] / total, sub)
            o_ref[:, lanes_of(p)] = result
            low_ref[:, lanes_of(p)] = result.astype(BF16)
            both = mx_scr[c, :, :1] + jnp.log(total)
            lse = jnp.where(lane == 2 * p, head_rows(both, 0, sub), lse_ref[...])
            lse_ref[...] = jnp.where(lane == 2 * p + 1, head_rows(both, 1, sub), lse)

    if count == PAIRS:
        group(0)
    else:
        lax.fori_loop(0, PAIRS // count, lambda g, c: (group(g), c)[1], 0)


ATTEND = lambda n: [
    ((together(n), 2 * ROWS, n), F32), ((together(n), 2 * ROWS, 128), F32), ((together(n), 2 * ROWS, 128), F32),
    ((together(n), 2 * ROWS, 128), F32), ((together(n), 2 * ROWS, 128), BF16),
]


def set_rows(target, parts, side):
    if len(parts) == 1:
        target[...] = parts[0][...]
        return
    rows = parts[0].shape[0]
    target[pl.ds(pl.multiple_of(side * rows, rows), rows), :] = parts[0][...]
    target[pl.ds(pl.multiple_of((1 - side) * rows, rows), rows), :] = parts[1][...]


def first_of(base, ends):
    first = jnp.int32(0)
    for end in ends[:-1]:
        first = jnp.where(base >= end, end, first)
    return first


def self_stage_kernel(n_parts, at_ref, len_ref, xe_ref, gain_ref, tiles, *refs):
    parts, refs = refs[:n_parts], refs[n_parts:]
    qkv_ref, w_ref, o_ref, low_ref, lse_ref, s_scr, mx_scr, l_scr, acc_scr, qs = refs
    chip, side = at_ref[0], at_ref[2]
    set_rows(w_ref, parts, side)
    width = w_ref.shape[0]
    step = 512

    def body(i, c):
        at = pl.multiple_of(i * step, step)
        wide = xe_ref[pl.ds(at, step), :width].astype(F32)
        value = (wide * rms_inverse(wide) * gain_ref[...]).astype(BF16)
        result = dot_nn(value, w_ref[...])
        for j in range(qkv_ref.shape[0]):
            qkv_ref[j, pl.ds(at, step), :] = result[:, 128 * j : 128 * j + 128].astype(BF16)
        return c

    lax.fori_loop(0, xe_ref.shape[0] // step, body, 0)

    starts, ends = spans(len_ref)
    base = pl.multiple_of(chip * ROWS, ROWS)
    j_min = first_of(base, ends) // ROWS
    full_from = first_of(base + ROWS - 1, ends)
    q_row = base + iota((ROWS, 1), 0)
    q_seg = seg_of(q_row, ends)

    rows = slice(0, 2 * ROWS)

    def visit(block):
        lax.fori_loop(j_min, chip + 1, lambda j, c: (block(j, rows), c)[1], 0)

    def visit_scores(block):
        def body(j, c):
            at = pl.multiple_of(j * ROWS, ROWS)
            plain = (at >= full_from) & (j < chip - 1)

            def with_bias(bias):
                def extra(p, raw):
                    return jnp.concatenate([raw[:ROWS] + bias(2 * p), raw[ROWS:] + bias(2 * p + 1)], axis=0)

                block(j, rows, extra)

            @pl.when(plain)
            def _():
                with_bias(lambda h: tiles[0, 0, h, :1, :1].astype(F32))

            @pl.when(jnp.logical_not(plain))
            def _():
                k_row = at + iota((1, ROWS), 1)
                masked = jnp.where((q_seg == seg_of(k_row, ends)) & (k_row <= q_row), 0.0, NEG)
                tile = jnp.maximum(j - chip + 2, 0)
                with_bias(lambda h: tiles[0, tile, h].astype(F32) + masked)

            return c

        lax.fori_loop(j_min, chip + 1, body, 0)

    attend(
        lambda p: qkv_ref[p, pl.ds(base, ROWS), :],
        lambda p, at: qkv_ref[PAIRS + p, pl.ds(at, ROWS), :],
        lambda p, at: qkv_ref[2 * PAIRS + p, pl.ds(at, ROWS), :],
        visit_scores, visit, ROWS, ROWS, s_scr, mx_scr, l_scr, acc_scr, qs, o_ref, low_ref, lse_ref,
    )


def add_heads(low_ref, other_ref, w_ref, core):
    own = pl.ds(pl.multiple_of(core * HALF, HALF), HALF)
    other = pl.ds(pl.multiple_of((1 - core) * HALF, HALF), HALF)
    return dot_nn(low_ref[...], w_ref[own, :]) + dot_nn(other_ref[...], w_ref[other, :])


def cross_stage_kernel(n_parts, at_ref, len_ref, enc_ref, deal_ref, xe_ref, gain_ref, low_ref, other_ref, *refs):
    outs, mates, parts, refs = refs[:n_parts], refs[n_parts : 2 * n_parts], refs[2 * n_parts : 3 * n_parts], refs[3 * n_parts :]
    mid_ref, in_ref, q_ref, kv_ref, o_ref, low2_ref, lse_ref, so_ref, co_ref, wc_ref, refs = *refs[:10], refs[10:]
    s_scr, mx_scr, l_scr, acc_scr, qs = refs
    chip, core, side = at_ref[0], at_ref[1], at_ref[2]
    set_rows(wc_ref, parts, side)
    for pieces, column in ((outs, core), (mates, 1 - core)):
        lanes = pl.ds(pl.multiple_of(column * HALF, 128), HALF)
        for i, piece in enumerate(pieces):
            rows = piece.shape[0]
            at = pl.multiple_of((side if i == 0 else 1 - side) * rows, rows) if n_parts > 1 else 0
            so_ref[pl.ds(at, rows), lanes] = piece[:, :HALF]
            co_ref[pl.ds(at, rows), lanes] = piece[:, HALF:]
    width = so_ref.shape[0]
    base = pl.multiple_of(chip * ROWS, ROWS)
    mid = xe_ref[pl.ds(base, ROWS), :width].astype(F32) + add_heads(low_ref, other_ref, so_ref, core)
    mid_ref[...] = mid
    normed = (mid * rms_inverse(mid) * gain_ref[...]).astype(BF16)
    in_ref[...] = normed
    q_ref[...] = dot_nn(normed, wc_ref[:, :HALF]).astype(BF16)
    step = 512

    def body(i, c):
        at = pl.multiple_of(i * step, step)
        result = dot_nn(xe_ref[pl.ds(at, step), width:], wc_ref[:, HALF:])
        for j in range(kv_ref.shape[0]):
            kv_ref[j, pl.ds(at, step), :] = result[:, 128 * j : 128 * j + 128].astype(BF16)
        return c

    lax.fori_loop(0, xe_ref.shape[0] // step, body, 0)
    _, over, mask = cross_flags(chip, len_ref, enc_ref, deal_ref)
    blocks = kv_ref.shape[1] // KEYS

    def visit(block):
        over(blocks, lambda j, r: block(j, stacked(r)))

    def visit_scores(block):
        def body(j, r):
            masked = mask(j, r)
            block(j, stacked(r), lambda p, raw: raw + jnp.concatenate([masked, masked], axis=0))

        over(blocks, body)

    attend(
        lambda p: q_ref[:, lanes_of(p)],
        lambda p, at: kv_ref[p, pl.ds(at, KEYS), :],
        lambda p, at: kv_ref[PAIRS + p, pl.ds(at, KEYS), :],
        visit_scores, visit, SUB, KEYS, s_scr, mx_scr, l_scr, acc_scr, qs, o_ref, low2_ref, lse_ref,
    )


def gelu_parts(value):
    tangent = jnp.tanh(GELU_C * (value + GELU_A * value * value * value))
    result = 0.5 * value * (1.0 + tangent)
    slope = 0.5 * (1.0 + tangent) + 0.5 * value * (1.0 - tangent * tangent) * GELU_C * (
        1.0 + 3.0 * GELU_A * value * value
    )
    return (result, slope)


def own_rows(core, rows):
    return pl.ds(pl.multiple_of(core * rows, rows), rows)


def ffn_stage_kernel(n_parts, at_ref, mid_ref, gain_ref, low_ref, other_ref, co_ref, cot_ref, mate_ref, *refs):
    inner, outer, refs = refs[:n_parts], refs[n_parts : 2 * n_parts], refs[2 * n_parts :]
    late_ref, in_ref, hid_ref, dpre_ref, cot_out, keep_ref, send_ref, e_ref, wi_ref, wo_ref, part_scr = refs
    core, side = at_ref[1], at_ref[2]
    rows = cot_ref.shape[0]
    set_rows(wi_ref, inner, side)
    set_rows(wo_ref, outer, side)
    cot_out[own_rows(core, rows), :] = cot_ref[...]
    cot_out[own_rows(1 - core, rows), :] = mate_ref[...]
    late = mid_ref[...] + add_heads(low_ref, other_ref, co_ref, core)
    late_ref[...] = late
    normed = (late * rms_inverse(late) * gain_ref[...]).astype(BF16)
    in_ref[...] = normed
    columns = 512

    def body(i, c):
        at = pl.multiple_of(i * columns, columns)
        activated, slope = gelu_parts(dot_nn(normed, wi_ref[:, pl.ds(at, columns)]))
        hid_ref[:, pl.ds(at, columns)] = activated.astype(BF16)
        grads = dot_nt(cot_out[...], wo_ref[pl.ds(at, columns), :])
        dpre_ref[:, pl.ds(at, columns)] = (grads * slope).astype(BF16)
        return c

    lax.fori_loop(0, wi_ref.shape[1] // columns, body, 0)
    e_ref[...] = dot_nt(dpre_ref[...], wi_ref[...])
    part_scr[...] = dot_nn(hid_ref[...], wo_ref[...])
    keep_ref[...] = part_scr[own_rows(core, rows), :] + late_ref[own_rows(core, rows), :]
    send_ref[...] = part_scr[own_rows(1 - core, rows), :]


def ffn_grads_kernel(n_sides, at_ref, hid_ref, cot_ref, in_ref, dpre_ref, *outs):
    side = at_ref[2]
    rows = in_ref.shape[1] // n_sides
    width = cot_ref.shape[1]
    if n_sides != 2:
        outs[0][...] = dot_tn(hid_ref[...], cot_ref[...])
        outs[1][...] = dot_tn(in_ref[...], dpre_ref[...])
        return
    keep_ref, send_ref = outs
    for owner in range(2):
        for mine, target in ((True, keep_ref), (False, send_ref)):

            @pl.when((side == owner) == mine)
            def _():
                for part in range(2):
                    units = slice((2 * owner + part) * rows, (2 * owner + part + 1) * rows)
                    block = dot_tn(hid_ref[:, units], cot_ref[...])
                    target[:, part * width : (part + 1) * width] = block.astype(target.dtype)
                block = dot_tn(in_ref[:, owner * rows : (owner + 1) * rows], dpre_ref[...])
                target[:, 2 * width :] = block.astype(target.dtype)


def norm_grad(value, gain, grad):
    inverse = rms_inverse(value)
    scaled = grad * gain
    cubed = inverse * inverse * inverse
    dvalue = inverse * scaled - value * cubed * jnp.mean(scaled * value, axis=-1, keepdims=True)
    return dvalue, jnp.sum(grad * value * inverse, axis=0, keepdims=True)


KEYS = 2 * ROWS
SUB = ROWS


def cross_flags(chip, len_ref, enc_ref, deal_ref):
    starts, ends = spans(len_ref)
    e_starts, e_ends = spans(enc_ref)
    base = chip * ROWS
    ranges = []
    for i in range(len(ends)):
        low, high = jnp.int32(0), jnp.int32(0)
        for e in range(len(e_ends)):
            hit = deal_ref[0, i] == e
            low = jnp.where(hit, e_starts[e], low)
            high = jnp.where(hit, e_ends[e], high)
        ranges.append((starts[i], ends[i], low, high))

    def wanted(at, first, count):
        found = jnp.bool_(False)
        for start, end, low, high in ranges:
            live = (start < base + first + count) & (end > base + first)
            found = found | (live & (low < at + KEYS) & (high > at))
        return found

    def visit(blocks, body):
        def inner(j, c):
            for r in range(ROWS // SUB):

                @pl.when(wanted(j * KEYS, r * SUB, SUB))
                def _():
                    body(j, r)

            return c

        lax.fori_loop(0, blocks, inner, 0)

    q_seg = seg_of(base + iota((ROWS, 1), 0), ends)
    q_pair = jnp.zeros((ROWS, 1), jnp.int32)
    for i in range(len(ends)):
        q_pair = q_pair + jnp.where(q_seg == i, deal_ref[0, i], 0)

    def mask(j, r):
        k_seg = seg_of(j * KEYS + iota((1, KEYS), 1), e_ends)
        return jnp.where(q_pair[r * SUB : (r + 1) * SUB] == k_seg, 0.0, NEG)

    return wanted, visit, mask


def stacked(r):
    return slice(2 * r * SUB, 2 * (r + 1) * SUB)


def row_stats(go_ref, o_ref, lse_ref, gs, lse_scr, delta_scr, sub=ROWS):
    lane = iota((ROWS, 128), 1)
    low = lane < HEAD_DIM
    for p in range(PAIRS):
        grads = go_ref[:, lanes_of(p)]
        gs[p] = split_pair(grads, sub)
        product = grads.astype(F32) * o_ref[:, lanes_of(p)]
        for i in range(2):
            part = jnp.where(low if i == 0 else ~low, product, 0.0)
            delta = jnp.sum(part, axis=1, keepdims=True)
            lse = jnp.sum(jnp.where(lane == 2 * p + i, lse_ref[...], 0.0), axis=1, keepdims=True)
            for at in range(0, ROWS, sub):
                rows = slice(2 * at + i * sub, 2 * at + (i + 1) * sub)
                delta_scr[p, rows] = jnp.broadcast_to(delta[at : at + sub], (sub, 128))
                lse_scr[p, rows] = jnp.broadcast_to(lse[at : at + sub], (sub, 128))


def self_query_grad_kernel(
    at_ref, len_ref, tiles, qkv_ref, go_ref, o_ref, lse_ref, dq_ref, dist_ref,
    qs, gs, lse_scr, delta_scr, dq_scr, ds_scr, far_scr,
):
    chip = at_ref[0]
    starts, ends = spans(len_ref)
    base = pl.multiple_of(chip * ROWS, ROWS)
    first = first_of(base, ends)
    row_stats(go_ref, o_ref, lse_ref, gs, lse_scr, delta_scr)

    def start(p):
        qs[p] = split_pair(qkv_ref[p, pl.ds(base, ROWS), :])

    each_pair(start)
    dq_scr[...] = jnp.zeros_like(dq_scr)
    ds_scr[...] = jnp.zeros_like(ds_scr)
    far_scr[...] = jnp.zeros_like(far_scr)
    full_from = first_of(base + ROWS - 1, ends)
    q_row = base + iota((ROWS, 1), 0)
    q_seg = seg_of(q_row, ends)

    def block(j, _):
        at = pl.multiple_of(j * ROWS, ROWS)
        plain = (at >= full_from) & (j < chip - 1)

        def gradients(extra, near):
            raws = [dot_nt(qs[p], qkv_ref[PAIRS + p, pl.ds(at, ROWS), :]) for p in range(PAIRS)]
            dprobs = [dot_nt(gs[p], qkv_ref[2 * PAIRS + p, pl.ds(at, ROWS), :]) for p in range(PAIRS)]
            for p in range(PAIRS):
                grads = []
                for i in range(2):
                    h = 2 * p + i
                    rows = slice(i * ROWS, (i + 1) * ROWS)
                    probs = jnp.exp(extra(h, raws[p][rows]) - lse_scr[p, rows, :1])
                    ds = (probs * (dprobs[p][rows] - delta_scr[p, rows, :1])).astype(BF16)
                    if near is None:
                        far_scr[h] += jnp.sum(ds.astype(F32).reshape(ROWS // 8, 8, ROWS), axis=0)
                    else:
                        ds_scr[near, h] += ds.astype(F32)
                    grads.append(ds)
                dq_scr[p] += dot_nn(jnp.concatenate(grads, axis=0), qkv_ref[PAIRS + p, pl.ds(at, ROWS), :])

        @pl.when(plain)
        def _():
            gradients(lambda h, raw: raw + tiles[0, 0, h, :1, :1].astype(F32), None)

        @pl.when(jnp.logical_not(plain))
        def _():
            k_row = at + iota((1, ROWS), 1)
            masked = jnp.where((q_seg == seg_of(k_row, ends)) & (k_row <= q_row), 0.0, NEG)
            tile = jnp.maximum(j - chip + 2, 0)
            gradients(lambda h, raw: raw + (tiles[0, tile, h].astype(F32) + masked), tile)

        return 0

    lax.fori_loop(first // ROWS, chip + 1, block, 0)
    dist_ref[...] = jnp.zeros_like(dist_ref)
    lanes = iota((1, 2 * ROWS), 1)
    for p in range(PAIRS):
        dq_ref[:, 128 * p : 128 * p + 128] = join_pair(dq_scr[p]).astype(BF16)

    def fold(h, c):
        folded = jnp.concatenate([ds_scr[1, h], ds_scr[2, h]], axis=1)
        rows = ROWS
        while rows > 1:
            rows //= 2
            folded = folded[:rows] + pltpu.roll(folded[rows:], 2 * ROWS - rows, 1)
        far = jnp.sum(ds_scr[0, h], axis=0, keepdims=True) + jnp.sum(far_scr[h], axis=0, keepdims=True)
        far = jnp.sum(far, axis=1, keepdims=True)
        dist_ref[pl.ds(h, 1), :] = folded + jnp.where(lanes == 2 * ROWS - 1, far, 0.0)
        return c

    lax.fori_loop(0, LOCAL, fold, 0)


def self_key_stage_kernel(
    n_sides, at_ref, len_ref, tiles, qkv_ref, message_ref, so_ref, dq_ref, w_ref, x_ref, gain_ref, small_ref,
    keep_ref, send_ref, *refs,
):
    *outs, go_ref, stat_ref, ks, vs, dk_scr, dv_scr, dqkv_scr, h_scr, e_scr, grads_ref = refs
    chip, core = at_ref[0], at_ref[1]
    starts, ends = spans(len_ref)
    base = pl.multiple_of(chip * ROWS, ROWS)
    last = ends[-1]
    for end in reversed(ends[:-1]):
        last = jnp.where(base + ROWS - 1 < end, end, last)
    stop = (last - 1) // ROWS + 1
    full_to = ends[-1]
    for end in reversed(ends[:-1]):
        full_to = jnp.where(base < end, end, full_to)
    heads = own_rows(core, HALF)
    half = ROWS // 2

    def receive(i, c):
        both = [message_ref[2 * i + e, :half, :] for e in range(2)]
        result = dot_nt(jnp.concatenate(both, axis=0), so_ref[heads, :])
        for p in range(PAIRS):
            go_ref[p, pl.ds(pl.multiple_of(i * ROWS, ROWS), ROWS), :] = result[:, 128 * p : 128 * p + 128].astype(BF16)
        parts = message_ref[2 * i + core, half:, :].astype(F32)
        stat_ref[i] = parts[:, :ROWS] + parts[:, ROWS : 2 * ROWS] + parts[:, 2 * ROWS :]
        return c

    lax.fori_loop(chip, stop, receive, 0)

    def start(p):
        ks[p] = split_pair(qkv_ref[PAIRS + p, pl.ds(base, ROWS), :])
        vs[p] = split_pair(qkv_ref[2 * PAIRS + p, pl.ds(base, ROWS), :])

    each_pair(start)
    dk_scr[...] = jnp.zeros_like(dk_scr)
    dv_scr[...] = jnp.zeros_like(dv_scr)
    k_row = base + iota((ROWS, 1), 0)
    k_seg = seg_of(k_row, ends)

    def block(i, _):
        at = pl.multiple_of(i * ROWS, ROWS)
        plain = (at + ROWS <= full_to) & (i > chip + 1)

        def gradients(extra):
            raws = [dot_nt(ks[p], qkv_ref[p, pl.ds(at, ROWS), :]) for p in range(PAIRS)]
            dprobs = [dot_nt(vs[p], go_ref[p, pl.ds(at, ROWS), :]) for p in range(PAIRS)]
            for p in range(PAIRS):
                weights, dscores = [], []
                for e in range(2):
                    rows = slice(e * ROWS, (e + 1) * ROWS)
                    h = 2 * p + e
                    probs = jnp.exp(extra(h, raws[p][rows]) - stat_ref[i, h : h + 1, :])
                    weights.append(probs.astype(BF16))
                    dscores.append((probs * (dprobs[p][rows] - stat_ref[i, 8 + h : 9 + h, :])).astype(BF16))
                dv_scr[p] += dot_nn(jnp.concatenate(weights, axis=0), go_ref[p, pl.ds(at, ROWS), :])
                dk_scr[p] += dot_nn(jnp.concatenate(dscores, axis=0), qkv_ref[p, pl.ds(at, ROWS), :])

        @pl.when(plain)
        def _():
            gradients(lambda h, raw: raw + tiles[1, 0, h, :1, :1].astype(F32))

        @pl.when(jnp.logical_not(plain))
        def _():
            q_row = at + iota((1, ROWS), 1)
            masked = jnp.where((k_seg == seg_of(q_row, ends)) & (k_row <= q_row), 0.0, NEG)
            tile = jnp.maximum(2 - (i - chip), 0)
            gradients(lambda h, raw: raw + (tiles[1, tile, h].astype(F32) + masked))

        return 0

    lax.fori_loop(chip, stop, block, 0)
    dqkv_scr[:, :HALF] = dq_ref[...]
    for p in range(PAIRS):
        dqkv_scr[:, HALF + 128 * p : HALF + 128 * p + 128] = join_pair(dk_scr[p]).astype(BF16)
        dqkv_scr[:, 2 * HALF + 128 * p : 2 * HALF + 128 * p + 128] = join_pair(dv_scr[p]).astype(BF16)
    e_scr[...] = dot_nt(dqkv_scr[...], w_ref[...])
    keep_ref[...] = e_scr[own_rows(core, half), :]
    send_ref[...] = e_scr[own_rows(1 - core, half), :]
    wide = x_ref[...].astype(F32)
    scaled = wide * rms_inverse(wide)
    h_scr[...] = (scaled * gain_ref[...]).astype(BF16)
    dgain = jnp.sum(e_scr[...] * scaled, axis=0, keepdims=True)
    dgain = jnp.transpose(jnp.where(iota((128, dgain.shape[1]), 0) == 0, dgain, 0.0))
    columns = grads_ref.shape[1]
    grads_ref[:, columns - 128 :] = (small_ref[...] + dgain).astype(BF16)
    step = 256
    for i in range(0, h_scr.shape[1], step):
        grads_ref[i : i + step, : 2 * HALF] = dot_tn(h_scr[:, i : i + step], dqkv_scr[:, HALF:]).astype(BF16)
    give(n_sides, at_ref[2], grads_ref, outs)


def cross_grad_stage_kernel(
    at_ref, len_ref, enc_ref, deal_ref, place_ref,
    e_ref, other_ref, late_ref, gain_ref, cot_ref, co_ref, q_ref, o_ref, lse_ref, kv_ref, wc_ref,
    grad_ref, low_ref, dgain_ref, dq_ref, keep_ref, send_ref, part_ref,
    go_ref, qs, gs, lse_scr, delta_scr, dq_scr, block_scr,
):
    chip, core = at_ref[0], at_ref[1]
    dvalue, dgain = norm_grad(late_ref[...], gain_ref[...], e_ref[...] + other_ref[...])
    dgain_ref[...] = dgain
    grad = cot_ref[...].astype(F32) + dvalue
    grad_ref[...] = grad
    low_ref[...] = grad.astype(BF16)
    go_ref[...] = dot_nt(low_ref[...], co_ref[own_rows(core, HALF), :]).astype(BF16)
    wanted, _, mask = cross_flags(chip, len_ref, enc_ref, deal_ref)
    row_stats(go_ref, o_ref, lse_ref, gs, lse_scr, delta_scr, SUB)
    for p in range(PAIRS):
        qs[p] = split_pair(q_ref[:, lanes_of(p)], SUB)
    dq_scr[...] = jnp.zeros_like(dq_scr)
    half = keep_ref.shape[0] // ROWS

    def gradients(j, rows, masked):
        at = pl.multiple_of(j * KEYS, KEYS)
        raws = [dot_nt(qs[p, rows], kv_ref[p, pl.ds(at, KEYS), :]) for p in range(PAIRS)]
        dprobs = [dot_nt(gs[p, rows], kv_ref[PAIRS + p, pl.ds(at, KEYS), :]) for p in range(PAIRS)]
        for p in range(PAIRS):
            probs = jnp.exp(raws[p] + masked - lse_scr[p, rows, :1])
            ds = (probs * (dprobs[p] - delta_scr[p, rows, :1])).astype(BF16)
            dq_scr[p, rows] += dot_nn(ds, kv_ref[p, pl.ds(at, KEYS), :])
            block_scr[:, lanes_of(p)] += dot_tn(ds, qs[p, rows])
            block_scr[:, lanes_of(PAIRS + p)] += dot_tn(probs.astype(BF16), gs[p, rows])

    def block(j, c):
        at = pl.multiple_of(j * KEYS, KEYS)
        hit = wanted(at, 0, ROWS)

        @pl.when(hit)
        def _():
            block_scr[...] = jnp.zeros_like(block_scr)
            for r in range(ROWS // SUB):

                @pl.when(wanted(at, r * SUB, SUB))
                def _():
                    masked = mask(j, r)
                    gradients(j, stacked(r), jnp.concatenate([masked, masked], axis=0))

        for i in range(KEYS // ROWS):
            place = place_ref[j * (KEYS // ROWS) + i]
            upper = (place >= half).astype(jnp.int32)
            to = pl.ds(pl.multiple_of((place - upper * half) * ROWS, ROWS), ROWS)
            for mine, target in ((True, keep_ref), (False, send_ref)):
                here = (upper == at_ref[3]) == mine

                @pl.when(here & hit)
                def _():
                    target[to, :] = block_scr[i * ROWS : (i + 1) * ROWS, :].astype(BF16)

                @pl.when(here & jnp.logical_not(hit))
                def _():
                    target[to, :] = jnp.zeros((ROWS, 2 * HALF), BF16)

        return c

    lax.fori_loop(0, kv_ref.shape[1] // KEYS, block, 0)
    for p in range(PAIRS):
        dq_ref[:, 128 * p : 128 * p + 128] = join_pair(dq_scr[p], SUB).astype(BF16)
    part_ref[...] = dot_nt(dq_ref[...], wc_ref[:, :HALF])


def self_grad_start_kernel(
    at_ref, e_ref, other_ref, mid_ref, gain_ref, late_grad_ref, so_ref, o_ref, lse_ref,
    grad_ref, low_ref, dgain_ref, go_ref, message_ref,
    stat_scr,
):
    core = at_ref[1]
    dvalue, dgain = norm_grad(mid_ref[...], gain_ref[...], e_ref[...] + other_ref[...])
    dgain_ref[...] = dgain
    grad = late_grad_ref[...] + dvalue
    grad_ref[...] = grad
    low_ref[...] = grad.astype(BF16)
    go_ref[...] = dot_nt(low_ref[...], so_ref[own_rows(core, HALF), :]).astype(BF16)
    half = ROWS // 2
    message_ref[:half, :] = low_ref[own_rows(core, half), :]
    lane = iota((ROWS, 128), 1)
    stat_scr[...] = lse_ref[...]

    def pair(p):
        product = go_ref[:, lanes_of(p)].astype(F32) * o_ref[:, lanes_of(p)]
        for i in range(2):
            part = jnp.where((lane < HEAD_DIM) if i == 0 else (lane >= HEAD_DIM), product, 0.0)
            stat_scr[...] = jnp.where(lane == 8 + 2 * p + i, jnp.sum(part, axis=1, keepdims=True), stat_scr[...])

    each_pair(pair)
    rest = jnp.transpose(stat_scr[...])[:16]
    for part in range(3):
        high = rest.astype(BF16)
        message_ref[half:, part * ROWS : (part + 1) * ROWS] = high
        rest = rest - high.astype(F32)


def projection_grads_kernel(
    n_sides, at_ref, low2_ref, other2_ref, b2_ref, in_ref, dq2_ref, low1_ref, other1_ref, b1_ref, x_ref, gain_ref, dq1_ref, *outs
):
    *outs, out_ref = outs
    core, side = at_ref[1], at_ref[2]
    lanes = pl.ds(pl.multiple_of(core * HALF, 128), HALF)
    for at, own, other, grad in ((0, low2_ref, other2_ref, b2_ref), (2 * HALF, low1_ref, other1_ref, b1_ref)):
        grads = grad[:, lanes]
        for which, part in ((core, own), (1 - core, other)):
            out_ref[own_rows(which, HALF), at : at + HALF] = dot_tn(part[...], grads).astype(BF16)
    out_ref[:, HALF : 2 * HALF] = dot_tn(in_ref[...], dq2_ref[...]).astype(BF16)
    wide = x_ref[...].astype(F32)
    normed = (wide * rms_inverse(wide) * gain_ref[...]).astype(BF16)
    out_ref[:, 3 * HALF :] = dot_tn(normed, dq1_ref[...]).astype(BF16)
    give(n_sides, side, out_ref, outs)


def give(n_sides, side, value, outs):
    if n_sides == 2:
        rows = value.shape[0] // 2
        outs[0][...] = value[own_rows(side, rows), :]
        outs[1][...] = value[own_rows(1 - side, rows), :]
    else:
        outs[0][...] = value[...]


def encoder_grads_kernel(n_sides, at_ref, dkv_ref, e_ref, wc_ref, keep_ref, send_ref, *outs):
    *outs, low_scr, e_scr, grads_ref = outs
    core = at_ref[1]
    half = ROWS // 2
    low_scr[...] = dkv_ref[...].astype(BF16)
    e_scr[...] = dot_nt(low_scr[...], wc_ref[:, HALF:])
    keep_ref[...] = e_scr[own_rows(core, half), :]
    send_ref[...] = e_scr[own_rows(1 - core, half), :]
    grads_ref[...] = dot_tn(e_ref[...], low_scr[...]).astype(BF16)
    give(n_sides, at_ref[2], grads_ref, outs)


def token_grads_kernel(at_ref, e_ref, other_ref, x_ref, gain_ref, grad_ref, out_ref):
    dvalue, _ = norm_grad(x_ref[...].astype(F32), gain_ref[...], e_ref[...] + other_ref[...])
    out_ref[...] = grad_ref[own_rows(at_ref[1], out_ref.shape[0]), :] + dvalue


def finish_late_kernel(count, at_ref, place_ref, own_ref, other_ref, *refs):
    *outs, one, two, three, table, small = refs
    core, place = at_ref[1], place_ref[0]
    rows = own_ref.shape[0] // count
    columns = slice(len(outs) * HALF, len(outs) * HALF + 128)
    for i in range(count):
        part = slice(i * rows, (i + 1) * rows)
        to = pl.ds(pl.multiple_of((place ^ i) * rows, rows), rows)
        for j, out in enumerate(outs):
            lanes = slice(j * HALF, (j + 1) * HALF)
            out[to, own_lanes(core)] = own_ref[part, lanes].astype(F32)
            out[to, own_lanes(1 - core)] = other_ref[part, lanes].astype(F32)
        small[to, :] = own_ref[part, columns].astype(F32) + other_ref[part, columns].astype(F32)
    turned = jnp.transpose(small[...])
    for i, out in enumerate((one, two, three)):
        out[...] = turned[i]
    table[...] = small[: table.shape[0], 3 : 3 + HEADS]


def own_lanes(core):
    return pl.ds(pl.multiple_of(core * HALF, 128), HALF)


def finish_kernel(order, parts_ref, outer_ref, inner_ref, *outs):
    rows = parts_ref.shape[1]
    width = outer_ref.shape[1]
    side = inner_ref.shape[0]
    unit = inner_ref.shape[1] // 4
    for i, (core, place) in enumerate(order):
        at = place * rows
        for half in range(2):
            top = (2 * core + half) * side + at
            outer_ref[top : top + rows, :] = parts_ref[i, :, half * width : (half + 1) * width].astype(F32)
            lanes = slice((2 * half + core) * unit, (2 * half + core + 1) * unit)
            inner_ref[at : at + rows, lanes] = parts_ref[i, :, 2 * width + half * unit : 2 * width + (half + 1) * unit].astype(F32)
    finish_columns_kernel(order, 4 * width, parts_ref, *outs)


def finish_columns_kernel(order, skip, parts_ref, *outs):
    rows = parts_ref.shape[1]
    for i, (core, place) in enumerate(order):
        at = slice(place * rows, (place + 1) * rows)
        for j, out in enumerate(outs):
            columns = slice(skip + j * HALF, skip + (j + 1) * HALF)
            out[at, core * HALF : (core + 1) * HALF] = parts_ref[i, :, columns].astype(F32)


def pack_kernel(groups, core_ref, *refs):
    count = sum(groups)
    ins, outs = list(refs[:count]), refs[count:]
    for size, out in zip(groups, outs):
        at = 0
        for _ in range(size):
            part = ins.pop(0)
            out[:, at : at + part.shape[1]] = part[...].astype(BF16)
            at += part.shape[1]


SMEM = pl.BlockSpec(memory_space=pltpu.SMEM)
VMEM = pl.BlockSpec(memory_space=pltpu.VMEM)


def call(kernel, scalars, arrays, outs, scratch, flops):
    moved = sum(a.size * a.dtype.itemsize for a in arrays) + sum(math.prod(s) * jnp.dtype(d).itemsize for s, d in outs)
    return pl.pallas_call(
        kernel,
        out_shape=[jax.ShapeDtypeStruct(s, d) for s, d in outs],
        in_specs=[SMEM] * len(scalars) + [VMEM] * len(arrays),
        out_specs=[VMEM] * len(outs),
        scratch_shapes=[pltpu.VMEM(s, d) for s, d in scratch],
        compiler_params=pltpu.CompilerParams(vmem_limit_bytes=VMEM_LIMIT),
        cost_estimate=pl.CostEstimate(flops=1, transcendentals=0, bytes_accessed=1),
    )(*scalars, *arrays)


TILES = ((3, LOCAL, ROWS, ROWS), F32)
FAR = ((LOCAL, 8, ROWS), F32)
STACK = ((PAIRS, 2 * ROWS, 128), BF16)
COLUMN = ((PAIRS, 2 * ROWS, 128), F32)
LANE = ((ROWS, 128), F32)


def pack(core, groups):
    flat = [item for group in groups for item in group]
    return pl.pallas_call(
        functools.partial(pack_kernel, [len(g) for g in groups]),
        grid_spec=pltpu.PrefetchScalarGridSpec(
            num_scalar_prefetch=1,
            grid=(1,),
            in_specs=[
                pl.BlockSpec(shape, functools.partial(lambda index, i, c: index(c[0]), index)) for _, shape, index in flat
            ],
            out_specs=[
                pl.BlockSpec((g[0][1][0], sum(s[1] for _, s, _ in g)), lambda i, c: (0, 0)) for g in groups
            ],
        ),
        out_shape=[jax.ShapeDtypeStruct((g[0][1][0], sum(s[1] for _, s, _ in g)), BF16) for g in groups],
        compiler_params=pltpu.CompilerParams(vmem_limit_bytes=VMEM_LIMIT),
    )(core, *(w for w, _, _ in flat))


def swap_core(value):
    return lax.ppermute(value, "core", [(0, 1), (1, 0)])


def gather_fsdp(own):
    count = lax.axis_size("fsdp")
    if count != 2:
        return [lax.all_gather(own, "fsdp", axis=0, tiled=True)]
    return [own, lax.ppermute(own, "fsdp", [(0, 1), (1, 0)])]


CHIPS = ("z", "y")
GROUP = ("z", "y", "core")


def gather_rows(own):
    return lax.all_gather(own, GROUP, axis=0, tiled=True)


def bits_of(axis):
    return range((lax.axis_size(axis) - 1).bit_length())


def swap_bit(value, axis, bit):
    return lax.ppermute(value, axis, [(i, i ^ (1 << bit)) for i in range(lax.axis_size(axis))])


def parted(terms, axis, bit):
    side = (lax.axis_index(axis) >> bit) & 1
    rows = terms[0].shape[0] // 2

    def half(which):
        return [lax.dynamic_slice_in_dim(t, which * rows, rows, 0) for t in terms]

    return half(side), total(half(1 - side)).astype(BF16)


def halve(terms, axis, bit):
    keep, send = parted(terms, axis, bit)
    return keep + [swap_bit(send, axis, bit)]


def total(terms):
    return sum(t.astype(F32) for t in terms[1:]) + terms[0].astype(F32)


def steps_of(*axes):
    return [(axis, bit) for axis in axes for bit in bits_of(axis)]


def scatter(terms, steps):
    for axis, bit in steps:
        terms = halve(terms, axis, bit)
    return terms


def scatter_fsdp(terms):
    return scatter(terms, [("fsdp", bit) for bit in reversed(bits_of("fsdp"))])


def places(steps):
    nz, ny = lax.axis_size("z"), lax.axis_size("y")
    found = []
    for z in range(nz):
        for y in range(ny):
            place = 0
            for axis, bit in steps:
                place = 2 * place + (((z if axis == "z" else y) >> bit) & 1)
            found.append(place)
    return found


def after(value, *earlier):
    return lax.optimization_barrier((value, *earlier))[0]


def on_device(
    tokens, encoded, cotangent, tgt_lengths, enc_lengths, deal,
    ln_self, ln_cross, ln_ffn, bias_table,
    self_query, self_key, self_value, self_output,
    cross_query, cross_key, cross_value, cross_output,
    ffn_inner, ffn_outer,
):
    core = lax.axis_index("core")
    fsdp = lax.axis_index("fsdp")
    n_fsdp = lax.axis_size("fsdp")
    chip = lax.axis_index(CHIPS)
    steps = steps_of("y", "z")
    y_side = (lax.axis_index("y") >> steps[0][1]) & 1
    at = jnp.stack([chip, core, fsdp, y_side]).astype(jnp.int32)
    core_ref = core.reshape(1).astype(jnp.int32)
    rows, width = tokens.shape
    n = 2 * rows * lax.axis_size(CHIPS)
    side = width // n_fsdp
    hidden_half = ffn_inner.shape[1] // 2
    unit = hidden_half // n_fsdp
    wide, flat = ((ROWS, width), F32), ((ROWS, width), BF16)

    def column(weight):
        return (weight, (side, HALF), lambda c: (0, c))

    (qkv_own,) = pack(core_ref, [[column(w) for w in (self_query, self_key, self_value)]])
    w_qkv = gather_fsdp(qkv_own)
    if unit % 128 == 0:
        inner_items = [(ffn_inner, (side, unit), functools.partial(lambda o, c: (0, 2 * o + c), o)) for o in range(n_fsdp)]
    else:
        inner_units = ffn_inner.reshape(side, n_fsdp, 2, unit)
        inner_units = lax.dynamic_index_in_dim(inner_units, core, 2, keepdims=False).reshape(side, hidden_half)
        inner_items = [(inner_units, (side, hidden_half), lambda c: (0, 0))]
    out_own, cross_own, inner_own, outer_own = pack(
        core_ref,
        [
            [column(w) for w in (self_output, cross_output)],
            [column(w) for w in (cross_query, cross_key, cross_value)],
            inner_items,
            [(ffn_outer, (unit, width), lambda c: (c, 0))],
        ],
    )
    w_out = gather_fsdp(out_own)
    w_cross = gather_fsdp(cross_own)
    inner_own, outer_own = after((inner_own, outer_own), w_cross[-1])
    w_inner, w_outer = gather_fsdp(inner_own), gather_fsdp(outer_own)
    w_out_mate = [swap_core(w) for w in w_out]
    cot_mate = swap_core(cotangent)

    small = jnp.concatenate([ln_self, ln_cross, ln_ffn, bias_table.reshape(-1)], axis=0).astype(BF16)[None]
    small = gather_fsdp(small)
    if len(small) == 2:
        small = jnp.where(fsdp == 0, jnp.concatenate(small, axis=0), jnp.concatenate(small[::-1], axis=0))
    else:
        small = small[0]
    gain_self, gain_cross, gain_ffn = (
        small[:, i * side : (i + 1) * side].reshape(1, width).astype(F32) for i in range(3)
    )
    table = small[:, 3 * side :].reshape(BUCKETS, HEADS)
    table = lax.dynamic_slice_in_dim(table, core * LOCAL, LOCAL, 1).astype(F32)
    onehots = np.concatenate([QK_ONEHOT, KQ_ONEHOT], axis=0)
    biases = jnp.einsum("bh,tb->ht", table, onehots, precision=lax.Precision.HIGHEST)
    biases = jnp.pad(biases.reshape(LOCAL, 2, 2 * ROWS).swapaxes(0, 1), ((0, 0), (0, 2), (0, 0)))
    (tiles,) = call(tiles_kernel, (), (biases.reshape(16, 2 * ROWS),), [((2, *TILES[0]), BF16)], [], 1)

    xe = gather_rows(jnp.concatenate([tokens, encoded], axis=1))
    qkv, w_qkv, attn_self, low_self, lse_self = call(
        functools.partial(self_stage_kernel, len(w_qkv)), (at, tgt_lengths), (xe, gain_self, tiles, *w_qkv),
        [((3 * PAIRS, n, 128), BF16), ((width, 3 * HALF), BF16), ((ROWS, HALF), F32), ((ROWS, HALF), BF16), LANE],
        ATTEND(n),
        2 * n * width * 3 * HALF + 4 * ROWS * n * HALF,
    )
    low_self_other = swap_core(low_self)

    x_mid, in_cross, q_cross, kv_cross, attn_cross, low_cross, lse_cross, w_so, w_co, w_cross = call(
        functools.partial(cross_stage_kernel, len(w_out)), (at, tgt_lengths, enc_lengths, deal),
        (xe, gain_cross, low_self, low_self_other, *w_out, *w_out_mate, *w_cross),
        [
            wide, flat, ((ROWS, HALF), BF16), ((2 * PAIRS, n, 128), BF16), ((ROWS, HALF), F32), ((ROWS, HALF), BF16), LANE,
            ((width, width), BF16), ((width, width), BF16), ((width, 3 * HALF), BF16),
        ],
        ATTEND(n),
        2 * n * width * 2 * HALF + 4 * ROWS * n * HALF,
    )
    low_cross_other = swap_core(low_cross)

    half_rows = ((rows, width), F32)
    x_late, in_ffn, hidden, d_pre, cot, out_keep, out_send, e_ffn = call(
        functools.partial(ffn_stage_kernel, len(w_inner)), (at,),
        (x_mid, gain_ffn, low_cross, low_cross_other, w_co, cotangent, cot_mate, *w_inner, *w_outer),
        [wide, flat, ((ROWS, hidden_half), BF16), ((ROWS, hidden_half), BF16), flat, half_rows, half_rows, wide],
        [((width, hidden_half), BF16), ((hidden_half, width), BF16), wide],
        8 * ROWS * width * hidden_half,
    )
    e_ffn_other = swap_core(e_ffn)
    output = out_keep + swap_core(out_send)

    place = places(steps)
    place_ref = jnp.asarray(np.array(place, np.int32))
    nz, ny = lax.axis_size("z"), lax.axis_size("y")
    y_place = [p // nz for p in place[:ny]]
    key_place_ref = jnp.asarray(np.array([y_place[y] * nz + z for z in range(nz) for y in range(ny)], np.int32))
    grad_late, late_low, d_gain_ffn, dq_cross, dkv_keep, dkv_send, e_cross = call(
        cross_grad_stage_kernel, (at, tgt_lengths, enc_lengths, deal, key_place_ref),
        (e_ffn, e_ffn_other, x_late, gain_ffn, cot, w_co, q_cross, attn_cross, lse_cross, kv_cross, w_cross),
        [wide, flat, ((1, width), F32), ((ROWS, HALF), BF16), ((n // 2, 2 * HALF), BF16), ((n // 2, 2 * HALF), BF16), wide],
        [((ROWS, HALF), BF16), STACK, STACK, COLUMN, COLUMN, COLUMN, ((KEYS, 2 * HALF), F32)],
        10 * ROWS * n * HALF,
    )
    e_cross_other = swap_core(e_cross)
    dkv_got = swap_bit(dkv_send, *steps[0])

    grad_mid, mid_low, d_gain_cross, go_self, message = call(
        self_grad_start_kernel, (at,), (e_cross, e_cross_other, x_mid, gain_cross, grad_late, w_so, attn_self, lse_self),
        [wide, flat, ((1, width), F32), ((ROWS, HALF), BF16), ((rows + 16, width), BF16)], [LANE],
        2 * ROWS * width * HALF,
    )
    ffn_out = (
        [((side, 4 * width), BF16), ((side, 4 * width), BF16)]
        if n_fsdp == 2
        else [((hidden_half, width), F32), ((width, hidden_half), F32)]
    )
    first = call(
        functools.partial(ffn_grads_kernel, n_fsdp), (at,), (hidden, cot, in_ffn, after(d_pre, message)), ffn_out, [],
        4 * ROWS * width * hidden_half,
    )
    if n_fsdp == 2:
        first_other = lax.ppermute(first[1], "fsdp", [(0, 1), (1, 0)])
        go_self = after(go_self, first[1])
    message = lax.all_gather(message, GROUP, axis=0)
    x_chip = lax.dynamic_slice(xe, (chip * ROWS, 0), (ROWS, width))
    e_chip = lax.dynamic_slice(xe, (chip * ROWS, width), (ROWS, width))
    dq_self, dist = call(
        self_query_grad_kernel, (at, tgt_lengths), (tiles, qkv, go_self, attn_self, lse_self),
        [((ROWS, HALF), BF16), ((8, 2 * ROWS), F32)],
        [STACK, STACK, COLUMN, COLUMN, COLUMN, TILES, FAR],
        6 * ROWS * n * HALF,
    )
    def given(columns):
        return [((width // 2, columns), BF16)] * 2 if n_fsdp == 2 else [((width, columns), BF16)]

    def over_fsdp(parts):
        if n_fsdp == 2:
            return [parts[0], lax.ppermute(parts[1], "fsdp", [(0, 1), (1, 0)])]
        return scatter_fsdp(parts)

    second = call(
        functools.partial(projection_grads_kernel, n_fsdp), (at,),
        (low_cross, low_cross_other, late_low, in_cross, dq_cross, low_self, low_self_other, mid_low, x_chip, gain_self, dq_self),
        given(4 * HALF), [((width, 4 * HALF), BF16)], 8 * ROWS * width * HALF,
    )
    d_table = jnp.einsum("ht,tb->bh", dist[:LOCAL], QK_ONEHOT, precision=lax.Precision.HIGHEST)
    d_table = jnp.zeros((BUCKETS, 2, LOCAL), F32).at[:, core].set(d_table).reshape(n_fsdp, -1, HEADS)
    d_table = jnp.pad(d_table, ((0, 0), (0, side - d_table.shape[1]), (0, 0))).reshape(width, HEADS)
    none = jnp.zeros((width, 1), F32)
    small = [none, 0.5 * d_gain_cross.reshape(width, 1), 0.5 * d_gain_ffn.reshape(width, 1), d_table]
    small = jnp.pad(jnp.concatenate(small, axis=1), ((0, 0), (0, 128 - 3 - HEADS)))

    if n_fsdp == 2:
        first = [first[0], first_other]
    else:
        outer = first[0].reshape(n_fsdp, 2, side, width)
        first = jnp.concatenate([outer[:, 0], outer[:, 1], first[1].reshape(n_fsdp, side, hidden_half)], axis=2)
        first = scatter_fsdp([first.reshape(width, -1)])
    *y_steps, z_near, z_far = steps
    dkv_cross = scatter(after([dkv_keep, dkv_got], second[-1]), y_steps[1:])
    dkv_cross = total(dkv_cross).astype(BF16)
    first = after(first, dkv_cross)
    second = over_fsdp(after(second, first[-1]))
    first_keep, first_sent = parted(first, *y_steps[0])
    first_got = swap_bit(first_sent, *y_steps[0])
    dkv_cross = lax.psum_scatter(dkv_cross, "z", scatter_dimension=0, tiled=True)

    e_keep, e_send, *fourth = call(
        functools.partial(self_key_stage_kernel, n_fsdp), (at, tgt_lengths),
        (tiles, qkv, after(message, first_sent), w_so, dq_self, w_qkv, x_chip, gain_self, small),
        [half_rows, half_rows, *given(2 * HALF + 128)],
        [
            ((PAIRS, n, 128), BF16), ((n // ROWS, 16, ROWS), F32), STACK, STACK, COLUMN, COLUMN,
            ((ROWS, 3 * HALF), BF16), flat, wide, ((width, 2 * HALF + 128), BF16),
        ],
        8 * ROWS * n * HALF,
    )
    fourth_sent = fourth[-1]
    fourth = over_fsdp(fourth)
    first = scatter(first_keep + [after(first_got, fourth_sent)], y_steps[1:])
    first_keep, first_sent = parted(first, *z_near)
    first_got = swap_bit(first_sent, *z_near)
    second, fourth = after((second, fourth), first_sent)
    second = jnp.concatenate([total(second), total(fourth)], axis=1).astype(BF16)
    second_keep, second_sent = parted([second], *y_steps[0])
    second_got = swap_bit(second_sent, *y_steps[0])
    enc_keep, enc_send, *third = call(
        functools.partial(encoder_grads_kernel, n_fsdp), (at,), (after(dkv_cross, second_sent), e_chip, w_cross),
        [half_rows, half_rows, *given(2 * HALF)],
        [((ROWS, 2 * HALF), BF16), wide, ((width, 2 * HALF), BF16)], 8 * ROWS * width * HALF,
    )
    third_sent = third[-1]
    third = over_fsdp(third)
    first_keep, first_sent = parted(first_keep + [after(first_got, third_sent)], *z_far)
    first_got = swap_bit(first_sent, *z_far)
    (grad_tokens,) = call(
        token_grads_kernel, (at,), (e_keep, swap_core(after(e_send, first_sent)), tokens, gain_self, grad_mid),
        [half_rows], [], 10 * rows * width,
    )
    enc_grad = enc_keep + swap_core(after(enc_send, first_sent))

    second = scatter(second_keep + [after(second_got, grad_tokens, enc_grad)], y_steps[1:])
    second_keep, second_sent = parted(second, *z_near)
    second_got = swap_bit(second_sent, *z_near)
    late_keep, late_sent = parted(after(third, second_sent), *y_steps[0])
    late_got = swap_bit(late_sent, *y_steps[0])
    first = total(first_keep + [after(first_got, late_sent)]).astype(BF16)
    second_keep, second_sent = parted(second_keep + [after(second_got, first)], *z_far)
    second_got = swap_bit(second_sent, *z_far)
    late = scatter(late_keep + [after(late_got, second_sent)], y_steps[1:])
    late_keep, late_sent = parted(late, *z_near)
    late_got = swap_bit(late_sent, *z_near)
    second = total(second_keep + [after(second_got, late_sent)]).astype(BF16)
    early = lax.all_gather(jnp.concatenate([first, second[:, : 4 * HALF]], axis=1), GROUP, axis=0)
    late = total(halve(late_keep + [after(late_got, second)], *z_far)).astype(BF16)
    late = jnp.concatenate([late, second[:, 4 * HALF :]], axis=1)
    for axis, bit in reversed(steps):
        late = jnp.concatenate([late, swap_bit(late, axis, bit)], axis=0)
    late_other = swap_core(late)
    early = after(early, late_other)

    matrix = ((side, width), F32)
    own_place = place_ref[chip].reshape(1)
    if side // len(place) % 8 == 0:
        g_ck, g_cv, g_sk, g_sv, *gains, g_table = call(
            functools.partial(finish_late_kernel, len(place)), (at, own_place), (late, late_other),
            [matrix] * 4 + [((side,), F32)] * 3 + [(bias_table.shape, F32)], [((side, 128), F32)], 8 * side * width,
        )
    else:
        blocks = jnp.stack([late, late_other]).reshape(2, len(place), side // len(place), -1)
        blocks = jnp.take(blocks, own_place[0] ^ jnp.arange(len(place), dtype=jnp.int32), axis=1)
        blocks = jnp.where(core == 0, blocks, blocks[::-1]).astype(F32).reshape(2, side, -1)
        g_ck, g_cv, g_sk, g_sv = (
            jnp.swapaxes(blocks[:, :, i : i + HALF], 0, 1).reshape(side, width) for i in range(0, 4 * HALF, HALF)
        )
        small = jnp.sum(blocks[:, :, 4 * HALF :], axis=0)
        gains = [small[:, i] for i in range(3)]
        g_table = small[: bias_table.shape[0], 3 : 3 + HEADS]
    order = [(c, p) for p in place for c in range(2)]
    if n_fsdp == 2:
        g_outer, g_inner, g_co, g_cq, g_so, g_sq = call(
            functools.partial(finish_kernel, order), (), (early,),
            [(ffn_outer.shape, F32), (ffn_inner.shape, F32), *[matrix] * 4], [], 8 * side * width,
        )
    else:
        sources = np.argsort([2 * p + c for c, p in order])
        pair = jnp.swapaxes(early[sources].reshape(len(place), 2, -1, early.shape[2]), 0, 1)
        pair = pair.reshape(2, side, -1).astype(F32)
        g_outer = pair[:, :, : 2 * width].reshape(2, side, 2, width)
        g_outer = jnp.swapaxes(g_outer, 1, 2).reshape(ffn_outer.shape)
        g_inner = jnp.transpose(pair[:, :, 2 * width : 4 * width].reshape(2, side, n_fsdp, unit), (1, 2, 0, 3))
        g_inner = g_inner.reshape(ffn_inner.shape)
        g_co, g_cq, g_so, g_sq = call(
            functools.partial(finish_columns_kernel, order, 4 * width), (), (early,), [matrix] * 4, [], 8 * side * width
        )

    return (
        output, grad_tokens, enc_grad,
        *gains, g_table,
        g_sq, g_sk, g_sv, g_so, g_cq, g_ck, g_cv, g_co, g_inner, g_outer,
    )


def solution(mesh):
    n_ctx, n_fsdp = mesh.shape["ctx"], mesh.shape["fsdp"]
    n_z = 4
    grid = Mesh(mesh.devices.reshape(n_z, n_ctx // (2 * n_z), 2, n_fsdp), ("z", "y", "core", "fsdp"))
    by_rows = P(("fsdp", "z", "y", "core"), None)
    split = P("fsdp", None)
    vector = P("fsdp")
    in_specs = (by_rows,) * 3 + (split,) * 3 + (vector,) * 3 + (split,) * 11
    out_specs = (by_rows,) * 3 + (vector,) * 3 + (split,) * 11
    return jax.shard_map(on_device, mesh=grid, in_specs=in_specs, out_specs=out_specs, check_vma=False)
```

```python
import functools
import math

import jax
import jax.numpy as jnp
import numpy as np
from jax import lax
from jax.experimental import pallas as pl
from jax.experimental.pallas import tpu as pltpu
from jax.sharding import Mesh
from jax.sharding import PartitionSpec as P

HEADS = 12
HEAD_DIM = 64
BUCKETS = 32
EPS = 1e-06
NEG = -1e30
GELU_C = 0.7978845608028654
GELU_A = 0.044715

LOCAL = HEADS // 2
PAIRS = LOCAL // 2
HALF = LOCAL * HEAD_DIM
ROWS = 256
VMEM_LIMIT = 56 << 20

F32 = jnp.float32
BF16 = jnp.bfloat16


def bucket_edges():
    edges = []
    for level in range(1, 16):
        distance = 16
        while int(math.log(distance / 16.0) / math.log(8.0) * 16.0) < level:
            distance += 1
        edges.append(distance)
    return edges


def buckets_of(distances):
    clipped = np.maximum(np.asarray(distances), 0)
    large = np.full(clipped.shape, 16)
    for edge in bucket_edges():
        large = large + (clipped >= edge)
    return np.where(clipped < 16, clipped, large)


LANES = np.arange(2 * ROWS)
QK_DISTANCE = np.where(LANES <= ROWS, ROWS - LANES, 3 * ROWS - LANES)
KQ_DISTANCE = LANES
QK_ONEHOT = np.eye(BUCKETS, dtype=np.float32)[buckets_of(QK_DISTANCE)]
KQ_ONEHOT = np.eye(BUCKETS, dtype=np.float32)[buckets_of(KQ_DISTANCE)]


def dot_nt(left, right):
    return lax.dot_general(left, right, (((1,), (1,)), ((), ())), preferred_element_type=F32)


def dot_tn(left, right):
    return lax.dot_general(left, right, (((0,), (0,)), ((), ())), preferred_element_type=F32)


def dot_nn(left, right):
    return lax.dot_general(left, right, (((1,), (0,)), ((), ())), preferred_element_type=F32)


def spans(ref):
    starts, ends, at = [], [], jnp.int32(0)
    for i in range(ref.shape[1]):
        starts.append(at)
        at = at + ref[0, i]
        ends.append(at)
    return starts, ends


def seg_of(index, ends):
    found = jnp.zeros(index.shape, jnp.int32)
    for end in ends[:-1]:
        found = found + (index >= end).astype(jnp.int32)
    return found


def iota(shape, axis):
    return lax.broadcasted_iota(jnp.int32, shape, axis)


def split_pair(pair, sub=ROWS):
    low = iota((sub, pair.shape[1]), 1) < HEAD_DIM
    zero = jnp.zeros((sub, pair.shape[1]), pair.dtype)
    parts = []
    for at in range(0, pair.shape[0], sub):
        part = pair[at : at + sub]
        parts += [jnp.where(low, part, zero), jnp.where(low, zero, part)]
    return jnp.concatenate(parts, axis=0)


def head_rows(both, e, sub=ROWS):
    parts = [both[at + e * sub : at + (e + 1) * sub] for at in range(0, both.shape[0], 2 * sub)]
    return parts[0] if len(parts) == 1 else jnp.concatenate(parts, axis=0)


def join_pair(both, sub=ROWS):
    first = head_rows(both, 0, sub)
    return jnp.where(iota(first.shape, 1) < HEAD_DIM, first, head_rows(both, 1, sub))


def tiles_kernel(bias_ref, tiles_ref):
    def head(h, c):
        for which in range(2):
            row = bias_ref[pl.ds(8 * which + h, 1), :]
            rolled = pltpu.roll(jnp.broadcast_to(row, (ROWS, 2 * ROWS)), 0, 1, stride=1, stride_axis=0)
            first, second = (1, 2) if which == 0 else (2, 1)
            tiles_ref[which, first, h] = rolled[:, :ROWS].astype(BF16)
            tiles_ref[which, second, h] = rolled[:, ROWS:].astype(BF16)
            tiles_ref[which, 0, h] = jnp.broadcast_to(row[:, 2 * ROWS - 1 :], (ROWS, ROWS)).astype(BF16)
        return c

    lax.fori_loop(0, LOCAL, head, 0)


def lanes_of(p):
    return slice(p * 128, p * 128 + 128) if isinstance(p, int) else pl.ds(pl.multiple_of(p * 128, 128), 128)


def each_pair(body):
    for p in range(PAIRS):
        body(p)


def rms_inverse(value):
    return lax.rsqrt(jnp.mean(value * value, axis=-1, keepdims=True) + EPS)


def together(n):
    return PAIRS if n <= 2048 else 1


def attend(queries, keys, values, visit_scores, visit, sub, step, s_scr, mx_scr, l_scr, acc_scr, qs, o_ref, low_ref, lse_ref):
    count = s_scr.shape[0]
    lse_ref[...] = jnp.zeros_like(lse_ref)
    lane = iota((ROWS, 128), 1)

    def group(g):
        for c in range(count):
            qs[c] = split_pair(queries(g * count + c), sub)
        mx_scr[...] = jnp.full_like(mx_scr, NEG)

        def scores(j, rows, extra):
            at = pl.multiple_of(j * step, step)
            raws = [dot_nt(qs[c, rows], keys(g * count + c, at)) for c in range(count)]
            for c in range(count):
                value = extra(g * count + c, raws[c])
                s_scr[c, rows, pl.ds(at, step)] = value
                mx_scr[c, rows] = functools.reduce(
                    jnp.maximum, [value[:, i : i + 128] for i in range(0, step, 128)], mx_scr[c, rows]
                )

        visit_scores(scores)
        for c in range(count):
            mx_scr[c] = jnp.broadcast_to(jnp.max(mx_scr[c], axis=1, keepdims=True), mx_scr.shape[1:])
        l_scr[...] = jnp.zeros_like(l_scr)
        acc_scr[...] = jnp.zeros_like(acc_scr)

        def weigh(j, rows):
            at = pl.multiple_of(j * step, step)
            for c in range(count):
                weights = jnp.exp(s_scr[c, rows, pl.ds(at, step)] - mx_scr[c, rows, :1])
                l_scr[c, rows] += sum(weights[:, i : i + 128] for i in range(128, step, 128)) + weights[:, :128]
                acc_scr[c, rows] += dot_nn(weights.astype(BF16), values(g * count + c, at))

        visit(weigh)
        for c in range(count):
            p = g * count + c
            total = jnp.sum(l_scr[c], axis=1, keepdims=True)
            result = join_pair(acc_scr[c] / total, sub)
            o_ref[:, lanes_of(p)] = result
            low_ref[:, lanes_of(p)] = result.astype(BF16)
            both = mx_scr[c, :, :1] + jnp.log(total)
            lse = jnp.where(lane == 2 * p, head_rows(both, 0, sub), lse_ref[...])
            lse_ref[...] = jnp.where(lane == 2 * p + 1, head_rows(both, 1, sub), lse)

    if count == PAIRS:
        group(0)
    else:
        lax.fori_loop(0, PAIRS // count, lambda g, c: (group(g), c)[1], 0)


ATTEND = lambda n: [
    ((together(n), 2 * ROWS, n), F32), ((together(n), 2 * ROWS, 128), F32), ((together(n), 2 * ROWS, 128), F32),
    ((together(n), 2 * ROWS, 128), F32), ((together(n), 2 * ROWS, 128), BF16),
]


def set_rows(target, parts, side):
    if len(parts) == 1:
        target[...] = parts[0][...]
        return
    rows = parts[0].shape[0]
    target[pl.ds(pl.multiple_of(side * rows, rows), rows), :] = parts[0][...]
    target[pl.ds(pl.multiple_of((1 - side) * rows, rows), rows), :] = parts[1][...]


def first_of(base, ends):
    first = jnp.int32(0)
    for end in ends[:-1]:
        first = jnp.where(base >= end, end, first)
    return first


def self_stage_kernel(n_parts, at_ref, len_ref, xe_ref, gain_ref, tiles, *refs):
    parts, refs = refs[:n_parts], refs[n_parts:]
    qkv_ref, w_ref, o_ref, low_ref, lse_ref, s_scr, mx_scr, l_scr, acc_scr, qs = refs
    chip, side = at_ref[0], at_ref[2]
    set_rows(w_ref, parts, side)
    width = w_ref.shape[0]
    step = 512

    def body(i, c):
        at = pl.multiple_of(i * step, step)
        wide = xe_ref[pl.ds(at, step), :width].astype(F32)
        value = (wide * rms_inverse(wide) * gain_ref[...]).astype(BF16)
        result = dot_nn(value, w_ref[...])
        for j in range(qkv_ref.shape[0]):
            qkv_ref[j, pl.ds(at, step), :] = result[:, 128 * j : 128 * j + 128].astype(BF16)
        return c

    lax.fori_loop(0, xe_ref.shape[0] // step, body, 0)

    starts, ends = spans(len_ref)
    base = pl.multiple_of(chip * ROWS, ROWS)
    j_min = first_of(base, ends) // ROWS
    full_from = first_of(base + ROWS - 1, ends)
    q_row = base + iota((ROWS, 1), 0)
    q_seg = seg_of(q_row, ends)

    rows = slice(0, 2 * ROWS)

    def visit(block):
        lax.fori_loop(j_min, chip + 1, lambda j, c: (block(j, rows), c)[1], 0)

    def visit_scores(block):
        def body(j, c):
            at = pl.multiple_of(j * ROWS, ROWS)
            plain = (at >= full_from) & (j < chip - 1)

            def with_bias(bias):
                def extra(p, raw):
                    return jnp.concatenate([raw[:ROWS] + bias(2 * p), raw[ROWS:] + bias(2 * p + 1)], axis=0)

                block(j, rows, extra)

            @pl.when(plain)
            def _():
                with_bias(lambda h: tiles[0, 0, h, :1, :1].astype(F32))

            @pl.when(jnp.logical_not(plain))
            def _():
                k_row = at + iota((1, ROWS), 1)
                masked = jnp.where((q_seg == seg_of(k_row, ends)) & (k_row <= q_row), 0.0, NEG)
                tile = jnp.maximum(j - chip + 2, 0)
                with_bias(lambda h: tiles[0, tile, h].astype(F32) + masked)

            return c

        lax.fori_loop(j_min, chip + 1, body, 0)

    attend(
        lambda p: qkv_ref[p, pl.ds(base, ROWS), :],
        lambda p, at: qkv_ref[PAIRS + p, pl.ds(at, ROWS), :],
        lambda p, at: qkv_ref[2 * PAIRS + p, pl.ds(at, ROWS), :],
        visit_scores, visit, ROWS, ROWS, s_scr, mx_scr, l_scr, acc_scr, qs, o_ref, low_ref, lse_ref,
    )


def add_heads(low_ref, other_ref, w_ref, core):
    own = pl.ds(pl.multiple_of(core * HALF, HALF), HALF)
    other = pl.ds(pl.multiple_of((1 - core) * HALF, HALF), HALF)
    return dot_nn(low_ref[...], w_ref[own, :]) + dot_nn(other_ref[...], w_ref[other, :])


def cross_stage_kernel(n_parts, at_ref, len_ref, enc_ref, deal_ref, xe_ref, gain_ref, low_ref, other_ref, *refs):
    outs, mates, parts, refs = refs[:n_parts], refs[n_parts : 2 * n_parts], refs[2 * n_parts : 3 * n_parts], refs[3 * n_parts :]
    mid_ref, in_ref, q_ref, kv_ref, o_ref, low2_ref, lse_ref, so_ref, co_ref, wc_ref, refs = *refs[:10], refs[10:]
    s_scr, mx_scr, l_scr, acc_scr, qs = refs
    chip, core, side = at_ref[0], at_ref[1], at_ref[2]
    set_rows(wc_ref, parts, side)
    for pieces, column in ((outs, core), (mates, 1 - core)):
        lanes = pl.ds(pl.multiple_of(column * HALF, 128), HALF)
        for i, piece in enumerate(pieces):
            rows = piece.shape[0]
            at = pl.multiple_of((side if i == 0 else 1 - side) * rows, rows) if n_parts > 1 else 0
            so_ref[pl.ds(at, rows), lanes] = piece[:, :HALF]
            co_ref[pl.ds(at, rows), lanes] = piece[:, HALF:]
    width = so_ref.shape[0]
    base = pl.multiple_of(chip * ROWS, ROWS)
    mid = xe_ref[pl.ds(base, ROWS), :width].astype(F32) + add_heads(low_ref, other_ref, so_ref, core)
    mid_ref[...] = mid
    normed = (mid * rms_inverse(mid) * gain_ref[...]).astype(BF16)
    in_ref[...] = normed
    q_ref[...] = dot_nn(normed, wc_ref[:, :HALF]).astype(BF16)
    step = 512

    def body(i, c):
        at = pl.multiple_of(i * step, step)
        result = dot_nn(xe_ref[pl.ds(at, step), width:], wc_ref[:, HALF:])
        for j in range(kv_ref.shape[0]):
            kv_ref[j, pl.ds(at, step), :] = result[:, 128 * j : 128 * j + 128].astype(BF16)
        return c

    lax.fori_loop(0, xe_ref.shape[0] // step, body, 0)
    _, over, mask = cross_flags(chip, len_ref, enc_ref, deal_ref)
    blocks = kv_ref.shape[1] // KEYS

    def visit(block):
        over(blocks, lambda j, r: block(j, stacked(r)))

    def visit_scores(block):
        def body(j, r):
            masked = mask(j, r)
            block(j, stacked(r), lambda p, raw: raw + jnp.concatenate([masked, masked], axis=0))

        over(blocks, body)

    attend(
        lambda p: q_ref[:, lanes_of(p)],
        lambda p, at: kv_ref[p, pl.ds(at, KEYS), :],
        lambda p, at: kv_ref[PAIRS + p, pl.ds(at, KEYS), :],
        visit_scores, visit, SUB, KEYS, s_scr, mx_scr, l_scr, acc_scr, qs, o_ref, low2_ref, lse_ref,
    )


def gelu_parts(value):
    tangent = jnp.tanh(GELU_C * (value + GELU_A * value * value * value))
    result = 0.5 * value * (1.0 + tangent)
    slope = 0.5 * (1.0 + tangent) + 0.5 * value * (1.0 - tangent * tangent) * GELU_C * (
        1.0 + 3.0 * GELU_A * value * value
    )
    return (result, slope)


def own_rows(core, rows):
    return pl.ds(pl.multiple_of(core * rows, rows), rows)


def ffn_stage_kernel(n_parts, at_ref, mid_ref, gain_ref, low_ref, other_ref, co_ref, cot_ref, mate_ref, *refs):
    inner, outer, refs = refs[:n_parts], refs[n_parts : 2 * n_parts], refs[2 * n_parts :]
    late_ref, in_ref, hid_ref, dpre_ref, cot_out, keep_ref, send_ref, e_ref, wi_ref, wo_ref, part_scr = refs
    core, side = at_ref[1], at_ref[2]
    rows = cot_ref.shape[0]
    set_rows(wi_ref, inner, side)
    set_rows(wo_ref, outer, side)
    cot_out[own_rows(core, rows), :] = cot_ref[...]
    cot_out[own_rows(1 - core, rows), :] = mate_ref[...]
    late = mid_ref[...] + add_heads(low_ref, other_ref, co_ref, core)
    late_ref[...] = late
    normed = (late * rms_inverse(late) * gain_ref[...]).astype(BF16)
    in_ref[...] = normed
    columns = 512

    def body(i, c):
        at = pl.multiple_of(i * columns, columns)
        activated, slope = gelu_parts(dot_nn(normed, wi_ref[:, pl.ds(at, columns)]))
        hid_ref[:, pl.ds(at, columns)] = activated.astype(BF16)
        grads = dot_nt(cot_out[...], wo_ref[pl.ds(at, columns), :])
        dpre_ref[:, pl.ds(at, columns)] = (grads * slope).astype(BF16)
        return c

    lax.fori_loop(0, wi_ref.shape[1] // columns, body, 0)
    e_ref[...] = dot_nt(dpre_ref[...], wi_ref[...])
    part_scr[...] = dot_nn(hid_ref[...], wo_ref[...])
    keep_ref[...] = part_scr[own_rows(core, rows), :] + late_ref[own_rows(core, rows), :]
    send_ref[...] = part_scr[own_rows(1 - core, rows), :]


def ffn_grads_kernel(n_sides, at_ref, hid_ref, cot_ref, in_ref, dpre_ref, *outs):
    side = at_ref[2]
    rows = in_ref.shape[1] // n_sides
    width = cot_ref.shape[1]
    if n_sides != 2:
        outs[0][...] = dot_tn(hid_ref[...], cot_ref[...])
        outs[1][...] = dot_tn(in_ref[...], dpre_ref[...])
        return
    keep_ref, send_ref = outs
    for owner in range(2):
        for mine, target in ((True, keep_ref), (False, send_ref)):

            @pl.when((side == owner) == mine)
            def _():
                for part in range(2):
                    units = slice((2 * owner + part) * rows, (2 * owner + part + 1) * rows)
                    block = dot_tn(hid_ref[:, units], cot_ref[...])
                    target[:, part * width : (part + 1) * width] = block.astype(target.dtype)
                block = dot_tn(in_ref[:, owner * rows : (owner + 1) * rows], dpre_ref[...])
                target[:, 2 * width :] = block.astype(target.dtype)


def norm_grad(value, gain, grad):
    inverse = rms_inverse(value)
    scaled = grad * gain
    cubed = inverse * inverse * inverse
    dvalue = inverse * scaled - value * cubed * jnp.mean(scaled * value, axis=-1, keepdims=True)
    return dvalue, jnp.sum(grad * value * inverse, axis=0, keepdims=True)


KEYS = 2 * ROWS
SUB = ROWS


def cross_flags(chip, len_ref, enc_ref, deal_ref):
    starts, ends = spans(len_ref)
    e_starts, e_ends = spans(enc_ref)
    base = chip * ROWS
    ranges = []
    for i in range(len(ends)):
        low, high = jnp.int32(0), jnp.int32(0)
        for e in range(len(e_ends)):
            hit = deal_ref[0, i] == e
            low = jnp.where(hit, e_starts[e], low)
            high = jnp.where(hit, e_ends[e], high)
        ranges.append((starts[i], ends[i], low, high))

    def wanted(at, first, count):
        found = jnp.bool_(False)
        for start, end, low, high in ranges:
            live = (start < base + first + count) & (end > base + first)
            found = found | (live & (low < at + KEYS) & (high > at))
        return found

    def visit(blocks, body):
        def inner(j, c):
            for r in range(ROWS // SUB):

                @pl.when(wanted(j * KEYS, r * SUB, SUB))
                def _():
                    body(j, r)

            return c

        lax.fori_loop(0, blocks, inner, 0)

    q_seg = seg_of(base + iota((ROWS, 1), 0), ends)
    q_pair = jnp.zeros((ROWS, 1), jnp.int32)
    for i in range(len(ends)):
        q_pair = q_pair + jnp.where(q_seg == i, deal_ref[0, i], 0)

    def mask(j, r):
        k_seg = seg_of(j * KEYS + iota((1, KEYS), 1), e_ends)
        return jnp.where(q_pair[r * SUB : (r + 1) * SUB] == k_seg, 0.0, NEG)

    return wanted, visit, mask


def stacked(r):
    return slice(2 * r * SUB, 2 * (r + 1) * SUB)


def row_stats(go_ref, o_ref, lse_ref, gs, lse_scr, delta_scr, sub=ROWS):
    lane = iota((ROWS, 128), 1)
    low = lane < HEAD_DIM
    for p in range(PAIRS):
        grads = go_ref[:, lanes_of(p)]
        gs[p] = split_pair(grads, sub)
        product = grads.astype(F32) * o_ref[:, lanes_of(p)]
        for i in range(2):
            part = jnp.where(low if i == 0 else ~low, product, 0.0)
            delta = jnp.sum(part, axis=1, keepdims=True)
            lse = jnp.sum(jnp.where(lane == 2 * p + i, lse_ref[...], 0.0), axis=1, keepdims=True)
            for at in range(0, ROWS, sub):
                rows = slice(2 * at + i * sub, 2 * at + (i + 1) * sub)
                delta_scr[p, rows] = jnp.broadcast_to(delta[at : at + sub], (sub, 128))
                lse_scr[p, rows] = jnp.broadcast_to(lse[at : at + sub], (sub, 128))


def self_query_grad_kernel(
    at_ref, len_ref, tiles, qkv_ref, go_ref, o_ref, lse_ref, dq_ref, dist_ref,
    qs, gs, lse_scr, delta_scr, dq_scr, ds_scr, far_scr,
):
    chip = at_ref[0]
    starts, ends = spans(len_ref)
    base = pl.multiple_of(chip * ROWS, ROWS)
    first = first_of(base, ends)
    row_stats(go_ref, o_ref, lse_ref, gs, lse_scr, delta_scr)

    def start(p):
        qs[p] = split_pair(qkv_ref[p, pl.ds(base, ROWS), :])

    each_pair(start)
    dq_scr[...] = jnp.zeros_like(dq_scr)
    ds_scr[...] = jnp.zeros_like(ds_scr)
    far_scr[...] = jnp.zeros_like(far_scr)
    full_from = first_of(base + ROWS - 1, ends)
    q_row = base + iota((ROWS, 1), 0)
    q_seg = seg_of(q_row, ends)

    def block(j, _):
        at = pl.multiple_of(j * ROWS, ROWS)
        plain = (at >= full_from) & (j < chip - 1)

        def gradients(extra, near):
            raws = [dot_nt(qs[p], qkv_ref[PAIRS + p, pl.ds(at, ROWS), :]) for p in range(PAIRS)]
            dprobs = [dot_nt(gs[p], qkv_ref[2 * PAIRS + p, pl.ds(at, ROWS), :]) for p in range(PAIRS)]
            for p in range(PAIRS):
                grads = []
                for i in range(2):
                    h = 2 * p + i
                    rows = slice(i * ROWS, (i + 1) * ROWS)
                    probs = jnp.exp(extra(h, raws[p][rows]) - lse_scr[p, rows, :1])
                    ds = (probs * (dprobs[p][rows] - delta_scr[p, rows, :1])).astype(BF16)
                    if near is None:
                        far_scr[h] += jnp.sum(ds.astype(F32).reshape(ROWS // 8, 8, ROWS), axis=0)
                    else:
                        ds_scr[near, h] += ds.astype(F32)
                    grads.append(ds)
                dq_scr[p] += dot_nn(jnp.concatenate(grads, axis=0), qkv_ref[PAIRS + p, pl.ds(at, ROWS), :])

        @pl.when(plain)
        def _():
            gradients(lambda h, raw: raw + tiles[0, 0, h, :1, :1].astype(F32), None)

        @pl.when(jnp.logical_not(plain))
        def _():
            k_row = at + iota((1, ROWS), 1)
            masked = jnp.where((q_seg == seg_of(k_row, ends)) & (k_row <= q_row), 0.0, NEG)
            tile = jnp.maximum(j - chip + 2, 0)
            gradients(lambda h, raw: raw + (tiles[0, tile, h].astype(F32) + masked), tile)

        return 0

    lax.fori_loop(first // ROWS, chip + 1, block, 0)
    dist_ref[...] = jnp.zeros_like(dist_ref)
    lanes = iota((1, 2 * ROWS), 1)
    for p in range(PAIRS):
        dq_ref[:, 128 * p : 128 * p + 128] = join_pair(dq_scr[p]).astype(BF16)

    def fold(h, c):
        folded = jnp.concatenate([ds_scr[1, h], ds_scr[2, h]], axis=1)
        rows = ROWS
        while rows > 1:
            rows //= 2
            folded = folded[:rows] + pltpu.roll(folded[rows:], 2 * ROWS - rows, 1)
        far = jnp.sum(ds_scr[0, h], axis=0, keepdims=True) + jnp.sum(far_scr[h], axis=0, keepdims=True)
        far = jnp.sum(far, axis=1, keepdims=True)
        dist_ref[pl.ds(h, 1), :] = folded + jnp.where(lanes == 2 * ROWS - 1, far, 0.0)
        return c

    lax.fori_loop(0, LOCAL, fold, 0)


def self_key_stage_kernel(
    n_sides, at_ref, len_ref, tiles, qkv_ref, message_ref, so_ref, dq_ref, w_ref, x_ref, gain_ref, small_ref,
    keep_ref, send_ref, *refs,
):
    *outs, go_ref, stat_ref, ks, vs, dk_scr, dv_scr, dqkv_scr, h_scr, e_scr, grads_ref = refs
    chip, core = at_ref[0], at_ref[1]
    starts, ends = spans(len_ref)
    base = pl.multiple_of(chip * ROWS, ROWS)
    last = ends[-1]
    for end in reversed(ends[:-1]):
        last = jnp.where(base + ROWS - 1 < end, end, last)
    stop = (last - 1) // ROWS + 1
    full_to = ends[-1]
    for end in reversed(ends[:-1]):
        full_to = jnp.where(base < end, end, full_to)
    heads = own_rows(core, HALF)
    half = ROWS // 2

    def receive(i, c):
        both = [message_ref[2 * i + e, :half, :] for e in range(2)]
        result = dot_nt(jnp.concatenate(both, axis=0), so_ref[heads, :])
        for p in range(PAIRS):
            go_ref[p, pl.ds(pl.multiple_of(i * ROWS, ROWS), ROWS), :] = result[:, 128 * p : 128 * p + 128].astype(BF16)
        parts = message_ref[2 * i + core, half:, :].astype(F32)
        stat_ref[i] = parts[:, :ROWS] + parts[:, ROWS : 2 * ROWS] + parts[:, 2 * ROWS :]
        return c

    lax.fori_loop(chip, stop, receive, 0)

    def start(p):
        ks[p] = split_pair(qkv_ref[PAIRS + p, pl.ds(base, ROWS), :])
        vs[p] = split_pair(qkv_ref[2 * PAIRS + p, pl.ds(base, ROWS), :])

    each_pair(start)
    dk_scr[...] = jnp.zeros_like(dk_scr)
    dv_scr[...] = jnp.zeros_like(dv_scr)
    k_row = base + iota((ROWS, 1), 0)
    k_seg = seg_of(k_row, ends)

    def block(i, _):
        at = pl.multiple_of(i * ROWS, ROWS)
        plain = (at + ROWS <= full_to) & (i > chip + 1)

        def gradients(extra):
            raws = [dot_nt(ks[p], qkv_ref[p, pl.ds(at, ROWS), :]) for p in range(PAIRS)]
            dprobs = [dot_nt(vs[p], go_ref[p, pl.ds(at, ROWS), :]) for p in range(PAIRS)]
            for p in range(PAIRS):
                weights, dscores = [], []
                for e in range(2):
                    rows = slice(e * ROWS, (e + 1) * ROWS)
                    h = 2 * p + e
                    probs = jnp.exp(extra(h, raws[p][rows]) - stat_ref[i, h : h + 1, :])
                    weights.append(probs.astype(BF16))
                    dscores.append((probs * (dprobs[p][rows] - stat_ref[i, 8 + h : 9 + h, :])).astype(BF16))
                dv_scr[p] += dot_nn(jnp.concatenate(weights, axis=0), go_ref[p, pl.ds(at, ROWS), :])
                dk_scr[p] += dot_nn(jnp.concatenate(dscores, axis=0), qkv_ref[p, pl.ds(at, ROWS), :])

        @pl.when(plain)
        def _():
            gradients(lambda h, raw: raw + tiles[1, 0, h, :1, :1].astype(F32))

        @pl.when(jnp.logical_not(plain))
        def _():
            q_row = at + iota((1, ROWS), 1)
            masked = jnp.where((k_seg == seg_of(q_row, ends)) & (k_row <= q_row), 0.0, NEG)
            tile = jnp.maximum(2 - (i - chip), 0)
            gradients(lambda h, raw: raw + (tiles[1, tile, h].astype(F32) + masked))

        return 0

    lax.fori_loop(chip, stop, block, 0)
    dqkv_scr[:, :HALF] = dq_ref[...]
    for p in range(PAIRS):
        dqkv_scr[:, HALF + 128 * p : HALF + 128 * p + 128] = join_pair(dk_scr[p]).astype(BF16)
        dqkv_scr[:, 2 * HALF + 128 * p : 2 * HALF + 128 * p + 128] = join_pair(dv_scr[p]).astype(BF16)
    e_scr[...] = dot_nt(dqkv_scr[...], w_ref[...])
    keep_ref[...] = e_scr[own_rows(core, half), :]
    send_ref[...] = e_scr[own_rows(1 - core, half), :]
    wide = x_ref[...].astype(F32)
    scaled = wide * rms_inverse(wide)
    h_scr[...] = (scaled * gain_ref[...]).astype(BF16)
    dgain = jnp.sum(e_scr[...] * scaled, axis=0, keepdims=True)
    dgain = jnp.transpose(jnp.where(iota((128, dgain.shape[1]), 0) == 0, dgain, 0.0))
    columns = grads_ref.shape[1]
    grads_ref[:, columns - 128 :] = (small_ref[...] + dgain).astype(BF16)
    step = 256
    for i in range(0, h_scr.shape[1], step):
        grads_ref[i : i + step, : 2 * HALF] = dot_tn(h_scr[:, i : i + step], dqkv_scr[:, HALF:]).astype(BF16)
    give(n_sides, at_ref[2], grads_ref, outs)


def cross_grad_stage_kernel(
    at_ref, len_ref, enc_ref, deal_ref, place_ref,
    e_ref, other_ref, late_ref, gain_ref, cot_ref, co_ref, q_ref, o_ref, lse_ref, kv_ref, wc_ref,
    grad_ref, low_ref, dgain_ref, dq_ref, keep_ref, send_ref, part_ref,
    go_ref, qs, gs, lse_scr, delta_scr, dq_scr, block_scr,
):
    chip, core = at_ref[0], at_ref[1]
    dvalue, dgain = norm_grad(late_ref[...], gain_ref[...], e_ref[...] + other_ref[...])
    dgain_ref[...] = dgain
    grad = cot_ref[...].astype(F32) + dvalue
    grad_ref[...] = grad
    low_ref[...] = grad.astype(BF16)
    go_ref[...] = dot_nt(low_ref[...], co_ref[own_rows(core, HALF), :]).astype(BF16)
    wanted, _, mask = cross_flags(chip, len_ref, enc_ref, deal_ref)
    row_stats(go_ref, o_ref, lse_ref, gs, lse_scr, delta_scr, SUB)
    for p in range(PAIRS):
        qs[p] = split_pair(q_ref[:, lanes_of(p)], SUB)
    dq_scr[...] = jnp.zeros_like(dq_scr)
    half = keep_ref.shape[0] // ROWS

    def gradients(j, rows, masked):
        at = pl.multiple_of(j * KEYS, KEYS)
        raws = [dot_nt(qs[p, rows], kv_ref[p, pl.ds(at, KEYS), :]) for p in range(PAIRS)]
        dprobs = [dot_nt(gs[p, rows], kv_ref[PAIRS + p, pl.ds(at, KEYS), :]) for p in range(PAIRS)]
        for p in range(PAIRS):
            probs = jnp.exp(raws[p] + masked - lse_scr[p, rows, :1])
            ds = (probs * (dprobs[p] - delta_scr[p, rows, :1])).astype(BF16)
            dq_scr[p, rows] += dot_nn(ds, kv_ref[p, pl.ds(at, KEYS), :])
            block_scr[:, lanes_of(p)] += dot_tn(ds, qs[p, rows])
            block_scr[:, lanes_of(PAIRS + p)] += dot_tn(probs.astype(BF16), gs[p, rows])

    def block(j, c):
        at = pl.multiple_of(j * KEYS, KEYS)
        hit = wanted(at, 0, ROWS)

        @pl.when(hit)
        def _():
            block_scr[...] = jnp.zeros_like(block_scr)
            for r in range(ROWS // SUB):

                @pl.when(wanted(at, r * SUB, SUB))
                def _():
                    masked = mask(j, r)
                    gradients(j, stacked(r), jnp.concatenate([masked, masked], axis=0))

        for i in range(KEYS // ROWS):
            place = place_ref[j * (KEYS // ROWS) + i]
            upper = (place >= half).astype(jnp.int32)
            to = pl.ds(pl.multiple_of((place - upper * half) * ROWS, ROWS), ROWS)
            for mine, target in ((True, keep_ref), (False, send_ref)):
                here = (upper == at_ref[3]) == mine

                @pl.when(here & hit)
                def _():
                    target[to, :] = block_scr[i * ROWS : (i + 1) * ROWS, :].astype(BF16)

                @pl.when(here & jnp.logical_not(hit))
                def _():
                    target[to, :] = jnp.zeros((ROWS, 2 * HALF), BF16)

        return c

    lax.fori_loop(0, kv_ref.shape[1] // KEYS, block, 0)
    for p in range(PAIRS):
        dq_ref[:, 128 * p : 128 * p + 128] = join_pair(dq_scr[p], SUB).astype(BF16)
    part_ref[...] = dot_nt(dq_ref[...], wc_ref[:, :HALF])


def self_grad_start_kernel(
    at_ref, e_ref, other_ref, mid_ref, gain_ref, late_grad_ref, so_ref, o_ref, lse_ref,
    grad_ref, low_ref, dgain_ref, go_ref, message_ref,
    stat_scr,
):
    core = at_ref[1]
    dvalue, dgain = norm_grad(mid_ref[...], gain_ref[...], e_ref[...] + other_ref[...])
    dgain_ref[...] = dgain
    grad = late_grad_ref[...] + dvalue
    grad_ref[...] = grad
    low_ref[...] = grad.astype(BF16)
    go_ref[...] = dot_nt(low_ref[...], so_ref[own_rows(core, HALF), :]).astype(BF16)
    half = ROWS // 2
    message_ref[:half, :] = low_ref[own_rows(core, half), :]
    lane = iota((ROWS, 128), 1)
    stat_scr[...] = lse_ref[...]

    def pair(p):
        product = go_ref[:, lanes_of(p)].astype(F32) * o_ref[:, lanes_of(p)]
        for i in range(2):
            part = jnp.where((lane < HEAD_DIM) if i == 0 else (lane >= HEAD_DIM), product, 0.0)
            stat_scr[...] = jnp.where(lane == 8 + 2 * p + i, jnp.sum(part, axis=1, keepdims=True), stat_scr[...])

    each_pair(pair)
    rest = jnp.transpose(stat_scr[...])[:16]
    for part in range(3):
        high = rest.astype(BF16)
        message_ref[half:, part * ROWS : (part + 1) * ROWS] = high
        rest = rest - high.astype(F32)


def projection_grads_kernel(
    n_sides, at_ref, low2_ref, other2_ref, b2_ref, in_ref, dq2_ref, low1_ref, other1_ref, b1_ref, x_ref, gain_ref, dq1_ref, *outs
):
    *outs, out_ref = outs
    core, side = at_ref[1], at_ref[2]
    lanes = pl.ds(pl.multiple_of(core * HALF, 128), HALF)
    for at, own, other, grad in ((0, low2_ref, other2_ref, b2_ref), (2 * HALF, low1_ref, other1_ref, b1_ref)):
        grads = grad[:, lanes]
        for which, part in ((core, own), (1 - core, other)):
            out_ref[own_rows(which, HALF), at : at + HALF] = dot_tn(part[...], grads).astype(BF16)
    out_ref[:, HALF : 2 * HALF] = dot_tn(in_ref[...], dq2_ref[...]).astype(BF16)
    wide = x_ref[...].astype(F32)
    normed = (wide * rms_inverse(wide) * gain_ref[...]).astype(BF16)
    out_ref[:, 3 * HALF :] = dot_tn(normed, dq1_ref[...]).astype(BF16)
    give(n_sides, side, out_ref, outs)


def give(n_sides, side, value, outs):
    if n_sides == 2:
        rows = value.shape[0] // 2
        outs[0][...] = value[own_rows(side, rows), :]
        outs[1][...] = value[own_rows(1 - side, rows), :]
    else:
        outs[0][...] = value[...]


def encoder_grads_kernel(n_sides, at_ref, dkv_ref, e_ref, wc_ref, keep_ref, send_ref, *outs):
    *outs, low_scr, e_scr, grads_ref = outs
    core = at_ref[1]
    half = ROWS // 2
    low_scr[...] = dkv_ref[...].astype(BF16)
    e_scr[...] = dot_nt(low_scr[...], wc_ref[:, HALF:])
    keep_ref[...] = e_scr[own_rows(core, half), :]
    send_ref[...] = e_scr[own_rows(1 - core, half), :]
    grads_ref[...] = dot_tn(e_ref[...], low_scr[...]).astype(BF16)
    give(n_sides, at_ref[2], grads_ref, outs)


def token_grads_kernel(at_ref, e_ref, other_ref, x_ref, gain_ref, grad_ref, out_ref):
    dvalue, _ = norm_grad(x_ref[...].astype(F32), gain_ref[...], e_ref[...] + other_ref[...])
    out_ref[...] = grad_ref[own_rows(at_ref[1], out_ref.shape[0]), :] + dvalue


def finish_late_kernel(count, at_ref, place_ref, own_ref, other_ref, *refs):
    *outs, one, two, three, table, small = refs
    core, place = at_ref[1], place_ref[0]
    rows = own_ref.shape[0] // count
    columns = slice(len(outs) * HALF, len(outs) * HALF + 128)
    for i in range(count):
        part = slice(i * rows, (i + 1) * rows)
        to = pl.ds(pl.multiple_of((place ^ i) * rows, rows), rows)
        for j, out in enumerate(outs):
            lanes = slice(j * HALF, (j + 1) * HALF)
            out[to, own_lanes(core)] = own_ref[part, lanes].astype(F32)
            out[to, own_lanes(1 - core)] = other_ref[part, lanes].astype(F32)
        small[to, :] = own_ref[part, columns].astype(F32) + other_ref[part, columns].astype(F32)
    turned = jnp.transpose(small[...])
    for i, out in enumerate((one, two, three)):
        out[...] = turned[i]
    table[...] = small[: table.shape[0], 3 : 3 + HEADS]


def own_lanes(core):
    return pl.ds(pl.multiple_of(core * HALF, 128), HALF)


def finish_kernel(order, parts_ref, outer_ref, inner_ref, *outs):
    rows = parts_ref.shape[1]
    width = outer_ref.shape[1]
    side = inner_ref.shape[0]
    unit = inner_ref.shape[1] // 4
    for i, (core, place) in enumerate(order):
        at = place * rows
        for half in range(2):
            top = (2 * core + half) * side + at
            outer_ref[top : top + rows, :] = parts_ref[i, :, half * width : (half + 1) * width].astype(F32)
            lanes = slice((2 * half + core) * unit, (2 * half + core + 1) * unit)
            inner_ref[at : at + rows, lanes] = parts_ref[i, :, 2 * width + half * unit : 2 * width + (half + 1) * unit].astype(F32)
    finish_columns_kernel(order, 4 * width, parts_ref, *outs)


def finish_columns_kernel(order, skip, parts_ref, *outs):
    rows = parts_ref.shape[1]
    for i, (core, place) in enumerate(order):
        at = slice(place * rows, (place + 1) * rows)
        for j, out in enumerate(outs):
            columns = slice(skip + j * HALF, skip + (j + 1) * HALF)
            out[at, core * HALF : (core + 1) * HALF] = parts_ref[i, :, columns].astype(F32)


def pack_kernel(groups, core_ref, *refs):
    count = sum(groups)
    ins, outs = list(refs[:count]), refs[count:]
    for size, out in zip(groups, outs):
        at = 0
        for _ in range(size):
            part = ins.pop(0)
            out[:, at : at + part.shape[1]] = part[...].astype(BF16)
            at += part.shape[1]


SMEM = pl.BlockSpec(memory_space=pltpu.SMEM)
VMEM = pl.BlockSpec(memory_space=pltpu.VMEM)


def call(kernel, scalars, arrays, outs, scratch, flops):
    moved = sum(a.size * a.dtype.itemsize for a in arrays) + sum(math.prod(s) * jnp.dtype(d).itemsize for s, d in outs)
    return pl.pallas_call(
        kernel,
        out_shape=[jax.ShapeDtypeStruct(s, d) for s, d in outs],
        in_specs=[SMEM] * len(scalars) + [VMEM] * len(arrays),
        out_specs=[VMEM] * len(outs),
        scratch_shapes=[pltpu.VMEM(s, d) for s, d in scratch],
        compiler_params=pltpu.CompilerParams(vmem_limit_bytes=VMEM_LIMIT),
        cost_estimate=pl.CostEstimate(flops=1, transcendentals=0, bytes_accessed=1),
    )(*scalars, *arrays)


TILES = ((3, LOCAL, ROWS, ROWS), F32)
FAR = ((LOCAL, 8, ROWS), F32)
STACK = ((PAIRS, 2 * ROWS, 128), BF16)
COLUMN = ((PAIRS, 2 * ROWS, 128), F32)
LANE = ((ROWS, 128), F32)


def pack(core, groups):
    flat = [item for group in groups for item in group]
    return pl.pallas_call(
        functools.partial(pack_kernel, [len(g) for g in groups]),
        grid_spec=pltpu.PrefetchScalarGridSpec(
            num_scalar_prefetch=1,
            grid=(1,),
            in_specs=[
                pl.BlockSpec(shape, functools.partial(lambda index, i, c: index(c[0]), index)) for _, shape, index in flat
            ],
            out_specs=[
                pl.BlockSpec((g[0][1][0], sum(s[1] for _, s, _ in g)), lambda i, c: (0, 0)) for g in groups
            ],
        ),
        out_shape=[jax.ShapeDtypeStruct((g[0][1][0], sum(s[1] for _, s, _ in g)), BF16) for g in groups],
        compiler_params=pltpu.CompilerParams(vmem_limit_bytes=VMEM_LIMIT),
    )(core, *(w for w, _, _ in flat))


def swap_core(value):
    return lax.ppermute(value, "core", [(0, 1), (1, 0)])


def gather_fsdp(own):
    count = lax.axis_size("fsdp")
    if count != 2:
        return [lax.all_gather(own, "fsdp", axis=0, tiled=True)]
    return [own, lax.ppermute(own, "fsdp", [(0, 1), (1, 0)])]


CHIPS = ("z", "y")
GROUP = ("z", "y", "core")


def gather_rows(own):
    return lax.all_gather(own, GROUP, axis=0, tiled=True)


def bits_of(axis):
    return range((lax.axis_size(axis) - 1).bit_length())


def swap_bit(value, axis, bit):
    return lax.ppermute(value, axis, [(i, i ^ (1 << bit)) for i in range(lax.axis_size(axis))])


def parted(terms, axis, bit):
    side = (lax.axis_index(axis) >> bit) & 1
    rows = terms[0].shape[0] // 2

    def half(which):
        return [lax.dynamic_slice_in_dim(t, which * rows, rows, 0) for t in terms]

    return half(side), total(half(1 - side)).astype(BF16)


def halve(terms, axis, bit):
    keep, send = parted(terms, axis, bit)
    return keep + [swap_bit(send, axis, bit)]


def total(terms):
    return sum(t.astype(F32) for t in terms[1:]) + terms[0].astype(F32)


def steps_of(*axes):
    return [(axis, bit) for axis in axes for bit in bits_of(axis)]


def scatter(terms, steps):
    for axis, bit in steps:
        terms = halve(terms, axis, bit)
    return terms


def scatter_fsdp(terms):
    return scatter(terms, [("fsdp", bit) for bit in reversed(bits_of("fsdp"))])


def places(steps):
    nz, ny = lax.axis_size("z"), lax.axis_size("y")
    found = []
    for z in range(nz):
        for y in range(ny):
            place = 0
            for axis, bit in steps:
                place = 2 * place + (((z if axis == "z" else y) >> bit) & 1)
            found.append(place)
    return found


def after(value, *earlier):
    return lax.optimization_barrier((value, *earlier))[0]


def on_device(
    tokens, encoded, cotangent, tgt_lengths, enc_lengths, deal,
    ln_self, ln_cross, ln_ffn, bias_table,
    self_query, self_key, self_value, self_output,
    cross_query, cross_key, cross_value, cross_output,
    ffn_inner, ffn_outer,
):
    core = lax.axis_index("core")
    fsdp = lax.axis_index("fsdp")
    n_fsdp = lax.axis_size("fsdp")
    chip = lax.axis_index(CHIPS)
    steps = steps_of("y", "z")
    y_side = (lax.axis_index("y") >> steps[0][1]) & 1
    at = jnp.stack([chip, core, fsdp, y_side]).astype(jnp.int32)
    core_ref = core.reshape(1).astype(jnp.int32)
    rows, width = tokens.shape
    n = 2 * rows * lax.axis_size(CHIPS)
    side = width // n_fsdp
    hidden_half = ffn_inner.shape[1] // 2
    unit = hidden_half // n_fsdp
    wide, flat = ((ROWS, width), F32), ((ROWS, width), BF16)

    def column(weight):
        return (weight, (side, HALF), lambda c: (0, c))

    (qkv_own,) = pack(core_ref, [[column(w) for w in (self_query, self_key, self_value)]])
    w_qkv = gather_fsdp(qkv_own)
    if unit % 128 == 0:
        inner_items = [(ffn_inner, (side, unit), functools.partial(lambda o, c: (0, 2 * o + c), o)) for o in range(n_fsdp)]
    else:
        inner_units = ffn_inner.reshape(side, n_fsdp, 2, unit)
        inner_units = lax.dynamic_index_in_dim(inner_units, core, 2, keepdims=False).reshape(side, hidden_half)
        inner_items = [(inner_units, (side, hidden_half), lambda c: (0, 0))]
    out_own, cross_own, inner_own, outer_own = pack(
        core_ref,
        [
            [column(w) for w in (self_output, cross_output)],
            [column(w) for w in (cross_query, cross_key, cross_value)],
            inner_items,
            [(ffn_outer, (unit, width), lambda c: (c, 0))],
        ],
    )
    w_out = gather_fsdp(out_own)
    w_cross = gather_fsdp(cross_own)
    inner_own, outer_own = after((inner_own, outer_own), w_cross[-1])
    w_inner, w_outer = gather_fsdp(inner_own), gather_fsdp(outer_own)
    w_out_mate = [swap_core(w) for w in w_out]
    cot_mate = swap_core(cotangent)

    small = jnp.concatenate([ln_self, ln_cross, ln_ffn, bias_table.reshape(-1)], axis=0).astype(BF16)[None]
    small = gather_fsdp(small)
    if len(small) == 2:
        small = jnp.where(fsdp == 0, jnp.concatenate(small, axis=0), jnp.concatenate(small[::-1], axis=0))
    else:
        small = small[0]
    gain_self, gain_cross, gain_ffn = (
        small[:, i * side : (i + 1) * side].reshape(1, width).astype(F32) for i in range(3)
    )
    table = small[:, 3 * side :].reshape(BUCKETS, HEADS)
    table = lax.dynamic_slice_in_dim(table, core * LOCAL, LOCAL, 1).astype(F32)
    onehots = np.concatenate([QK_ONEHOT, KQ_ONEHOT], axis=0)
    biases = jnp.einsum("bh,tb->ht", table, onehots, precision=lax.Precision.HIGHEST)
    biases = jnp.pad(biases.reshape(LOCAL, 2, 2 * ROWS).swapaxes(0, 1), ((0, 0), (0, 2), (0, 0)))
    (tiles,) = call(tiles_kernel, (), (biases.reshape(16, 2 * ROWS),), [((2, *TILES[0]), BF16)], [], 1)

    xe = gather_rows(jnp.concatenate([tokens, encoded], axis=1))
    qkv, w_qkv, attn_self, low_self, lse_self = call(
        functools.partial(self_stage_kernel, len(w_qkv)), (at, tgt_lengths), (xe, gain_self, tiles, *w_qkv),
        [((3 * PAIRS, n, 128), BF16), ((width, 3 * HALF), BF16), ((ROWS, HALF), F32), ((ROWS, HALF), BF16), LANE],
        ATTEND(n),
        2 * n * width * 3 * HALF + 4 * ROWS * n * HALF,
    )
    low_self_other = swap_core(low_self)

    x_mid, in_cross, q_cross, kv_cross, attn_cross, low_cross, lse_cross, w_so, w_co, w_cross = call(
        functools.partial(cross_stage_kernel, len(w_out)), (at, tgt_lengths, enc_lengths, deal),
        (xe, gain_cross, low_self, low_self_other, *w_out, *w_out_mate, *w_cross),
        [
            wide, flat, ((ROWS, HALF), BF16), ((2 * PAIRS, n, 128), BF16), ((ROWS, HALF), F32), ((ROWS, HALF), BF16), LANE,
            ((width, width), BF16), ((width, width), BF16), ((width, 3 * HALF), BF16),
        ],
        ATTEND(n),
        2 * n * width * 2 * HALF + 4 * ROWS * n * HALF,
    )
    low_cross_other = swap_core(low_cross)

    half_rows = ((rows, width), F32)
    x_late, in_ffn, hidden, d_pre, cot, out_keep, out_send, e_ffn = call(
        functools.partial(ffn_stage_kernel, len(w_inner)), (at,),
        (x_mid, gain_ffn, low_cross, low_cross_other, w_co, cotangent, cot_mate, *w_inner, *w_outer),
        [wide, flat, ((ROWS, hidden_half), BF16), ((ROWS, hidden_half), BF16), flat, half_rows, half_rows, wide],
        [((width, hidden_half), BF16), ((hidden_half, width), BF16), wide],
        8 * ROWS * width * hidden_half,
    )
    e_ffn_other = swap_core(e_ffn)
    output = out_keep + swap_core(out_send)

    place = places(steps)
    place_ref = jnp.asarray(np.array(place, np.int32))
    nz, ny = lax.axis_size("z"), lax.axis_size("y")
    y_place = [p // nz for p in place[:ny]]
    key_place_ref = jnp.asarray(np.array([y_place[y] * nz + z for z in range(nz) for y in range(ny)], np.int32))
    grad_late, late_low, d_gain_ffn, dq_cross, dkv_keep, dkv_send, e_cross = call(
        cross_grad_stage_kernel, (at, tgt_lengths, enc_lengths, deal, key_place_ref),
        (e_ffn, e_ffn_other, x_late, gain_ffn, cot, w_co, q_cross, attn_cross, lse_cross, kv_cross, w_cross),
        [wide, flat, ((1, width), F32), ((ROWS, HALF), BF16), ((n // 2, 2 * HALF), BF16), ((n // 2, 2 * HALF), BF16), wide],
        [((ROWS, HALF), BF16), STACK, STACK, COLUMN, COLUMN, COLUMN, ((KEYS, 2 * HALF), F32)],
        10 * ROWS * n * HALF,
    )
    e_cross_other = swap_core(e_cross)
    dkv_got = swap_bit(dkv_send, *steps[0])

    grad_mid, mid_low, d_gain_cross, go_self, message = call(
        self_grad_start_kernel, (at,), (e_cross, e_cross_other, x_mid, gain_cross, grad_late, w_so, attn_self, lse_self),
        [wide, flat, ((1, width), F32), ((ROWS, HALF), BF16), ((rows + 16, width), BF16)], [LANE],
        2 * ROWS * width * HALF,
    )
    ffn_out = (
        [((side, 4 * width), BF16), ((side, 4 * width), BF16)]
        if n_fsdp == 2
        else [((hidden_half, width), F32), ((width, hidden_half), F32)]
    )
    first = call(
        functools.partial(ffn_grads_kernel, n_fsdp), (at,), (hidden, cot, in_ffn, after(d_pre, message)), ffn_out, [],
        4 * ROWS * width * hidden_half,
    )
    if n_fsdp == 2:
        first_other = lax.ppermute(first[1], "fsdp", [(0, 1), (1, 0)])
        go_self = after(go_self, first[1])
    message = lax.all_gather(message, GROUP, axis=0)
    x_chip = lax.dynamic_slice(xe, (chip * ROWS, 0), (ROWS, width))
    e_chip = lax.dynamic_slice(xe, (chip * ROWS, width), (ROWS, width))
    dq_self, dist = call(
        self_query_grad_kernel, (at, tgt_lengths), (tiles, qkv, go_self, attn_self, lse_self),
        [((ROWS, HALF), BF16), ((8, 2 * ROWS), F32)],
        [STACK, STACK, COLUMN, COLUMN, COLUMN, TILES, FAR],
        6 * ROWS * n * HALF,
    )
    def given(columns):
        return [((width // 2, columns), BF16)] * 2 if n_fsdp == 2 else [((width, columns), BF16)]

    def over_fsdp(parts):
        if n_fsdp == 2:
            return [parts[0], lax.ppermute(parts[1], "fsdp", [(0, 1), (1, 0)])]
        return scatter_fsdp(parts)

    second = call(
        functools.partial(projection_grads_kernel, n_fsdp), (at,),
        (low_cross, low_cross_other, late_low, in_cross, dq_cross, low_self, low_self_other, mid_low, x_chip, gain_self, dq_self),
        given(4 * HALF), [((width, 4 * HALF), BF16)], 8 * ROWS * width * HALF,
    )
    d_table = jnp.einsum("ht,tb->bh", dist[:LOCAL], QK_ONEHOT, precision=lax.Precision.HIGHEST)
    d_table = jnp.zeros((BUCKETS, 2, LOCAL), F32).at[:, core].set(d_table).reshape(n_fsdp, -1, HEADS)
    d_table = jnp.pad(d_table, ((0, 0), (0, side - d_table.shape[1]), (0, 0))).reshape(width, HEADS)
    none = jnp.zeros((width, 1), F32)
    small = [none, 0.5 * d_gain_cross.reshape(width, 1), 0.5 * d_gain_ffn.reshape(width, 1), d_table]
    small = jnp.pad(jnp.concatenate(small, axis=1), ((0, 0), (0, 128 - 3 - HEADS)))

    if n_fsdp == 2:
        first = [first[0], first_other]
    else:
        outer = first[0].reshape(n_fsdp, 2, side, width)
        first = jnp.concatenate([outer[:, 0], outer[:, 1], first[1].reshape(n_fsdp, side, hidden_half)], axis=2)
        first = scatter_fsdp([first.reshape(width, -1)])
    *y_steps, z_near, z_far = steps
    dkv_cross = scatter(after([dkv_keep, dkv_got], second[-1]), y_steps[1:])
    dkv_cross = total(dkv_cross).astype(BF16)
    first = after(first, dkv_cross)
    second = over_fsdp(after(second, first[-1]))
    first_keep, first_sent = parted(first, *y_steps[0])
    first_got = swap_bit(first_sent, *y_steps[0])
    dkv_cross = lax.psum_scatter(dkv_cross, "z", scatter_dimension=0, tiled=True)

    e_keep, e_send, *fourth = call(
        functools.partial(self_key_stage_kernel, n_fsdp), (at, tgt_lengths),
        (tiles, qkv, after(message, first_sent), w_so, dq_self, w_qkv, x_chip, gain_self, small),
        [half_rows, half_rows, *given(2 * HALF + 128)],
        [
            ((PAIRS, n, 128), BF16), ((n // ROWS, 16, ROWS), F32), STACK, STACK, COLUMN, COLUMN,
            ((ROWS, 3 * HALF), BF16), flat, wide, ((width, 2 * HALF + 128), BF16),
        ],
        8 * ROWS * n * HALF,
    )
    fourth_sent = fourth[-1]
    fourth = over_fsdp(fourth)
    first = scatter(first_keep + [after(first_got, fourth_sent)], y_steps[1:])
    first_keep, first_sent = parted(first, *z_near)
    first_got = swap_bit(first_sent, *z_near)
    second_keep, second_sent = parted(after(second, first_sent), *y_steps[0])
    second_got = swap_bit(second_sent, *y_steps[0])
    fourth_keep, fourth_sent = parted(after(fourth, second_sent), *y_steps[0])
    fourth_got = swap_bit(fourth_sent, *y_steps[0])
    enc_keep, enc_send, *third = call(
        functools.partial(encoder_grads_kernel, n_fsdp), (at,), (after(dkv_cross, fourth_sent), e_chip, w_cross),
        [half_rows, half_rows, *given(2 * HALF)],
        [((ROWS, 2 * HALF), BF16), wide, ((width, 2 * HALF), BF16)], 8 * ROWS * width * HALF,
    )
    third_sent = third[-1]
    third = over_fsdp(third)
    first_keep, first_sent = parted(first_keep + [after(first_got, third_sent)], *z_far)
    first_got = swap_bit(first_sent, *z_far)

    second_got, fourth_got = after((second_got, fourth_got), first_sent)
    second = total(scatter(second_keep + [second_got], y_steps[1:]))
    fourth = total(scatter(fourth_keep + [fourth_got], y_steps[1:]))
    second = jnp.concatenate([second, fourth], axis=1).astype(BF16)
    second_keep, second_sent = parted([second], *z_near)
    second_got = swap_bit(second_sent, *z_near)
    (grad_tokens,) = call(
        token_grads_kernel, (at,), (e_keep, swap_core(after(e_send, second_sent)), tokens, gain_self, grad_mid),
        [half_rows], [], 10 * rows * width,
    )
    enc_grad = enc_keep + swap_core(after(enc_send, second_sent))
    second_got = after(second_got, grad_tokens, enc_grad)
    late_keep, late_sent = parted(after(third, second_sent), *y_steps[0])
    late_got = swap_bit(late_sent, *y_steps[0])
    first = total(first_keep + [after(first_got, late_sent)]).astype(BF16)
    second_keep, second_sent = parted(second_keep + [after(second_got, first)], *z_far)
    second_got = swap_bit(second_sent, *z_far)
    late = scatter(late_keep + [after(late_got, second_sent)], y_steps[1:])
    late_keep, late_sent = parted(late, *z_near)
    late_got = swap_bit(late_sent, *z_near)
    second = total(second_keep + [after(second_got, late_sent)]).astype(BF16)
    early = lax.all_gather(jnp.concatenate([first, second[:, : 4 * HALF]], axis=1), GROUP, axis=0)
    late = total(halve(late_keep + [after(late_got, second)], *z_far)).astype(BF16)
    late = jnp.concatenate([late, second[:, 4 * HALF :]], axis=1)
    for axis, bit in reversed(steps):
        late = jnp.concatenate([late, swap_bit(late, axis, bit)], axis=0)
    late_other = swap_core(late)
    early = after(early, late_other)

    matrix = ((side, width), F32)
    own_place = place_ref[chip].reshape(1)
    if side // len(place) % 8 == 0:
        g_ck, g_cv, g_sk, g_sv, *gains, g_table = call(
            functools.partial(finish_late_kernel, len(place)), (at, own_place), (late, late_other),
            [matrix] * 4 + [((side,), F32)] * 3 + [(bias_table.shape, F32)], [((side, 128), F32)], 8 * side * width,
        )
    else:
        blocks = jnp.stack([late, late_other]).reshape(2, len(place), side // len(place), -1)
        blocks = jnp.take(blocks, own_place[0] ^ jnp.arange(len(place), dtype=jnp.int32), axis=1)
        blocks = jnp.where(core == 0, blocks, blocks[::-1]).astype(F32).reshape(2, side, -1)
        g_ck, g_cv, g_sk, g_sv = (
            jnp.swapaxes(blocks[:, :, i : i + HALF], 0, 1).reshape(side, width) for i in range(0, 4 * HALF, HALF)
        )
        small = jnp.sum(blocks[:, :, 4 * HALF :], axis=0)
        gains = [small[:, i] for i in range(3)]
        g_table = small[: bias_table.shape[0], 3 : 3 + HEADS]
    order = [(c, p) for p in place for c in range(2)]
    if n_fsdp == 2:
        g_outer, g_inner, g_co, g_cq, g_so, g_sq = call(
            functools.partial(finish_kernel, order), (), (early,),
            [(ffn_outer.shape, F32), (ffn_inner.shape, F32), *[matrix] * 4], [], 8 * side * width,
        )
    else:
        sources = np.argsort([2 * p + c for c, p in order])
        pair = jnp.swapaxes(early[sources].reshape(len(place), 2, -1, early.shape[2]), 0, 1)
        pair = pair.reshape(2, side, -1).astype(F32)
        g_outer = pair[:, :, : 2 * width].reshape(2, side, 2, width)
        g_outer = jnp.swapaxes(g_outer, 1, 2).reshape(ffn_outer.shape)
        g_inner = jnp.transpose(pair[:, :, 2 * width : 4 * width].reshape(2, side, n_fsdp, unit), (1, 2, 0, 3))
        g_inner = g_inner.reshape(ffn_inner.shape)
        g_co, g_cq, g_so, g_sq = call(
            functools.partial(finish_columns_kernel, order, 4 * width), (), (early,), [matrix] * 4, [], 8 * side * width
        )

    return (
        output, grad_tokens, enc_grad,
        *gains, g_table,
        g_sq, g_sk, g_sv, g_so, g_cq, g_ck, g_cv, g_co, g_inner, g_outer,
    )


def solution(mesh):
    n_ctx, n_fsdp = mesh.shape["ctx"], mesh.shape["fsdp"]
    n_z = 4
    grid = Mesh(mesh.devices.reshape(n_z, n_ctx // (2 * n_z), 2, n_fsdp), ("z", "y", "core", "fsdp"))
    by_rows = P(("fsdp", "z", "y", "core"), None)
    split = P("fsdp", None)
    vector = P("fsdp")
    in_specs = (by_rows,) * 3 + (split,) * 3 + (vector,) * 3 + (split,) * 11
    out_specs = (by_rows,) * 3 + (vector,) * 3 + (split,) * 11
    return jax.shard_map(on_device, mesh=grid, in_specs=in_specs, out_specs=out_specs, check_vma=False)
```

```python
import functools
import math

import jax
import jax.numpy as jnp
import numpy as np
from jax import lax
from jax.experimental import pallas as pl
from jax.experimental.pallas import tpu as pltpu
from jax.sharding import Mesh
from jax.sharding import PartitionSpec as P

HEADS = 12
HEAD_DIM = 64
BUCKETS = 32
EPS = 1e-06
NEG = -1e30
GELU_C = 0.7978845608028654
GELU_A = 0.044715

LOCAL = HEADS // 2
PAIRS = LOCAL // 2
HALF = LOCAL * HEAD_DIM
ROWS = 256
VMEM_LIMIT = 56 << 20

F32 = jnp.float32
BF16 = jnp.bfloat16


def bucket_edges():
    edges = []
    for level in range(1, 16):
        distance = 16
        while int(math.log(distance / 16.0) / math.log(8.0) * 16.0) < level:
            distance += 1
        edges.append(distance)
    return edges


def buckets_of(distances):
    clipped = np.maximum(np.asarray(distances), 0)
    large = np.full(clipped.shape, 16)
    for edge in bucket_edges():
        large = large + (clipped >= edge)
    return np.where(clipped < 16, clipped, large)


LANES = np.arange(2 * ROWS)
QK_DISTANCE = np.where(LANES <= ROWS, ROWS - LANES, 3 * ROWS - LANES)
KQ_DISTANCE = LANES
QK_ONEHOT = np.eye(BUCKETS, dtype=np.float32)[buckets_of(QK_DISTANCE)]
KQ_ONEHOT = np.eye(BUCKETS, dtype=np.float32)[buckets_of(KQ_DISTANCE)]


def dot_nt(left, right):
    return lax.dot_general(left, right, (((1,), (1,)), ((), ())), preferred_element_type=F32)


def dot_tn(left, right):
    return lax.dot_general(left, right, (((0,), (0,)), ((), ())), preferred_element_type=F32)


def dot_nn(left, right):
    return lax.dot_general(left, right, (((1,), (0,)), ((), ())), preferred_element_type=F32)


def spans(ref):
    starts, ends, at = [], [], jnp.int32(0)
    for i in range(ref.shape[1]):
        starts.append(at)
        at = at + ref[0, i]
        ends.append(at)
    return starts, ends


def seg_of(index, ends):
    found = jnp.zeros(index.shape, jnp.int32)
    for end in ends[:-1]:
        found = found + (index >= end).astype(jnp.int32)
    return found


def iota(shape, axis):
    return lax.broadcasted_iota(jnp.int32, shape, axis)


def split_pair(pair, sub=ROWS):
    low = iota((sub, pair.shape[1]), 1) < HEAD_DIM
    zero = jnp.zeros((sub, pair.shape[1]), pair.dtype)
    parts = []
    for at in range(0, pair.shape[0], sub):
        part = pair[at : at + sub]
        parts += [jnp.where(low, part, zero), jnp.where(low, zero, part)]
    return jnp.concatenate(parts, axis=0)


def head_rows(both, e, sub=ROWS):
    parts = [both[at + e * sub : at + (e + 1) * sub] for at in range(0, both.shape[0], 2 * sub)]
    return parts[0] if len(parts) == 1 else jnp.concatenate(parts, axis=0)


def join_pair(both, sub=ROWS):
    first = head_rows(both, 0, sub)
    return jnp.where(iota(first.shape, 1) < HEAD_DIM, first, head_rows(both, 1, sub))


def tiles_kernel(bias_ref, tiles_ref):
    def head(h, c):
        for which in range(2):
            row = bias_ref[pl.ds(8 * which + h, 1), :]
            rolled = pltpu.roll(jnp.broadcast_to(row, (ROWS, 2 * ROWS)), 0, 1, stride=1, stride_axis=0)
            first, second = (1, 2) if which == 0 else (2, 1)
            tiles_ref[which, first, h] = rolled[:, :ROWS].astype(BF16)
            tiles_ref[which, second, h] = rolled[:, ROWS:].astype(BF16)
            tiles_ref[which, 0, h] = jnp.broadcast_to(row[:, 2 * ROWS - 1 :], (ROWS, ROWS)).astype(BF16)
        return c

    lax.fori_loop(0, LOCAL, head, 0)


def lanes_of(p):
    return slice(p * 128, p * 128 + 128) if isinstance(p, int) else pl.ds(pl.multiple_of(p * 128, 128), 128)


def each_pair(body):
    for p in range(PAIRS):
        body(p)


def rms_inverse(value):
    return lax.rsqrt(jnp.mean(value * value, axis=-1, keepdims=True) + EPS)


def together(n):
    return PAIRS if n <= 2048 else 1


def attend(queries, keys, values, visit_scores, visit, sub, step, s_scr, mx_scr, l_scr, acc_scr, qs, o_ref, low_ref, lse_ref):
    count = s_scr.shape[0]
    lse_ref[...] = jnp.zeros_like(lse_ref)
    lane = iota((ROWS, 128), 1)

    def group(g):
        for c in range(count):
            qs[c] = split_pair(queries(g * count + c), sub)
        mx_scr[...] = jnp.full_like(mx_scr, NEG)

        def scores(j, rows, extra):
            at = pl.multiple_of(j * step, step)
            raws = [dot_nt(qs[c, rows], keys(g * count + c, at)) for c in range(count)]
            for c in range(count):
                value = extra(g * count + c, raws[c])
                s_scr[c, rows, pl.ds(at, step)] = value
                mx_scr[c, rows] = functools.reduce(
                    jnp.maximum, [value[:, i : i + 128] for i in range(0, step, 128)], mx_scr[c, rows]
                )

        visit_scores(scores)
        for c in range(count):
            mx_scr[c] = jnp.broadcast_to(jnp.max(mx_scr[c], axis=1, keepdims=True), mx_scr.shape[1:])
        l_scr[...] = jnp.zeros_like(l_scr)
        acc_scr[...] = jnp.zeros_like(acc_scr)

        def weigh(j, rows):
            at = pl.multiple_of(j * step, step)
            for c in range(count):
                weights = jnp.exp(s_scr[c, rows, pl.ds(at, step)] - mx_scr[c, rows, :1])
                l_scr[c, rows] += sum(weights[:, i : i + 128] for i in range(128, step, 128)) + weights[:, :128]
                acc_scr[c, rows] += dot_nn(weights.astype(BF16), values(g * count + c, at))

        visit(weigh)
        for c in range(count):
            p = g * count + c
            total = jnp.sum(l_scr[c], axis=1, keepdims=True)
            result = join_pair(acc_scr[c] / total, sub)
            o_ref[:, lanes_of(p)] = result
            low_ref[:, lanes_of(p)] = result.astype(BF16)
            both = mx_scr[c, :, :1] + jnp.log(total)
            lse = jnp.where(lane == 2 * p, head_rows(both, 0, sub), lse_ref[...])
            lse_ref[...] = jnp.where(lane == 2 * p + 1, head_rows(both, 1, sub), lse)

    if count == PAIRS:
        group(0)
    else:
        lax.fori_loop(0, PAIRS // count, lambda g, c: (group(g), c)[1], 0)


ATTEND = lambda n: [
    ((together(n), 2 * ROWS, n), F32), ((together(n), 2 * ROWS, 128), F32), ((together(n), 2 * ROWS, 128), F32),
    ((together(n), 2 * ROWS, 128), F32), ((together(n), 2 * ROWS, 128), BF16),
]


def set_rows(target, parts, side):
    if len(parts) == 1:
        target[...] = parts[0][...]
        return
    rows = parts[0].shape[0]
    target[pl.ds(pl.multiple_of(side * rows, rows), rows), :] = parts[0][...]
    target[pl.ds(pl.multiple_of((1 - side) * rows, rows), rows), :] = parts[1][...]


def first_of(base, ends):
    first = jnp.int32(0)
    for end in ends[:-1]:
        first = jnp.where(base >= end, end, first)
    return first


def self_stage_kernel(n_parts, at_ref, len_ref, xe_ref, gain_ref, tiles, *refs):
    parts, refs = refs[:n_parts], refs[n_parts:]
    qkv_ref, w_ref, o_ref, low_ref, lse_ref, s_scr, mx_scr, l_scr, acc_scr, qs = refs
    chip, side = at_ref[0], at_ref[2]
    set_rows(w_ref, parts, side)
    width = w_ref.shape[0]
    step = 512

    def body(i, c):
        at = pl.multiple_of(i * step, step)
        wide = xe_ref[pl.ds(at, step), :width].astype(F32)
        value = (wide * rms_inverse(wide) * gain_ref[...]).astype(BF16)
        result = dot_nn(value, w_ref[...])
        for j in range(qkv_ref.shape[0]):
            qkv_ref[j, pl.ds(at, step), :] = result[:, 128 * j : 128 * j + 128].astype(BF16)
        return c

    lax.fori_loop(0, xe_ref.shape[0] // step, body, 0)

    starts, ends = spans(len_ref)
    base = pl.multiple_of(chip * ROWS, ROWS)
    j_min = first_of(base, ends) // ROWS
    full_from = first_of(base + ROWS - 1, ends)
    q_row = base + iota((ROWS, 1), 0)
    q_seg = seg_of(q_row, ends)

    rows = slice(0, 2 * ROWS)

    def visit(block):
        lax.fori_loop(j_min, chip + 1, lambda j, c: (block(j, rows), c)[1], 0)

    def visit_scores(block):
        def body(j, c):
            at = pl.multiple_of(j * ROWS, ROWS)
            plain = (at >= full_from) & (j < chip - 1)

            def with_bias(bias):
                def extra(p, raw):
                    return jnp.concatenate([raw[:ROWS] + bias(2 * p), raw[ROWS:] + bias(2 * p + 1)], axis=0)

                block(j, rows, extra)

            @pl.when(plain)
            def _():
                with_bias(lambda h: tiles[0, 0, h, :1, :1].astype(F32))

            @pl.when(jnp.logical_not(plain))
            def _():
                k_row = at + iota((1, ROWS), 1)
                masked = jnp.where((q_seg == seg_of(k_row, ends)) & (k_row <= q_row), 0.0, NEG)
                tile = jnp.maximum(j - chip + 2, 0)
                with_bias(lambda h: tiles[0, tile, h].astype(F32) + masked)

            return c

        lax.fori_loop(j_min, chip + 1, body, 0)

    attend(
        lambda p: qkv_ref[p, pl.ds(base, ROWS), :],
        lambda p, at: qkv_ref[PAIRS + p, pl.ds(at, ROWS), :],
        lambda p, at: qkv_ref[2 * PAIRS + p, pl.ds(at, ROWS), :],
        visit_scores, visit, ROWS, ROWS, s_scr, mx_scr, l_scr, acc_scr, qs, o_ref, low_ref, lse_ref,
    )


def add_heads(low_ref, other_ref, w_ref, core):
    own = pl.ds(pl.multiple_of(core * HALF, HALF), HALF)
    other = pl.ds(pl.multiple_of((1 - core) * HALF, HALF), HALF)
    return dot_nn(low_ref[...], w_ref[own, :]) + dot_nn(other_ref[...], w_ref[other, :])


def cross_stage_kernel(n_parts, at_ref, len_ref, enc_ref, deal_ref, xe_ref, gain_ref, low_ref, other_ref, *refs):
    outs, mates, parts, refs = refs[:n_parts], refs[n_parts : 2 * n_parts], refs[2 * n_parts : 3 * n_parts], refs[3 * n_parts :]
    mid_ref, in_ref, q_ref, kv_ref, o_ref, low2_ref, lse_ref, so_ref, co_ref, wc_ref, refs = *refs[:10], refs[10:]
    s_scr, mx_scr, l_scr, acc_scr, qs = refs
    chip, core, side = at_ref[0], at_ref[1], at_ref[2]
    set_rows(wc_ref, parts, side)
    for pieces, column in ((outs, core), (mates, 1 - core)):
        lanes = pl.ds(pl.multiple_of(column * HALF, 128), HALF)
        for i, piece in enumerate(pieces):
            rows = piece.shape[0]
            at = pl.multiple_of((side if i == 0 else 1 - side) * rows, rows) if n_parts > 1 else 0
            so_ref[pl.ds(at, rows), lanes] = piece[:, :HALF]
            co_ref[pl.ds(at, rows), lanes] = piece[:, HALF:]
    width = so_ref.shape[0]
    base = pl.multiple_of(chip * ROWS, ROWS)
    mid = xe_ref[pl.ds(base, ROWS), :width].astype(F32) + add_heads(low_ref, other_ref, so_ref, core)
    mid_ref[...] = mid
    normed = (mid * rms_inverse(mid) * gain_ref[...]).astype(BF16)
    in_ref[...] = normed
    q_ref[...] = dot_nn(normed, wc_ref[:, :HALF]).astype(BF16)
    step = 512

    def body(i, c):
        at = pl.multiple_of(i * step, step)
        result = dot_nn(xe_ref[pl.ds(at, step), width:], wc_ref[:, HALF:])
        for j in range(kv_ref.shape[0]):
            kv_ref[j, pl.ds(at, step), :] = result[:, 128 * j : 128 * j + 128].astype(BF16)
        return c

    lax.fori_loop(0, xe_ref.shape[0] // step, body, 0)
    _, over, mask = cross_flags(chip, len_ref, enc_ref, deal_ref)
    blocks = kv_ref.shape[1] // KEYS

    def visit(block):
        over(blocks, lambda j, r: block(j, stacked(r)))

    def visit_scores(block):
        def body(j, r):
            masked = mask(j, r)
            block(j, stacked(r), lambda p, raw: raw + jnp.concatenate([masked, masked], axis=0))

        over(blocks, body)

    attend(
        lambda p: q_ref[:, lanes_of(p)],
        lambda p, at: kv_ref[p, pl.ds(at, KEYS), :],
        lambda p, at: kv_ref[PAIRS + p, pl.ds(at, KEYS), :],
        visit_scores, visit, SUB, KEYS, s_scr, mx_scr, l_scr, acc_scr, qs, o_ref, low2_ref, lse_ref,
    )


def gelu_parts(value):
    tangent = jnp.tanh(GELU_C * (value + GELU_A * value * value * value))
    result = 0.5 * value * (1.0 + tangent)
    slope = 0.5 * (1.0 + tangent) + 0.5 * value * (1.0 - tangent * tangent) * GELU_C * (
        1.0 + 3.0 * GELU_A * value * value
    )
    return (result, slope)


def own_rows(core, rows):
    return pl.ds(pl.multiple_of(core * rows, rows), rows)


def ffn_stage_kernel(n_parts, at_ref, mid_ref, gain_ref, low_ref, other_ref, co_ref, cot_ref, mate_ref, *refs):
    inner, outer, refs = refs[:n_parts], refs[n_parts : 2 * n_parts], refs[2 * n_parts :]
    late_ref, in_ref, hid_ref, dpre_ref, cot_out, keep_ref, send_ref, e_ref, wi_ref, wo_ref, part_scr = refs
    core, side = at_ref[1], at_ref[2]
    rows = cot_ref.shape[0]
    set_rows(wi_ref, inner, side)
    set_rows(wo_ref, outer, side)
    cot_out[own_rows(core, rows), :] = cot_ref[...]
    cot_out[own_rows(1 - core, rows), :] = mate_ref[...]
    late = mid_ref[...] + add_heads(low_ref, other_ref, co_ref, core)
    late_ref[...] = late
    normed = (late * rms_inverse(late) * gain_ref[...]).astype(BF16)
    in_ref[...] = normed
    columns = 512

    def body(i, c):
        at = pl.multiple_of(i * columns, columns)
        activated, slope = gelu_parts(dot_nn(normed, wi_ref[:, pl.ds(at, columns)]))
        hid_ref[:, pl.ds(at, columns)] = activated.astype(BF16)
        grads = dot_nt(cot_out[...], wo_ref[pl.ds(at, columns), :])
        dpre_ref[:, pl.ds(at, columns)] = (grads * slope).astype(BF16)
        return c

    lax.fori_loop(0, wi_ref.shape[1] // columns, body, 0)
    e_ref[...] = dot_nt(dpre_ref[...], wi_ref[...])
    part_scr[...] = dot_nn(hid_ref[...], wo_ref[...])
    keep_ref[...] = part_scr[own_rows(core, rows), :] + late_ref[own_rows(core, rows), :]
    send_ref[...] = part_scr[own_rows(1 - core, rows), :]


def ffn_grads_kernel(n_sides, at_ref, hid_ref, cot_ref, in_ref, dpre_ref, *outs):
    side = at_ref[2]
    rows = in_ref.shape[1] // n_sides
    width = cot_ref.shape[1]
    if n_sides != 2:
        outs[0][...] = dot_tn(hid_ref[...], cot_ref[...])
        outs[1][...] = dot_tn(in_ref[...], dpre_ref[...])
        return
    keep_ref, send_ref = outs
    for owner in range(2):
        for mine, target in ((True, keep_ref), (False, send_ref)):

            @pl.when((side == owner) == mine)
            def _():
                for part in range(2):
                    units = slice((2 * owner + part) * rows, (2 * owner + part + 1) * rows)
                    block = dot_tn(hid_ref[:, units], cot_ref[...])
                    target[:, part * width : (part + 1) * width] = block.astype(target.dtype)
                block = dot_tn(in_ref[:, owner * rows : (owner + 1) * rows], dpre_ref[...])
                target[:, 2 * width :] = block.astype(target.dtype)


def norm_grad(value, gain, grad):
    inverse = rms_inverse(value)
    scaled = grad * gain
    cubed = inverse * inverse * inverse
    dvalue = inverse * scaled - value * cubed * jnp.mean(scaled * value, axis=-1, keepdims=True)
    return dvalue, jnp.sum(grad * value * inverse, axis=0, keepdims=True)


KEYS = 2 * ROWS
SUB = ROWS


def cross_flags(chip, len_ref, enc_ref, deal_ref):
    starts, ends = spans(len_ref)
    e_starts, e_ends = spans(enc_ref)
    base = chip * ROWS
    ranges = []
    for i in range(len(ends)):
        low, high = jnp.int32(0), jnp.int32(0)
        for e in range(len(e_ends)):
            hit = deal_ref[0, i] == e
            low = jnp.where(hit, e_starts[e], low)
            high = jnp.where(hit, e_ends[e], high)
        ranges.append((starts[i], ends[i], low, high))

    def wanted(at, first, count):
        found = jnp.bool_(False)
        for start, end, low, high in ranges:
            live = (start < base + first + count) & (end > base + first)
            found = found | (live & (low < at + KEYS) & (high > at))
        return found

    def visit(blocks, body):
        def inner(j, c):
            for r in range(ROWS // SUB):

                @pl.when(wanted(j * KEYS, r * SUB, SUB))
                def _():
                    body(j, r)

            return c

        lax.fori_loop(0, blocks, inner, 0)

    q_seg = seg_of(base + iota((ROWS, 1), 0), ends)
    q_pair = jnp.zeros((ROWS, 1), jnp.int32)
    for i in range(len(ends)):
        q_pair = q_pair + jnp.where(q_seg == i, deal_ref[0, i], 0)

    def mask(j, r):
        k_seg = seg_of(j * KEYS + iota((1, KEYS), 1), e_ends)
        return jnp.where(q_pair[r * SUB : (r + 1) * SUB] == k_seg, 0.0, NEG)

    return wanted, visit, mask


def stacked(r):
    return slice(2 * r * SUB, 2 * (r + 1) * SUB)


def row_stats(go_ref, o_ref, lse_ref, gs, lse_scr, delta_scr, sub=ROWS):
    lane = iota((ROWS, 128), 1)
    low = lane < HEAD_DIM
    for p in range(PAIRS):
        grads = go_ref[:, lanes_of(p)]
        gs[p] = split_pair(grads, sub)
        product = grads.astype(F32) * o_ref[:, lanes_of(p)]
        for i in range(2):
            part = jnp.where(low if i == 0 else ~low, product, 0.0)
            delta = jnp.sum(part, axis=1, keepdims=True)
            lse = jnp.sum(jnp.where(lane == 2 * p + i, lse_ref[...], 0.0), axis=1, keepdims=True)
            for at in range(0, ROWS, sub):
                rows = slice(2 * at + i * sub, 2 * at + (i + 1) * sub)
                delta_scr[p, rows] = jnp.broadcast_to(delta[at : at + sub], (sub, 128))
                lse_scr[p, rows] = jnp.broadcast_to(lse[at : at + sub], (sub, 128))


def self_query_grad_kernel(
    at_ref, len_ref, tiles, qkv_ref, go_ref, o_ref, lse_ref, dq_ref, dist_ref,
    qs, gs, lse_scr, delta_scr, dq_scr, ds_scr, far_scr,
):
    chip = at_ref[0]
    starts, ends = spans(len_ref)
    base = pl.multiple_of(chip * ROWS, ROWS)
    first = first_of(base, ends)
    row_stats(go_ref, o_ref, lse_ref, gs, lse_scr, delta_scr)

    def start(p):
        qs[p] = split_pair(qkv_ref[p, pl.ds(base, ROWS), :])

    each_pair(start)
    dq_scr[...] = jnp.zeros_like(dq_scr)
    ds_scr[...] = jnp.zeros_like(ds_scr)
    far_scr[...] = jnp.zeros_like(far_scr)
    full_from = first_of(base + ROWS - 1, ends)
    q_row = base + iota((ROWS, 1), 0)
    q_seg = seg_of(q_row, ends)

    def block(j, _):
        at = pl.multiple_of(j * ROWS, ROWS)
        plain = (at >= full_from) & (j < chip - 1)

        def gradients(extra, near):
            raws = [dot_nt(qs[p], qkv_ref[PAIRS + p, pl.ds(at, ROWS), :]) for p in range(PAIRS)]
            dprobs = [dot_nt(gs[p], qkv_ref[2 * PAIRS + p, pl.ds(at, ROWS), :]) for p in range(PAIRS)]
            for p in range(PAIRS):
                grads = []
                for i in range(2):
                    h = 2 * p + i
                    rows = slice(i * ROWS, (i + 1) * ROWS)
                    probs = jnp.exp(extra(h, raws[p][rows]) - lse_scr[p, rows, :1])
                    ds = (probs * (dprobs[p][rows] - delta_scr[p, rows, :1])).astype(BF16)
                    if near is None:
                        far_scr[h] += jnp.sum(ds.astype(F32).reshape(ROWS // 8, 8, ROWS), axis=0)
                    else:
                        ds_scr[near, h] += ds.astype(F32)
                    grads.append(ds)
                dq_scr[p] += dot_nn(jnp.concatenate(grads, axis=0), qkv_ref[PAIRS + p, pl.ds(at, ROWS), :])

        @pl.when(plain)
        def _():
            gradients(lambda h, raw: raw + tiles[0, 0, h, :1, :1].astype(F32), None)

        @pl.when(jnp.logical_not(plain))
        def _():
            k_row = at + iota((1, ROWS), 1)
            masked = jnp.where((q_seg == seg_of(k_row, ends)) & (k_row <= q_row), 0.0, NEG)
            tile = jnp.maximum(j - chip + 2, 0)
            gradients(lambda h, raw: raw + (tiles[0, tile, h].astype(F32) + masked), tile)

        return 0

    lax.fori_loop(first // ROWS, chip + 1, block, 0)
    dist_ref[...] = jnp.zeros_like(dist_ref)
    lanes = iota((1, 2 * ROWS), 1)
    for p in range(PAIRS):
        dq_ref[:, 128 * p : 128 * p + 128] = join_pair(dq_scr[p]).astype(BF16)

    def fold(h, c):
        folded = jnp.concatenate([ds_scr[1, h], ds_scr[2, h]], axis=1)
        rows = ROWS
        while rows > 1:
            rows //= 2
            folded = folded[:rows] + pltpu.roll(folded[rows:], 2 * ROWS - rows, 1)
        far = jnp.sum(ds_scr[0, h], axis=0, keepdims=True) + jnp.sum(far_scr[h], axis=0, keepdims=True)
        far = jnp.sum(far, axis=1, keepdims=True)
        dist_ref[pl.ds(h, 1), :] = folded + jnp.where(lanes == 2 * ROWS - 1, far, 0.0)
        return c

    lax.fori_loop(0, LOCAL, fold, 0)


def self_key_stage_kernel(
    n_sides, at_ref, len_ref, tiles, qkv_ref, message_ref, so_ref, dq_ref, w_ref, x_ref, gain_ref, small_ref,
    keep_ref, send_ref, *refs,
):
    *outs, go_ref, stat_ref, ks, vs, dk_scr, dv_scr, dqkv_scr, h_scr, e_scr, grads_ref = refs
    chip, core = at_ref[0], at_ref[1]
    starts, ends = spans(len_ref)
    base = pl.multiple_of(chip * ROWS, ROWS)
    last = ends[-1]
    for end in reversed(ends[:-1]):
        last = jnp.where(base + ROWS - 1 < end, end, last)
    stop = (last - 1) // ROWS + 1
    full_to = ends[-1]
    for end in reversed(ends[:-1]):
        full_to = jnp.where(base < end, end, full_to)
    heads = own_rows(core, HALF)
    half = ROWS // 2

    def receive(i, c):
        both = [message_ref[2 * i + e, :half, :] for e in range(2)]
        result = dot_nt(jnp.concatenate(both, axis=0), so_ref[heads, :])
        for p in range(PAIRS):
            go_ref[p, pl.ds(pl.multiple_of(i * ROWS, ROWS), ROWS), :] = result[:, 128 * p : 128 * p + 128].astype(BF16)
        parts = message_ref[2 * i + core, half:, :].astype(F32)
        stat_ref[i] = parts[:, :ROWS] + parts[:, ROWS : 2 * ROWS] + parts[:, 2 * ROWS :]
        return c

    lax.fori_loop(chip, stop, receive, 0)

    def start(p):
        ks[p] = split_pair(qkv_ref[PAIRS + p, pl.ds(base, ROWS), :])
        vs[p] = split_pair(qkv_ref[2 * PAIRS + p, pl.ds(base, ROWS), :])

    each_pair(start)
    dk_scr[...] = jnp.zeros_like(dk_scr)
    dv_scr[...] = jnp.zeros_like(dv_scr)
    k_row = base + iota((ROWS, 1), 0)
    k_seg = seg_of(k_row, ends)

    def block(i, _):
        at = pl.multiple_of(i * ROWS, ROWS)
        plain = (at + ROWS <= full_to) & (i > chip + 1)

        def gradients(extra):
            raws = [dot_nt(ks[p], qkv_ref[p, pl.ds(at, ROWS), :]) for p in range(PAIRS)]
            dprobs = [dot_nt(vs[p], go_ref[p, pl.ds(at, ROWS), :]) for p in range(PAIRS)]
            for p in range(PAIRS):
                weights, dscores = [], []
                for e in range(2):
                    rows = slice(e * ROWS, (e + 1) * ROWS)
                    h = 2 * p + e
                    probs = jnp.exp(extra(h, raws[p][rows]) - stat_ref[i, h : h + 1, :])
                    weights.append(probs.astype(BF16))
                    dscores.append((probs * (dprobs[p][rows] - stat_ref[i, 8 + h : 9 + h, :])).astype(BF16))
                dv_scr[p] += dot_nn(jnp.concatenate(weights, axis=0), go_ref[p, pl.ds(at, ROWS), :])
                dk_scr[p] += dot_nn(jnp.concatenate(dscores, axis=0), qkv_ref[p, pl.ds(at, ROWS), :])

        @pl.when(plain)
        def _():
            gradients(lambda h, raw: raw + tiles[1, 0, h, :1, :1].astype(F32))

        @pl.when(jnp.logical_not(plain))
        def _():
            q_row = at + iota((1, ROWS), 1)
            masked = jnp.where((k_seg == seg_of(q_row, ends)) & (k_row <= q_row), 0.0, NEG)
            tile = jnp.maximum(2 - (i - chip), 0)
            gradients(lambda h, raw: raw + (tiles[1, tile, h].astype(F32) + masked))

        return 0

    lax.fori_loop(chip, stop, block, 0)
    dqkv_scr[:, :HALF] = dq_ref[...]
    for p in range(PAIRS):
        dqkv_scr[:, HALF + 128 * p : HALF + 128 * p + 128] = join_pair(dk_scr[p]).astype(BF16)
        dqkv_scr[:, 2 * HALF + 128 * p : 2 * HALF + 128 * p + 128] = join_pair(dv_scr[p]).astype(BF16)
    e_scr[...] = dot_nt(dqkv_scr[...], w_ref[...])
    keep_ref[...] = e_scr[own_rows(core, half), :]
    send_ref[...] = e_scr[own_rows(1 - core, half), :]
    wide = x_ref[...].astype(F32)
    scaled = wide * rms_inverse(wide)
    h_scr[...] = (scaled * gain_ref[...]).astype(BF16)
    dgain = jnp.sum(e_scr[...] * scaled, axis=0, keepdims=True)
    dgain = jnp.transpose(jnp.where(iota((128, dgain.shape[1]), 0) == 0, dgain, 0.0))
    columns = grads_ref.shape[1]
    grads_ref[:, columns - 128 :] = (small_ref[...] + dgain).astype(BF16)
    step = 256
    for i in range(0, h_scr.shape[1], step):
        grads_ref[i : i + step, : 2 * HALF] = dot_tn(h_scr[:, i : i + step], dqkv_scr[:, HALF:]).astype(BF16)
    give(n_sides, at_ref[2], grads_ref, outs)


def cross_grad_stage_kernel(
    at_ref, len_ref, enc_ref, deal_ref, place_ref,
    e_ref, other_ref, late_ref, gain_ref, cot_ref, co_ref, q_ref, o_ref, lse_ref, kv_ref, wc_ref,
    grad_ref, low_ref, dgain_ref, dq_ref, keep_ref, send_ref, part_ref,
    go_ref, qs, gs, lse_scr, delta_scr, dq_scr, block_scr,
):
    chip, core = at_ref[0], at_ref[1]
    dvalue, dgain = norm_grad(late_ref[...], gain_ref[...], e_ref[...] + other_ref[...])
    dgain_ref[...] = dgain
    grad = cot_ref[...].astype(F32) + dvalue
    grad_ref[...] = grad
    low_ref[...] = grad.astype(BF16)
    go_ref[...] = dot_nt(low_ref[...], co_ref[own_rows(core, HALF), :]).astype(BF16)
    wanted, _, mask = cross_flags(chip, len_ref, enc_ref, deal_ref)
    row_stats(go_ref, o_ref, lse_ref, gs, lse_scr, delta_scr, SUB)
    for p in range(PAIRS):
        qs[p] = split_pair(q_ref[:, lanes_of(p)], SUB)
    dq_scr[...] = jnp.zeros_like(dq_scr)
    half = keep_ref.shape[0] // ROWS

    def gradients(j, rows, masked):
        at = pl.multiple_of(j * KEYS, KEYS)
        raws = [dot_nt(qs[p, rows], kv_ref[p, pl.ds(at, KEYS), :]) for p in range(PAIRS)]
        dprobs = [dot_nt(gs[p, rows], kv_ref[PAIRS + p, pl.ds(at, KEYS), :]) for p in range(PAIRS)]
        for p in range(PAIRS):
            probs = jnp.exp(raws[p] + masked - lse_scr[p, rows, :1])
            ds = (probs * (dprobs[p] - delta_scr[p, rows, :1])).astype(BF16)
            dq_scr[p, rows] += dot_nn(ds, kv_ref[p, pl.ds(at, KEYS), :])
            block_scr[:, lanes_of(p)] += dot_tn(ds, qs[p, rows])
            block_scr[:, lanes_of(PAIRS + p)] += dot_tn(probs.astype(BF16), gs[p, rows])

    def block(j, c):
        at = pl.multiple_of(j * KEYS, KEYS)
        hit = wanted(at, 0, ROWS)

        @pl.when(hit)
        def _():
            block_scr[...] = jnp.zeros_like(block_scr)
            for r in range(ROWS // SUB):

                @pl.when(wanted(at, r * SUB, SUB))
                def _():
                    masked = mask(j, r)
                    gradients(j, stacked(r), jnp.concatenate([masked, masked], axis=0))

        for i in range(KEYS // ROWS):
            place = place_ref[j * (KEYS // ROWS) + i]
            upper = (place >= half).astype(jnp.int32)
            to = pl.ds(pl.multiple_of((place - upper * half) * ROWS, ROWS), ROWS)
            for mine, target in ((True, keep_ref), (False, send_ref)):
                here = (upper == at_ref[3]) == mine

                @pl.when(here & hit)
                def _():
                    target[to, :] = block_scr[i * ROWS : (i + 1) * ROWS, :].astype(BF16)

                @pl.when(here & jnp.logical_not(hit))
                def _():
                    target[to, :] = jnp.zeros((ROWS, 2 * HALF), BF16)

        return c

    lax.fori_loop(0, kv_ref.shape[1] // KEYS, block, 0)
    for p in range(PAIRS):
        dq_ref[:, 128 * p : 128 * p + 128] = join_pair(dq_scr[p], SUB).astype(BF16)
    part_ref[...] = dot_nt(dq_ref[...], wc_ref[:, :HALF])


def self_grad_start_kernel(
    at_ref, e_ref, other_ref, mid_ref, gain_ref, late_grad_ref, so_ref, o_ref, lse_ref,
    grad_ref, low_ref, dgain_ref, go_ref, message_ref,
    stat_scr,
):
    core = at_ref[1]
    dvalue, dgain = norm_grad(mid_ref[...], gain_ref[...], e_ref[...] + other_ref[...])
    dgain_ref[...] = dgain
    grad = late_grad_ref[...] + dvalue
    grad_ref[...] = grad
    low_ref[...] = grad.astype(BF16)
    go_ref[...] = dot_nt(low_ref[...], so_ref[own_rows(core, HALF), :]).astype(BF16)
    half = ROWS // 2
    message_ref[:half, :] = low_ref[own_rows(core, half), :]
    lane = iota((ROWS, 128), 1)
    stat_scr[...] = lse_ref[...]

    def pair(p):
        product = go_ref[:, lanes_of(p)].astype(F32) * o_ref[:, lanes_of(p)]
        for i in range(2):
            part = jnp.where((lane < HEAD_DIM) if i == 0 else (lane >= HEAD_DIM), product, 0.0)
            stat_scr[...] = jnp.where(lane == 8 + 2 * p + i, jnp.sum(part, axis=1, keepdims=True), stat_scr[...])

    each_pair(pair)
    rest = jnp.transpose(stat_scr[...])[:16]
    for part in range(3):
        high = rest.astype(BF16)
        message_ref[half:, part * ROWS : (part + 1) * ROWS] = high
        rest = rest - high.astype(F32)


def projection_grads_kernel(
    n_sides, at_ref, low2_ref, other2_ref, b2_ref, in_ref, dq2_ref, low1_ref, other1_ref, b1_ref, x_ref, gain_ref, dq1_ref, *outs
):
    *outs, out_ref = outs
    core, side = at_ref[1], at_ref[2]
    lanes = pl.ds(pl.multiple_of(core * HALF, 128), HALF)
    for at, own, other, grad in ((0, low2_ref, other2_ref, b2_ref), (2 * HALF, low1_ref, other1_ref, b1_ref)):
        grads = grad[:, lanes]
        for which, part in ((core, own), (1 - core, other)):
            out_ref[own_rows(which, HALF), at : at + HALF] = dot_tn(part[...], grads).astype(BF16)
    out_ref[:, HALF : 2 * HALF] = dot_tn(in_ref[...], dq2_ref[...]).astype(BF16)
    wide = x_ref[...].astype(F32)
    normed = (wide * rms_inverse(wide) * gain_ref[...]).astype(BF16)
    out_ref[:, 3 * HALF :] = dot_tn(normed, dq1_ref[...]).astype(BF16)
    give(n_sides, side, out_ref, outs)


def give(n_sides, side, value, outs):
    if n_sides == 2:
        rows = value.shape[0] // 2
        outs[0][...] = value[own_rows(side, rows), :]
        outs[1][...] = value[own_rows(1 - side, rows), :]
    else:
        outs[0][...] = value[...]


def encoder_grads_kernel(n_sides, at_ref, dkv_ref, e_ref, wc_ref, keep_ref, send_ref, *outs):
    *outs, low_scr, e_scr, grads_ref = outs
    core = at_ref[1]
    half = ROWS // 2
    low_scr[...] = dkv_ref[...].astype(BF16)
    e_scr[...] = dot_nt(low_scr[...], wc_ref[:, HALF:])
    keep_ref[...] = e_scr[own_rows(core, half), :]
    send_ref[...] = e_scr[own_rows(1 - core, half), :]
    grads_ref[...] = dot_tn(e_ref[...], low_scr[...]).astype(BF16)
    give(n_sides, at_ref[2], grads_ref, outs)


def token_grads_kernel(at_ref, e_ref, other_ref, x_ref, gain_ref, grad_ref, out_ref):
    dvalue, _ = norm_grad(x_ref[...].astype(F32), gain_ref[...], e_ref[...] + other_ref[...])
    out_ref[...] = grad_ref[own_rows(at_ref[1], out_ref.shape[0]), :] + dvalue


def finish_late_kernel(count, at_ref, place_ref, own_ref, other_ref, *refs):
    *outs, one, two, three, table, small = refs
    core, place = at_ref[1], place_ref[0]
    rows = own_ref.shape[0] // count
    columns = slice(len(outs) * HALF, len(outs) * HALF + 128)
    for i in range(count):
        part = slice(i * rows, (i + 1) * rows)
        to = pl.ds(pl.multiple_of((place ^ i) * rows, rows), rows)
        for j, out in enumerate(outs):
            lanes = slice(j * HALF, (j + 1) * HALF)
            out[to, own_lanes(core)] = own_ref[part, lanes].astype(F32)
            out[to, own_lanes(1 - core)] = other_ref[part, lanes].astype(F32)
        small[to, :] = own_ref[part, columns].astype(F32) + other_ref[part, columns].astype(F32)
    turned = jnp.transpose(small[...])
    for i, out in enumerate((one, two, three)):
        out[...] = turned[i]
    table[...] = small[: table.shape[0], 3 : 3 + HEADS]


def own_lanes(core):
    return pl.ds(pl.multiple_of(core * HALF, 128), HALF)


def finish_kernel(order, parts_ref, outer_ref, inner_ref, *outs):
    rows = parts_ref.shape[1]
    width = outer_ref.shape[1]
    side = inner_ref.shape[0]
    unit = inner_ref.shape[1] // 4
    for i, (core, place) in enumerate(order):
        at = place * rows
        for half in range(2):
            top = (2 * core + half) * side + at
            outer_ref[top : top + rows, :] = parts_ref[i, :, half * width : (half + 1) * width].astype(F32)
            lanes = slice((2 * half + core) * unit, (2 * half + core + 1) * unit)
            inner_ref[at : at + rows, lanes] = parts_ref[i, :, 2 * width + half * unit : 2 * width + (half + 1) * unit].astype(F32)
    finish_columns_kernel(order, 4 * width, parts_ref, *outs)


def finish_columns_kernel(order, skip, parts_ref, *outs):
    rows = parts_ref.shape[1]
    for i, (core, place) in enumerate(order):
        at = slice(place * rows, (place + 1) * rows)
        for j, out in enumerate(outs):
            columns = slice(skip + j * HALF, skip + (j + 1) * HALF)
            out[at, core * HALF : (core + 1) * HALF] = parts_ref[i, :, columns].astype(F32)


def pack_kernel(groups, core_ref, *refs):
    count = sum(groups)
    ins, outs = list(refs[:count]), refs[count:]
    for size, out in zip(groups, outs):
        at = 0
        for _ in range(size):
            part = ins.pop(0)
            out[:, at : at + part.shape[1]] = part[...].astype(BF16)
            at += part.shape[1]


SMEM = pl.BlockSpec(memory_space=pltpu.SMEM)
VMEM = pl.BlockSpec(memory_space=pltpu.VMEM)


def call(kernel, scalars, arrays, outs, scratch, flops):
    moved = sum(a.size * a.dtype.itemsize for a in arrays) + sum(math.prod(s) * jnp.dtype(d).itemsize for s, d in outs)
    return pl.pallas_call(
        kernel,
        out_shape=[jax.ShapeDtypeStruct(s, d) for s, d in outs],
        in_specs=[SMEM] * len(scalars) + [VMEM] * len(arrays),
        out_specs=[VMEM] * len(outs),
        scratch_shapes=[pltpu.VMEM(s, d) for s, d in scratch],
        compiler_params=pltpu.CompilerParams(vmem_limit_bytes=VMEM_LIMIT),
        cost_estimate=pl.CostEstimate(flops=1, transcendentals=0, bytes_accessed=1),
    )(*scalars, *arrays)


TILES = ((3, LOCAL, ROWS, ROWS), F32)
FAR = ((LOCAL, 8, ROWS), F32)
STACK = ((PAIRS, 2 * ROWS, 128), BF16)
COLUMN = ((PAIRS, 2 * ROWS, 128), F32)
LANE = ((ROWS, 128), F32)


def pack(core, groups):
    flat = [item for group in groups for item in group]
    return pl.pallas_call(
        functools.partial(pack_kernel, [len(g) for g in groups]),
        grid_spec=pltpu.PrefetchScalarGridSpec(
            num_scalar_prefetch=1,
            grid=(1,),
            in_specs=[
                pl.BlockSpec(shape, functools.partial(lambda index, i, c: index(c[0]), index)) for _, shape, index in flat
            ],
            out_specs=[
                pl.BlockSpec((g[0][1][0], sum(s[1] for _, s, _ in g)), lambda i, c: (0, 0)) for g in groups
            ],
        ),
        out_shape=[jax.ShapeDtypeStruct((g[0][1][0], sum(s[1] for _, s, _ in g)), BF16) for g in groups],
        compiler_params=pltpu.CompilerParams(vmem_limit_bytes=VMEM_LIMIT),
    )(core, *(w for w, _, _ in flat))


def swap_core(value):
    return lax.ppermute(value, "core", [(0, 1), (1, 0)])


def gather_fsdp(own):
    count = lax.axis_size("fsdp")
    if count != 2:
        return [lax.all_gather(own, "fsdp", axis=0, tiled=True)]
    return [own, lax.ppermute(own, "fsdp", [(0, 1), (1, 0)])]


CHIPS = ("z", "y")
GROUP = ("z", "y", "core")


def gather_rows(own):
    return lax.all_gather(own, GROUP, axis=0, tiled=True)


def bits_of(axis):
    return range((lax.axis_size(axis) - 1).bit_length())


def swap_bit(value, axis, bit):
    return lax.ppermute(value, axis, [(i, i ^ (1 << bit)) for i in range(lax.axis_size(axis))])


def parted(terms, axis, bit):
    side = (lax.axis_index(axis) >> bit) & 1
    rows = terms[0].shape[0] // 2

    def half(which):
        return [lax.dynamic_slice_in_dim(t, which * rows, rows, 0) for t in terms]

    return half(side), total(half(1 - side)).astype(BF16)


def halve(terms, axis, bit):
    keep, send = parted(terms, axis, bit)
    return keep + [swap_bit(send, axis, bit)]


def total(terms):
    return sum(t.astype(F32) for t in terms[1:]) + terms[0].astype(F32)


def steps_of(*axes):
    return [(axis, bit) for axis in axes for bit in bits_of(axis)]


def scatter(terms, steps):
    for axis, bit in steps:
        terms = halve(terms, axis, bit)
    return terms


def scatter_fsdp(terms):
    return scatter(terms, [("fsdp", bit) for bit in reversed(bits_of("fsdp"))])


def places(steps):
    nz, ny = lax.axis_size("z"), lax.axis_size("y")
    found = []
    for z in range(nz):
        for y in range(ny):
            place = 0
            for axis, bit in steps:
                place = 2 * place + (((z if axis == "z" else y) >> bit) & 1)
            found.append(place)
    return found


def after(value, *earlier):
    return lax.optimization_barrier((value, *earlier))[0]


def on_device(
    tokens, encoded, cotangent, tgt_lengths, enc_lengths, deal,
    ln_self, ln_cross, ln_ffn, bias_table,
    self_query, self_key, self_value, self_output,
    cross_query, cross_key, cross_value, cross_output,
    ffn_inner, ffn_outer,
):
    core = lax.axis_index("core")
    fsdp = lax.axis_index("fsdp")
    n_fsdp = lax.axis_size("fsdp")
    chip = lax.axis_index(CHIPS)
    steps = steps_of("y", "z")
    y_side = (lax.axis_index("y") >> steps[0][1]) & 1
    at = jnp.stack([chip, core, fsdp, y_side]).astype(jnp.int32)
    core_ref = core.reshape(1).astype(jnp.int32)
    rows, width = tokens.shape
    n = 2 * rows * lax.axis_size(CHIPS)
    side = width // n_fsdp
    hidden_half = ffn_inner.shape[1] // 2
    unit = hidden_half // n_fsdp
    wide, flat = ((ROWS, width), F32), ((ROWS, width), BF16)

    def column(weight):
        return (weight, (side, HALF), lambda c: (0, c))

    (qkv_own,) = pack(core_ref, [[column(w) for w in (self_query, self_key, self_value)]])
    w_qkv = gather_fsdp(qkv_own)
    if unit % 128 == 0:
        inner_items = [(ffn_inner, (side, unit), functools.partial(lambda o, c: (0, 2 * o + c), o)) for o in range(n_fsdp)]
    else:
        inner_units = ffn_inner.reshape(side, n_fsdp, 2, unit)
        inner_units = lax.dynamic_index_in_dim(inner_units, core, 2, keepdims=False).reshape(side, hidden_half)
        inner_items = [(inner_units, (side, hidden_half), lambda c: (0, 0))]
    out_own, cross_own, inner_own, outer_own = pack(
        core_ref,
        [
            [column(w) for w in (self_output, cross_output)],
            [column(w) for w in (cross_query, cross_key, cross_value)],
            inner_items,
            [(ffn_outer, (unit, width), lambda c: (c, 0))],
        ],
    )
    w_out = gather_fsdp(out_own)
    w_cross = gather_fsdp(cross_own)
    inner_own, outer_own = after((inner_own, outer_own), w_cross[-1])
    w_inner, w_outer = gather_fsdp(inner_own), gather_fsdp(outer_own)
    w_out_mate = [swap_core(w) for w in w_out]
    cot_mate = swap_core(cotangent)

    small = jnp.concatenate([ln_self, ln_cross, ln_ffn, bias_table.reshape(-1)], axis=0).astype(BF16)[None]
    small = gather_fsdp(small)
    if len(small) == 2:
        small = jnp.where(fsdp == 0, jnp.concatenate(small, axis=0), jnp.concatenate(small[::-1], axis=0))
    else:
        small = small[0]
    gain_self, gain_cross, gain_ffn = (
        small[:, i * side : (i + 1) * side].reshape(1, width).astype(F32) for i in range(3)
    )
    table = small[:, 3 * side :].reshape(BUCKETS, HEADS)
    table = lax.dynamic_slice_in_dim(table, core * LOCAL, LOCAL, 1).astype(F32)
    onehots = np.concatenate([QK_ONEHOT, KQ_ONEHOT], axis=0)
    biases = jnp.einsum("bh,tb->ht", table, onehots, precision=lax.Precision.HIGHEST)
    biases = jnp.pad(biases.reshape(LOCAL, 2, 2 * ROWS).swapaxes(0, 1), ((0, 0), (0, 2), (0, 0)))
    (tiles,) = call(tiles_kernel, (), (biases.reshape(16, 2 * ROWS),), [((2, *TILES[0]), BF16)], [], 1)

    xe = gather_rows(jnp.concatenate([tokens, encoded], axis=1))
    qkv, w_qkv, attn_self, low_self, lse_self = call(
        functools.partial(self_stage_kernel, len(w_qkv)), (at, tgt_lengths), (xe, gain_self, tiles, *w_qkv),
        [((3 * PAIRS, n, 128), BF16), ((width, 3 * HALF), BF16), ((ROWS, HALF), F32), ((ROWS, HALF), BF16), LANE],
        ATTEND(n),
        2 * n * width * 3 * HALF + 4 * ROWS * n * HALF,
    )
    low_self_other = swap_core(low_self)

    x_mid, in_cross, q_cross, kv_cross, attn_cross, low_cross, lse_cross, w_so, w_co, w_cross = call(
        functools.partial(cross_stage_kernel, len(w_out)), (at, tgt_lengths, enc_lengths, deal),
        (xe, gain_cross, low_self, low_self_other, *w_out, *w_out_mate, *w_cross),
        [
            wide, flat, ((ROWS, HALF), BF16), ((2 * PAIRS, n, 128), BF16), ((ROWS, HALF), F32), ((ROWS, HALF), BF16), LANE,
            ((width, width), BF16), ((width, width), BF16), ((width, 3 * HALF), BF16),
        ],
        ATTEND(n),
        2 * n * width * 2 * HALF + 4 * ROWS * n * HALF,
    )
    low_cross_other = swap_core(low_cross)

    half_rows = ((rows, width), F32)
    x_late, in_ffn, hidden, d_pre, cot, out_keep, out_send, e_ffn = call(
        functools.partial(ffn_stage_kernel, len(w_inner)), (at,),
        (x_mid, gain_ffn, low_cross, low_cross_other, w_co, cotangent, cot_mate, *w_inner, *w_outer),
        [wide, flat, ((ROWS, hidden_half), BF16), ((ROWS, hidden_half), BF16), flat, half_rows, half_rows, wide],
        [((width, hidden_half), BF16), ((hidden_half, width), BF16), wide],
        8 * ROWS * width * hidden_half,
    )
    e_ffn_other = swap_core(e_ffn)
    output = out_keep + swap_core(out_send)

    place = places(steps)
    place_ref = jnp.asarray(np.array(place, np.int32))
    nz, ny = lax.axis_size("z"), lax.axis_size("y")
    y_place = [p // nz for p in place[:ny]]
    key_place_ref = jnp.asarray(np.array([y_place[y] * nz + z for z in range(nz) for y in range(ny)], np.int32))
    grad_late, late_low, d_gain_ffn, dq_cross, dkv_keep, dkv_send, e_cross = call(
        cross_grad_stage_kernel, (at, tgt_lengths, enc_lengths, deal, key_place_ref),
        (e_ffn, e_ffn_other, x_late, gain_ffn, cot, w_co, q_cross, attn_cross, lse_cross, kv_cross, w_cross),
        [wide, flat, ((1, width), F32), ((ROWS, HALF), BF16), ((n // 2, 2 * HALF), BF16), ((n // 2, 2 * HALF), BF16), wide],
        [((ROWS, HALF), BF16), STACK, STACK, COLUMN, COLUMN, COLUMN, ((KEYS, 2 * HALF), F32)],
        10 * ROWS * n * HALF,
    )
    e_cross_other = swap_core(e_cross)
    dkv_got = swap_bit(dkv_send, *steps[0])

    grad_mid, mid_low, d_gain_cross, go_self, message = call(
        self_grad_start_kernel, (at,), (e_cross, e_cross_other, x_mid, gain_cross, grad_late, w_so, attn_self, lse_self),
        [wide, flat, ((1, width), F32), ((ROWS, HALF), BF16), ((rows + 16, width), BF16)], [LANE],
        2 * ROWS * width * HALF,
    )
    ffn_out = (
        [((side, 4 * width), BF16), ((side, 4 * width), BF16)]
        if n_fsdp == 2
        else [((hidden_half, width), F32), ((width, hidden_half), F32)]
    )
    first = call(
        functools.partial(ffn_grads_kernel, n_fsdp), (at,), (hidden, cot, in_ffn, after(d_pre, message)), ffn_out, [],
        4 * ROWS * width * hidden_half,
    )
    if n_fsdp == 2:
        first_other = lax.ppermute(first[1], "fsdp", [(0, 1), (1, 0)])
        go_self = after(go_self, first[1])
    message = lax.all_gather(message, GROUP, axis=0)
    x_chip = lax.dynamic_slice(xe, (chip * ROWS, 0), (ROWS, width))
    e_chip = lax.dynamic_slice(xe, (chip * ROWS, width), (ROWS, width))
    dq_self, dist = call(
        self_query_grad_kernel, (at, tgt_lengths), (tiles, qkv, go_self, attn_self, lse_self),
        [((ROWS, HALF), BF16), ((8, 2 * ROWS), F32)],
        [STACK, STACK, COLUMN, COLUMN, COLUMN, TILES, FAR],
        6 * ROWS * n * HALF,
    )
    def given(columns):
        return [((width // 2, columns), BF16)] * 2 if n_fsdp == 2 else [((width, columns), BF16)]

    def over_fsdp(parts):
        if n_fsdp == 2:
            return [parts[0], lax.ppermute(parts[1], "fsdp", [(0, 1), (1, 0)])]
        return scatter_fsdp(parts)

    second = call(
        functools.partial(projection_grads_kernel, n_fsdp), (at,),
        (low_cross, low_cross_other, late_low, in_cross, dq_cross, low_self, low_self_other, mid_low, x_chip, gain_self, dq_self),
        given(4 * HALF), [((width, 4 * HALF), BF16)], 8 * ROWS * width * HALF,
    )
    d_table = jnp.einsum("ht,tb->bh", dist[:LOCAL], QK_ONEHOT, precision=lax.Precision.HIGHEST)
    d_table = jnp.zeros((BUCKETS, 2, LOCAL), F32).at[:, core].set(d_table).reshape(n_fsdp, -1, HEADS)
    d_table = jnp.pad(d_table, ((0, 0), (0, side - d_table.shape[1]), (0, 0))).reshape(width, HEADS)
    none = jnp.zeros((width, 1), F32)
    small = [none, 0.5 * d_gain_cross.reshape(width, 1), 0.5 * d_gain_ffn.reshape(width, 1), d_table]
    small = jnp.pad(jnp.concatenate(small, axis=1), ((0, 0), (0, 128 - 3 - HEADS)))

    if n_fsdp == 2:
        first = [first[0], first_other]
    else:
        outer = first[0].reshape(n_fsdp, 2, side, width)
        first = jnp.concatenate([outer[:, 0], outer[:, 1], first[1].reshape(n_fsdp, side, hidden_half)], axis=2)
        first = scatter_fsdp([first.reshape(width, -1)])
    *y_steps, z_near, z_far = steps
    dkv_cross = scatter(after([dkv_keep, dkv_got], second[-1]), y_steps[1:])
    dkv_cross = total(dkv_cross).astype(BF16)
    first = after(first, dkv_cross)
    second = over_fsdp(after(second, first[-1]))
    first_keep, first_sent = parted(first, *y_steps[0])
    first_got = swap_bit(first_sent, *y_steps[0])
    dkv_cross = lax.psum_scatter(dkv_cross, "z", scatter_dimension=0, tiled=True)

    e_keep, e_send, *fourth = call(
        functools.partial(self_key_stage_kernel, n_fsdp), (at, tgt_lengths),
        (tiles, qkv, after(message, first_sent), w_so, dq_self, w_qkv, x_chip, gain_self, small),
        [half_rows, half_rows, *given(2 * HALF + 128)],
        [
            ((PAIRS, n, 128), BF16), ((n // ROWS, 16, ROWS), F32), STACK, STACK, COLUMN, COLUMN,
            ((ROWS, 3 * HALF), BF16), flat, wide, ((width, 2 * HALF + 128), BF16),
        ],
        8 * ROWS * n * HALF,
    )
    fourth_sent = fourth[-1]
    fourth = over_fsdp(fourth)
    first = scatter(first_keep + [after(first_got, fourth_sent)], y_steps[1:])
    first_keep, first_sent = parted(first, *z_near)
    first_got = swap_bit(first_sent, *z_near)
    second_keep, second_sent = parted(after(second, first_sent), *y_steps[0])
    second_got = swap_bit(second_sent, *y_steps[0])
    enc_keep, enc_send, *third = call(
        functools.partial(encoder_grads_kernel, n_fsdp), (at,), (after(dkv_cross, second_sent), e_chip, w_cross),
        [half_rows, half_rows, *given(2 * HALF)],
        [((ROWS, 2 * HALF), BF16), wide, ((width, 2 * HALF), BF16)], 8 * ROWS * width * HALF,
    )
    third_sent = third[-1]
    third = over_fsdp(third)
    fourth_keep, fourth_sent = parted(after(fourth, third_sent), *y_steps[0])
    fourth_got = swap_bit(fourth_sent, *y_steps[0])
    first_keep, first_sent = parted(first_keep + [after(first_got, fourth_sent)], *z_far)
    first_got = swap_bit(first_sent, *z_far)

    second_got, fourth_got = after((second_got, fourth_got), first_sent)
    second = total(scatter(second_keep + [second_got], y_steps[1:]))
    fourth = total(scatter(fourth_keep + [fourth_got], y_steps[1:]))
    second = jnp.concatenate([second, fourth], axis=1).astype(BF16)
    second_keep, second_sent = parted([second], *z_near)
    second_got = swap_bit(second_sent, *z_near)
    (grad_tokens,) = call(
        token_grads_kernel, (at,), (e_keep, swap_core(after(e_send, second_sent)), tokens, gain_self, grad_mid),
        [half_rows], [], 10 * rows * width,
    )
    enc_grad = enc_keep + swap_core(after(enc_send, second_sent))
    second_got = after(second_got, grad_tokens, enc_grad)
    late_keep, late_sent = parted(after(third, second_sent), *y_steps[0])
    late_got = swap_bit(late_sent, *y_steps[0])
    first = total(first_keep + [after(first_got, late_sent)]).astype(BF16)
    second_keep, second_sent = parted(second_keep + [after(second_got, first)], *z_far)
    second_got = swap_bit(second_sent, *z_far)
    late = scatter(late_keep + [after(late_got, second_sent)], y_steps[1:])
    late_keep, late_sent = parted(late, *z_near)
    late_got = swap_bit(late_sent, *z_near)
    second = total(second_keep + [after(second_got, late_sent)]).astype(BF16)
    early = lax.all_gather(jnp.concatenate([first, second[:, : 4 * HALF]], axis=1), GROUP, axis=0)
    late = total(halve(late_keep + [after(late_got, second)], *z_far)).astype(BF16)
    late = jnp.concatenate([late, second[:, 4 * HALF :]], axis=1)
    for axis, bit in reversed(steps):
        late = jnp.concatenate([late, swap_bit(late, axis, bit)], axis=0)
    late_other = swap_core(late)
    early = after(early, late_other)

    matrix = ((side, width), F32)
    own_place = place_ref[chip].reshape(1)
    if side // len(place) % 8 == 0:
        g_ck, g_cv, g_sk, g_sv, *gains, g_table = call(
            functools.partial(finish_late_kernel, len(place)), (at, own_place), (late, late_other),
            [matrix] * 4 + [((side,), F32)] * 3 + [(bias_table.shape, F32)], [((side, 128), F32)], 8 * side * width,
        )
    else:
        blocks = jnp.stack([late, late_other]).reshape(2, len(place), side // len(place), -1)
        blocks = jnp.take(blocks, own_place[0] ^ jnp.arange(len(place), dtype=jnp.int32), axis=1)
        blocks = jnp.where(core == 0, blocks, blocks[::-1]).astype(F32).reshape(2, side, -1)
        g_ck, g_cv, g_sk, g_sv = (
            jnp.swapaxes(blocks[:, :, i : i + HALF], 0, 1).reshape(side, width) for i in range(0, 4 * HALF, HALF)
        )
        small = jnp.sum(blocks[:, :, 4 * HALF :], axis=0)
        gains = [small[:, i] for i in range(3)]
        g_table = small[: bias_table.shape[0], 3 : 3 + HEADS]
    order = [(c, p) for p in place for c in range(2)]
    if n_fsdp == 2:
        g_outer, g_inner, g_co, g_cq, g_so, g_sq = call(
            functools.partial(finish_kernel, order), (), (early,),
            [(ffn_outer.shape, F32), (ffn_inner.shape, F32), *[matrix] * 4], [], 8 * side * width,
        )
    else:
        sources = np.argsort([2 * p + c for c, p in order])
        pair = jnp.swapaxes(early[sources].reshape(len(place), 2, -1, early.shape[2]), 0, 1)
        pair = pair.reshape(2, side, -1).astype(F32)
        g_outer = pair[:, :, : 2 * width].reshape(2, side, 2, width)
        g_outer = jnp.swapaxes(g_outer, 1, 2).reshape(ffn_outer.shape)
        g_inner = jnp.transpose(pair[:, :, 2 * width : 4 * width].reshape(2, side, n_fsdp, unit), (1, 2, 0, 3))
        g_inner = g_inner.reshape(ffn_inner.shape)
        g_co, g_cq, g_so, g_sq = call(
            functools.partial(finish_columns_kernel, order, 4 * width), (), (early,), [matrix] * 4, [], 8 * side * width
        )

    return (
        output, grad_tokens, enc_grad,
        *gains, g_table,
        g_sq, g_sk, g_sv, g_so, g_cq, g_ck, g_cv, g_co, g_inner, g_outer,
    )


def solution(mesh):
    n_ctx, n_fsdp = mesh.shape["ctx"], mesh.shape["fsdp"]
    n_z = 4
    grid = Mesh(mesh.devices.reshape(n_z, n_ctx // (2 * n_z), 2, n_fsdp), ("z", "y", "core", "fsdp"))
    by_rows = P(("fsdp", "z", "y", "core"), None)
    split = P("fsdp", None)
    vector = P("fsdp")
    in_specs = (by_rows,) * 3 + (split,) * 3 + (vector,) * 3 + (split,) * 11
    out_specs = (by_rows,) * 3 + (vector,) * 3 + (split,) * 11
    return jax.shard_map(on_device, mesh=grid, in_specs=in_specs, out_specs=out_specs, check_vma=False)
```
